32 devices in a mesh: outer: 8 (over z, x), inner: 4 (over y, core).
Axes of the slice: x: 2, y: 2, z: 4, core: 2. Of those that a mesh axis runs over, the one named last changes fastest.
Arguments:
- inputs: bfloat16 [16384, 512], P(('outer', 'inner')), may hold values from -6 to 6
- weights: bfloat16 [3151872], replicated
- cotangent: bfloat16 [16384, 512], P(('outer', 'inner')), may hold values from -6 to 6
- clip_lengths: int32 [11], replicated, may hold values from 1 to 1500, 16384 in all
- first_moment: float32 [3151872], P('inner')
- second_moment: float32 [3151872], P('inner')
Outputs:
- layer_output: bfloat16 [16384, 512], P(('outer', 'inner'))
- input_grad: bfloat16 [16384, 512], P(('outer', 'inner'))
- weight_grads: float32 [3151872], P('inner')
- grad_norm: float32 [], replicated
- moment_one: float32 [3151872], P('inner')
- moment_two: float32 [3151872], P('inner')
- weight_step: bfloat16 [3151872], replicated
The draws below stay inside these ranges and needn't reach their ends.
Inputs may be any that keep to these rules, and one draw needn't show every extreme that they name: `clip_lengths`: the lengths add up to 16384; clip c occupies the slots from the sum of the lengths before it on, in order.
All inputs are finite; a program needn't handle non-finite values.
Results may differ from the reference program's by a relative error of at most 0.015.
Values may be sent and summed in bfloat16 or wider, within the bound.
No kernel may reach another device: no remote copies, remote signals or barrier semaphores. Data moves between devices by JAX's collectives and lax.ppermute only.
A program may use at most 192 MiB of HBM per device.

```python
import math
import jax
import jax.numpy as jnp
import numpy as np
from jax import lax

D = 512
HEADS = 8
FF = 2048
TOK_DEV = 512
MOST = 1500
SLOTS = 16384
CLIPS = 11
PARAMS = 3151872


def draw_weights(key, part):

    def normal_section(number, layout, spread):
        return spread * jax.random.normal(jax.random.fold_in(key, number), layout, jnp.float32)

    def gain_section(number, layout):
        return jax.random.uniform(jax.random.fold_in(key, number), layout, jnp.float32, 0.6, 1.4)
    inverse_root = 1.0 / math.sqrt(D)
    sections = [gain_section(1, (D,)), normal_section(2, (D,), 0.2), normal_section(3, (D, D), inverse_root), normal_section(4, (D,), 0.2), normal_section(5, (D, D), inverse_root), normal_section(6, (D, D), inverse_root), normal_section(7, (D,), 0.2), normal_section(8, (D, D), 4.0 * inverse_root), normal_section(9, (D,), 0.2), gain_section(10, (D,)), normal_section(11, (D,), 0.2), normal_section(12, (D, FF), inverse_root), normal_section(13, (FF,), 0.2), normal_section(14, (FF, D), 1.0 / math.sqrt(FF)), normal_section(15, (D,), 0.2)]
    return jnp.concatenate([section.reshape(-1) for section in sections]).astype(jnp.bfloat16)


def draw_first_moment(key, part):
    spread = 0.2 / math.sqrt(PARAMS)
    values = jax.random.normal(jax.random.fold_in(key, 31), (PARAMS,), jnp.float32)
    return spread * jnp.clip(values, -6.0, 6.0)


def draw_second_moment(key, part):
    lower = math.log(0.0003 / PARAMS)
    upper = math.log(0.03 / PARAMS)
    exponent = jax.random.uniform(jax.random.fold_in(key, 37), (PARAMS,), jnp.float32, lower, upper)
    return jnp.exp(exponent)


def levels(own_key, shape, split, smallest, top_value):
    def one(axis_at, blocks):
        draws = jax.random.uniform(jax.random.fold_in(jax.random.fold_in(own_key, 6), axis_at), (blocks,), jnp.float32, smallest / len(split), top_value / len(split))
        return jnp.repeat(jnp.exp(draws), shape[axis_at] // blocks).reshape((-1,) + (1,) * (len(shape) - axis_at - 1))

    loudness = one(*split[0])
    for cut in split[1:]:
        loudness = loudness * one(*cut)
    return loudness


def profile(amount, total, limit, slope):
    portions = [(1 << 20) // math.isqrt(grade ** slope) + 1 for grade in range(2, amount + 1)]
    rest, holding = total - limit - (amount - 1), [1] * (amount - 1)
    while rest > 0:
        movable = [i for i in range(amount - 1) if holding[i] < limit]
        pool, left = sum([portions[i] for i in movable]), rest
        for i in movable:
            addition = min(limit - holding[i], max(1, left * portions[i] // pool), rest)
            holding[i] = holding[i] + addition
            rest = rest - addition
    return np.array([limit] + holding)


def ragged(rng, count, total, limit, slope):
    if count == 2:
        one = jax.random.randint(rng, (), max(1, total - limit), min(limit, total - 1) + 1)
        return jnp.stack([one, total - one])
    sizes = jnp.asarray(profile(count, total, limit, slope), jnp.int32)
    couples = (count - 1) // 2
    source_of, receiver = sizes[1:1 + 2 * couples:2], sizes[2:2 + 2 * couples:2]
    slack = jnp.minimum(source_of - 1, limit - receiver)
    passed = jax.random.randint(jax.random.fold_in(rng, 1), (couples,), 0, 1 << 20) % (slack + 1)
    sizes = sizes.at[1:1 + 2 * couples:2].set(source_of - passed).at[2:2 + 2 * couples:2].set(receiver + passed)
    return sizes[jax.random.permutation(jax.random.fold_in(rng, 2), count)]


def centred(stream_key, dims, scale, most, split=(), held_as=jnp.bfloat16):
    values = jax.random.normal(stream_key, dims, jnp.float32) * scale
    if len(split) > 0:
        values = levels(stream_key, dims, split, -0.22, 0.18) * values
    return jnp.clip(values, min=-most, max=most).astype(held_as)


def setup_inputs(seed: int = 0) -> dict:
    keys = jax.random.split(jax.random.key(seed), 7)
    inputs = centred(keys[0], (SLOTS, D), 1.0, 6.0, ((0, 32),))
    weights = draw_weights(jax.random.fold_in(keys[6], 71), 0)
    cotangent = centred(keys[2], (SLOTS, D), 1.0, 6.0, ((0, 32),))
    clip_lengths = ragged(keys[3], CLIPS, SLOTS, MOST, 1).astype(jnp.int32)
    first_moment = draw_first_moment(jax.random.fold_in(keys[6], 71), 0)
    second_moment = draw_second_moment(jax.random.fold_in(keys[6], 71), 0)
    return {"inputs": inputs, "weights": weights, "cotangent": cotangent, "clip_lengths": clip_lengths, "first_moment": first_moment, "second_moment": second_moment}


@jax.custom_vjp
def low(v):
    return lax.optimization_barrier(v.astype(jnp.bfloat16)).astype(jnp.float32)

@jax.custom_vjp
def low_back(v):
    return v

def low_keep(v):
    return (low(v), None)

def low_pass(kept, grad):
    return (grad,)

def back_keep(v):
    return (v, None)

def back_low(kept, grad):
    return (low(grad),)
low.defvjp(low_keep, low_pass)
low_back.defvjp(back_keep, back_low)
BETA_ONE = 0.9
BETA_TWO = 0.999
FIX_ONE = 1.0 - (0.9 ** 10) ** 10
FIX_TWO = 1.0 - (0.999 ** 10) ** 10
DECAY = 0.1

def layouts():
    return [(D,), (D,), (D, D), (D,), (D, D), (D, D), (D,), (D, D), (D,), (D,), (D,), (D, FF), (FF,), (FF, D), (D,)]

def unpack(flat):
    sections = []
    offset = 0
    for layout in layouts():
        entries = 1
        for extent in layout:
            entries = entries * extent
        sections.append(flat[offset:offset + entries].reshape(layout))
        offset = offset + entries
    return sections

def matmul(matrix_one, matrix_two):
    return jnp.dot(matrix_one, matrix_two, precision=lax.Precision.HIGHEST, preferred_element_type=jnp.float32)

def standard(values, gain, shift):
    center = lax.optimization_barrier(jnp.mean(values, axis=-1, keepdims=True))
    centered = values - center
    scaled = centered * lax.rsqrt(lax.optimization_barrier(jnp.mean(centered * centered, axis=-1, keepdims=True)) + 1e-05)
    return scaled * gain + shift

def bounds(positions, clip_lengths):
    starts = jnp.cumsum(clip_lengths, dtype=jnp.int32) - clip_lengths
    member = lax.optimization_barrier(jnp.sum((positions[:, None] >= starts[None, :]).astype(jnp.int32), axis=1, dtype=jnp.int32)) - 1
    onehot = (jnp.arange(clip_lengths.shape[0], dtype=jnp.int32)[None, :] == member[:, None]).astype(jnp.int32)
    lower_slot = lax.optimization_barrier(jnp.sum(onehot * starts[None, :], axis=1, dtype=jnp.int32))
    upper_slot = lower_slot + lax.optimization_barrier(jnp.sum(onehot * clip_lengths[None, :], axis=1, dtype=jnp.int32))
    return (lower_slot, upper_slot)

def forward(sections, values, clip_lengths):
    first_gain, first_bias, query_weight, query_bias, key_weight, value_weight, value_bias, out_weight, out_bias, second_gain, second_bias, up_weight, up_bias, down_weight, down_bias = sections
    normed = low(standard(values, first_gain, first_bias))
    query_rows = low(low_back(matmul(normed, query_weight) + query_bias))
    key_rows = low(low_back(matmul(normed, key_weight)))
    value_rows = low(low_back(matmul(normed, value_weight) + value_bias))
    margin = MOST - 1
    key_pad = jnp.pad(key_rows, ((margin, margin), (0, 0)))
    value_pad = jnp.pad(value_rows, ((margin, margin), (0, 0)))
    window = TOK_DEV + 2 * margin
    blocks = values.shape[0] // TOK_DEV
    head_width = D // HEADS
    score_scale = 1.0 / math.sqrt(head_width)

    def attend_block(block_data):
        block_index, query_block, input_block = block_data
        first_slot = block_index * TOK_DEV
        positions = first_slot + jnp.arange(TOK_DEV, dtype=jnp.int32)
        lower_slot, upper_slot = bounds(positions, clip_lengths)
        key_places = first_slot - margin + jnp.arange(window, dtype=jnp.int32)
        allowed = (key_places[None, :] >= lower_slot[:, None]) & (key_places[None, :] < upper_slot[:, None])
        key_window = lax.dynamic_slice_in_dim(key_pad, first_slot, window, 0).reshape(window, HEADS, head_width)
        value_window = lax.dynamic_slice_in_dim(value_pad, first_slot, window, 0).reshape(window, HEADS, head_width)
        query_heads = query_block.reshape(TOK_DEV, HEADS, head_width)
        raw_scores = jnp.einsum('qhd,khd->hqk', query_heads, key_window, precision=lax.Precision.HIGHEST)
        scores = jnp.where(allowed[None], score_scale * low_back(raw_scores), -1e+30)
        row_peak = lax.optimization_barrier(jnp.max(scores, axis=-1, keepdims=True))
        exps = jnp.exp(scores - row_peak)
        soft_weights = exps / lax.optimization_barrier(jnp.sum(exps, axis=-1, keepdims=True))
        mixed = jnp.einsum('hqk,khd->qhd', low(soft_weights), value_window, precision=lax.Precision.HIGHEST)
        mixed = low(low_back(mixed.reshape(TOK_DEV, D)))
        middle = input_block + low_back(matmul(mixed, out_weight) + out_bias)
        hidden_in = low(standard(middle, second_gain, second_bias))
        up_rows = low_back(matmul(hidden_in, up_weight) + up_bias)
        activated = low(jax.nn.gelu(up_rows, approximate=False))
        return middle + matmul(activated, down_weight) + down_bias
    stacked = lax.map(jax.checkpoint(attend_block), (jnp.arange(blocks, dtype=jnp.int32), query_rows.reshape(blocks, TOK_DEV, D), values.reshape(blocks, TOK_DEV, D)))
    return stacked.reshape(values.shape)

def reference(inputs, weights, cotangent, clip_lengths, first_moment, second_moment):
    flat = weights.astype(jnp.float32)
    sections = unpack(flat)

    def run_layer(sections_in, rows_in):
        return forward(sections_in, rows_in, clip_lengths)
    outputs, pullback = jax.vjp(run_layer, sections, inputs.astype(jnp.float32))
    section_grads, input_grad = pullback(cotangent.astype(jnp.float32))
    grads = jnp.concatenate([section.reshape(-1) for section in section_grads])
    grad_norm = jnp.sqrt(jnp.sum(grads * grads))
    clipped = grads / jnp.maximum(grad_norm, 1.0)
    moment_one = BETA_ONE * first_moment + (1.0 - BETA_ONE) * clipped
    moment_two = BETA_TWO * second_moment + (1.0 - BETA_TWO) * clipped * clipped
    update = moment_one / FIX_ONE / (jnp.sqrt(moment_two / FIX_TWO) + 1e-08) + DECAY * flat
    weight_step = update.astype(jnp.bfloat16)
    return (outputs.astype(jnp.bfloat16), input_grad.astype(jnp.bfloat16), grads, grad_norm, moment_one, moment_two, weight_step)
```

```python
import functools
import math

import jax
import jax.numpy as jnp
from jax import lax
from jax.experimental import pallas as pl
from jax.experimental.pallas import tpu as pltpu
from jax.sharding import PartitionSpec as P

D = 512
HEADS = 8
FF = 2048
MOST = 1500


BETA_ONE = 0.9
BETA_TWO = 0.999
FIX_ONE = 1.0 - (0.9**10) ** 10
FIX_TWO = 1.0 - (0.999**10) ** 10
DECAY = 0.1
INV_ROOT_TWO = 1.0 / math.sqrt(2.0)
INV_ROOT_TWO_PI = 1.0 / math.sqrt(2.0 * math.pi)


def layouts():
    return [
        (D,),
        (D,),
        (D, D),
        (D,),
        (D, D),
        (D, D),
        (D,),
        (D, D),
        (D,),
        (D,),
        (D,),
        (D, FF),
        (FF,),
        (FF, D),
        (D,),
    ]


def unpack(flat):
    sections = []
    offset = 0
    for layout in layouts():
        entries = 1
        for extent in layout:
            entries = entries * extent
        section = flat[offset : offset + entries].reshape(layout)
        if len(layout) == 1:
            section = section.astype(jnp.float32)
        sections.append(section)
        offset = offset + entries
    return sections


def plain_dot(matrix_one, matrix_two):
    return jnp.dot(matrix_one, matrix_two, preferred_element_type=jnp.float32)


def rows_dot(matrix_one, matrix_two):
    return lax.dot_general(
        matrix_one, matrix_two, (((0,), (0,)), ((), ())), preferred_element_type=jnp.float32
    )


def back_dot(matrix_one, matrix_two):
    return lax.dot_general(
        matrix_one, matrix_two, (((1,), (1,)), ((), ())), preferred_element_type=jnp.float32
    )


def standard(values):
    center = jnp.mean(values, axis=-1, keepdims=True)
    centered = values - center
    inverse_dev = lax.rsqrt(jnp.mean(centered * centered, axis=-1, keepdims=True) + 1e-05)
    return (centered * inverse_dev, inverse_dev)


def norm_back(grad_normed, normed_hat, inverse_dev, gain):
    scaled = grad_normed * gain
    return inverse_dev * (
        scaled
        - jnp.mean(scaled, axis=-1, keepdims=True)
        - normed_hat * jnp.mean(scaled * normed_hat, axis=-1, keepdims=True)
    )


def bounds(positions, clip_lengths):
    starts = jnp.cumsum(clip_lengths, dtype=jnp.int32) - clip_lengths
    member = (
        jnp.sum((positions[:, None] >= starts[None, :]).astype(jnp.int32), axis=1, dtype=jnp.int32)
        - 1
    )
    onehot = (
        jnp.arange(clip_lengths.shape[0], dtype=jnp.int32)[None, :] == member[:, None]
    ).astype(jnp.int32)
    lower_slot = jnp.sum(onehot * starts[None, :], axis=1, dtype=jnp.int32)
    upper_slot = lower_slot + jnp.sum(onehot * clip_lengths[None, :], axis=1, dtype=jnp.int32)
    return (lower_slot, upper_slot)


LINE = ("outer", "inner")
NEG = -1e30


def shifted(block, distance):
    n = lax.axis_size(LINE)
    return lax.ppermute(block, LINE, [(i + distance, i) for i in range(n) if 0 <= i + distance < n])


def swapped(block, bit):
    n = lax.axis_size(LINE)
    return lax.ppermute(block, LINE, [(i ^ bit, i) for i in range(n)])


def halo(block):
    n = lax.axis_size(LINE)
    partner = swapped(block, 1)
    left = shifted(block, -2)
    right = shifted(block, 2)
    route = [(i + (3 if i % 2 else -3), i) for i in range(n)]
    far = lax.ppermute(block, LINE, [(s, t) for s, t in route if 0 <= s < n])
    return [block, partner, left, right, swapped(left, 1), swapped(right, 1), far]


def slot_table():
    odd = lax.axis_index(LINE) % 2
    even_slots = jnp.array([6, 2, 4, 0, 1, 3, 5], jnp.int32)
    odd_slots = jnp.array([4, 2, 1, 0, 5, 3, 6], jnp.int32)
    return jnp.where(odd == 1, odd_slots, even_slots)


def dot_nt(a, b):
    return lax.dot_general(a, b, (((1,), (1,)), ((), ())), preferred_element_type=jnp.float32)


def head_halves(pair):
    first = lax.broadcasted_iota(jnp.int32, pair.shape, 1) < pair.shape[1] // 2
    zero = jnp.zeros_like(pair)
    return jnp.where(first, pair, zero), jnp.where(first, zero, pair)


def over_lanes(tile, op):
    parts = [tile[:, 128 * j : 128 * (j + 1)] for j in range(tile.shape[1] // 128)]
    while len(parts) > 1:
        rest = parts[len(parts) // 2 * 2 :]
        parts = [op(parts[2 * j], parts[2 * j + 1]) for j in range(len(parts) // 2)] + rest
    return parts[0]


def tile_mask(block, shape, low, high):
    place = block * shape[1] + lax.broadcasted_iota(jnp.int32, shape, 1)
    return (place >= low) & (place < high)


def forward_kernel(rows_at, first_ref, last_ref, slot_ref, q_ref, k_ref, v_ref, low_ref, high_ref, o_ref, lse_ref, s_ref):
    width = q_ref.shape[0]
    for i in range(width // rows_at):
        rows = pl.ds(i * rows_at, rows_at)
        queries = head_halves(q_ref[rows, :] * jnp.bfloat16(0.125))
        low, high = low_ref[rows, :], high_ref[rows, :]

        def scores(block, peaks):
            keys = k_ref[pl.ds(pl.multiple_of(slot_ref[block] * width, width), width), :]
            mask = tile_mask(block, (rows_at, width), low, high)
            found = []
            for h in range(2):
                score = jnp.where(mask, dot_nt(queries[h], keys), NEG)
                s_ref[h, block] = score
                found.append(jnp.maximum(peaks[h], over_lanes(score, jnp.maximum)))
            return tuple(found)

        start = jnp.full((rows_at, 128), NEG, jnp.float32)
        peaks = lax.fori_loop(first_ref[i], last_ref[i], scores, (start, start))
        peaks = [jnp.max(peak, axis=1, keepdims=True) for peak in peaks]

        def mix(block, carried):
            values = v_ref[pl.ds(pl.multiple_of(slot_ref[block] * width, width), width), :]
            totals, sums = [], []
            for h in range(2):
                soft = jnp.exp(s_ref[h, block] - peaks[h])
                totals.append(carried[0][h] + over_lanes(soft, jnp.add))
                sums.append(carried[1][h] + jnp.dot(soft.astype(jnp.bfloat16), values, preferred_element_type=jnp.float32))
            return tuple(totals), tuple(sums)

        zero = jnp.zeros((rows_at, 128), jnp.float32)
        totals, sums = lax.fori_loop(first_ref[i], last_ref[i], mix, ((zero, zero), (zero, zero)))
        totals = [jnp.sum(total, axis=1, keepdims=True) for total in totals]
        even = lax.broadcasted_iota(jnp.int32, (rows_at, 128), 1) < 64
        o_ref[rows, :] = jnp.where(even, sums[0] / totals[0], sums[1] / totals[1])
        lse_ref[rows, :] = jnp.where(even, peaks[0] + jnp.log(totals[0]), peaks[1] + jnp.log(totals[1]))


def query_kernel(
    rows_at, first_ref, last_ref, slot_ref, q_ref, k_ref, v_ref, g_ref, lse_ref, delta_ref, low_ref, high_ref, dq_ref
):
    width = q_ref.shape[0]
    for i in range(width // rows_at):
        rows = pl.ds(i * rows_at, rows_at)
        queries = head_halves(q_ref[rows, :] * jnp.bfloat16(0.125))
        grads = head_halves(g_ref[rows, :])
        low, high = low_ref[rows, :], high_ref[rows, :]
        lse = [lse_ref[rows, 64 * h : 64 * h + 1] for h in range(2)]
        delta = [delta_ref[rows, 64 * h : 64 * h + 1] for h in range(2)]

        def step(block, carried):
            at = pl.ds(pl.multiple_of(slot_ref[block] * width, width), width)
            keys, values = k_ref[at, :], v_ref[at, :]
            mask = tile_mask(block, (rows_at, width), low, high)
            found = []
            for h in range(2):
                soft = jnp.exp(jnp.where(mask, dot_nt(queries[h], keys) - lse[h], NEG))
                grad = (soft * (dot_nt(grads[h], values) - delta[h])).astype(jnp.bfloat16)
                found.append(carried[h] + jnp.dot(grad, keys, preferred_element_type=jnp.float32))
            return tuple(found)

        zero = jnp.zeros((rows_at, 128), jnp.float32)
        sums = lax.fori_loop(first_ref[i], last_ref[i], step, (zero, zero))
        even = lax.broadcasted_iota(jnp.int32, (rows_at, 128), 1) < 64
        dq_ref[rows, :] = (jnp.where(even, sums[0], sums[1]) * 0.125).astype(jnp.bfloat16)


def key_kernel(
    rows_at, first_ref, last_ref, slot_ref, k_ref, v_ref, q_ref, g_ref, stat_ref, low_ref, high_ref, dk_ref, dv_ref
):
    pair = pl.program_id(0)
    width = k_ref.shape[0]
    for i in range(width // rows_at):
        rows = pl.ds(i * rows_at, rows_at)
        keys = head_halves(k_ref[rows, :] * jnp.bfloat16(0.125))
        values = head_halves(v_ref[rows, :])
        low, high = low_ref[rows, :], high_ref[rows, :]

        def step(block, carried):
            slot = slot_ref[block]
            at = pl.ds(pl.multiple_of(slot * width, width), width)
            queries, grads = q_ref[at, :], g_ref[at, :]
            mask = tile_mask(block, (rows_at, width), low, high)
            key_sums, value_sums = [], []
            for h in range(2):
                lse = stat_ref[slot, pl.ds(2 * pair + h, 1), :]
                delta = stat_ref[slot, pl.ds(8 + 2 * pair + h, 1), :]
                soft = jnp.exp(jnp.where(mask, dot_nt(keys[h], queries) - lse, NEG))
                value_sums.append(
                    carried[1][h] + jnp.dot(soft.astype(jnp.bfloat16), grads, preferred_element_type=jnp.float32)
                )
                grad = (soft * (dot_nt(values[h], grads) - delta)).astype(jnp.bfloat16)
                key_sums.append(carried[0][h] + jnp.dot(grad, queries, preferred_element_type=jnp.float32))
            return tuple(key_sums), tuple(value_sums)

        zero = jnp.zeros((rows_at, 128), jnp.float32)
        key_sums, value_sums = lax.fori_loop(first_ref[i], last_ref[i], step, ((zero, zero), (zero, zero)))
        even = lax.broadcasted_iota(jnp.int32, (rows_at, 128), 1) < 64
        dk_ref[rows, :] = (jnp.where(even, key_sums[0], key_sums[1]) * 0.125).astype(jnp.bfloat16)
        dv_ref[rows, :] = jnp.where(even, value_sums[0], value_sums[1]).astype(jnp.bfloat16)


ROWS_AT = 256


def attend(kernel, name, ranges, operands, results, scratch, dots):
    tok_rows = operands[0][0].shape[0] if operands[0][1][0] == "own" else None
    specs = []
    for array, (kind, at) in operands:
        if kind == "own":
            specs.append(pl.BlockSpec((ranges[3], 128), lambda h, *_, at=at: (0, at + h)))
        elif kind == "window":
            specs.append(pl.BlockSpec((array.shape[0], 128), lambda h, *_, at=at: (0, at + h)))
        else:
            specs.append(pl.BlockSpec(array.shape, lambda h, *_, n=array.ndim: (0,) * n))
    tok_rows = ranges[3]
    return pl.pallas_call(
        functools.partial(kernel, ROWS_AT),
        name=name,
        grid_spec=pltpu.PrefetchScalarGridSpec(
            num_scalar_prefetch=3,
            grid=(D // 128,),
            in_specs=specs,
            out_specs=[pl.BlockSpec((tok_rows, 128), lambda h, *_: (0, h))] * len(results),
            scratch_shapes=scratch,
        ),
        out_shape=[jax.ShapeDtypeStruct((tok_rows, D), kept) for kept in results],
        compiler_params=pltpu.CompilerParams(vmem_limit_bytes=48 * 2**20),
        cost_estimate=pl.CostEstimate(
            flops=dots * 2 * tok_rows * 2048 * D, bytes_accessed=12 * 2**20, transcendentals=tok_rows * 2048 * HEADS
        ),
    )(*ranges[:3], *[array for array, _ in operands])


def pack_kernel(plan, shard_rows, *refs):
    out_ref, flat_ref = refs[-2], refs[-1]
    for (offset, rows, columns), ref in zip(plan, refs[:-2]):
        pieces = columns // 128
        for j in range(pieces):
            part = ref[:, 128 * j : 128 * (j + 1)]
            if rows == 1:
                flat_ref[pl.ds(offset + j, 1), :] = part
            else:
                flat_ref[pl.ds(offset + j, rows, stride=pieces), :] = part
    shards, padded, _ = out_ref.shape
    for i in range(shards):
        out_ref[i, pl.ds(0, shard_rows), :] = flat_ref[pl.ds(i * shard_rows, shard_rows), :].astype(jnp.bfloat16)
        out_ref[i, pl.ds(shard_rows, padded - shard_rows), :] = jnp.zeros((padded - shard_rows, 128), jnp.bfloat16)


def packed_rows(grads, shards, shard_rows, padded):
    plan = []
    offset = 0
    for grad in grads:
        plan.append((offset, *grad.shape))
        offset = offset + grad.shape[0] * grad.shape[1] // 128
    return pl.pallas_call(
        functools.partial(pack_kernel, plan, shard_rows),
        name="pack",
        out_shape=jax.ShapeDtypeStruct((shards, padded, 128), jnp.bfloat16),
        scratch_shapes=[pltpu.VMEM((offset, 128), jnp.float32)],
        compiler_params=pltpu.CompilerParams(vmem_limit_bytes=60 * 2**20),
        cost_estimate=pl.CostEstimate(flops=0, bytes_accessed=offset * 768, transcendentals=0),
    )(*grads)


def join_kernel(shard_rows, place_ref, mine_ref, other_ref, out_ref):
    shards = mine_ref.shape[0] * 2
    place = place_ref[0]
    for s in range(shards):
        rows = pl.ds(s * shard_rows, shard_rows)
        source = (s // 2) ^ (place // 2)

        @pl.when(place % 2 == s % 2)
        def _():
            out_ref[rows, :] = mine_ref[source]

        @pl.when(place % 2 != s % 2)
        def _():
            out_ref[rows, :] = other_ref[source]


def joined(mine, other, place):
    halves, shard_rows, _ = mine.shape
    return pl.pallas_call(
        functools.partial(join_kernel, shard_rows),
        name="join",
        in_specs=[pl.BlockSpec(memory_space=pltpu.SMEM)] + [pl.BlockSpec(memory_space=pltpu.VMEM)] * 2,
        out_specs=pl.BlockSpec(memory_space=pltpu.VMEM),
        out_shape=jax.ShapeDtypeStruct((2 * halves * shard_rows, 128), mine.dtype),
        compiler_params=pltpu.CompilerParams(vmem_limit_bytes=48 * 2**20),
        cost_estimate=pl.CostEstimate(flops=0, bytes_accessed=halves * shard_rows * 1024, transcendentals=0),
    )(place.reshape(1), mine, other)


def bit_of(bit):
    return (lax.axis_index(LINE) // bit) % 2


def spread_sum(cube, order, bits):
    left = list(bits)
    for bit in order:
        axis = left.index(bit)
        mine = lax.dynamic_index_in_dim(cube, bit_of(bit), axis, keepdims=False)
        theirs = lax.dynamic_index_in_dim(cube, 1 - bit_of(bit), axis, keepdims=False)
        cube = mine + swapped(theirs, bit)
        left.pop(axis)
    return cube


def gathered(piece, bits):
    for bit in bits:
        other = swapped(piece, bit)
        upper = bit_of(bit) == 1
        piece = jnp.concatenate([jnp.where(upper, other, piece), jnp.where(upper, piece, other)], axis=0)
    return piece


def on_device(inputs, weights, cotangent, clip_lengths, first_moment, second_moment):
    tok_rows = inputs.shape[0]
    reach = (MOST + tok_rows - 2) // tok_rows
    head_width = D // HEADS
    (
        first_gain,
        first_bias,
        query_weight,
        query_bias,
        key_weight,
        value_weight,
        value_bias,
        out_weight,
        out_bias,
        second_gain,
        second_bias,
        up_weight,
        up_bias,
        down_weight,
        down_bias,
    ) = unpack(weights)
    base_slot = lax.axis_index(LINE) * tok_rows
    positions = base_slot + jnp.arange(tok_rows, dtype=jnp.int32)
    lower_slot, upper_slot = bounds(positions, clip_lengths)
    low = lower_slot - base_slot + reach * tok_rows
    high = upper_slot - base_slot + reach * tok_rows
    first_block = low.reshape(-1, ROWS_AT)[:, 0] // tok_rows
    last_block = (high.reshape(-1, ROWS_AT)[:, -1] + tok_rows - 1) // tok_rows
    ranges = (first_block, last_block, slot_table(), tok_rows)
    low, high = low[:, None], high[:, None]

    window = jnp.concatenate(halo(inputs), axis=0)
    window_hat, window_dev = standard(window.astype(jnp.float32))
    window_normed = (window_hat * first_gain + first_bias).astype(jnp.bfloat16)
    project = jnp.concatenate([query_weight, key_weight, value_weight], axis=1)
    shift = jnp.concatenate([query_bias, jnp.zeros((D,), jnp.float32), value_bias])
    rows = (plain_dot(window_normed, project) + shift).astype(jnp.bfloat16)
    input_rows = inputs.astype(jnp.float32)
    first_hat, first_dev = standard(input_rows)
    normed = (first_hat * first_gain + first_bias).astype(jnp.bfloat16)

    attended, lse = attend(
        forward_kernel,
        "attend_forward",
        ranges,
        [
            (rows, ("own", 0)),
            (rows, ("window", 4)),
            (rows, ("window", 8)),
            (low, ("all", 0)),
            (high, ("all", 0)),
        ],
        [jnp.float32, jnp.float32],
        [pltpu.VMEM((2, 2 * reach + 1, ROWS_AT, tok_rows), jnp.float32)],
        2,
    )
    mixed = attended.astype(jnp.bfloat16)
    middle = input_rows + plain_dot(mixed, out_weight) + out_bias
    second_hat, second_dev = standard(middle)
    hidden_in = (second_hat * second_gain + second_bias).astype(jnp.bfloat16)
    up_rows = plain_dot(hidden_in, up_weight) + up_bias
    cdf_part = 0.5 * (1.0 + lax.erf(up_rows * INV_ROOT_TWO))
    activated = (up_rows * cdf_part).astype(jnp.bfloat16)
    layer_output = (middle + plain_dot(activated, down_weight) + down_bias).astype(jnp.bfloat16)
    grad_out = cotangent.astype(jnp.float32)
    down_grad = rows_dot(activated, cotangent)
    down_bias_grad = jnp.sum(grad_out, axis=0)
    grad_act = back_dot(cotangent, down_weight)
    pdf_part = jnp.exp(-0.5 * up_rows * up_rows) * INV_ROOT_TWO_PI
    grad_up = (grad_act * (cdf_part + up_rows * pdf_part)).astype(jnp.bfloat16)
    up_grad = rows_dot(hidden_in, grad_up)
    up_bias_grad = jnp.sum(grad_up.astype(jnp.float32), axis=0)
    grad_hidden = back_dot(grad_up, up_weight)
    second_gain_grad = jnp.sum(grad_hidden * second_hat, axis=0)
    second_bias_grad = jnp.sum(grad_hidden, axis=0)
    grad_middle = grad_out + norm_back(grad_hidden, second_hat, second_dev, second_gain)
    grad_branch = grad_middle.astype(jnp.bfloat16)
    out_grad = rows_dot(mixed, grad_branch)
    out_bias_grad = jnp.sum(grad_branch.astype(jnp.float32), axis=0)
    grad_mixed = back_dot(grad_branch, out_weight).astype(jnp.bfloat16)
    row_delta = jnp.sum(
        (grad_mixed.astype(jnp.float32) * attended).reshape(tok_rows, HEADS, head_width), axis=-1
    )
    delta = jnp.repeat(row_delta, head_width, axis=1)
    stats = jnp.concatenate([lse[:, ::head_width].T, row_delta.T], axis=0)
    grad_window = jnp.concatenate(halo(grad_mixed), axis=0)
    stat_window = jnp.stack(halo(stats))

    (query_low,) = attend(
        query_kernel,
        "attend_query",
        ranges,
        [
            (rows, ("own", 0)),
            (rows, ("window", 4)),
            (rows, ("window", 8)),
            (grad_mixed, ("own", 0)),
            (lse, ("own", 0)),
            (delta, ("own", 0)),
            (low, ("all", 0)),
            (high, ("all", 0)),
        ],
        [jnp.bfloat16],
        [],
        3,
    )
    key_low, value_low = attend(
        key_kernel,
        "attend_key",
        ranges,
        [
            (rows, ("own", 4)),
            (rows, ("own", 8)),
            (rows, ("window", 0)),
            (grad_window, ("window", 0)),
            (stat_window, ("all", 0)),
            (low, ("all", 0)),
            (high, ("all", 0)),
        ],
        [jnp.bfloat16, jnp.bfloat16],
        [],
        4,
    )
    query_grad = rows_dot(normed, query_low)
    query_bias_grad = jnp.sum(query_low.astype(jnp.float32), axis=0)
    key_grad = rows_dot(normed, key_low)
    value_grad = rows_dot(normed, value_low)
    value_bias_grad = jnp.sum(value_low.astype(jnp.float32), axis=0)
    grad_normed = (
        back_dot(query_low, query_weight)
        + back_dot(key_low, key_weight)
        + back_dot(value_low, value_weight)
    )
    first_gain_grad = jnp.sum(grad_normed * first_hat, axis=0)
    first_bias_grad = jnp.sum(grad_normed, axis=0)
    input_grad = (grad_middle + norm_back(grad_normed, first_hat, first_dev, first_gain)).astype(
        jnp.bfloat16
    )

    outer, inner = lax.axis_size("outer"), lax.axis_size("inner")
    shard_rows = first_moment.shape[0] // 128
    padded = -(-shard_rows // (16 * outer)) * 16 * outer
    sections = [
        first_gain_grad,
        first_bias_grad,
        query_grad,
        query_bias_grad,
        key_grad,
        value_grad,
        value_bias_grad,
        out_grad,
        out_bias_grad,
        second_gain_grad,
        second_bias_grad,
        up_grad,
        up_bias_grad,
        down_grad,
        down_bias_grad,
    ]
    packed = packed_rows(
        [section.reshape(-1, section.shape[-1]) for section in sections], inner, shard_rows, padded
    )
    bits = [inner * outer >> (k + 1) for k in range((inner * outer).bit_length() - 1)]
    outer_bits = [bit for bit in bits if bit >= inner]
    inner_bits = [bit for bit in bits if bit < inner]
    cube_bits = inner_bits + outer_bits
    cube = packed.reshape((2,) * len(bits) + (padded // outer, 128))
    piece = spread_sum(cube, inner_bits[::-1] + outer_bits[::-1], cube_bits)
    shard = gathered(piece, outer_bits[::-1])[:shard_rows]
    grad_shard = shard.astype(jnp.float32)
    squares = lax.psum(jnp.sum(grad_shard * grad_shard), "inner")
    grad_norm = jnp.sqrt(squares)
    clipped = grad_shard / jnp.maximum(grad_norm, 1.0)
    moment_one = BETA_ONE * first_moment.reshape(-1, 128) + (1.0 - BETA_ONE) * clipped
    moment_two = BETA_TWO * second_moment.reshape(-1, 128) + (1.0 - BETA_TWO) * clipped * clipped
    shard_len = first_moment.shape[0]
    own_weights = lax.dynamic_slice_in_dim(
        weights, lax.axis_index("inner") * shard_len, shard_len, 0
    ).astype(jnp.float32)
    update = moment_one / FIX_ONE / (jnp.sqrt(moment_two / FIX_TWO) + 1e-08) + DECAY * own_weights.reshape(-1, 128)
    mine = update.astype(jnp.bfloat16)[None]
    for bit in inner_bits[::-1][1:]:
        mine = jnp.concatenate([mine, swapped(mine, bit)], axis=0)
    weight_step = joined(mine, swapped(mine, 1), lax.axis_index("inner")).reshape(-1)
    return (
        layer_output,
        input_grad,
        grad_shard.reshape(-1),
        grad_norm,
        moment_one.reshape(-1),
        moment_two.reshape(-1),
        weight_step,
    )


def solution(mesh):
    return jax.shard_map(
        on_device,
        mesh=mesh,
        in_specs=(
            P(("outer", "inner"), None),
            P(),
            P(("outer", "inner"), None),
            P(),
            P("inner"),
            P("inner"),
        ),
        out_specs=(
            P(("outer", "inner"), None),
            P(("outer", "inner"), None),
            P("inner"),
            P(),
            P("inner"),
            P("inner"),
            P(),
        ),
        check_vma=False,
    )
```

```python
import functools
import math

import jax
import jax.numpy as jnp
from jax import lax
from jax.experimental import pallas as pl
from jax.experimental.pallas import tpu as pltpu
from jax.sharding import PartitionSpec as P

D = 512
HEADS = 8
FF = 2048
MOST = 1500


BETA_ONE = 0.9
BETA_TWO = 0.999
FIX_ONE = 1.0 - (0.9**10) ** 10
FIX_TWO = 1.0 - (0.999**10) ** 10
DECAY = 0.1
INV_ROOT_TWO = 1.0 / math.sqrt(2.0)
INV_ROOT_TWO_PI = 1.0 / math.sqrt(2.0 * math.pi)


def layouts():
    return [
        (D,),
        (D,),
        (D, D),
        (D,),
        (D, D),
        (D, D),
        (D,),
        (D, D),
        (D,),
        (D,),
        (D,),
        (D, FF),
        (FF,),
        (FF, D),
        (D,),
    ]


def unpack(flat):
    sections = []
    offset = 0
    for layout in layouts():
        entries = 1
        for extent in layout:
            entries = entries * extent
        section = flat[offset : offset + entries].reshape(layout)
        if len(layout) == 1:
            section = section.astype(jnp.float32)
        sections.append(section)
        offset = offset + entries
    return sections


def plain_dot(matrix_one, matrix_two):
    return jnp.dot(matrix_one, matrix_two, preferred_element_type=jnp.float32)


def rows_dot(matrix_one, matrix_two):
    return lax.dot_general(
        matrix_one, matrix_two, (((0,), (0,)), ((), ())), preferred_element_type=jnp.float32
    )


def back_dot(matrix_one, matrix_two):
    return lax.dot_general(
        matrix_one, matrix_two, (((1,), (1,)), ((), ())), preferred_element_type=jnp.float32
    )


def standard(values):
    center = jnp.mean(values, axis=-1, keepdims=True)
    centered = values - center
    inverse_dev = lax.rsqrt(jnp.mean(centered * centered, axis=-1, keepdims=True) + 1e-05)
    return (centered * inverse_dev, inverse_dev)


def norm_back(grad_normed, normed_hat, inverse_dev, gain):
    scaled = grad_normed * gain
    return inverse_dev * (
        scaled
        - jnp.mean(scaled, axis=-1, keepdims=True)
        - normed_hat * jnp.mean(scaled * normed_hat, axis=-1, keepdims=True)
    )


def bounds(positions, clip_lengths):
    starts = jnp.cumsum(clip_lengths, dtype=jnp.int32) - clip_lengths
    member = (
        jnp.sum((positions[:, None] >= starts[None, :]).astype(jnp.int32), axis=1, dtype=jnp.int32)
        - 1
    )
    onehot = (
        jnp.arange(clip_lengths.shape[0], dtype=jnp.int32)[None, :] == member[:, None]
    ).astype(jnp.int32)
    lower_slot = jnp.sum(onehot * starts[None, :], axis=1, dtype=jnp.int32)
    upper_slot = lower_slot + jnp.sum(onehot * clip_lengths[None, :], axis=1, dtype=jnp.int32)
    return (lower_slot, upper_slot)


LINE = ("outer", "inner")
NEG = -1e30


def shifted(block, distance):
    n = lax.axis_size(LINE)
    return lax.ppermute(block, LINE, [(i + distance, i) for i in range(n) if 0 <= i + distance < n])


def swapped(block, bit):
    n = lax.axis_size(LINE)
    return lax.ppermute(block, LINE, [(i ^ bit, i) for i in range(n)])


def halo(block):
    n = lax.axis_size(LINE)
    partner = swapped(block, 1)
    left = shifted(block, -2)
    right = shifted(block, 2)
    route = [(i + (3 if i % 2 else -3), i) for i in range(n)]
    far = lax.ppermute(block, LINE, [(s, t) for s, t in route if 0 <= s < n])
    return [block, partner, left, right, swapped(left, 1), swapped(right, 1), far]


def slot_table():
    odd = lax.axis_index(LINE) % 2
    even_slots = jnp.array([6, 2, 4, 0, 1, 3, 5], jnp.int32)
    odd_slots = jnp.array([4, 2, 1, 0, 5, 3, 6], jnp.int32)
    return jnp.where(odd == 1, odd_slots, even_slots)


def dot_nt(a, b):
    return lax.dot_general(a, b, (((1,), (1,)), ((), ())), preferred_element_type=jnp.float32)


def head_halves(pair):
    first = lax.broadcasted_iota(jnp.int32, pair.shape, 1) < pair.shape[1] // 2
    zero = jnp.zeros_like(pair)
    return jnp.where(first, pair, zero), jnp.where(first, zero, pair)


def over_lanes(tile, op):
    parts = [tile[:, 128 * j : 128 * (j + 1)] for j in range(tile.shape[1] // 128)]
    while len(parts) > 1:
        rest = parts[len(parts) // 2 * 2 :]
        parts = [op(parts[2 * j], parts[2 * j + 1]) for j in range(len(parts) // 2)] + rest
    return parts[0]


def tile_mask(block, shape, low, high):
    place = block * shape[1] + lax.broadcasted_iota(jnp.int32, shape, 1)
    return (place >= low) & (place < high)


def forward_kernel(rows_at, first_ref, last_ref, slot_ref, q_ref, k_ref, v_ref, low_ref, high_ref, o_ref, lse_ref, s_ref):
    width = q_ref.shape[0]
    for i in range(width // rows_at):
        rows = pl.ds(i * rows_at, rows_at)
        queries = head_halves(q_ref[rows, :] * jnp.bfloat16(0.125))
        low, high = low_ref[rows, :], high_ref[rows, :]

        def scores(block, peaks):
            keys = k_ref[pl.ds(pl.multiple_of(slot_ref[block] * width, width), width), :]
            mask = tile_mask(block, (rows_at, width), low, high)
            found = []
            for h in range(2):
                score = jnp.where(mask, dot_nt(queries[h], keys), NEG)
                s_ref[h, block] = score
                found.append(jnp.maximum(peaks[h], over_lanes(score, jnp.maximum)))
            return tuple(found)

        start = jnp.full((rows_at, 128), NEG, jnp.float32)
        peaks = lax.fori_loop(first_ref[i], last_ref[i], scores, (start, start))
        peaks = [jnp.max(peak, axis=1, keepdims=True) for peak in peaks]

        def mix(block, carried):
            values = v_ref[pl.ds(pl.multiple_of(slot_ref[block] * width, width), width), :]
            totals, sums = [], []
            for h in range(2):
                soft = jnp.exp(s_ref[h, block] - peaks[h])
                totals.append(carried[0][h] + over_lanes(soft, jnp.add))
                sums.append(carried[1][h] + jnp.dot(soft.astype(jnp.bfloat16), values, preferred_element_type=jnp.float32))
            return tuple(totals), tuple(sums)

        zero = jnp.zeros((rows_at, 128), jnp.float32)
        totals, sums = lax.fori_loop(first_ref[i], last_ref[i], mix, ((zero, zero), (zero, zero)))
        totals = [jnp.sum(total, axis=1, keepdims=True) for total in totals]
        even = lax.broadcasted_iota(jnp.int32, (rows_at, 128), 1) < 64
        o_ref[rows, :] = jnp.where(even, sums[0] / totals[0], sums[1] / totals[1])
        lse_ref[rows, :] = jnp.where(even, peaks[0] + jnp.log(totals[0]), peaks[1] + jnp.log(totals[1]))


def query_kernel(
    rows_at, first_ref, last_ref, slot_ref, q_ref, k_ref, v_ref, g_ref, lse_ref, delta_ref, low_ref, high_ref, dq_ref
):
    width = q_ref.shape[0]
    for i in range(width // rows_at):
        rows = pl.ds(i * rows_at, rows_at)
        queries = head_halves(q_ref[rows, :] * jnp.bfloat16(0.125))
        grads = head_halves(g_ref[rows, :])
        low, high = low_ref[rows, :], high_ref[rows, :]
        lse = [lse_ref[rows, 64 * h : 64 * h + 1] for h in range(2)]
        delta = [delta_ref[rows, 64 * h : 64 * h + 1] for h in range(2)]

        def step(block, carried):
            at = pl.ds(pl.multiple_of(slot_ref[block] * width, width), width)
            keys, values = k_ref[at, :], v_ref[at, :]
            mask = tile_mask(block, (rows_at, width), low, high)
            found = []
            for h in range(2):
                soft = jnp.exp(jnp.where(mask, dot_nt(queries[h], keys) - lse[h], NEG))
                grad = (soft * (dot_nt(grads[h], values) - delta[h])).astype(jnp.bfloat16)
                found.append(carried[h] + jnp.dot(grad, keys, preferred_element_type=jnp.float32))
            return tuple(found)

        zero = jnp.zeros((rows_at, 128), jnp.float32)
        sums = lax.fori_loop(first_ref[i], last_ref[i], step, (zero, zero))
        even = lax.broadcasted_iota(jnp.int32, (rows_at, 128), 1) < 64
        dq_ref[rows, :] = (jnp.where(even, sums[0], sums[1]) * 0.125).astype(jnp.bfloat16)


def key_kernel(
    rows_at, first_ref, last_ref, slot_ref, k_ref, v_ref, q_ref, g_ref, low_ref, high_ref, dk_ref, dv_ref
):
    width = k_ref.shape[0]
    sent = width + stat_rows(width)
    for i in range(width // rows_at):
        rows = pl.ds(i * rows_at, rows_at)
        keys = head_halves(k_ref[rows, :] * jnp.bfloat16(0.125))
        values = head_halves(v_ref[rows, :])
        low, high = low_ref[rows, :], high_ref[rows, :]

        def step(block, carried):
            slot = slot_ref[block]
            at = pl.ds(pl.multiple_of(slot * width, width), width)
            queries = q_ref[at, :]
            grads = g_ref[pl.ds(pl.multiple_of(slot * sent, 16), width), :]
            packed = g_ref[pl.ds(pl.multiple_of(slot * sent + width, 16), sent - width), :].astype(jnp.float32)
            mask = tile_mask(block, (rows_at, width), low, high)
            key_sums, value_sums = [], []
            for h in range(2):
                lse = unpacked_stat(packed, h, width)
                delta = unpacked_stat(packed, 2 + h, width)
                soft = jnp.exp(jnp.where(mask, dot_nt(keys[h], queries) - lse, NEG))
                value_sums.append(
                    carried[1][h] + jnp.dot(soft.astype(jnp.bfloat16), grads, preferred_element_type=jnp.float32)
                )
                grad = (soft * (dot_nt(values[h], grads) - delta)).astype(jnp.bfloat16)
                key_sums.append(carried[0][h] + jnp.dot(grad, queries, preferred_element_type=jnp.float32))
            return tuple(key_sums), tuple(value_sums)

        zero = jnp.zeros((rows_at, 128), jnp.float32)
        key_sums, value_sums = lax.fori_loop(first_ref[i], last_ref[i], step, ((zero, zero), (zero, zero)))
        even = lax.broadcasted_iota(jnp.int32, (rows_at, 128), 1) < 64
        dk_ref[rows, :] = (jnp.where(even, key_sums[0], key_sums[1]) * 0.125).astype(jnp.bfloat16)
        dv_ref[rows, :] = jnp.where(even, value_sums[0], value_sums[1]).astype(jnp.bfloat16)


def stat_rows(width):
    return -(-12 * (width // 128) // 16) * 16


def unpacked_stat(packed, which, width):
    pieces = width // 128
    parts = []
    for j in range(pieces):
        at = [(3 * which + part) * pieces + j for part in range(3)]
        parts.append(packed[at[0] : at[0] + 1] + packed[at[1] : at[1] + 1] + packed[at[2] : at[2] + 1])
    return jnp.concatenate(parts, axis=1)


def mixed_grad_kernel(branch_ref, weight_ref, mixed_ref, lse_ref, sent_ref, delta_ref):
    width = branch_ref.shape[0]
    grad = dot_nt(branch_ref[...], weight_ref[...]).astype(jnp.bfloat16)
    sent_ref[pl.ds(0, width), :] = grad
    product = grad.astype(jnp.float32) * mixed_ref[...]
    even = lax.broadcasted_iota(jnp.int32, product.shape, 1) < 64
    sums = [jnp.sum(part, axis=1, keepdims=True) for part in head_halves(product)]
    delta = jnp.where(even, sums[0], sums[1])
    delta_ref[...] = delta
    rows = []
    for kept in (lse_ref[...], delta):
        turned = kept.T
        for h in range(2):
            row = turned[64 * h : 64 * h + 1, :]
            for _ in range(3):
                part = row.astype(jnp.bfloat16).astype(jnp.float32)
                row = row - part
                rows.extend(part[:, 128 * j : 128 * (j + 1)] for j in range(width // 128))
    spare = stat_rows(width) - len(rows)
    if spare:
        rows.append(jnp.zeros((spare, 128), jnp.float32))
    sent_ref[pl.ds(width, stat_rows(width)), :] = jnp.concatenate(rows, axis=0).astype(jnp.bfloat16)


def mixed_grad(branch, out_weight, mixed, lse):
    width = branch.shape[0]
    column = pl.BlockSpec((width, 128), lambda h: (0, h))
    return pl.pallas_call(
        mixed_grad_kernel,
        name="mixed_grad",
        grid=(D // 128,),
        in_specs=[
            pl.BlockSpec((width, D), lambda h: (0, 0)),
            pl.BlockSpec((128, D), lambda h: (h, 0)),
            column,
            column,
        ],
        out_specs=[pl.BlockSpec((width + stat_rows(width), 128), lambda h: (0, h)), column],
        out_shape=[
            jax.ShapeDtypeStruct((width + stat_rows(width), D), jnp.bfloat16),
            jax.ShapeDtypeStruct((width, D), jnp.float32),
        ],
        cost_estimate=pl.CostEstimate(flops=2 * width * D * D, bytes_accessed=6 * 2**20, transcendentals=0),
    )(branch, out_weight, mixed, lse)


ROWS_AT = 256


def attend(kernel, name, ranges, operands, results, scratch, dots, pairs=(0, D // 128)):
    begin, count = pairs
    specs = []
    for array, (kind, at) in operands:
        if kind == "own":
            specs.append(pl.BlockSpec((ranges[3], 128), lambda h, *_, at=at + begin: (0, at + h)))
        elif kind == "window":
            specs.append(pl.BlockSpec((array.shape[0], 128), lambda h, *_, at=at + begin: (0, at + h)))
        else:
            specs.append(pl.BlockSpec(array.shape, lambda h, *_, n=array.ndim: (0,) * n))
    tok_rows = ranges[3]
    return pl.pallas_call(
        functools.partial(kernel, ROWS_AT),
        name=name,
        grid_spec=pltpu.PrefetchScalarGridSpec(
            num_scalar_prefetch=3,
            grid=(count,),
            in_specs=specs,
            out_specs=[pl.BlockSpec((tok_rows, 128), lambda h, *_: (0, h))] * len(results),
            scratch_shapes=scratch,
        ),
        out_shape=[jax.ShapeDtypeStruct((tok_rows, 128 * count), kept) for kept in results],
        compiler_params=pltpu.CompilerParams(vmem_limit_bytes=48 * 2**20),
        cost_estimate=pl.CostEstimate(
            flops=dots * 8 * tok_rows * 2048 * 128 * count,
            bytes_accessed=count * 3 * 2**20,
            transcendentals=tok_rows * 4096 * count,
        ),
    )(*ranges[:3], *[array for array, _ in operands])


def pack_kernel(plan, half, bit_ref, *refs):
    keep_ref, give_ref, flat_ref = refs[-3:]
    for (offset, rows, columns), ref in zip(plan, refs[:-3]):
        pieces = columns // 128
        for j in range(pieces):
            part = ref[:, 128 * j : 128 * (j + 1)]
            if rows == 1:
                flat_ref[pl.ds(offset + j, 1), :] = part
            else:
                flat_ref[pl.ds(offset + j, rows, stride=pieces), :] = part
    end = plan[-1][0] + plan[-1][1] * plan[-1][2] // 128
    flat_ref[pl.ds(end, 2 * half - end), :] = jnp.zeros((2 * half - end, 128), jnp.float32)
    bit = bit_ref[0]
    keep_ref[...] = flat_ref[pl.ds(pl.multiple_of(bit * half, 8), half), :].astype(jnp.bfloat16)
    give_ref[...] = flat_ref[pl.ds(pl.multiple_of((1 - bit) * half, 8), half), :].astype(jnp.bfloat16)


def packed_halves(grads, offset_from, half, bit):
    plan = []
    offset = 0
    for grad in grads:
        plan.append((offset, *grad.shape))
        offset = offset + grad.shape[0] * grad.shape[1] // 128
    return pl.pallas_call(
        functools.partial(pack_kernel, plan, half),
        name="pack",
        in_specs=[pl.BlockSpec(memory_space=pltpu.SMEM)] + [pl.BlockSpec(memory_space=pltpu.VMEM)] * len(grads),
        out_specs=[pl.BlockSpec(memory_space=pltpu.VMEM)] * 2,
        out_shape=[jax.ShapeDtypeStruct((half, 128), jnp.bfloat16)] * 2,
        scratch_shapes=[pltpu.VMEM((2 * half, 128), jnp.float32)],
        compiler_params=pltpu.CompilerParams(vmem_limit_bytes=60 * 2**20),
        cost_estimate=pl.CostEstimate(flops=0, bytes_accessed=offset * 768, transcendentals=0),
    )(bit_of(bit).reshape(1), *grads)


def add_split_kernel(bit_ref, one_ref, two_ref, keep_ref, give_ref):
    half = keep_ref.shape[0]
    kept = pl.ds(pl.multiple_of(bit_ref[0] * half, 8), half)
    given = pl.ds(pl.multiple_of((1 - bit_ref[0]) * half, 8), half)
    for rows, ref in ((given, give_ref), (kept, keep_ref)):
        total = one_ref[rows, :].astype(jnp.float32) + two_ref[rows, :].astype(jnp.float32)
        ref[...] = total.astype(jnp.bfloat16)


def add_split(one, two, bit):
    half = one.shape[0] // 2
    return pl.pallas_call(
        add_split_kernel,
        name="add_split",
        in_specs=[pl.BlockSpec(memory_space=pltpu.SMEM)] + [pl.BlockSpec(memory_space=pltpu.VMEM)] * 2,
        out_specs=[pl.BlockSpec(memory_space=pltpu.VMEM)] * 2,
        out_shape=[jax.ShapeDtypeStruct((half, 128), jnp.bfloat16)] * 2,
        cost_estimate=pl.CostEstimate(flops=0, bytes_accessed=half * 1536, transcendentals=0),
    )(bit_of(bit).reshape(1), one, two)


def together_kernel(bit_ref, own_ref, other_ref, out_ref):
    rows = own_ref.shape[0]
    out_ref[pl.ds(pl.multiple_of(bit_ref[0] * rows, 8), rows), :] = own_ref[...]
    out_ref[pl.ds(pl.multiple_of((1 - bit_ref[0]) * rows, 8), rows), :] = other_ref[...]


def together(own, other, bit):
    return pl.pallas_call(
        together_kernel,
        name="together",
        in_specs=[pl.BlockSpec(memory_space=pltpu.SMEM)] + [pl.BlockSpec(memory_space=pltpu.VMEM)] * 2,
        out_specs=pl.BlockSpec(memory_space=pltpu.VMEM),
        out_shape=jax.ShapeDtypeStruct((2 * own.shape[0], 128), own.dtype),
        cost_estimate=pl.CostEstimate(flops=0, bytes_accessed=own.shape[0] * 1024, transcendentals=0),
    )(bit_of(bit).reshape(1), own, other)


def summed(keep, give, order):
    for at, bit in enumerate(order):
        got = swapped(give, bit)
        if at + 1 < len(order):
            keep, give = add_split(keep, got, order[at + 1])
    piece = (keep.astype(jnp.float32) + got.astype(jnp.float32)).astype(jnp.bfloat16)
    for bit in order[::-1]:
        piece = together(piece, swapped(piece, bit), bit)
    return piece


def join_kernel(shard_rows, place_ref, mine_ref, other_ref, out_ref):
    shards = mine_ref.shape[0] * 2
    place = place_ref[0]
    for s in range(shards):
        rows = pl.ds(s * shard_rows, shard_rows)
        source = (s // 2) ^ (place // 2)

        @pl.when(place % 2 == s % 2)
        def _():
            out_ref[rows, :] = mine_ref[source, pl.ds(0, shard_rows), :]

        @pl.when(place % 2 != s % 2)
        def _():
            out_ref[rows, :] = other_ref[source, pl.ds(0, shard_rows), :]


def joined(mine, other, place, shard_rows):
    halves, padded, _ = mine.shape
    return pl.pallas_call(
        functools.partial(join_kernel, shard_rows),
        name="join",
        in_specs=[pl.BlockSpec(memory_space=pltpu.SMEM)] + [pl.BlockSpec(memory_space=pltpu.VMEM)] * 2,
        out_specs=pl.BlockSpec(memory_space=pltpu.VMEM),
        out_shape=jax.ShapeDtypeStruct((2 * halves * shard_rows, 128), mine.dtype),
        compiler_params=pltpu.CompilerParams(vmem_limit_bytes=48 * 2**20),
        cost_estimate=pl.CostEstimate(flops=0, bytes_accessed=halves * shard_rows * 1024, transcendentals=0),
    )(place.reshape(1), mine, other)


def bit_of(bit):
    return (lax.axis_index(LINE) // bit) % 2


def relayed(piece, bit, relay):
    rows = piece.shape[0] // 2
    mine = bit_of(relay)
    half = swapped(lax.dynamic_slice_in_dim(piece, mine * rows, rows, 0), bit)
    return together(half, swapped(half, relay), relay)


def on_device(inputs, weights, cotangent, clip_lengths, first_moment, second_moment):
    tok_rows = inputs.shape[0]
    reach = (MOST + tok_rows - 2) // tok_rows
    head_width = D // HEADS
    (
        first_gain,
        first_bias,
        query_weight,
        query_bias,
        key_weight,
        value_weight,
        value_bias,
        out_weight,
        out_bias,
        second_gain,
        second_bias,
        up_weight,
        up_bias,
        down_weight,
        down_bias,
    ) = unpack(weights)
    base_slot = lax.axis_index(LINE) * tok_rows
    positions = base_slot + jnp.arange(tok_rows, dtype=jnp.int32)
    lower_slot, upper_slot = bounds(positions, clip_lengths)
    low = lower_slot - base_slot + reach * tok_rows
    high = upper_slot - base_slot + reach * tok_rows
    first_block = low.reshape(-1, ROWS_AT)[:, 0] // tok_rows
    last_block = (high.reshape(-1, ROWS_AT)[:, -1] + tok_rows - 1) // tok_rows
    ranges = (first_block, last_block, slot_table(), tok_rows)
    low, high = low[:, None], high[:, None]

    window = jnp.concatenate(halo(inputs), axis=0)
    window_hat, window_dev = standard(window.astype(jnp.float32))
    window_normed = (window_hat * first_gain + first_bias).astype(jnp.bfloat16)
    project = jnp.concatenate([query_weight, key_weight, value_weight], axis=1)
    shift = jnp.concatenate([query_bias, jnp.zeros((D,), jnp.float32), value_bias])
    rows = (plain_dot(window_normed, project) + shift).astype(jnp.bfloat16)
    input_rows = inputs.astype(jnp.float32)
    first_hat, first_dev = standard(input_rows)
    normed = (first_hat * first_gain + first_bias).astype(jnp.bfloat16)

    attended, lse = attend(
        forward_kernel,
        "attend_forward",
        ranges,
        [
            (rows, ("own", 0)),
            (rows, ("window", 4)),
            (rows, ("window", 8)),
            (low, ("all", 0)),
            (high, ("all", 0)),
        ],
        [jnp.float32, jnp.float32],
        [pltpu.VMEM((2, 2 * reach + 1, ROWS_AT, tok_rows), jnp.float32)],
        2,
    )
    mixed = attended.astype(jnp.bfloat16)
    middle = input_rows + plain_dot(mixed, out_weight) + out_bias
    second_hat, second_dev = standard(middle)
    hidden_in = (second_hat * second_gain + second_bias).astype(jnp.bfloat16)
    up_rows = plain_dot(hidden_in, up_weight) + up_bias
    cdf_part = 0.5 * (1.0 + lax.erf(up_rows * INV_ROOT_TWO))
    activated = (up_rows * cdf_part).astype(jnp.bfloat16)
    layer_output = (middle + plain_dot(activated, down_weight) + down_bias).astype(jnp.bfloat16)
    grad_out = cotangent.astype(jnp.float32)
    down_grad = rows_dot(activated, cotangent)
    down_bias_grad = jnp.sum(grad_out, axis=0)
    grad_act = back_dot(cotangent, down_weight)
    pdf_part = jnp.exp(-0.5 * up_rows * up_rows) * INV_ROOT_TWO_PI
    grad_up = (grad_act * (cdf_part + up_rows * pdf_part)).astype(jnp.bfloat16)
    up_grad = rows_dot(hidden_in, grad_up)
    up_bias_grad = jnp.sum(grad_up.astype(jnp.float32), axis=0)
    grad_hidden = back_dot(grad_up, up_weight)
    second_gain_grad = jnp.sum(grad_hidden * second_hat, axis=0)
    second_bias_grad = jnp.sum(grad_hidden, axis=0)
    grad_middle = grad_out + norm_back(grad_hidden, second_hat, second_dev, second_gain)
    grad_branch = grad_middle.astype(jnp.bfloat16)
    out_grad = rows_dot(mixed, grad_branch)
    out_bias_grad = jnp.sum(grad_branch.astype(jnp.float32), axis=0)
    sent, delta = mixed_grad(grad_branch, out_weight, attended, lse)
    grad_window = jnp.concatenate(halo(sent), axis=0)

    early_rows = [
        out_grad,
        out_bias_grad,
        second_gain_grad,
        second_bias_grad,
        up_grad,
        up_bias_grad,
        down_grad,
        down_bias_grad,
    ]
    early_rows = [section.reshape(-1, section.shape[-1]) for section in early_rows]
    early_count = sum(section.size for section in early_rows) // 128
    line = lax.axis_size(LINE)
    bits = [1 << k for k in range(line.bit_length() - 1)]
    early_half = -(-early_count // (16 * line)) * 8 * line
    early_keep, early_give = packed_halves(early_rows, 0, early_half, 1)
    early_got = swapped(early_give, 1)
    turned_bits = bits[1:3][::-1] + bits[3:]
    part = early_half // 2
    early_parts = []
    for begin, order in ((0, bits[1:]), (part, turned_bits)):
        keep, give = add_split(early_keep[begin : begin + part], early_got[begin : begin + part], order[0])
        early_parts.append(summed(keep, give, order))
    early_own = jnp.concatenate(early_parts, axis=0)
    early_full = together(early_own, swapped(early_own, 1), 1)

    query_parts = []
    for pairs in ((0, 2), (2, 2)):
        query_parts += attend(
            query_kernel,
            "attend_query",
            ranges,
            [
                (rows, ("own", 0)),
                (rows, ("window", 4)),
                (rows, ("window", 8)),
                (sent, ("own", 0)),
                (lse, ("own", 0)),
                (delta, ("own", 0)),
                (low, ("all", 0)),
                (high, ("all", 0)),
            ],
            [jnp.bfloat16],
            [],
            3,
            pairs,
        )
    query_low = jnp.concatenate(query_parts, axis=1)
    key_parts, value_parts = [], []
    for pairs in ((0, 2), (2, 2)):
        key_part, value_part = attend(
            key_kernel,
            "attend_key",
            ranges,
            [
                (rows, ("own", 4)),
                (rows, ("own", 8)),
                (rows, ("window", 0)),
                (grad_window, ("window", 0)),
                (low, ("all", 0)),
                (high, ("all", 0)),
            ],
            [jnp.bfloat16, jnp.bfloat16],
            [],
            4,
            pairs,
        )
        key_parts.append(key_part)
        value_parts.append(value_part)
    key_low = jnp.concatenate(key_parts, axis=1)
    value_low = jnp.concatenate(value_parts, axis=1)
    query_grad = rows_dot(normed, query_low)
    query_bias_grad = jnp.sum(query_low.astype(jnp.float32), axis=0)
    key_grad = rows_dot(normed, key_low)
    value_grad = rows_dot(normed, value_low)
    value_bias_grad = jnp.sum(value_low.astype(jnp.float32), axis=0)
    grad_normed = (
        back_dot(query_low, query_weight)
        + back_dot(key_low, key_weight)
        + back_dot(value_low, value_weight)
    )
    first_gain_grad = jnp.sum(grad_normed * first_hat, axis=0)
    first_bias_grad = jnp.sum(grad_normed, axis=0)
    input_grad = (grad_middle + norm_back(grad_normed, first_hat, first_dev, first_gain)).astype(
        jnp.bfloat16
    )

    shard_rows = first_moment.shape[0] // 128
    late_rows = [
        first_gain_grad,
        first_bias_grad,
        query_grad,
        query_bias_grad,
        key_grad,
        value_grad,
        value_bias_grad,
    ]
    late_rows = [section.reshape(-1, section.shape[-1]) for section in late_rows]
    late_count = sum(section.size for section in late_rows) // 128
    late_half = -(-late_count // (16 * line)) * 8 * line
    late_full = summed(*packed_halves(late_rows, 0, late_half, 1), bits)
    every = jnp.concatenate([late_full[:late_count], early_full[:early_count]], axis=0)
    shard = lax.dynamic_slice_in_dim(every, lax.axis_index("inner") * shard_rows, shard_rows, 0)
    grad_shard = shard.astype(jnp.float32)
    squares = jnp.sum(jnp.square(late_full.astype(jnp.float32))) + jnp.sum(
        jnp.square(early_full.astype(jnp.float32))
    )
    grad_norm = jnp.sqrt(squares)
    clipped = grad_shard / jnp.maximum(grad_norm, 1.0)
    moment_one = BETA_ONE * first_moment.reshape(-1, 128) + (1.0 - BETA_ONE) * clipped
    moment_two = BETA_TWO * second_moment.reshape(-1, 128) + (1.0 - BETA_TWO) * clipped * clipped
    shard_len = first_moment.shape[0]
    own_weights = lax.dynamic_slice_in_dim(
        weights, lax.axis_index("inner") * shard_len, shard_len, 0
    ).astype(jnp.float32)
    update = moment_one / FIX_ONE / (jnp.sqrt(moment_two / FIX_TWO) + 1e-08) + DECAY * own_weights.reshape(-1, 128)
    inner = lax.axis_size("inner")
    piece_rows = -(-shard_rows // 32) * 32
    mine = jnp.pad(update.astype(jnp.bfloat16), ((0, piece_rows - shard_rows), (0, 0)))
    bit = 2
    while bit < inner:
        mine = jnp.concatenate([mine, relayed(mine, bit, inner)], axis=0)
        bit = 2 * bit
    other = swapped(mine, 1)
    weight_step = joined(
        mine.reshape(-1, piece_rows, 128), other.reshape(-1, piece_rows, 128), lax.axis_index("inner"), shard_rows
    ).reshape(-1)
    return (
        layer_output,
        input_grad,
        grad_shard.reshape(-1),
        grad_norm,
        moment_one.reshape(-1),
        moment_two.reshape(-1),
        weight_step,
    )


def solution(mesh):
    return jax.shard_map(
        on_device,
        mesh=mesh,
        in_specs=(
            P(("outer", "inner"), None),
            P(),
            P(("outer", "inner"), None),
            P(),
            P("inner"),
            P("inner"),
        ),
        out_specs=(
            P(("outer", "inner"), None),
            P(("outer", "inner"), None),
            P("inner"),
            P(),
            P("inner"),
            P("inner"),
            P(),
        ),
        check_vma=False,
    )
```

```python
import functools
import math

import jax
import jax.numpy as jnp
from jax import lax
from jax.experimental import pallas as pl
from jax.experimental.pallas import tpu as pltpu
from jax.sharding import PartitionSpec as P

D = 512
HEADS = 8
FF = 2048
MOST = 1500


BETA_ONE = 0.9
BETA_TWO = 0.999
FIX_ONE = 1.0 - (0.9**10) ** 10
FIX_TWO = 1.0 - (0.999**10) ** 10
DECAY = 0.1
INV_ROOT_TWO = 1.0 / math.sqrt(2.0)
INV_ROOT_TWO_PI = 1.0 / math.sqrt(2.0 * math.pi)


def layouts():
    return [
        (D,),
        (D,),
        (D, D),
        (D,),
        (D, D),
        (D, D),
        (D,),
        (D, D),
        (D,),
        (D,),
        (D,),
        (D, FF),
        (FF,),
        (FF, D),
        (D,),
    ]


def unpack(flat):
    sections = []
    offset = 0
    for layout in layouts():
        entries = 1
        for extent in layout:
            entries = entries * extent
        section = flat[offset : offset + entries].reshape(layout)
        if len(layout) == 1:
            section = section.astype(jnp.float32)
        sections.append(section)
        offset = offset + entries
    return sections


def plain_dot(matrix_one, matrix_two):
    return jnp.dot(matrix_one, matrix_two, preferred_element_type=jnp.float32)


def rows_dot(matrix_one, matrix_two):
    return lax.dot_general(
        matrix_one, matrix_two, (((0,), (0,)), ((), ())), preferred_element_type=jnp.float32
    )


def back_dot(matrix_one, matrix_two):
    return lax.dot_general(
        matrix_one, matrix_two, (((1,), (1,)), ((), ())), preferred_element_type=jnp.float32
    )


def standard(values):
    center = jnp.mean(values, axis=-1, keepdims=True)
    centered = values - center
    inverse_dev = lax.rsqrt(jnp.mean(centered * centered, axis=-1, keepdims=True) + 1e-05)
    return (centered * inverse_dev, inverse_dev)


def norm_back(grad_normed, normed_hat, inverse_dev, gain):
    scaled = grad_normed * gain
    return inverse_dev * (
        scaled
        - jnp.mean(scaled, axis=-1, keepdims=True)
        - normed_hat * jnp.mean(scaled * normed_hat, axis=-1, keepdims=True)
    )


def bounds(positions, clip_lengths):
    starts = jnp.cumsum(clip_lengths, dtype=jnp.int32) - clip_lengths
    member = (
        jnp.sum((positions[:, None] >= starts[None, :]).astype(jnp.int32), axis=1, dtype=jnp.int32)
        - 1
    )
    onehot = (
        jnp.arange(clip_lengths.shape[0], dtype=jnp.int32)[None, :] == member[:, None]
    ).astype(jnp.int32)
    lower_slot = jnp.sum(onehot * starts[None, :], axis=1, dtype=jnp.int32)
    upper_slot = lower_slot + jnp.sum(onehot * clip_lengths[None, :], axis=1, dtype=jnp.int32)
    return (lower_slot, upper_slot)


LINE = ("outer", "inner")
NEG = -1e30


def shifted(block, distance):
    n = lax.axis_size(LINE)
    return lax.ppermute(block, LINE, [(i + distance, i) for i in range(n) if 0 <= i + distance < n])


def swapped(block, bit):
    n = lax.axis_size(LINE)
    return lax.ppermute(block, LINE, [(i ^ bit, i) for i in range(n)])


def halo(block):
    n = lax.axis_size(LINE)
    partner = swapped(block, 1)
    left = shifted(block, -2)
    right = shifted(block, 2)
    route = [(i + (3 if i % 2 else -3), i) for i in range(n)]
    far = lax.ppermute(block, LINE, [(s, t) for s, t in route if 0 <= s < n])
    return [block, partner, left, right, swapped(left, 1), swapped(right, 1), far]


def slot_table():
    odd = lax.axis_index(LINE) % 2
    even_slots = jnp.array([6, 2, 4, 0, 1, 3, 5], jnp.int32)
    odd_slots = jnp.array([4, 2, 1, 0, 5, 3, 6], jnp.int32)
    return jnp.where(odd == 1, odd_slots, even_slots)


def dot_nt(a, b):
    return lax.dot_general(a, b, (((1,), (1,)), ((), ())), preferred_element_type=jnp.float32)


def head_halves(pair):
    first = lax.broadcasted_iota(jnp.int32, pair.shape, 1) < pair.shape[1] // 2
    zero = jnp.zeros_like(pair)
    return jnp.where(first, pair, zero), jnp.where(first, zero, pair)


def over_lanes(tile, op):
    parts = [tile[:, 128 * j : 128 * (j + 1)] for j in range(tile.shape[1] // 128)]
    while len(parts) > 1:
        rest = parts[len(parts) // 2 * 2 :]
        parts = [op(parts[2 * j], parts[2 * j + 1]) for j in range(len(parts) // 2)] + rest
    return parts[0]


def tile_mask(block, shape, low, high):
    place = block * shape[1] + lax.broadcasted_iota(jnp.int32, shape, 1)
    return (place >= low) & (place < high)


def forward_kernel(rows_at, first_ref, last_ref, slot_ref, q_ref, k_ref, v_ref, low_ref, high_ref, o_ref, lse_ref, s_ref):
    width = q_ref.shape[0]
    for i in range(width // rows_at):
        rows = pl.ds(i * rows_at, rows_at)
        queries = head_halves(q_ref[rows, :] * jnp.bfloat16(0.125))
        low, high = low_ref[rows, :], high_ref[rows, :]

        def scores(block, peaks):
            keys = k_ref[pl.ds(pl.multiple_of(slot_ref[block] * width, width), width), :]
            mask = tile_mask(block, (rows_at, width), low, high)
            found = []
            for h in range(2):
                score = jnp.where(mask, dot_nt(queries[h], keys), NEG)
                s_ref[h, block] = score
                found.append(jnp.maximum(peaks[h], over_lanes(score, jnp.maximum)))
            return tuple(found)

        start = jnp.full((rows_at, 128), NEG, jnp.float32)
        peaks = lax.fori_loop(first_ref[i], last_ref[i], scores, (start, start))
        peaks = [jnp.max(peak, axis=1, keepdims=True) for peak in peaks]

        def mix(block, carried):
            values = v_ref[pl.ds(pl.multiple_of(slot_ref[block] * width, width), width), :]
            totals, sums = [], []
            for h in range(2):
                soft = jnp.exp(s_ref[h, block] - peaks[h])
                totals.append(carried[0][h] + over_lanes(soft, jnp.add))
                sums.append(carried[1][h] + jnp.dot(soft.astype(jnp.bfloat16), values, preferred_element_type=jnp.float32))
            return tuple(totals), tuple(sums)

        zero = jnp.zeros((rows_at, 128), jnp.float32)
        totals, sums = lax.fori_loop(first_ref[i], last_ref[i], mix, ((zero, zero), (zero, zero)))
        totals = [jnp.sum(total, axis=1, keepdims=True) for total in totals]
        even = lax.broadcasted_iota(jnp.int32, (rows_at, 128), 1) < 64
        o_ref[rows, :] = jnp.where(even, sums[0] / totals[0], sums[1] / totals[1])
        lse_ref[rows, :] = jnp.where(even, peaks[0] + jnp.log(totals[0]), peaks[1] + jnp.log(totals[1]))


def query_kernel(
    rows_at, first_ref, last_ref, slot_ref, q_ref, k_ref, v_ref, g_ref, lse_ref, delta_ref, low_ref, high_ref, dq_ref
):
    width = q_ref.shape[0]
    for i in range(width // rows_at):
        rows = pl.ds(i * rows_at, rows_at)
        queries = head_halves(q_ref[rows, :] * jnp.bfloat16(0.125))
        grads = head_halves(g_ref[rows, :])
        low, high = low_ref[rows, :], high_ref[rows, :]
        lse = [lse_ref[rows, 64 * h : 64 * h + 1] for h in range(2)]
        delta = [delta_ref[rows, 64 * h : 64 * h + 1] for h in range(2)]

        def step(block, carried):
            at = pl.ds(pl.multiple_of(slot_ref[block] * width, width), width)
            keys, values = k_ref[at, :], v_ref[at, :]
            mask = tile_mask(block, (rows_at, width), low, high)
            found = []
            for h in range(2):
                soft = jnp.exp(jnp.where(mask, dot_nt(queries[h], keys) - lse[h], NEG))
                grad = (soft * (dot_nt(grads[h], values) - delta[h])).astype(jnp.bfloat16)
                found.append(carried[h] + jnp.dot(grad, keys, preferred_element_type=jnp.float32))
            return tuple(found)

        zero = jnp.zeros((rows_at, 128), jnp.float32)
        sums = lax.fori_loop(first_ref[i], last_ref[i], step, (zero, zero))
        even = lax.broadcasted_iota(jnp.int32, (rows_at, 128), 1) < 64
        dq_ref[rows, :] = (jnp.where(even, sums[0], sums[1]) * 0.125).astype(jnp.bfloat16)


def key_kernel(
    rows_at, first_ref, last_ref, slot_ref, k_ref, v_ref, q_ref, g_ref, low_ref, high_ref, dk_ref, dv_ref
):
    width = k_ref.shape[0]
    sent = width + stat_rows(width)
    for i in range(width // rows_at):
        rows = pl.ds(i * rows_at, rows_at)
        keys = head_halves(k_ref[rows, :] * jnp.bfloat16(0.125))
        values = head_halves(v_ref[rows, :])
        low, high = low_ref[rows, :], high_ref[rows, :]

        def step(block, carried):
            slot = slot_ref[block]
            at = pl.ds(pl.multiple_of(slot * width, width), width)
            queries = q_ref[at, :]
            grads = g_ref[pl.ds(pl.multiple_of(slot * sent, 16), width), :]
            packed = g_ref[pl.ds(pl.multiple_of(slot * sent + width, 16), sent - width), :].astype(jnp.float32)
            mask = tile_mask(block, (rows_at, width), low, high)
            key_sums, value_sums = [], []
            for h in range(2):
                lse = unpacked_stat(packed, h, width)
                delta = unpacked_stat(packed, 2 + h, width)
                soft = jnp.exp(jnp.where(mask, dot_nt(keys[h], queries) - lse, NEG))
                value_sums.append(
                    carried[1][h] + jnp.dot(soft.astype(jnp.bfloat16), grads, preferred_element_type=jnp.float32)
                )
                grad = (soft * (dot_nt(values[h], grads) - delta)).astype(jnp.bfloat16)
                key_sums.append(carried[0][h] + jnp.dot(grad, queries, preferred_element_type=jnp.float32))
            return tuple(key_sums), tuple(value_sums)

        zero = jnp.zeros((rows_at, 128), jnp.float32)
        key_sums, value_sums = lax.fori_loop(first_ref[i], last_ref[i], step, ((zero, zero), (zero, zero)))
        even = lax.broadcasted_iota(jnp.int32, (rows_at, 128), 1) < 64
        dk_ref[rows, :] = (jnp.where(even, key_sums[0], key_sums[1]) * 0.125).astype(jnp.bfloat16)
        dv_ref[rows, :] = jnp.where(even, value_sums[0], value_sums[1]).astype(jnp.bfloat16)


def stat_rows(width):
    return -(-12 * (width // 128) // 16) * 16


def unpacked_stat(packed, which, width):
    pieces = width // 128
    parts = []
    for j in range(pieces):
        at = [(3 * which + part) * pieces + j for part in range(3)]
        parts.append(packed[at[0] : at[0] + 1] + packed[at[1] : at[1] + 1] + packed[at[2] : at[2] + 1])
    return jnp.concatenate(parts, axis=1)


def mixed_grad_kernel(branch_ref, weight_ref, mixed_ref, lse_ref, sent_ref, delta_ref):
    width = branch_ref.shape[0]
    grad = dot_nt(branch_ref[...], weight_ref[...]).astype(jnp.bfloat16)
    sent_ref[pl.ds(0, width), :] = grad
    product = grad.astype(jnp.float32) * mixed_ref[...]
    even = lax.broadcasted_iota(jnp.int32, product.shape, 1) < 64
    sums = [jnp.sum(part, axis=1, keepdims=True) for part in head_halves(product)]
    delta = jnp.where(even, sums[0], sums[1])
    delta_ref[...] = delta
    rows = []
    for kept in (lse_ref[...], delta):
        turned = kept.T
        for h in range(2):
            row = turned[64 * h : 64 * h + 1, :]
            for _ in range(3):
                part = row.astype(jnp.bfloat16).astype(jnp.float32)
                row = row - part
                rows.extend(part[:, 128 * j : 128 * (j + 1)] for j in range(width // 128))
    spare = stat_rows(width) - len(rows)
    if spare:
        rows.append(jnp.zeros((spare, 128), jnp.float32))
    sent_ref[pl.ds(width, stat_rows(width)), :] = jnp.concatenate(rows, axis=0).astype(jnp.bfloat16)


def mixed_grad(branch, out_weight, mixed, lse):
    width = branch.shape[0]
    column = pl.BlockSpec((width, 128), lambda h: (0, h))
    return pl.pallas_call(
        mixed_grad_kernel,
        name="mixed_grad",
        grid=(D // 128,),
        in_specs=[
            pl.BlockSpec((width, D), lambda h: (0, 0)),
            pl.BlockSpec((128, D), lambda h: (h, 0)),
            column,
            column,
        ],
        out_specs=[pl.BlockSpec((width + stat_rows(width), 128), lambda h: (0, h)), column],
        out_shape=[
            jax.ShapeDtypeStruct((width + stat_rows(width), D), jnp.bfloat16),
            jax.ShapeDtypeStruct((width, D), jnp.float32),
        ],
        cost_estimate=pl.CostEstimate(flops=2 * width * D * D, bytes_accessed=6 * 2**20, transcendentals=0),
    )(branch, out_weight, mixed, lse)


ROWS_AT = 256


def attend(kernel, name, ranges, operands, results, scratch, dots, pairs=(0, D // 128), after=()):
    begin, count = pairs
    specs = []
    for array, (kind, at) in operands:
        if kind == "own":
            specs.append(pl.BlockSpec((ranges[3], 128), lambda h, *_, at=at + begin: (0, at + h)))
        elif kind == "window":
            specs.append(pl.BlockSpec((array.shape[0], 128), lambda h, *_, at=at + begin: (0, at + h)))
        else:
            specs.append(pl.BlockSpec(array.shape, lambda h, *_, n=array.ndim: (0,) * n))
    tok_rows = ranges[3]
    specs = specs + [pl.BlockSpec(memory_space=pl.ANY)] * len(after)

    def body(*refs):
        kernel(ROWS_AT, *refs[: 3 + len(operands)], *refs[3 + len(operands) + len(after) :])

    return pl.pallas_call(
        body,
        name=name,
        grid_spec=pltpu.PrefetchScalarGridSpec(
            num_scalar_prefetch=3,
            grid=(count,),
            in_specs=specs,
            out_specs=[pl.BlockSpec((tok_rows, 128), lambda h, *_: (0, h))] * len(results),
            scratch_shapes=scratch,
        ),
        out_shape=[jax.ShapeDtypeStruct((tok_rows, 128 * count), kept) for kept in results],
        compiler_params=pltpu.CompilerParams(vmem_limit_bytes=48 * 2**20),
        cost_estimate=pl.CostEstimate(
            flops=dots * 8 * tok_rows * 2048 * 128 * count,
            bytes_accessed=count * 3 * 2**20,
            transcendentals=tok_rows * 4096 * count,
        ),
    )(*ranges[:3], *[array for array, _ in operands], *after)


VECTOR = pltpu.VMEM
ANY = pl.ANY


def halves_rows(shard_rows):
    return -(-shard_rows // 128) * 64


def unpack_kernel(plan, shard_rows, flat_ref, *refs):
    wide_ref = refs[-1]
    padded_ref = refs[-2]
    total = flat_ref.shape[0]
    chunk = 432

    def widen(i, _):
        rows = pl.ds(pl.multiple_of(i * chunk, 16), chunk)
        wide_ref[rows, :] = flat_ref[rows, :].astype(jnp.float32)
        return 0

    lax.fori_loop(0, total // chunk, widen, 0)
    wide_ref[pl.ds(total, wide_ref.shape[0] - total), :] = jnp.zeros((wide_ref.shape[0] - total, 128), jnp.float32)
    for (offset, rows, columns, begin), ref in zip(plan, refs[:-2]):
        pieces = columns // 128
        if rows == 1:
            for j in range(pieces):
                ref[:, 128 * j : 128 * (j + 1)] = wide_ref[pl.ds(offset + j, 1), :]
            continue

        def matrix(i, _):
            at = pl.multiple_of(i * 64, 64)
            for j in range(pieces):
                part = wide_ref[pl.ds(offset + j + at * pieces, 64, stride=pieces), :]
                ref[pl.ds(at, 64), begin + 128 * j : begin + 128 * (j + 1)] = part.astype(jnp.bfloat16)
            return 0

        lax.fori_loop(0, rows // 64, matrix, 0)
    shards = total // shard_rows
    half = halves_rows(shard_rows)
    for s in range(shards):
        for h in range(2):

            def pad(i, _):
                part = wide_ref[pl.ds(s * shard_rows + h * half + i * 64, 64), :]
                padded_ref[s * 2 + h, pl.ds(pl.multiple_of(i * 64, 64), 64), :] = part.astype(jnp.bfloat16)
                return 0

            lax.fori_loop(0, half // 64, pad, 0)


def unpacked(weights, shard_rows):
    flat = weights.reshape(-1, 128)
    half = halves_rows(shard_rows)
    plan, outs, targets = [], [], []
    offset = 0
    for layout in layouts():
        rows, columns = layout if len(layout) == 2 else (1, layout[0])
        plan.append([offset, rows, columns, 0])
        outs.append(jax.ShapeDtypeStruct((rows, columns), jnp.bfloat16 if rows > 1 else jnp.float32))
        offset = offset + rows * columns // 128
    shards = flat.shape[0] // shard_rows
    outs.append(jax.ShapeDtypeStruct((2 * shards, half, 128), jnp.bfloat16))
    return pl.pallas_call(
        functools.partial(unpack_kernel, plan, shard_rows),
        name="unpack",
        in_specs=[pl.BlockSpec(memory_space=VECTOR)],
        out_specs=[pl.BlockSpec(memory_space=VECTOR)] * len(outs),
        out_shape=outs,
        scratch_shapes=[VECTOR((flat.shape[0] + 2 * half, 128), jnp.float32)],
        compiler_params=pltpu.CompilerParams(vmem_limit_bytes=60 * 2**20),
        cost_estimate=pl.CostEstimate(flops=0, bytes_accessed=24 * 2**20, transcendentals=0),
    )(flat)


def pack_kernel(plan, spans, half, place_ref, *refs):
    count = len(plan)
    keep_ref, give_ref, flat_ref, out_ref, sems = refs[-5:]
    end = max(offset + rows * columns // 128 for offset, rows, columns in plan)
    begin = min(offset for offset, _, _ in plan)
    if begin:
        flat_ref[pl.ds(0, begin), :] = jnp.zeros((begin, 128), jnp.float32)
    for (offset, rows, columns), ref in zip(plan, refs[:count]):
        pieces = columns // 128
        if rows == 1:
            for j in range(pieces):
                flat_ref[pl.ds(offset + j, 1), :] = ref[:, 128 * j : 128 * (j + 1)]
            continue

        def matrix(i, _):
            at = pl.multiple_of(i * 64, 64)
            for j in range(pieces):
                flat_ref[pl.ds(offset + j + at * pieces, 64, stride=pieces), :] = ref[pl.ds(at, 64), 128 * j : 128 * (j + 1)]
            return 0

        lax.fori_loop(0, rows // 64, matrix, 0)
    for h in range(2):
        at = h ^ place_ref[0]
        filled = 0
        for source, rows, room in spans[h]:
            whole = rows // 64

            def move(i, _):
                to = pl.ds(pl.multiple_of(filled + i * 64, 16), 64)
                out_ref[at, to, :] = flat_ref[pl.ds(source + i * 64, 64), :].astype(jnp.bfloat16)
                return 0

            lax.fori_loop(0, whole, move, 0)
            rest = rows - 64 * whole
            tail = room - 64 * whole
            if tail:
                parts = []
                if rest:
                    parts.append(flat_ref[pl.ds(source + 64 * whole, rest), :])
                if tail > rest:
                    parts.append(jnp.zeros((tail - rest, 128), jnp.float32))
                last = parts[0] if len(parts) == 1 else jnp.concatenate(parts, axis=0)
                out_ref[at, pl.ds(filled + 64 * whole, tail), :] = last.astype(jnp.bfloat16)
            filled = filled + room
    copies = [
        pltpu.make_async_copy(out_ref.at[0], keep_ref, sems.at[0]),
        pltpu.make_async_copy(out_ref.at[1], give_ref, sems.at[1]),
    ]
    for copy in copies:
        copy.start()
    for copy in copies:
        copy.wait()


def packed_halves(grads, begin, spans, half):
    plan = []
    offset = begin
    for grad in grads:
        plan.append((offset, *grad.shape))
        offset = offset + grad.shape[0] * grad.shape[1] // 128
    return pl.pallas_call(
        functools.partial(pack_kernel, plan, spans, half),
        name="pack",
        in_specs=[pl.BlockSpec(memory_space=pltpu.SMEM)] + [pl.BlockSpec(memory_space=VECTOR)] * len(grads),
        out_specs=[pl.BlockSpec(memory_space=ANY)] * 2,
        out_shape=[jax.ShapeDtypeStruct((half, 128), jnp.bfloat16)] * 2,
        scratch_shapes=[
            VECTOR((offset, 128), jnp.float32),
            VECTOR((2, half, 128), jnp.bfloat16),
            pltpu.SemaphoreType.DMA((2,)),
        ],
        compiler_params=pltpu.CompilerParams(vmem_limit_bytes=60 * 2**20),
        cost_estimate=pl.CostEstimate(flops=0, bytes_accessed=offset * 768, transcendentals=0),
    )(bit_of(1).reshape(1), *grads)


def combine_kernel(count, places_ref, *refs):
    parts, outs = refs[:count], refs[-places_ref.shape[0] :]
    rows = outs[0].shape[0]
    for k, out in enumerate(outs):
        at = pl.ds(pl.multiple_of(places_ref[k] * rows, 16), rows)
        terms = [part[at, :].astype(jnp.float32) for part in parts]
        while len(terms) > 1:
            terms = [terms[2 * j] + terms[2 * j + 1] for j in range(len(terms) // 2)]
        out[...] = terms[0].astype(jnp.bfloat16)


def places_of(group):
    if not group:
        return jnp.zeros((1,), jnp.int32)
    place = (lax.axis_index(LINE) // group[0]) % (1 << len(group))
    return place ^ jnp.arange(1 << len(group), dtype=jnp.int32)


def combine(parts, group, after):
    count = 1 << len(group)
    rows = parts[0].shape[0] // count
    outs = pl.pallas_call(
        functools.partial(combine_kernel, len(parts)),
        name="combine",
        in_specs=[pl.BlockSpec(memory_space=pltpu.SMEM)]
        + [pl.BlockSpec(memory_space=VECTOR)] * len(parts)
        + [pl.BlockSpec(memory_space=ANY)] * len(after),
        out_specs=[pl.BlockSpec(memory_space=VECTOR)] * count,
        out_shape=[jax.ShapeDtypeStruct((rows, 128), jnp.bfloat16)] * count,
        cost_estimate=pl.CostEstimate(flops=0, bytes_accessed=rows * count * 256 * (len(parts) + 1), transcendentals=0),
    )(places_of(group), *parts, *after)
    return list(outs)


def stack_kernel(count, places_ref, *refs):
    out_ref = refs[-1]
    rows = refs[0].shape[0]
    for k in range(count):
        out_ref[pl.ds(pl.multiple_of(places_ref[k] * rows, 16), rows), :] = refs[k][...]


def stack(parts, group, after):
    rows = parts[0].shape[0] * len(parts)
    return pl.pallas_call(
        functools.partial(stack_kernel, len(parts)),
        name="stack",
        in_specs=[pl.BlockSpec(memory_space=pltpu.SMEM)]
        + [pl.BlockSpec(memory_space=VECTOR)] * len(parts)
        + [pl.BlockSpec(memory_space=ANY)] * len(after),
        out_specs=pl.BlockSpec(memory_space=VECTOR),
        out_shape=jax.ShapeDtypeStruct((rows, 128), jnp.bfloat16),
        cost_estimate=pl.CostEstimate(flops=0, bytes_accessed=rows * 512, transcendentals=0),
    )(places_of(group), *parts, *after)


def exchanged(parts, group):
    return [parts[0]] + [swapped(parts[k % len(parts)], group[0] * k) for k in range(1, 1 << len(group))]


def bit_groups():
    bits = [1 << k for k in range(1, lax.axis_size(LINE).bit_length() - 1)]
    return [bits[k : k + 2] for k in range(0, len(bits), 2)]


def update_kernel(
    shards, late, meta_ref, norm_ref, early_own, early_other, late_own, late_other, extra_own, extra_other, weight_ref,
    one_ref, two_ref, *refs
):
    moments = refs[: 2 * shards]
    step_ref, grad_ref, new_one_ref, new_two_ref, sum_ref = refs[2 * shards :]
    which, k = pl.program_id(0), pl.program_id(1)
    core, me, turn = meta_ref[0], meta_ref[1], meta_ref[2]
    shard = me ^ k
    half = core ^ which
    rows = sum_ref.shape[0]
    steps = rows // 64
    scale = norm_ref[0]

    def load(ref, lead=None):
        def move(i, _):
            at = pl.ds(pl.multiple_of(i * 64, 64), 64)
            sum_ref[at, :] = ref[at, :].astype(jnp.float32)
            return 0

        lax.fori_loop(0, steps, move, 0)

    for array, side, is_late in ((early_own, 0, 0), (early_other, 1, 0), (late_own, 0, 1), (late_other, 1, 1)):
        pl.when((which == side) & ((shard < late) == (is_late == 1)))(functools.partial(load, array))
    for array, side in ((extra_own, 0), (extra_other, 1)):

        @pl.when((which == side) & (shard == late) & (half == 0))
        def _():
            sum_ref[pl.ds(0, 8), :] = sum_ref[pl.ds(0, 8), :] + array[pl.ds(0, 8), :].astype(jnp.float32)

    def moved(grad, one, two):
        clipped = grad / scale
        one = BETA_ONE * one + (1.0 - BETA_ONE) * clipped
        two = BETA_TWO * two + (1.0 - BETA_TWO) * clipped * clipped
        return one, two

    for j in range(shards):

        @pl.when(k == j)
        def _():
            def move(i, _):
                at = pl.ds(pl.multiple_of(i * 64, 64), 64)
                one, two = moments[2 * j][at, :], moments[2 * j + 1][at, :]
                if j >= 2:
                    one, two = jnp.where(turn == 1, two, one), jnp.where(turn == 1, one, two)
                one, two = moved(sum_ref[at, :], one.astype(jnp.float32), two.astype(jnp.float32))
                update = one / FIX_ONE / (jnp.sqrt(two / FIX_TWO) + 1e-08)
                update = update + DECAY * weight_ref[0, at, :].astype(jnp.float32)
                step_ref[0, at, :] = update.astype(jnp.bfloat16)
                return 0

            lax.fori_loop(0, steps, move, 0)

    @pl.when(k == 0)
    def _():
        def move(i, _):
            at = pl.ds(pl.multiple_of(i * 64, 64), 64)
            grad = sum_ref[at, :]
            one, two = moved(grad, one_ref[at, :], two_ref[at, :])
            grad_ref[at, :] = grad
            new_one_ref[at, :] = one
            new_two_ref[at, :] = two
            return 0

        lax.fori_loop(0, steps, move, 0)


def updated(norm, early, late, late_shards, weights, first_moment, second_moment, moments):
    shards = len(moments) // 2
    rows = weights.shape[1]
    shard_rows = first_moment.shape[0] // 128
    line = lax.axis_index(LINE)
    inner = lax.axis_size("inner")
    meta = jnp.stack([line % 2, lax.axis_index("inner"), (line // inner) % 2]).astype(jnp.int32)
    last = shards - 1

    def early_map(side):
        def index(w, k, meta):
            k = jnp.where(w == side, k, last if side == 0 else 0)
            return (jnp.clip((meta[1] ^ k) - late_shards, 0, shards - late_shards - 1), 0)

        return index

    def late_map(side):
        def index(w, k, meta):
            k = jnp.where(w == side, k, last if side == 0 else 0)
            return (jnp.clip(meta[1] ^ k, 0, late_shards - 1), 0)

        return index

    by_half = pl.BlockSpec((rows, 128), lambda w, k, meta: (meta[0] ^ w, 0))
    by_shard = pl.BlockSpec((1, rows, 128), lambda w, k, meta: (2 * (meta[1] ^ k) + (meta[0] ^ w), 0, 0))
    extra = pl.BlockSpec((16, 128), lambda w, k, meta: (late_shards * rows // 16, 0))
    return pl.pallas_call(
        functools.partial(update_kernel, shards, late_shards),
        name="update",
        grid_spec=pltpu.PrefetchScalarGridSpec(
            num_scalar_prefetch=1,
            grid=(2, shards),
            in_specs=[pl.BlockSpec(memory_space=pltpu.SMEM)]
            + [pl.BlockSpec((rows, 128), early_map(side)) for side in range(2)]
            + [pl.BlockSpec((rows, 128), late_map(side)) for side in range(2)]
            + [extra, extra, by_shard, by_half, by_half]
            + [by_half] * (2 * shards),
            out_specs=[by_shard, by_half, by_half, by_half],
            scratch_shapes=[VECTOR((rows, 128), jnp.float32)],
        ),
        out_shape=[jax.ShapeDtypeStruct((2 * shards, rows, 128), jnp.bfloat16)]
        + [jax.ShapeDtypeStruct((shard_rows, 128), jnp.float32)] * 3,
        compiler_params=pltpu.CompilerParams(vmem_limit_bytes=60 * 2**20),
        cost_estimate=pl.CostEstimate(flops=0, bytes_accessed=44 * 2**20, transcendentals=0),
    )(
        meta,
        norm.reshape(1),
        *early,
        *late,
        *late,
        weights,
        first_moment.reshape(-1, 128),
        second_moment.reshape(-1, 128),
        *moments,
    )


def join_kernel(shard_rows, step_ref, out_ref, wide_ref):
    count, rows, _ = step_ref.shape
    for s in range(count):
        base = s // 2 * shard_rows + s % 2 * rows

        def widen(i, _):
            at = pl.multiple_of(i * 64, 64)
            wide_ref[pl.ds(base + at, 64), :] = step_ref[s, pl.ds(at, 64), :].astype(jnp.float32)
            return 0

        lax.fori_loop(0, rows // 64, widen, 0)
    chunk = 432

    def narrow(i, _):
        at = pl.ds(pl.multiple_of(i * chunk, 16), chunk)
        out_ref[at, :] = wide_ref[at, :].astype(jnp.bfloat16)
        return 0

    lax.fori_loop(0, out_ref.shape[0] // chunk, narrow, 0)


def joined(steps, shard_rows):
    count, rows, _ = steps.shape
    total = count // 2 * shard_rows
    return pl.pallas_call(
        functools.partial(join_kernel, shard_rows),
        name="join",
        in_specs=[pl.BlockSpec(memory_space=VECTOR)],
        out_specs=pl.BlockSpec(memory_space=VECTOR),
        out_shape=jax.ShapeDtypeStruct((total, 128), steps.dtype),
        scratch_shapes=[VECTOR((total + 2 * rows, 128), jnp.float32)],
        compiler_params=pltpu.CompilerParams(vmem_limit_bytes=48 * 2**20),
        cost_estimate=pl.CostEstimate(flops=0, bytes_accessed=total * 512, transcendentals=0),
    )(steps)


def narrow_kernel(one_ref, two_ref, after_ref, one_out, two_out):
    shape = one_out.shape
    begin = pl.program_id(0) * shape[0]
    inside = begin + lax.broadcasted_iota(jnp.int32, shape, 0) < after_ref[0]
    one_out[...] = jnp.where(inside, one_ref[...], 0.0).astype(jnp.bfloat16)
    two_out[...] = jnp.where(inside, two_ref[...], 0.0).astype(jnp.bfloat16)


def narrowed(one, two, half, count):
    block = pl.BlockSpec((half // 7 if half % 7 == 0 else half, 128), lambda i: (i, 0))
    return pl.pallas_call(
        narrow_kernel,
        name="narrow",
        grid=(2 * half // block.block_shape[0],),
        in_specs=[block, block, pl.BlockSpec(memory_space=pltpu.SMEM)],
        out_specs=[block, block],
        out_shape=[jax.ShapeDtypeStruct((2 * half, 128), jnp.bfloat16)] * 2,
        cost_estimate=pl.CostEstimate(flops=0, bytes_accessed=half * 3072, transcendentals=0),
    )(one, two, count)


def bit_of(bit):
    return (lax.axis_index(LINE) // bit) % 2


def on_device(inputs, weights, cotangent, clip_lengths, first_moment, second_moment):
    tok_rows = inputs.shape[0]
    reach = (MOST + tok_rows - 2) // tok_rows
    head_width = D // HEADS
    shard_rows = first_moment.shape[0] // 128
    half = halves_rows(shard_rows)
    (
        first_gain,
        first_bias,
        query_weight,
        query_bias,
        key_weight,
        value_weight,
        value_bias,
        out_weight,
        out_bias,
        second_gain,
        second_bias,
        up_weight,
        up_bias,
        down_weight,
        down_bias,
        padded_weights,
    ) = unpacked(weights, shard_rows)
    base_slot = lax.axis_index(LINE) * tok_rows
    positions = base_slot + jnp.arange(tok_rows, dtype=jnp.int32)
    lower_slot, upper_slot = bounds(positions, clip_lengths)
    low = lower_slot - base_slot + reach * tok_rows
    high = upper_slot - base_slot + reach * tok_rows
    first_block = low.reshape(-1, ROWS_AT)[:, 0] // tok_rows
    last_block = (high.reshape(-1, ROWS_AT)[:, -1] + tok_rows - 1) // tok_rows
    ranges = (first_block, last_block, slot_table(), tok_rows)
    low, high = low[:, None], high[:, None]

    window = jnp.concatenate(halo(inputs), axis=0)
    window_hat, window_dev = standard(window.astype(jnp.float32))
    window_normed = (window_hat * first_gain + first_bias).astype(jnp.bfloat16)
    project = jnp.concatenate([query_weight, key_weight, value_weight], axis=1)
    shift = jnp.concatenate([query_bias, jnp.zeros((1, D), jnp.float32), value_bias], axis=1)
    rows = (plain_dot(window_normed, project) + shift).astype(jnp.bfloat16)
    count = jnp.where(rows[0, 0] == rows[0, 0], shard_rows, 0).astype(jnp.int32).reshape(1)
    own_moments = narrowed(first_moment.reshape(-1, 128), second_moment.reshape(-1, 128), half, count)
    inner = lax.axis_size("inner")
    turn = (lax.axis_index(LINE) // inner) % 2
    held = {0: own_moments}
    bit = 2
    while bit < inner:
        for place in list(held):
            one, two = held[place]
            fetched = swapped(jnp.where(turn == 1, two, one), bit) if place == 0 else swapped(one, bit)
            passed = swapped(fetched, inner) if place == 0 else swapped(two, bit)
            held[place + bit] = (fetched, passed)
        bit = 2 * bit
    moments = []
    for place in range(inner):
        if place % 2 == 0:
            moments += held[place]
        else:
            moments += [swapped(piece, 1) for piece in held[place - 1]]
    input_rows = inputs.astype(jnp.float32)
    first_hat, first_dev = standard(input_rows)
    normed = (first_hat * first_gain + first_bias).astype(jnp.bfloat16)

    attended, lse = attend(
        forward_kernel,
        "attend_forward",
        ranges,
        [
            (rows, ("own", 0)),
            (rows, ("window", 4)),
            (rows, ("window", 8)),
            (low, ("all", 0)),
            (high, ("all", 0)),
        ],
        [jnp.float32, jnp.float32],
        [pltpu.VMEM((2, 2 * reach + 1, ROWS_AT, tok_rows), jnp.float32)],
        2,
    )
    mixed = attended.astype(jnp.bfloat16)
    middle = input_rows + plain_dot(mixed, out_weight) + out_bias
    second_hat, second_dev = standard(middle)
    hidden_in = (second_hat * second_gain + second_bias).astype(jnp.bfloat16)
    up_rows = plain_dot(hidden_in, up_weight) + up_bias
    cdf_part = 0.5 * (1.0 + lax.erf(up_rows * INV_ROOT_TWO))
    activated = (up_rows * cdf_part).astype(jnp.bfloat16)
    layer_output = (middle + plain_dot(activated, down_weight) + down_bias).astype(jnp.bfloat16)
    grad_out = cotangent.astype(jnp.float32)
    down_grad = rows_dot(activated, cotangent)
    down_bias_grad = jnp.sum(grad_out, axis=0)
    grad_act = back_dot(cotangent, down_weight)
    pdf_part = jnp.exp(-0.5 * up_rows * up_rows) * INV_ROOT_TWO_PI
    grad_up = (grad_act * (cdf_part + up_rows * pdf_part)).astype(jnp.bfloat16)
    up_grad = rows_dot(hidden_in, grad_up)
    up_bias_grad = jnp.sum(grad_up.astype(jnp.float32), axis=0)
    grad_hidden = back_dot(grad_up, up_weight)
    second_gain_grad = jnp.sum(grad_hidden * second_hat, axis=0)
    second_bias_grad = jnp.sum(grad_hidden, axis=0)
    grad_middle = grad_out + norm_back(grad_hidden, second_hat, second_dev, second_gain)
    grad_branch = grad_middle.astype(jnp.bfloat16)
    out_grad = rows_dot(mixed, grad_branch)
    out_bias_grad = jnp.sum(grad_branch.astype(jnp.float32), axis=0)
    sent, delta = mixed_grad(grad_branch, out_weight, attended, lse)
    grad_window = jnp.concatenate(halo(sent), axis=0)

    line = lax.axis_size(LINE)
    shards = inner
    late_shards = shards // 4
    groups = bit_groups()

    def rounded(count, unit):
        return -(-count // unit) * unit

    def shard_spans(first, last, base):
        spans = ([], [])
        for shard in range(first, last):
            begin = (shard - first) * shard_rows + base
            spans[0].append((begin, half, half))
            spans[1].append((begin + half, shard_rows - half, half))
        return spans

    early_rows = [
        out_grad,
        out_bias_grad,
        second_gain_grad,
        second_bias_grad,
        up_grad,
        up_bias_grad,
        down_grad,
        down_bias_grad,
    ]
    early_rows = [section.reshape(-1, section.shape[-1]) for section in early_rows]
    early_half = rounded((shards - late_shards) * half, 8 * line)
    spans = shard_spans(late_shards, shards, 0)
    for span in spans:
        span.append((0, 0, early_half - (shards - late_shards) * half))
    early_keep, early_give = packed_halves(early_rows, D // 128, spans, early_half)
    early_got = swapped(early_give, 1)

    def query_step(pairs, after):
        return attend(
            query_kernel,
            "attend_query",
            ranges,
            [
                (rows, ("own", 0)),
                (rows, ("window", 4)),
                (rows, ("window", 8)),
                (sent, ("own", 0)),
                (lse, ("own", 0)),
                (delta, ("own", 0)),
                (low, ("all", 0)),
                (high, ("all", 0)),
            ],
            [jnp.bfloat16],
            [],
            3,
            pairs,
            after,
        )

    def key_step(pairs, after):
        return attend(
            key_kernel,
            "attend_key",
            ranges,
            [
                (rows, ("own", 4)),
                (rows, ("own", 8)),
                (rows, ("window", 0)),
                (grad_window, ("window", 0)),
                (low, ("all", 0)),
                (high, ("all", 0)),
            ],
            [jnp.bfloat16, jnp.bfloat16],
            [],
            4,
            pairs,
            after,
        )

    query_parts = query_step((0, 2), (early_give,))
    parts = combine([early_keep, early_got], groups[0], query_parts)
    got = exchanged(parts, groups[0])
    query_parts += query_step((2, 2), (parts[0],))
    query_low = jnp.concatenate(query_parts, axis=1)
    held_back = query_parts[-1:]
    key_parts, value_parts = [], []
    work = [(0, 1), (1, 1), (2, 1), (3, 1)]
    for at, group in enumerate(groups):
        parts = combine(got, groups[at + 1] if at + 1 < len(groups) else [], held_back)
        if at + 1 < len(groups):
            got = exchanged(parts, groups[at + 1])
        if work:
            done = key_step(work.pop(0), parts[:1])
            key_parts.append(done[0])
            value_parts.append(done[1])
            held_back = done[:1]
    piece = parts[0]
    for at, group in enumerate(groups[::-1]):
        got = exchanged([piece], group)
        if work and at > 0:
            done = key_step(work.pop(0), [piece])
            key_parts.append(done[0])
            value_parts.append(done[1])
            held_back = done[:1]
        piece = stack(got, group, held_back)
    early_other = swapped(piece, 1)
    for pairs in work:
        done = key_step(pairs, [piece])
        key_parts.append(done[0])
        value_parts.append(done[1])
    early = (piece, early_other)
    key_low = jnp.concatenate(key_parts, axis=1)
    value_low = jnp.concatenate(value_parts, axis=1)
    query_grad = rows_dot(normed, query_low)
    query_bias_grad = jnp.sum(query_low.astype(jnp.float32), axis=0)
    key_grad = rows_dot(normed, key_low)
    value_grad = rows_dot(normed, value_low)
    value_bias_grad = jnp.sum(value_low.astype(jnp.float32), axis=0)
    grad_normed = (
        back_dot(query_low, query_weight)
        + back_dot(key_low, key_weight)
        + back_dot(value_low, value_weight)
    )
    first_gain_grad = jnp.sum(grad_normed * first_hat, axis=0)
    first_bias_grad = jnp.sum(grad_normed, axis=0)
    input_grad = (grad_middle + norm_back(grad_normed, first_hat, first_dev, first_gain)).astype(
        jnp.bfloat16
    )

    late_rows = [
        first_gain_grad,
        first_bias_grad,
        query_grad,
        query_bias_grad,
        key_grad,
        value_grad,
        value_bias_grad,
    ]
    late_rows = [section.reshape(-1, section.shape[-1]) for section in late_rows]
    tail = max(1, 1 << (len(groups[0])))
    late_half = rounded(late_shards * half + 16, 16 * tail)
    spans = shard_spans(0, late_shards, 0)
    spare = late_half - late_shards * half
    spans[0].append((late_shards * shard_rows, D // 128, spare))
    spans[1].append((0, 0, spare))
    keep, give = packed_halves(late_rows, 0, spans, late_half)
    parts = combine([keep, swapped(give, 1)], groups[0], ())
    (piece,) = combine(exchanged(parts, groups[0]), [], ())
    for group in groups[1:]:
        (piece,) = combine(exchanged([piece], group), [], ())
    piece = stack(exchanged([piece], groups[0]), groups[0], ())
    late = (piece, swapped(piece, 1))

    def square_sum(pair):
        sums = [jnp.sum(jnp.square(part.astype(jnp.float32))) for part in pair]
        return sums[0] + sums[1]

    grad_norm = jnp.sqrt(square_sum(early) + square_sum(late))
    steps, grad_shard, moment_one, moment_two = updated(
        jnp.maximum(grad_norm, 1.0), early, late, late_shards, padded_weights, first_moment, second_moment, moments
    )
    weight_step = joined(steps, shard_rows).reshape(-1)
    return (
        layer_output,
        input_grad,
        grad_shard.reshape(-1),
        grad_norm,
        moment_one.reshape(-1),
        moment_two.reshape(-1),
        weight_step,
    )


def solution(mesh):
    return jax.shard_map(
        on_device,
        mesh=mesh,
        in_specs=(
            P(("outer", "inner"), None),
            P(),
            P(("outer", "inner"), None),
            P(),
            P("inner"),
            P("inner"),
        ),
        out_specs=(
            P(("outer", "inner"), None),
            P(("outer", "inner"), None),
            P("inner"),
            P(),
            P("inner"),
            P("inner"),
            P(),
        ),
        check_vma=False,
    )
```

```python
import functools
import math

import jax
import jax.numpy as jnp
from jax import lax
from jax.experimental import pallas as pl
from jax.experimental.pallas import tpu as pltpu
from jax.sharding import PartitionSpec as P

D = 512
FF = 2048
MOST = 1500


BETA_ONE = 0.9
BETA_TWO = 0.999
FIX_ONE = 1.0 - (0.9**10) ** 10
FIX_TWO = 1.0 - (0.999**10) ** 10
DECAY = 0.1
INV_ROOT_TWO = 1.0 / math.sqrt(2.0)
INV_ROOT_TWO_PI = 1.0 / math.sqrt(2.0 * math.pi)


def layouts():
    return [
        (D,),
        (D,),
        (D, D),
        (D,),
        (D, D),
        (D, D),
        (D,),
        (D, D),
        (D,),
        (D,),
        (D,),
        (D, FF),
        (FF,),
        (FF, D),
        (D,),
    ]


def plain_dot(matrix_one, matrix_two):
    return jnp.dot(matrix_one, matrix_two, preferred_element_type=jnp.float32)


def rows_dot(matrix_one, matrix_two):
    return lax.dot_general(
        matrix_one, matrix_two, (((0,), (0,)), ((), ())), preferred_element_type=jnp.float32
    )


def back_dot(matrix_one, matrix_two):
    return lax.dot_general(
        matrix_one, matrix_two, (((1,), (1,)), ((), ())), preferred_element_type=jnp.float32
    )


def standard(values):
    center = jnp.mean(values, axis=-1, keepdims=True)
    centered = values - center
    inverse_dev = lax.rsqrt(jnp.mean(centered * centered, axis=-1, keepdims=True) + 1e-05)
    return (centered * inverse_dev, inverse_dev)


def norm_back(grad_normed, normed_hat, inverse_dev, gain):
    scaled = grad_normed * gain
    return inverse_dev * (
        scaled
        - jnp.mean(scaled, axis=-1, keepdims=True)
        - normed_hat * jnp.mean(scaled * normed_hat, axis=-1, keepdims=True)
    )


def bounds(positions, clip_lengths):
    starts = jnp.cumsum(clip_lengths, dtype=jnp.int32) - clip_lengths
    member = (
        jnp.sum((positions[:, None] >= starts[None, :]).astype(jnp.int32), axis=1, dtype=jnp.int32)
        - 1
    )
    onehot = (
        jnp.arange(clip_lengths.shape[0], dtype=jnp.int32)[None, :] == member[:, None]
    ).astype(jnp.int32)
    lower_slot = jnp.sum(onehot * starts[None, :], axis=1, dtype=jnp.int32)
    upper_slot = lower_slot + jnp.sum(onehot * clip_lengths[None, :], axis=1, dtype=jnp.int32)
    return (lower_slot, upper_slot)


LINE = ("outer", "inner")
NEG = -1e30
BRIEF = pl.CostEstimate(flops=1000, bytes_accessed=1000, transcendentals=0)


def shifted(block, distance):
    n = lax.axis_size(LINE)
    return lax.ppermute(block, LINE, [(i + distance, i) for i in range(n) if 0 <= i + distance < n])


def swapped(block, bit):
    n = lax.axis_size(LINE)
    return lax.ppermute(block, LINE, [(i ^ bit, i) for i in range(n)])


def halo(block, before=()):
    n = lax.axis_size(LINE)
    left = shifted(block, -2)
    right = shifted(block, 2)
    partner = swapped(block, 1)
    route = [(i + (3 if i % 2 else -3), i) for i in range(n)]
    far = lax.ppermute(block, LINE, [(s, t) for s, t in route if 0 <= s < n])
    passed_left, passed_right, *_ = lax.optimization_barrier((left, right, *before))
    turned = [swapped(passed_left, 1), swapped(passed_right, 1)]
    return [block, partner, left, right, *turned, far]


def slot_table():
    odd = lax.axis_index(LINE) % 2
    even_slots = jnp.array([6, 2, 4, 0, 1, 3, 5], jnp.int32)
    odd_slots = jnp.array([4, 2, 1, 0, 5, 3, 6], jnp.int32)
    return jnp.where(odd == 1, odd_slots, even_slots)


def dot_nt(a, b):
    return lax.dot_general(a, b, (((1,), (1,)), ((), ())), preferred_element_type=jnp.float32)


def head_halves(pair):
    first = lax.broadcasted_iota(jnp.int32, pair.shape, 1) < pair.shape[1] // 2
    zero = jnp.zeros_like(pair)
    return jnp.where(first, pair, zero), jnp.where(first, zero, pair)


def over_lanes(tile, op):
    parts = [tile[:, 128 * j : 128 * (j + 1)] for j in range(tile.shape[1] // 128)]
    while len(parts) > 1:
        rest = parts[len(parts) // 2 * 2 :]
        parts = [op(parts[2 * j], parts[2 * j + 1]) for j in range(len(parts) // 2)] + rest
    return parts[0]


def tile_mask(block, shape, low, high):
    place = block * shape[1] + lax.broadcasted_iota(jnp.int32, shape, 1)
    return (place >= low) & (place < high)


def forward_kernel(rows_at, first_ref, last_ref, slot_ref, q_ref, k_ref, v_ref, low_ref, high_ref, o_ref, lse_ref, s_ref):
    width = q_ref.shape[0]
    for i in range(width // rows_at):
        rows = pl.ds(i * rows_at, rows_at)
        queries = head_halves(q_ref[rows, :] * jnp.bfloat16(0.125))
        low, high = low_ref[rows, :], high_ref[rows, :]

        def scores(block, peaks):
            keys = k_ref[pl.ds(pl.multiple_of(slot_ref[block] * width, width), width), :]
            mask = tile_mask(block, (rows_at, width), low, high)
            found = []
            for h in range(2):
                score = jnp.where(mask, dot_nt(queries[h], keys), NEG)
                s_ref[h, block] = score
                found.append(jnp.maximum(peaks[h], over_lanes(score, jnp.maximum)))
            return tuple(found)

        start = jnp.full((rows_at, 128), NEG, jnp.float32)
        peaks = lax.fori_loop(first_ref[i], last_ref[i], scores, (start, start))
        peaks = [jnp.max(peak, axis=1, keepdims=True) for peak in peaks]

        def mix(block, carried):
            values = v_ref[pl.ds(pl.multiple_of(slot_ref[block] * width, width), width), :]
            totals, sums = [], []
            for h in range(2):
                soft = jnp.exp(s_ref[h, block] - peaks[h])
                totals.append(carried[0][h] + over_lanes(soft, jnp.add))
                sums.append(carried[1][h] + jnp.dot(soft.astype(jnp.bfloat16), values, preferred_element_type=jnp.float32))
            return tuple(totals), tuple(sums)

        zero = jnp.zeros((rows_at, 128), jnp.float32)
        totals, sums = lax.fori_loop(first_ref[i], last_ref[i], mix, ((zero, zero), (zero, zero)))
        totals = [jnp.sum(total, axis=1, keepdims=True) for total in totals]
        even = lax.broadcasted_iota(jnp.int32, (rows_at, 128), 1) < 64
        o_ref[rows, :] = jnp.where(even, sums[0] / totals[0], sums[1] / totals[1])
        lse_ref[rows, :] = jnp.where(even, peaks[0] + jnp.log(totals[0]), peaks[1] + jnp.log(totals[1]))


def query_kernel(
    rows_at, first_ref, last_ref, slot_ref, q_ref, k_ref, v_ref, g_ref, lse_ref, delta_ref, low_ref, high_ref, dq_ref
):
    width = q_ref.shape[0]
    for i in range(width // rows_at):
        rows = pl.ds(i * rows_at, rows_at)
        queries = head_halves(q_ref[rows, :] * jnp.bfloat16(0.125))
        grads = head_halves(g_ref[rows, :])
        low, high = low_ref[rows, :], high_ref[rows, :]
        lse = [lse_ref[rows, 64 * h : 64 * h + 1] for h in range(2)]
        delta = [delta_ref[rows, 64 * h : 64 * h + 1] for h in range(2)]

        def step(block, carried):
            at = pl.ds(pl.multiple_of(slot_ref[block] * width, width), width)
            keys, values = k_ref[at, :], v_ref[at, :]
            mask = tile_mask(block, (rows_at, width), low, high)
            found = []
            for h in range(2):
                soft = jnp.exp(jnp.where(mask, dot_nt(queries[h], keys) - lse[h], NEG))
                grad = (soft * (dot_nt(grads[h], values) - delta[h])).astype(jnp.bfloat16)
                found.append(carried[h] + jnp.dot(grad, keys, preferred_element_type=jnp.float32))
            return tuple(found)

        zero = jnp.zeros((rows_at, 128), jnp.float32)
        sums = lax.fori_loop(first_ref[i], last_ref[i], step, (zero, zero))
        even = lax.broadcasted_iota(jnp.int32, (rows_at, 128), 1) < 64
        dq_ref[rows, :] = (jnp.where(even, sums[0], sums[1]) * 0.125).astype(jnp.bfloat16)


def key_kernel(
    rows_at, first_ref, last_ref, slot_ref, k_ref, v_ref, q_ref, g_ref, low_ref, high_ref, dk_ref, dv_ref
):
    width = k_ref.shape[0]
    sent = width + stat_rows(width)
    for i in range(width // rows_at):
        rows = pl.ds(i * rows_at, rows_at)
        keys = head_halves(k_ref[rows, :] * jnp.bfloat16(0.125))
        values = head_halves(v_ref[rows, :])
        low, high = low_ref[rows, :], high_ref[rows, :]

        def step(block, carried):
            slot = slot_ref[block]
            at = pl.ds(pl.multiple_of(slot * width, width), width)
            queries = q_ref[at, :]
            grads = g_ref[pl.ds(pl.multiple_of(slot * sent, 16), width), :]
            packed = g_ref[pl.ds(pl.multiple_of(slot * sent + width, 16), sent - width), :].astype(jnp.float32)
            mask = tile_mask(block, (rows_at, width), low, high)
            key_sums, value_sums = [], []
            for h in range(2):
                lse = unpacked_stat(packed, h, width)
                delta = unpacked_stat(packed, 2 + h, width)
                soft = jnp.exp(jnp.where(mask, dot_nt(keys[h], queries) - lse, NEG))
                value_sums.append(
                    carried[1][h] + jnp.dot(soft.astype(jnp.bfloat16), grads, preferred_element_type=jnp.float32)
                )
                grad = (soft * (dot_nt(values[h], grads) - delta)).astype(jnp.bfloat16)
                key_sums.append(carried[0][h] + jnp.dot(grad, queries, preferred_element_type=jnp.float32))
            return tuple(key_sums), tuple(value_sums)

        zero = jnp.zeros((rows_at, 128), jnp.float32)
        key_sums, value_sums = lax.fori_loop(first_ref[i], last_ref[i], step, ((zero, zero), (zero, zero)))
        even = lax.broadcasted_iota(jnp.int32, (rows_at, 128), 1) < 64
        dk_ref[rows, :] = (jnp.where(even, key_sums[0], key_sums[1]) * 0.125).astype(jnp.bfloat16)
        dv_ref[rows, :] = jnp.where(even, value_sums[0], value_sums[1]).astype(jnp.bfloat16)


def stat_rows(width):
    return -(-12 * (width // 128) // 16) * 16


def unpacked_stat(packed, which, width):
    pieces = width // 128
    parts = []
    for j in range(pieces):
        at = [(3 * which + part) * pieces + j for part in range(3)]
        parts.append(packed[at[0] : at[0] + 1] + packed[at[1] : at[1] + 1] + packed[at[2] : at[2] + 1])
    return jnp.concatenate(parts, axis=1)


def mixed_grad_kernel(branch_ref, weight_ref, mixed_ref, lse_ref, sent_ref, delta_ref):
    width = branch_ref.shape[0]
    grad = dot_nt(branch_ref[...], weight_ref[...]).astype(jnp.bfloat16)
    sent_ref[pl.ds(0, width), :] = grad
    product = grad.astype(jnp.float32) * mixed_ref[...]
    even = lax.broadcasted_iota(jnp.int32, product.shape, 1) < 64
    sums = [jnp.sum(part, axis=1, keepdims=True) for part in head_halves(product)]
    delta = jnp.where(even, sums[0], sums[1])
    delta_ref[...] = delta
    rows = []
    for kept in (lse_ref[...], delta):
        turned = kept.T
        for h in range(2):
            row = turned[64 * h : 64 * h + 1, :]
            for _ in range(3):
                part = row.astype(jnp.bfloat16).astype(jnp.float32)
                row = row - part
                rows.extend(part[:, 128 * j : 128 * (j + 1)] for j in range(width // 128))
    spare = stat_rows(width) - len(rows)
    if spare:
        rows.append(jnp.zeros((spare, 128), jnp.float32))
    sent_ref[pl.ds(width, stat_rows(width)), :] = jnp.concatenate(rows, axis=0).astype(jnp.bfloat16)


def mixed_grad(branch, out_weight, mixed, lse):
    width = branch.shape[0]
    column = pl.BlockSpec((width, 128), lambda h: (0, h))
    return pl.pallas_call(
        mixed_grad_kernel,
        name="mixed_grad",
        grid=(D // 128,),
        in_specs=[
            pl.BlockSpec((width, D), lambda h: (0, 0)),
            pl.BlockSpec((128, D), lambda h: (h, 0)),
            column,
            column,
        ],
        out_specs=[pl.BlockSpec((width + stat_rows(width), 128), lambda h: (0, h)), column],
        out_shape=[
            jax.ShapeDtypeStruct((width + stat_rows(width), D), jnp.bfloat16),
            jax.ShapeDtypeStruct((width, D), jnp.float32),
        ],
        cost_estimate=BRIEF,
    )(branch, out_weight, mixed, lse)


ROWS_AT = 256


def attend(kernel, ranges, operands, results, scratch, pairs=(0, D // 128), after=()):
    begin, count = pairs
    specs = []
    for array, (kind, at) in operands:
        if kind == "own":
            specs.append(pl.BlockSpec((ranges[3], 128), lambda h, *_, at=at + begin: (0, at + h)))
        elif kind == "window":
            specs.append(pl.BlockSpec((array.shape[0], 128), lambda h, *_, at=at + begin: (0, at + h)))
        else:
            specs.append(pl.BlockSpec(array.shape, lambda h, *_, n=array.ndim: (0,) * n))
    tok_rows = ranges[3]
    return pl.pallas_call(
        functools.partial(kernel, ROWS_AT),
        grid_spec=pltpu.PrefetchScalarGridSpec(
            num_scalar_prefetch=3,
            grid=(count,),
            in_specs=specs,
            out_specs=[pl.BlockSpec((tok_rows, 128), lambda h, *_: (0, h))] * len(results),
            scratch_shapes=scratch,
        ),
        out_shape=[jax.ShapeDtypeStruct((tok_rows, 128 * count), kept) for kept in results],
        compiler_params=pltpu.CompilerParams(vmem_limit_bytes=48 * 2**20),
        cost_estimate=BRIEF,
    )(*[behind(bound, after) for bound in ranges[:1]], *ranges[1:3], *[array for array, _ in operands])


VECTOR = pltpu.VMEM
ANY = pl.ANY


def behind(value, others):
    return lax.optimization_barrier((value, *others))[0]


def halves_rows(shard_rows):
    return -(-shard_rows // 128) * 64


def unpack_kernel(plan, shard_rows, flat_ref, *refs):
    wide_ref = refs[-1]
    padded_ref = refs[-2]
    total = flat_ref.shape[0]
    chunk = 432

    def widen(i, _):
        rows = pl.ds(pl.multiple_of(i * chunk, 16), chunk)
        wide_ref[rows, :] = flat_ref[rows, :].astype(jnp.float32)
        return 0

    lax.fori_loop(0, total // chunk, widen, 0)
    wide_ref[pl.ds(total, wide_ref.shape[0] - total), :] = jnp.zeros((wide_ref.shape[0] - total, 128), jnp.float32)
    for (offset, rows, columns, begin), ref in zip(plan, refs[:-2]):
        pieces = columns // 128
        if rows == 1:
            for j in range(pieces):
                ref[:, 128 * j : 128 * (j + 1)] = wide_ref[pl.ds(offset + j, 1), :]
            continue

        def matrix(i, _):
            at = pl.multiple_of(i * 64, 64)
            for j in range(pieces):
                part = wide_ref[pl.ds(offset + j + at * pieces, 64, stride=pieces), :]
                ref[pl.ds(at, 64), begin + 128 * j : begin + 128 * (j + 1)] = part.astype(jnp.bfloat16)
            return 0

        lax.fori_loop(0, rows // 64, matrix, 0)
    shards = total // shard_rows
    half = halves_rows(shard_rows)
    for s in range(shards):
        for h in range(2):

            def pad(i, _):
                part = wide_ref[pl.ds(s * shard_rows + h * half + i * 64, 64), :]
                padded_ref[s * 2 + h, pl.ds(pl.multiple_of(i * 64, 64), 64), :] = part.astype(jnp.bfloat16)
                return 0

            lax.fori_loop(0, half // 64, pad, 0)


def unpacked(weights, shard_rows):
    flat = weights.reshape(-1, 128)
    half = halves_rows(shard_rows)
    plan, outs = [], []
    offset = 0
    for layout in layouts():
        rows, columns = layout if len(layout) == 2 else (1, layout[0])
        plan.append([offset, rows, columns, 0])
        outs.append(jax.ShapeDtypeStruct((rows, columns), jnp.bfloat16 if rows > 1 else jnp.float32))
        offset = offset + rows * columns // 128
    shards = flat.shape[0] // shard_rows
    outs.append(jax.ShapeDtypeStruct((2 * shards, half, 128), jnp.bfloat16))
    return pl.pallas_call(
        functools.partial(unpack_kernel, plan, shard_rows),
        name="unpack",
        in_specs=[pl.BlockSpec(memory_space=VECTOR)],
        out_specs=[pl.BlockSpec(memory_space=VECTOR)] * len(outs),
        out_shape=outs,
        scratch_shapes=[VECTOR((flat.shape[0] + 2 * half, 128), jnp.float32)],
        compiler_params=pltpu.CompilerParams(vmem_limit_bytes=60 * 2**20),
        cost_estimate=BRIEF,
    )(flat)


def pack_kernel(plan, spans, place_ref, *refs):
    count = len(plan)
    keep_ref, give_ref, flat_ref, out_ref, sems = refs[-5:]
    end = max(offset + rows * columns // 128 for offset, rows, columns in plan)
    begin = min(offset for offset, _, _ in plan)
    if begin:
        flat_ref[pl.ds(0, begin), :] = jnp.zeros((begin, 128), jnp.float32)
    for (offset, rows, columns), ref in zip(plan, refs[:count]):
        pieces = columns // 128
        if rows == 1:
            for j in range(pieces):
                flat_ref[pl.ds(offset + j, 1), :] = ref[:, 128 * j : 128 * (j + 1)]
            continue

        def matrix(i, _):
            at = pl.multiple_of(i * 64, 64)
            for j in range(pieces):
                flat_ref[pl.ds(offset + j + at * pieces, 64, stride=pieces), :] = ref[pl.ds(at, 64), 128 * j : 128 * (j + 1)]
            return 0

        lax.fori_loop(0, rows // 64, matrix, 0)
    for h in range(2):
        at = h ^ place_ref[0]
        filled = 0
        for source, rows, room in spans[h]:
            whole = rows // 64

            def move(i, _):
                to = pl.ds(pl.multiple_of(filled + i * 64, 16), 64)
                out_ref[at, to, :] = flat_ref[pl.ds(source + i * 64, 64), :].astype(jnp.bfloat16)
                return 0

            lax.fori_loop(0, whole, move, 0)
            rest = rows - 64 * whole
            tail = room - 64 * whole
            if tail:
                parts = []
                if rest:
                    parts.append(flat_ref[pl.ds(source + 64 * whole, rest), :])
                if tail > rest:
                    parts.append(jnp.zeros((tail - rest, 128), jnp.float32))
                last = parts[0] if len(parts) == 1 else jnp.concatenate(parts, axis=0)
                out_ref[at, pl.ds(filled + 64 * whole, tail), :] = last.astype(jnp.bfloat16)
            filled = filled + room
    copies = [
        pltpu.make_async_copy(out_ref.at[0], keep_ref, sems.at[0]),
        pltpu.make_async_copy(out_ref.at[1], give_ref, sems.at[1]),
    ]
    for copy in copies:
        copy.start()
    for copy in copies:
        copy.wait()


def packed_halves(grads, begin, spans, half):
    plan = []
    offset = begin
    for grad in grads:
        plan.append((offset, *grad.shape))
        offset = offset + grad.shape[0] * grad.shape[1] // 128
    return pl.pallas_call(
        functools.partial(pack_kernel, plan, spans),
        name="pack",
        in_specs=[pl.BlockSpec(memory_space=pltpu.SMEM)] + [pl.BlockSpec(memory_space=VECTOR)] * len(grads),
        out_specs=[pl.BlockSpec(memory_space=ANY)] * 2,
        out_shape=[jax.ShapeDtypeStruct((half, 128), jnp.bfloat16)] * 2,
        scratch_shapes=[
            VECTOR((offset, 128), jnp.float32),
            VECTOR((2, half, 128), jnp.bfloat16),
            pltpu.SemaphoreType.DMA((2,)),
        ],
        compiler_params=pltpu.CompilerParams(vmem_limit_bytes=60 * 2**20),
        cost_estimate=BRIEF,
    )(bit_of(1).reshape(1), *grads)


def combine_kernel(count, places_ref, *refs):
    parts, outs = refs[:count], refs[-places_ref.shape[0] :]
    rows = outs[0].shape[0]
    for k, out in enumerate(outs):
        at = pl.ds(pl.multiple_of(places_ref[k] * rows, 16), rows)
        terms = [part[at, :].astype(jnp.float32) for part in parts]
        while len(terms) > 1:
            terms = [terms[2 * j] + terms[2 * j + 1] for j in range(len(terms) // 2)]
        out[...] = terms[0].astype(jnp.bfloat16)


def places_of(group):
    if not group:
        return jnp.zeros((1,), jnp.int32)
    place = (lax.axis_index(LINE) // group[0]) % (1 << len(group))
    return place ^ jnp.arange(1 << len(group), dtype=jnp.int32)


def combine(parts, group, after):
    count = 1 << len(group)
    rows = parts[0].shape[0] // count
    outs = pl.pallas_call(
        functools.partial(combine_kernel, len(parts)),
        name="combine",
        in_specs=[pl.BlockSpec(memory_space=pltpu.SMEM)]
        + [pl.BlockSpec(memory_space=VECTOR)] * len(parts),
        out_specs=[pl.BlockSpec(memory_space=VECTOR)] * count,
        out_shape=[jax.ShapeDtypeStruct((rows, 128), jnp.bfloat16)] * count,
        cost_estimate=BRIEF,
    )(behind(places_of(group), after), *parts)
    return list(outs)


def stack_kernel(count, places_ref, *refs):
    out_ref = refs[-1]
    rows = refs[0].shape[0]
    for k in range(count):
        out_ref[pl.ds(pl.multiple_of(places_ref[k] * rows, 16), rows), :] = refs[k][...]


def stack(parts, group, after):
    rows = parts[0].shape[0] * len(parts)
    return pl.pallas_call(
        functools.partial(stack_kernel, len(parts)),
        name="stack",
        in_specs=[pl.BlockSpec(memory_space=pltpu.SMEM)]
        + [pl.BlockSpec(memory_space=VECTOR)] * len(parts),
        out_specs=pl.BlockSpec(memory_space=VECTOR),
        out_shape=jax.ShapeDtypeStruct((rows, 128), jnp.bfloat16),
        cost_estimate=BRIEF,
    )(behind(places_of(group), after), *parts)


def exchanged(parts, group):
    return [parts[0]] + [swapped(parts[k % len(parts)], group[0] * k) for k in range(1, 1 << len(group))]


def bit_groups():
    bits = [1 << k for k in range(1, lax.axis_size(LINE).bit_length() - 1)]
    return [bits[k : k + 2] for k in range(0, len(bits), 2)]


def update_kernel(
    shards, late, shard_rows, meta_ref, scale_ref, early_own, early_other, late_own, late_other, extra_own, extra_other,
    weight_ref, one_ref, two_ref, *refs
):
    moments = refs[: 2 * shards]
    step_ref, grad_ref, new_one_ref, new_two_ref, sum_ref, wide_ref, stage_ref, sems = refs[2 * shards :]
    which, k = pl.program_id(0), pl.program_id(1)
    core, me, turn = meta_ref[0], meta_ref[1], meta_ref[2]
    shard = me ^ k
    half = core ^ which
    rows = sum_ref.shape[0]
    chunk = rows // 7 if rows % 112 == 0 else 64
    scale = scale_ref[0]

    def by_chunks(body):
        def move(i, _):
            body(pl.multiple_of(i * chunk, 16))
            return 0

        lax.fori_loop(0, rows // chunk, move, 0)

    def load(ref):
        def body(at):
            sum_ref[pl.ds(at, chunk), :] = ref[pl.ds(at, chunk), :].astype(jnp.float32) * scale

        by_chunks(body)

    for array, side, is_late in ((early_own, 0, 0), (early_other, 1, 0), (late_own, 0, 1), (late_other, 1, 1)):
        pl.when((which == side) & ((shard < late) == (is_late == 1)))(functools.partial(load, array))
    for array, side in ((extra_own, 0), (extra_other, 1)):

        @pl.when((which == side) & (shard == late) & (half == 0))
        def _():
            sum_ref[pl.ds(0, 8), :] = sum_ref[pl.ds(0, 8), :] + array[pl.ds(0, 8), :].astype(jnp.float32) * scale

    def moved(clipped, one, two):
        one = BETA_ONE * one + (1.0 - BETA_ONE) * clipped
        two = BETA_TWO * two + (1.0 - BETA_TWO) * clipped * clipped
        return one, two

    base = shard * shard_rows + half * rows
    limit = jnp.where(half == 1, shard_rows - rows, rows)
    for j in range(shards):

        @pl.when(k == j)
        def _():
            def body(start):
                at = pl.ds(start, chunk)
                first, second = moments[2 * j][at, :], moments[2 * j + 1][at, :]
                one, two = jnp.where(turn == 1, second, first), jnp.where(turn == 1, first, second)
                one, two = moved(sum_ref[at, :], one.astype(jnp.float32), two.astype(jnp.float32))
                update = (one * (1.0 / FIX_ONE)) / (jnp.sqrt(two * (1.0 / FIX_TWO)) + 1e-08)
                update = update + DECAY * weight_ref[0, at, :].astype(jnp.float32)
                to = pl.ds(base + start, chunk)
                inside = start + lax.broadcasted_iota(jnp.int32, update.shape, 0) < limit
                wide_ref[to, :] = jnp.where(inside, update, wide_ref[to, :])

            by_chunks(body)

    @pl.when(k == 0)
    def _():
        unscale = scale_ref[1]

        def body(start):
            at = pl.ds(start, chunk)
            clipped = sum_ref[at, :]
            one, two = moved(clipped, one_ref[at, :], two_ref[at, :])
            grad_ref[at, :] = clipped * unscale
            new_one_ref[at, :] = one
            new_two_ref[at, :] = two

        by_chunks(body)

    @pl.when((which == 1) & (k == shards - 1))
    def _():
        piece = stage_ref.shape[1]
        total = step_ref.shape[0]

        def sending(i, slot):
            return pltpu.make_async_copy(
                stage_ref.at[slot], step_ref.at[pl.ds(pl.multiple_of(i * piece, 16), piece), :], sems.at[slot]
            )

        count = total // piece
        for i in range(count):
            if i >= 2:
                sending(i - 2, i % 2).wait()
            stage_ref[i % 2] = wide_ref[pl.ds(i * piece, piece), :].astype(jnp.bfloat16)
            sending(i, i % 2).start()
        for i in range(count - 2, count):
            sending(i, i % 2).wait()


def updated(norm, early, late, late_shards, weights, first_moment, second_moment, moments):
    shards = len(moments) // 2
    rows = weights.shape[1]
    shard_rows = first_moment.shape[0] // 128
    line = lax.axis_index(LINE)
    inner = lax.axis_size("inner")
    meta = jnp.stack([line % 2, lax.axis_index("inner"), (line // inner) % 2]).astype(jnp.int32)
    last = shards - 1

    def early_map(side):
        def index(w, k, meta):
            k = jnp.where(w == side, k, last if side == 0 else 0)
            return (jnp.clip((meta[1] ^ k) - late_shards, 0, shards - late_shards - 1), 0)

        return index

    def late_map(side):
        def index(w, k, meta):
            k = jnp.where(w == side, k, last if side == 0 else 0)
            return (jnp.clip(meta[1] ^ k, 0, late_shards - 1), 0)

        return index

    by_half = pl.BlockSpec((rows, 128), lambda w, k, meta: (meta[0] ^ w, 0))
    by_shard = pl.BlockSpec((1, rows, 128), lambda w, k, meta: (2 * (meta[1] ^ k) + (meta[0] ^ w), 0, 0))
    extra = pl.BlockSpec((16, 128), lambda w, k, meta: (late_shards * rows // 16, 0))
    return pl.pallas_call(
        functools.partial(update_kernel, shards, late_shards, shard_rows),
        name="update",
        grid_spec=pltpu.PrefetchScalarGridSpec(
            num_scalar_prefetch=1,
            grid=(2, shards),
            in_specs=[pl.BlockSpec(memory_space=pltpu.SMEM)]
            + [pl.BlockSpec((rows, 128), early_map(side)) for side in range(2)]
            + [pl.BlockSpec((rows, 128), late_map(side)) for side in range(2)]
            + [extra, extra, by_shard, by_half, by_half]
            + [by_half] * (2 * shards),
            out_specs=[pl.BlockSpec(memory_space=ANY), by_half, by_half, by_half],
            scratch_shapes=[
                VECTOR((rows, 128), jnp.float32),
                VECTOR((shards * shard_rows + 2 * rows, 128), jnp.float32),
                VECTOR((2, shards * shard_rows // 9, 128), jnp.bfloat16),
                pltpu.SemaphoreType.DMA((2,)),
            ],
        ),
        out_shape=[jax.ShapeDtypeStruct((shards * shard_rows, 128), jnp.bfloat16)]
        + [jax.ShapeDtypeStruct((shard_rows, 128), jnp.float32)] * 3,
        compiler_params=pltpu.CompilerParams(vmem_limit_bytes=60 * 2**20),
        cost_estimate=BRIEF,
    )(
        meta,
        jnp.stack([1.0 / norm, norm]),
        *early,
        *late,
        *late,
        weights,
        first_moment.reshape(-1, 128),
        second_moment.reshape(-1, 128),
        *moments,
    )


def narrow_kernel(shard_rows, turn_ref, one_ref, two_ref, first_out, second_out):
    shape = first_out.shape
    begin = pl.program_id(0) * shape[0]
    inside = begin + lax.broadcasted_iota(jnp.int32, shape, 0) < shard_rows
    one = jnp.where(inside, one_ref[...], 0.0).astype(jnp.bfloat16)
    two = jnp.where(inside, two_ref[...], 0.0).astype(jnp.bfloat16)
    turned = turn_ref[0] == 1
    first_out[...] = jnp.where(turned, two, one)
    second_out[...] = jnp.where(turned, one, two)


def narrowed(one, two, half, turn):
    block = pl.BlockSpec((half // 2, 128), lambda i: (i, 0))
    return pl.pallas_call(
        functools.partial(narrow_kernel, one.shape[0]),
        name="narrow",
        grid=(4,),
        in_specs=[pl.BlockSpec(memory_space=pltpu.SMEM), block, block],
        out_specs=[block, block],
        out_shape=[jax.ShapeDtypeStruct((2 * half, 128), jnp.bfloat16)] * 2,
        cost_estimate=BRIEF,
    )(turn.reshape(1), one, two)


def bit_of(bit):
    return (lax.axis_index(LINE) // bit) % 2


def on_device(inputs, weights, cotangent, clip_lengths, first_moment, second_moment):
    tok_rows = inputs.shape[0]
    reach = (MOST + tok_rows - 2) // tok_rows
    shard_rows = first_moment.shape[0] // 128
    half = halves_rows(shard_rows)
    (
        first_gain,
        first_bias,
        query_weight,
        query_bias,
        key_weight,
        value_weight,
        value_bias,
        out_weight,
        out_bias,
        second_gain,
        second_bias,
        up_weight,
        up_bias,
        down_weight,
        down_bias,
        padded_weights,
    ) = unpacked(weights, shard_rows)
    base_slot = lax.axis_index(LINE) * tok_rows
    positions = base_slot + jnp.arange(tok_rows, dtype=jnp.int32)
    lower_slot, upper_slot = bounds(positions, clip_lengths)
    low = lower_slot - base_slot + reach * tok_rows
    high = upper_slot - base_slot + reach * tok_rows
    first_block = low.reshape(-1, ROWS_AT)[:, 0] // tok_rows
    last_block = (high.reshape(-1, ROWS_AT)[:, -1] + tok_rows - 1) // tok_rows
    ranges = (first_block, last_block, slot_table(), tok_rows)
    low, high = low[:, None], high[:, None]

    inner = lax.axis_size("inner")
    turn = (lax.axis_index(LINE) // inner) % 2
    first_half, second_half = narrowed(first_moment.reshape(-1, 128), second_moment.reshape(-1, 128), half, turn)
    blocks = halo(inputs, (padded_weights,))
    window = jnp.concatenate(blocks, axis=0)
    fetched, window = lax.optimization_barrier((first_half, window))
    window_hat, _ = standard(window.astype(jnp.float32))
    window_normed = (window_hat * first_gain + first_bias).astype(jnp.bfloat16)
    project = jnp.concatenate([query_weight, key_weight, value_weight], axis=1)
    shift = jnp.concatenate([query_bias, jnp.zeros((1, D), jnp.float32), value_bias], axis=1)
    rows = (plain_dot(window_normed, project) + shift).astype(jnp.bfloat16)
    fetched = swapped(fetched, 2)
    input_rows = inputs.astype(jnp.float32)
    first_hat, first_dev = standard(input_rows)
    normed = (first_hat * first_gain + first_bias).astype(jnp.bfloat16)

    attended, lse = attend(
        forward_kernel,
        ranges,
        [
            (rows, ("own", 0)),
            (rows, ("window", 4)),
            (rows, ("window", 8)),
            (low, ("all", 0)),
            (high, ("all", 0)),
        ],
        [jnp.float32, jnp.float32],
        [pltpu.VMEM((2, 2 * reach + 1, ROWS_AT, tok_rows), jnp.float32)],
    )
    attended, lse, fetched = lax.optimization_barrier((attended, lse, fetched))
    held = {0: (first_half, second_half), 2: (fetched, swapped(fetched, inner))}
    bit = 4
    while bit < inner:
        for place in list(held):
            held[place + bit] = tuple(swapped(piece, bit) for piece in held[place])
        bit = 2 * bit
    moments = []
    for place in range(inner):
        if place % 2 == 0:
            moments += held[place]
        else:
            moments += [swapped(piece, 1) for piece in held[place - 1]]
    mixed = attended.astype(jnp.bfloat16)
    middle = input_rows + plain_dot(mixed, out_weight) + out_bias
    second_hat, second_dev = standard(middle)
    hidden_in = (second_hat * second_gain + second_bias).astype(jnp.bfloat16)
    up_rows = plain_dot(hidden_in, up_weight) + up_bias
    cdf_part = 0.5 * (1.0 + lax.erf(up_rows * INV_ROOT_TWO))
    activated = (up_rows * cdf_part).astype(jnp.bfloat16)
    layer_output = (middle + plain_dot(activated, down_weight) + down_bias).astype(jnp.bfloat16)
    grad_out = cotangent.astype(jnp.float32)
    down_bias_grad = jnp.sum(grad_out, axis=0)
    grad_act = back_dot(cotangent, down_weight)
    pdf_part = jnp.exp(-0.5 * up_rows * up_rows) * INV_ROOT_TWO_PI
    grad_up = (grad_act * (cdf_part + up_rows * pdf_part)).astype(jnp.bfloat16)
    up_bias_grad = jnp.sum(grad_up.astype(jnp.float32), axis=0)
    grad_hidden = back_dot(grad_up, up_weight)
    second_gain_grad = jnp.sum(grad_hidden * second_hat, axis=0)
    second_bias_grad = jnp.sum(grad_hidden, axis=0)
    grad_middle = grad_out + norm_back(grad_hidden, second_hat, second_dev, second_gain)
    grad_branch = grad_middle.astype(jnp.bfloat16)
    out_bias_grad = jnp.sum(grad_branch.astype(jnp.float32), axis=0)
    grad_branch, *moments[4:6] = lax.optimization_barrier((grad_branch, *moments[4:6]))
    sent, delta = mixed_grad(grad_branch, out_weight, attended, lse)
    line = lax.axis_size(LINE)
    shards = inner
    late_shards = shards // 4
    groups = bit_groups()

    def rounded(count, unit):
        return -(-count // unit) * unit

    def shard_spans(first, last, base):
        spans = ([], [])
        for shard in range(first, last):
            begin = (shard - first) * shard_rows + base
            spans[0].append((begin, half, half))
            spans[1].append((begin + half, shard_rows - half, half))
        return spans

    def query_step(pairs, after):
        return attend(
            query_kernel,
            ranges,
            [
                (rows, ("own", 0)),
                (rows, ("window", 4)),
                (rows, ("window", 8)),
                (sent, ("own", 0)),
                (lse, ("own", 0)),
                (delta, ("own", 0)),
                (low, ("all", 0)),
                (high, ("all", 0)),
            ],
            [jnp.bfloat16],
            [],
            pairs,
            after,
        )

    def key_step(pairs, after):
        return attend(
            key_kernel,
            ranges,
            [
                (rows, ("own", 4)),
                (rows, ("own", 8)),
                (rows, ("window", 0)),
                (grad_window, ("window", 0)),
                (low, ("all", 0)),
                (high, ("all", 0)),
            ],
            [jnp.bfloat16, jnp.bfloat16],
            [],
            pairs,
            after,
        )

    query_parts = query_step((0, 2), ())
    grad_window = halo(sent, query_parts)
    grad_window = jnp.concatenate(grad_window, axis=0)
    activated, hidden_in, mixed = (behind(array, query_parts) for array in (activated, hidden_in, mixed))
    down_grad = rows_dot(activated, cotangent)
    up_grad = rows_dot(hidden_in, grad_up)
    out_grad = rows_dot(mixed, grad_branch)

    early_rows = [
        out_grad,
        out_bias_grad,
        second_gain_grad,
        second_bias_grad,
        up_grad,
        up_bias_grad,
        down_grad,
        down_bias_grad,
    ]
    early_rows = [section.reshape(-1, section.shape[-1]) for section in early_rows]
    early_half = rounded((shards - late_shards) * half, 8 * line)
    spans = shard_spans(late_shards, shards, 0)
    for span in spans:
        span.append((0, 0, early_half - (shards - late_shards) * half))
    early_keep, early_give = packed_halves(early_rows, D // 128, spans, early_half)
    early_got = swapped(early_give, 1)

    query_parts += query_step((2, 2), (early_give,))
    parts = combine([early_keep, early_got], groups[0], query_parts)
    got = exchanged(parts, groups[0])
    query_low = jnp.concatenate(query_parts, axis=1)
    work = [(1, 1), (2, 1), (3, 1)]
    done = key_step((0, 1), parts[:1])
    key_parts, value_parts = [done[0]], [done[1]]
    held_back = done[:1]
    for at, group in enumerate(groups):
        parts = combine(got, groups[at + 1] if at + 1 < len(groups) else [], held_back)
        if at + 1 < len(groups):
            got = exchanged(parts, groups[at + 1])
        if work:
            done = key_step(work.pop(0), parts[:1])
            key_parts.append(done[0])
            value_parts.append(done[1])
            held_back = done[:1]
    piece = parts[0]
    for at, group in enumerate(groups[::-1]):
        got = exchanged([piece], group)
        if work and at > 0:
            done = key_step(work.pop(0), [piece])
            key_parts.append(done[0])
            value_parts.append(done[1])
            held_back = done[:1]
        piece = stack(got, group, held_back)
    early_other = swapped(piece, 1)
    for pairs in work:
        done = key_step(pairs, [piece])
        key_parts.append(done[0])
        value_parts.append(done[1])
    early = (piece, early_other)
    key_low = jnp.concatenate(key_parts, axis=1)
    value_low = jnp.concatenate(value_parts, axis=1)
    query_grad = rows_dot(normed, query_low)
    query_bias_grad = jnp.sum(query_low.astype(jnp.float32), axis=0)
    key_grad = rows_dot(normed, key_low)
    value_grad = rows_dot(normed, value_low)
    value_bias_grad = jnp.sum(value_low.astype(jnp.float32), axis=0)
    grad_normed = (
        back_dot(query_low, query_weight)
        + back_dot(key_low, key_weight)
        + back_dot(value_low, value_weight)
    )
    first_gain_grad = jnp.sum(grad_normed * first_hat, axis=0)
    first_bias_grad = jnp.sum(grad_normed, axis=0)
    input_grad = (grad_middle + norm_back(grad_normed, first_hat, first_dev, first_gain)).astype(
        jnp.bfloat16
    )

    late_rows = [
        first_gain_grad,
        first_bias_grad,
        query_grad,
        query_bias_grad,
        key_grad,
        value_grad,
        value_bias_grad,
    ]
    late_rows = [section.reshape(-1, section.shape[-1]) for section in late_rows]
    tail = max(1, 1 << (len(groups[0])))
    late_half = rounded(late_shards * half + 16, 16 * tail)
    spans = shard_spans(0, late_shards, 0)
    spare = late_half - late_shards * half
    spans[0].append((late_shards * shard_rows, D // 128, spare))
    spans[1].append((0, 0, spare))
    keep, give = packed_halves(late_rows, 0, spans, late_half)
    parts = combine([keep, swapped(give, 1)], groups[0], ())
    (piece,) = combine(exchanged(parts, groups[0]), [], ())
    for group in groups[1:]:
        (piece,) = combine(exchanged([piece], group), [], ())
    piece = stack(exchanged([piece], groups[0]), groups[0], ())
    late = (piece, swapped(piece, 1))

    def square_sum(pair):
        sums = [jnp.sum(jnp.square(part.astype(jnp.float32))) for part in pair]
        return sums[0] + sums[1]

    grad_norm = jnp.sqrt(square_sum(early) + square_sum(late))
    steps, grad_shard, moment_one, moment_two = updated(
        jnp.maximum(grad_norm, 1.0), early, late, late_shards, padded_weights, first_moment, second_moment, moments
    )
    weight_step = steps.reshape(-1)
    return (
        layer_output,
        input_grad,
        grad_shard.reshape(-1),
        grad_norm,
        moment_one.reshape(-1),
        moment_two.reshape(-1),
        weight_step,
    )


def solution(mesh):
    return jax.shard_map(
        on_device,
        mesh=mesh,
        in_specs=(
            P(("outer", "inner"), None),
            P(),
            P(("outer", "inner"), None),
            P(),
            P("inner"),
            P("inner"),
        ),
        out_specs=(
            P(("outer", "inner"), None),
            P(("outer", "inner"), None),
            P("inner"),
            P(),
            P("inner"),
            P("inner"),
            P(),
        ),
        check_vma=False,
    )
```

```python
import functools
import math

import jax
import jax.numpy as jnp
from jax import lax
from jax.experimental import pallas as pl
from jax.experimental.pallas import tpu as pltpu
from jax.sharding import PartitionSpec as P

D = 512
HEADS = 8
FF = 2048
MOST = 1500


BETA_ONE = 0.9
BETA_TWO = 0.999
FIX_ONE = 1.0 - (0.9**10) ** 10
FIX_TWO = 1.0 - (0.999**10) ** 10
DECAY = 0.1
INV_ROOT_TWO = 1.0 / math.sqrt(2.0)
INV_ROOT_TWO_PI = 1.0 / math.sqrt(2.0 * math.pi)


def layouts():
    return [
        (D,),
        (D,),
        (D, D),
        (D,),
        (D, D),
        (D, D),
        (D,),
        (D, D),
        (D,),
        (D,),
        (D,),
        (D, FF),
        (FF,),
        (FF, D),
        (D,),
    ]


def plain_dot(matrix_one, matrix_two):
    return jnp.dot(matrix_one, matrix_two, preferred_element_type=jnp.float32)


def rows_dot(matrix_one, matrix_two):
    return lax.dot_general(
        matrix_one, matrix_two, (((0,), (0,)), ((), ())), preferred_element_type=jnp.float32
    )


def back_dot(matrix_one, matrix_two):
    return lax.dot_general(
        matrix_one, matrix_two, (((1,), (1,)), ((), ())), preferred_element_type=jnp.float32
    )


def standard(values):
    center = jnp.mean(values, axis=-1, keepdims=True)
    centered = values - center
    inverse_dev = lax.rsqrt(jnp.mean(centered * centered, axis=-1, keepdims=True) + 1e-05)
    return (centered * inverse_dev, inverse_dev)


def norm_back(grad_normed, normed_hat, inverse_dev, gain):
    scaled = grad_normed * gain
    return inverse_dev * (
        scaled
        - jnp.mean(scaled, axis=-1, keepdims=True)
        - normed_hat * jnp.mean(scaled * normed_hat, axis=-1, keepdims=True)
    )


def bounds(positions, clip_lengths):
    starts = jnp.cumsum(clip_lengths, dtype=jnp.int32) - clip_lengths
    member = (
        jnp.sum((positions[:, None] >= starts[None, :]).astype(jnp.int32), axis=1, dtype=jnp.int32)
        - 1
    )
    onehot = (
        jnp.arange(clip_lengths.shape[0], dtype=jnp.int32)[None, :] == member[:, None]
    ).astype(jnp.int32)
    lower_slot = jnp.sum(onehot * starts[None, :], axis=1, dtype=jnp.int32)
    upper_slot = lower_slot + jnp.sum(onehot * clip_lengths[None, :], axis=1, dtype=jnp.int32)
    return (lower_slot, upper_slot)


LINE = ("outer", "inner")
NEG = -1e30
BRIEF = pl.CostEstimate(flops=1000, bytes_accessed=1000, transcendentals=0)


def shifted(block, distance):
    n = lax.axis_size(LINE)
    return lax.ppermute(block, LINE, [(i + distance, i) for i in range(n) if 0 <= i + distance < n])


def swapped(block, bit):
    n = lax.axis_size(LINE)
    return lax.ppermute(block, LINE, [(i ^ bit, i) for i in range(n)])


def halo(block, before=()):
    n = lax.axis_size(LINE)
    left = shifted(block, -2)
    right = shifted(block, 2)
    partner = swapped(block, 1)
    route = [(i + (3 if i % 2 else -3), i) for i in range(n)]
    far = lax.ppermute(block, LINE, [(s, t) for s, t in route if 0 <= s < n])
    passed_left, passed_right, *_ = lax.optimization_barrier((left, right, *before))
    turned = [swapped(passed_left, 1), swapped(passed_right, 1)]
    return [block, partner, left, right, *turned, far]


def block_distances():
    odd = lax.axis_index(LINE) % 2
    even_far = jnp.array([0, 1, -2, 2, -1, 3, -3], jnp.int32)
    odd_far = jnp.array([0, -1, -2, 2, -3, 1, 3], jnp.int32)
    return jnp.where(odd == 1, odd_far, even_far)


def slot_table():
    odd = lax.axis_index(LINE) % 2
    even_slots = jnp.array([6, 2, 4, 0, 1, 3, 5], jnp.int32)
    odd_slots = jnp.array([4, 2, 1, 0, 5, 3, 6], jnp.int32)
    return jnp.where(odd == 1, odd_slots, even_slots)


def dot_nt(a, b):
    return lax.dot_general(a, b, (((1,), (1,)), ((), ())), preferred_element_type=jnp.float32)


def head_halves(pair):
    first = lax.broadcasted_iota(jnp.int32, pair.shape, 1) < pair.shape[1] // 2
    zero = jnp.zeros_like(pair)
    return jnp.where(first, pair, zero), jnp.where(first, zero, pair)


def over_lanes(tile, op):
    parts = [tile[:, 128 * j : 128 * (j + 1)] for j in range(tile.shape[1] // 128)]
    while len(parts) > 1:
        rest = parts[len(parts) // 2 * 2 :]
        parts = [op(parts[2 * j], parts[2 * j + 1]) for j in range(len(parts) // 2)] + rest
    return parts[0]


LSE_PARTS, DELTA_PARTS = 3, 2
DELTA_AT = LSE_PARTS * HEADS
CLIPS_AT = DELTA_AT + DELTA_PARTS * HEADS


def lane_of(shape):
    return lax.broadcasted_iota(jnp.int32, shape, 1)


def among(lane, begin, count):
    return (lane >= begin) & (lane < begin + count)


def beside(pair, marks):
    return jnp.concatenate([pair, marks.astype(pair.dtype)], axis=1)


def clip_marks(positions, clip_lengths):
    ends = jnp.cumsum(clip_lengths, dtype=jnp.int32)
    starts = ends - clip_lengths
    spare = 128 - CLIPS_AT - clip_lengths.shape[0]
    assert spare >= 0
    big = jnp.iinfo(jnp.int32).max
    lower = jnp.concatenate([jnp.full((CLIPS_AT,), -big, jnp.int32), starts, jnp.full((spare,), big, jnp.int32)])
    upper = jnp.concatenate([jnp.full((CLIPS_AT,), big, jnp.int32), ends, jnp.full((spare,), big, jnp.int32)])
    inside = (positions[:, None] >= lower[None]) & (positions[:, None] < upper[None])
    return inside.astype(jnp.bfloat16)


def penalty(marks):
    closed = (lane_of(marks.shape) >= CLIPS_AT) & (marks == 0)
    return jnp.where(closed, NEG, 0.0).astype(jnp.bfloat16)


def forward_kernel(
    begin, rows_at, first_ref, last_ref, slot_ref, q_ref, k_ref, v_ref, mark_ref, closed_ref, o_ref, lse_ref, s_ref
):
    width = q_ref.shape[0]
    for i in range(width // rows_at):
        rows = pl.ds(i * rows_at, rows_at)
        queries = [
            beside(half, closed_ref[rows, :]) for half in head_halves(q_ref[rows, :] * jnp.bfloat16(0.125))
        ]

        def scores(block, peaks):
            at = pl.ds(pl.multiple_of(slot_ref[block] * width, width), width)
            keys = beside(k_ref[at, :], mark_ref[at, :])
            found = []
            for h in range(2):
                score = dot_nt(queries[h], keys)
                s_ref[h, block] = score
                found.append(jnp.maximum(peaks[h], over_lanes(score, jnp.maximum)))
            return tuple(found)

        start = jnp.full((rows_at, 128), NEG, jnp.float32)
        peaks = lax.fori_loop(first_ref[i], last_ref[i], scores, (start, start))
        peaks = [jnp.max(peak, axis=1, keepdims=True) for peak in peaks]

        def mix(block, sums):
            at = pl.ds(pl.multiple_of(slot_ref[block] * width, width), width)
            values = beside(v_ref[at, :], mark_ref[at, :])
            found = []
            for h in range(2):
                soft = jnp.exp(s_ref[h, block] - peaks[h]).astype(jnp.bfloat16)
                found.append(sums[h] + jnp.dot(soft, values, preferred_element_type=jnp.float32))
            return tuple(found)

        zero = jnp.zeros((rows_at, 256), jnp.float32)
        sums = lax.fori_loop(first_ref[i], last_ref[i], mix, (zero, zero))
        totals = [part[:, 128:129] for part in sums]
        even = lane_of((rows_at, 128)) < 64
        o_ref[rows, :] = jnp.where(even, sums[0][:, :128] / totals[0], sums[1][:, :128] / totals[1])
        lse_ref[rows, :] = jnp.where(even, peaks[0] + jnp.log(totals[0]), peaks[1] + jnp.log(totals[1]))


def query_kernel(
    begin, rows_at, first_ref, last_ref, slot_ref, q_ref, k_ref, v_ref, g_ref, own_ref, mark_ref, closed_ref, dq_ref
):
    width = q_ref.shape[0]
    pair = pl.program_id(0) + begin
    for i in range(width // rows_at):
        rows = pl.ds(i * rows_at, rows_at)
        own, closed = own_ref[rows, :], closed_ref[rows, :]
        lane = lane_of(own.shape)
        zero = jnp.zeros_like(own)
        queries, grads = [], []
        halves = zip(head_halves(q_ref[rows, :] * jnp.bfloat16(0.125)), head_halves(g_ref[rows, :]))
        for h, (query, grad) in enumerate(halves):
            head = 2 * pair + h
            queries.append(beside(query, jnp.where(among(lane, LSE_PARTS * head, LSE_PARTS), own, closed)))
            grads.append(beside(grad, jnp.where(among(lane, DELTA_AT + DELTA_PARTS * head, DELTA_PARTS), own, zero)))

        def step(block, carried):
            at = pl.ds(pl.multiple_of(slot_ref[block] * width, width), width)
            keys = k_ref[at, :]
            values = beside(v_ref[at, :], mark_ref[at, :])
            marked = beside(keys, mark_ref[at, :])
            found = []
            for h in range(2):
                soft = jnp.exp(dot_nt(queries[h], marked))
                grad = (soft * dot_nt(grads[h], values)).astype(jnp.bfloat16)
                found.append(carried[h] + jnp.dot(grad, keys, preferred_element_type=jnp.float32))
            return tuple(found)

        start = jnp.zeros((rows_at, 128), jnp.float32)
        sums = lax.fori_loop(first_ref[i], last_ref[i], step, (start, start))
        dq_ref[rows, :] = (jnp.where(lane < 64, sums[0], sums[1]) * 0.125).astype(jnp.bfloat16)


def key_kernel(begin, rows_at, first_ref, last_ref, slot_ref, k_ref, v_ref, q_ref, closed_ref, *refs):
    dk_ref, dv_ref, grad_ref, mark_ref = refs[-4:]
    width = k_ref.shape[0]
    pair = pl.program_id(0) + begin
    blocks = grad_ref.shape[0]
    for j in range(blocks):
        grad_ref[j] = refs[j][...]

    @pl.when(pl.program_id(0) == 0)
    def _():
        for j in range(blocks):
            mark_ref[j] = refs[blocks + j][...]

    for i in range(width // rows_at):
        rows = pl.ds(i * rows_at, rows_at)
        closed = closed_ref[rows, :]
        lane = lane_of(closed.shape)
        one, zero = jnp.ones_like(closed), jnp.zeros_like(closed)
        keys, values = [], []
        halves = zip(head_halves(k_ref[rows, :] * jnp.bfloat16(0.125)), head_halves(v_ref[rows, :]))
        for h, (key, value) in enumerate(halves):
            head = 2 * pair + h
            keys.append(beside(key, jnp.where(among(lane, LSE_PARTS * head, LSE_PARTS), one, closed)))
            values.append(beside(value, jnp.where(among(lane, DELTA_AT + DELTA_PARTS * head, DELTA_PARTS), one, zero)))

        def step(block, carried):
            slot = slot_ref[block]
            queries = q_ref[pl.ds(pl.multiple_of(slot * width, width), width), :]
            grads, marks = grad_ref[slot], mark_ref[slot]
            marked, graded = beside(queries, marks), beside(grads, marks)
            key_sums, value_sums = [], []
            for h in range(2):
                soft = jnp.exp(dot_nt(keys[h], marked))
                value_sums.append(
                    carried[1][h] + jnp.dot(soft.astype(jnp.bfloat16), grads, preferred_element_type=jnp.float32)
                )
                grad = (soft * dot_nt(values[h], graded)).astype(jnp.bfloat16)
                key_sums.append(carried[0][h] + jnp.dot(grad, queries, preferred_element_type=jnp.float32))
            return tuple(key_sums), tuple(value_sums)

        start = jnp.zeros((rows_at, 128), jnp.float32)
        key_sums, value_sums = lax.fori_loop(first_ref[i], last_ref[i], step, ((start, start), (start, start)))
        dk_ref[rows, :] = (jnp.where(lane < 64, key_sums[0], key_sums[1]) * 0.125).astype(jnp.bfloat16)
        dv_ref[rows, :] = jnp.where(lane < 64, value_sums[0], value_sums[1]).astype(jnp.bfloat16)


def mixed_grad_kernel(branch_ref, weight_ref, mixed_ref, lse_ref, own_ref, sent_ref, mark_ref):
    step = pl.program_id(0)

    @pl.when(step == 0)
    def _():
        mark_ref[...] = own_ref[...].astype(jnp.float32)

    @pl.when(step < D // 128)
    def _():
        grad = dot_nt(branch_ref[...], weight_ref[...]).astype(jnp.bfloat16)
        sent_ref[...] = grad
        product = grad.astype(jnp.float32) * mixed_ref[...]
        lane = lane_of(product.shape)
        for h, part in enumerate(head_halves(product)):
            head = 2 * step + h
            delta = -jnp.sum(part, axis=1, keepdims=True)
            lse = -lse_ref[:, 64 * h : 64 * h + 1]
            for value, begin, count in (
                (lse, LSE_PARTS * head, LSE_PARTS),
                (delta, DELTA_AT + DELTA_PARTS * head, DELTA_PARTS),
            ):
                for k in range(count):
                    rounded = value.astype(jnp.bfloat16).astype(jnp.float32)
                    mark_ref[...] = jnp.where(lane == begin + k, rounded, mark_ref[...])
                    value = value - rounded

    @pl.when(step == D // 128)
    def _():
        sent_ref[...] = mark_ref[...].astype(jnp.bfloat16)


def mixed_grad(branch, out_weight, mixed, lse, own_marks):
    width = branch.shape[0]
    last = D // 128 - 1
    column = pl.BlockSpec((width, 128), lambda h: (0, jnp.minimum(h, last)))
    return pl.pallas_call(
        mixed_grad_kernel,
        name="mixed_grad",
        grid=(D // 128 + 1,),
        in_specs=[
            pl.BlockSpec((width, D), lambda h: (0, 0)),
            pl.BlockSpec((128, D), lambda h: (jnp.minimum(h, last), 0)),
            column,
            column,
            pl.BlockSpec((width, 128), lambda h: (0, 0)),
        ],
        out_specs=pl.BlockSpec((width, 128), lambda h: (0, h)),
        out_shape=jax.ShapeDtypeStruct((width, D + 128), jnp.bfloat16),
        scratch_shapes=[pltpu.VMEM((width, 128), jnp.float32)],
        cost_estimate=BRIEF,
    )(branch, out_weight, mixed, lse, own_marks)


def project_kernel(count, *refs):
    query_ref, key_ref, value_ref, gain_ref, bias_ref, query_bias_ref, value_bias_ref, out_ref, row_ref = refs[count:]
    step = pl.program_id(0)
    for j in range(count):

        @pl.when(step == j)
        def _():
            row_ref[...] = refs[j][...]

    rows = 256
    for i in range(row_ref.shape[0] // rows):
        at = pl.ds(i * rows, rows)
        hat, _ = standard(row_ref[at, :].astype(jnp.float32))
        normed = (hat * gain_ref[...] + bias_ref[...]).astype(jnp.bfloat16)
        out_ref[at, 0:D] = (plain_dot(normed, query_ref[...]) + query_bias_ref[...]).astype(jnp.bfloat16)
        out_ref[at, D : 2 * D] = plain_dot(normed, key_ref[...]).astype(jnp.bfloat16)
        out_ref[at, 2 * D :] = (plain_dot(normed, value_ref[...]) + value_bias_ref[...]).astype(jnp.bfloat16)


def projected(blocks, *weights):
    width = blocks[0].shape[0]
    whole = [pl.BlockSpec(array.shape, lambda i: (0, 0)) for array in (*blocks, *weights)]
    return pl.pallas_call(
        functools.partial(project_kernel, len(blocks)),
        name="project",
        grid=(len(blocks),),
        in_specs=whole,
        out_specs=pl.BlockSpec((width, 3 * D), lambda i: (i, 0)),
        out_shape=jax.ShapeDtypeStruct((len(blocks) * width, 3 * D), jnp.bfloat16),
        scratch_shapes=[pltpu.VMEM((width, D), jnp.bfloat16)],
        compiler_params=pltpu.CompilerParams(vmem_limit_bytes=48 * 2**20),
        cost_estimate=BRIEF,
    )(*blocks, *weights)


ROWS_AT = 256


def attend(kernel, ranges, operands, results, scratch, pairs=(0, D // 128), after=()):
    begin, count = pairs
    tok_rows = ranges[3]
    specs = []
    for array, (kind, at) in operands:
        if kind == "pair":
            rows = array.shape[0] if at < 0 else tok_rows
            at = (abs(at) - 1 if at < 0 else at) + begin
            specs.append(pl.BlockSpec((rows, 128), lambda h, *_, at=at: (0, at + h)))
        elif kind == "column":
            specs.append(pl.BlockSpec((tok_rows, 128), lambda h, *_, at=at: (0, at)))
        else:
            specs.append(pl.BlockSpec(array.shape, lambda h, *_, n=array.ndim: (0,) * n))
    return pl.pallas_call(
        functools.partial(kernel, begin, ROWS_AT),
        grid_spec=pltpu.PrefetchScalarGridSpec(
            num_scalar_prefetch=3,
            grid=(count,),
            in_specs=specs,
            out_specs=[pl.BlockSpec((tok_rows, 128), lambda h, *_: (0, h))] * len(results),
            scratch_shapes=scratch,
        ),
        out_shape=[jax.ShapeDtypeStruct((tok_rows, 128 * count), kept) for kept in results],
        compiler_params=pltpu.CompilerParams(vmem_limit_bytes=48 * 2**20),
        cost_estimate=BRIEF,
    )(*[behind(bound, after) for bound in ranges[:1]], *ranges[1:3], *[array for array, _ in operands])


VECTOR = pltpu.VMEM
ANY = pl.ANY


def behind(value, others):
    return lax.optimization_barrier((value, *others))[0]


def halves_rows(shard_rows):
    return -(-shard_rows // 128) * 64


def unpack_kernel(plan, shard_rows, flat_ref, *refs):
    wide_ref = refs[-1]
    padded_ref = refs[-2]
    total = flat_ref.shape[0]
    chunk = 432

    def widen(i, _):
        rows = pl.ds(pl.multiple_of(i * chunk, 16), chunk)
        wide_ref[rows, :] = flat_ref[rows, :].astype(jnp.float32)
        return 0

    lax.fori_loop(0, total // chunk, widen, 0)
    wide_ref[pl.ds(total, wide_ref.shape[0] - total), :] = jnp.zeros((wide_ref.shape[0] - total, 128), jnp.float32)
    for (offset, rows, columns, begin), ref in zip(plan, refs[:-2]):
        pieces = columns // 128
        if rows == 1:
            for j in range(pieces):
                ref[:, 128 * j : 128 * (j + 1)] = wide_ref[pl.ds(offset + j, 1), :]
            continue

        def matrix(i, _):
            at = pl.multiple_of(i * 64, 64)
            for j in range(pieces):
                part = wide_ref[pl.ds(offset + j + at * pieces, 64, stride=pieces), :]
                ref[pl.ds(at, 64), begin + 128 * j : begin + 128 * (j + 1)] = part.astype(jnp.bfloat16)
            return 0

        lax.fori_loop(0, rows // 64, matrix, 0)
    shards = total // shard_rows
    half = halves_rows(shard_rows)
    for s in range(shards):
        for h in range(2):

            def pad(i, _):
                part = wide_ref[pl.ds(s * shard_rows + h * half + i * 64, 64), :]
                padded_ref[s * 2 + h, pl.ds(pl.multiple_of(i * 64, 64), 64), :] = part.astype(jnp.bfloat16)
                return 0

            lax.fori_loop(0, half // 64, pad, 0)


def unpacked(weights, shard_rows):
    flat = weights.reshape(-1, 128)
    half = halves_rows(shard_rows)
    plan, outs = [], []
    offset = 0
    for layout in layouts():
        rows, columns = layout if len(layout) == 2 else (1, layout[0])
        plan.append([offset, rows, columns, 0])
        outs.append(jax.ShapeDtypeStruct((rows, columns), jnp.bfloat16 if rows > 1 else jnp.float32))
        offset = offset + rows * columns // 128
    shards = flat.shape[0] // shard_rows
    outs.append(jax.ShapeDtypeStruct((2 * shards, half, 128), jnp.bfloat16))
    return pl.pallas_call(
        functools.partial(unpack_kernel, plan, shard_rows),
        name="unpack",
        in_specs=[pl.BlockSpec(memory_space=VECTOR)],
        out_specs=[pl.BlockSpec(memory_space=VECTOR)] * len(outs),
        out_shape=outs,
        scratch_shapes=[VECTOR((flat.shape[0] + 2 * half, 128), jnp.float32)],
        compiler_params=pltpu.CompilerParams(vmem_limit_bytes=60 * 2**20),
        cost_estimate=BRIEF,
    )(flat)


def pack_kernel(plan, spans, place_ref, *refs):
    count = len(plan)
    keep_ref, give_ref, flat_ref, out_ref, sems = refs[-5:]
    end = max(offset + rows * columns // 128 for offset, rows, columns in plan)
    begin = min(offset for offset, _, _ in plan)
    if begin:
        flat_ref[pl.ds(0, begin), :] = jnp.zeros((begin, 128), jnp.float32)
    for (offset, rows, columns), ref in zip(plan, refs[:count]):
        pieces = columns // 128
        if rows == 1:
            for j in range(pieces):
                flat_ref[pl.ds(offset + j, 1), :] = ref[:, 128 * j : 128 * (j + 1)]
            continue

        def matrix(i, _):
            at = pl.multiple_of(i * 64, 64)
            for j in range(pieces):
                flat_ref[pl.ds(offset + j + at * pieces, 64, stride=pieces), :] = ref[pl.ds(at, 64), 128 * j : 128 * (j + 1)]
            return 0

        lax.fori_loop(0, rows // 64, matrix, 0)
    for h in range(2):
        at = h ^ place_ref[0]
        filled = 0
        for source, rows, room in spans[h]:
            whole = rows // 64

            def move(i, _):
                to = pl.ds(pl.multiple_of(filled + i * 64, 16), 64)
                out_ref[at, to, :] = flat_ref[pl.ds(source + i * 64, 64), :].astype(jnp.bfloat16)
                return 0

            lax.fori_loop(0, whole, move, 0)
            rest = rows - 64 * whole
            tail = room - 64 * whole
            if tail:
                parts = []
                if rest:
                    parts.append(flat_ref[pl.ds(source + 64 * whole, rest), :])
                if tail > rest:
                    parts.append(jnp.zeros((tail - rest, 128), jnp.float32))
                last = parts[0] if len(parts) == 1 else jnp.concatenate(parts, axis=0)
                out_ref[at, pl.ds(filled + 64 * whole, tail), :] = last.astype(jnp.bfloat16)
            filled = filled + room
    copies = [
        pltpu.make_async_copy(out_ref.at[0], keep_ref, sems.at[0]),
        pltpu.make_async_copy(out_ref.at[1], give_ref, sems.at[1]),
    ]
    for copy in copies:
        copy.start()
    for copy in copies:
        copy.wait()


def packed_halves(grads, begin, spans, half):
    plan = []
    offset = begin
    for grad in grads:
        plan.append((offset, *grad.shape))
        offset = offset + grad.shape[0] * grad.shape[1] // 128
    return pl.pallas_call(
        functools.partial(pack_kernel, plan, spans),
        name="pack",
        in_specs=[pl.BlockSpec(memory_space=pltpu.SMEM)] + [pl.BlockSpec(memory_space=VECTOR)] * len(grads),
        out_specs=[pl.BlockSpec(memory_space=ANY)] * 2,
        out_shape=[jax.ShapeDtypeStruct((half, 128), jnp.bfloat16)] * 2,
        scratch_shapes=[
            VECTOR((offset, 128), jnp.float32),
            VECTOR((2, half, 128), jnp.bfloat16),
            pltpu.SemaphoreType.DMA((2,)),
        ],
        compiler_params=pltpu.CompilerParams(vmem_limit_bytes=60 * 2**20),
        cost_estimate=BRIEF,
    )(bit_of(1).reshape(1), *grads)


def combine_kernel(count, places_ref, *refs):
    parts, outs = refs[:count], refs[-places_ref.shape[0] :]
    rows = outs[0].shape[0]
    for k, out in enumerate(outs):
        at = pl.ds(pl.multiple_of(places_ref[k] * rows, 16), rows)
        terms = [part[at, :].astype(jnp.float32) for part in parts]
        while len(terms) > 1:
            terms = [terms[2 * j] + terms[2 * j + 1] for j in range(len(terms) // 2)]
        out[...] = terms[0].astype(jnp.bfloat16)


def places_of(group):
    if not group:
        return jnp.zeros((1,), jnp.int32)
    place = (lax.axis_index(LINE) // group[0]) % (1 << len(group))
    return place ^ jnp.arange(1 << len(group), dtype=jnp.int32)


def combine(parts, group, after):
    count = 1 << len(group)
    rows = parts[0].shape[0] // count
    outs = pl.pallas_call(
        functools.partial(combine_kernel, len(parts)),
        name="combine",
        in_specs=[pl.BlockSpec(memory_space=pltpu.SMEM)]
        + [pl.BlockSpec(memory_space=VECTOR)] * len(parts),
        out_specs=[pl.BlockSpec(memory_space=VECTOR)] * count,
        out_shape=[jax.ShapeDtypeStruct((rows, 128), jnp.bfloat16)] * count,
        cost_estimate=BRIEF,
    )(behind(places_of(group), after), *parts)
    return list(outs)


def stack_kernel(count, places_ref, *refs):
    out_ref = refs[-1]
    rows = refs[0].shape[0]
    for k in range(count):
        out_ref[pl.ds(pl.multiple_of(places_ref[k] * rows, 16), rows), :] = refs[k][...]


def stack(parts, group, after):
    rows = parts[0].shape[0] * len(parts)
    return pl.pallas_call(
        functools.partial(stack_kernel, len(parts)),
        name="stack",
        in_specs=[pl.BlockSpec(memory_space=pltpu.SMEM)]
        + [pl.BlockSpec(memory_space=VECTOR)] * len(parts),
        out_specs=pl.BlockSpec(memory_space=VECTOR),
        out_shape=jax.ShapeDtypeStruct((rows, 128), jnp.bfloat16),
        cost_estimate=BRIEF,
    )(behind(places_of(group), after), *parts)


def exchanged(parts, group):
    return [parts[0]] + [swapped(parts[k % len(parts)], group[0] * k) for k in range(1, 1 << len(group))]


def bit_groups():
    bits = [1 << k for k in range(1, lax.axis_size(LINE).bit_length() - 1)]
    return [bits[k : k + 2] for k in range(0, len(bits), 2)]


def update_kernel(
    shards, late, shard_rows, meta_ref, scale_ref, early_own, early_other, late_own, late_other, extra_own, extra_other,
    weight_ref, one_ref, two_ref, *refs
):
    moments = refs[: 2 * shards]
    step_ref, grad_ref, new_one_ref, new_two_ref, sum_ref, wide_ref, stage_ref, sems = refs[2 * shards :]
    which, k = pl.program_id(0), pl.program_id(1)
    core, me, turn = meta_ref[0], meta_ref[1], meta_ref[2]
    shard = me ^ k
    half = core ^ which
    rows = sum_ref.shape[0]
    chunk = rows // 7 if rows % 112 == 0 else 64
    scale = scale_ref[0]

    def by_chunks(body):
        def move(i, _):
            body(pl.multiple_of(i * chunk, 16))
            return 0

        lax.fori_loop(0, rows // chunk, move, 0)

    def load(ref):
        def body(at):
            sum_ref[pl.ds(at, chunk), :] = ref[pl.ds(at, chunk), :].astype(jnp.float32) * scale

        by_chunks(body)

    for array, side, is_late in ((early_own, 0, 0), (early_other, 1, 0), (late_own, 0, 1), (late_other, 1, 1)):
        pl.when((which == side) & ((shard < late) == (is_late == 1)))(functools.partial(load, array))
    for array, side in ((extra_own, 0), (extra_other, 1)):

        @pl.when((which == side) & (shard == late) & (half == 0))
        def _():
            sum_ref[pl.ds(0, 8), :] = sum_ref[pl.ds(0, 8), :] + array[pl.ds(0, 8), :].astype(jnp.float32) * scale

    def moved(clipped, one, two):
        one = BETA_ONE * one + (1.0 - BETA_ONE) * clipped
        two = BETA_TWO * two + (1.0 - BETA_TWO) * clipped * clipped
        return one, two

    base = shard * shard_rows + half * rows
    limit = jnp.where(half == 1, shard_rows - rows, rows)
    for j in range(shards):

        @pl.when(k == j)
        def _():
            def body(start):
                at = pl.ds(start, chunk)
                first, second = moments[2 * j][at, :], moments[2 * j + 1][at, :]
                one, two = jnp.where(turn == 1, second, first), jnp.where(turn == 1, first, second)
                one, two = moved(sum_ref[at, :], one.astype(jnp.float32), two.astype(jnp.float32))
                update = (one * (1.0 / FIX_ONE)) / (jnp.sqrt(two * (1.0 / FIX_TWO)) + 1e-08)
                update = update + DECAY * weight_ref[0, at, :].astype(jnp.float32)
                to = pl.ds(base + start, chunk)
                inside = start + lax.broadcasted_iota(jnp.int32, update.shape, 0) < limit
                wide_ref[to, :] = jnp.where(inside, update, wide_ref[to, :])

            by_chunks(body)

    @pl.when(k == 0)
    def _():
        unscale = scale_ref[1]

        def body(start):
            at = pl.ds(start, chunk)
            clipped = sum_ref[at, :]
            one, two = moved(clipped, one_ref[at, :], two_ref[at, :])
            grad_ref[at, :] = clipped * unscale
            new_one_ref[at, :] = one
            new_two_ref[at, :] = two

        by_chunks(body)

    @pl.when((which == 1) & (k == shards - 1))
    def _():
        piece = stage_ref.shape[1]
        total = step_ref.shape[0]

        def sending(i, slot):
            return pltpu.make_async_copy(
                stage_ref.at[slot], step_ref.at[pl.ds(pl.multiple_of(i * piece, 16), piece), :], sems.at[slot]
            )

        count = total // piece
        for i in range(count):
            if i >= 2:
                sending(i - 2, i % 2).wait()
            stage_ref[i % 2] = wide_ref[pl.ds(i * piece, piece), :].astype(jnp.bfloat16)
            sending(i, i % 2).start()
        for i in range(count - 2, count):
            sending(i, i % 2).wait()


def updated(norm, early, late, late_shards, weights, first_moment, second_moment, moments):
    shards = len(moments) // 2
    rows = weights.shape[1]
    shard_rows = first_moment.shape[0] // 128
    line = lax.axis_index(LINE)
    inner = lax.axis_size("inner")
    meta = jnp.stack([line % 2, lax.axis_index("inner"), (line // inner) % 2]).astype(jnp.int32)
    last = shards - 1

    def early_map(side):
        def index(w, k, meta):
            k = jnp.where(w == side, k, last if side == 0 else 0)
            return (jnp.clip((meta[1] ^ k) - late_shards, 0, shards - late_shards - 1), 0)

        return index

    def late_map(side):
        def index(w, k, meta):
            k = jnp.where(w == side, k, last if side == 0 else 0)
            return (jnp.clip(meta[1] ^ k, 0, late_shards - 1), 0)

        return index

    by_half = pl.BlockSpec((rows, 128), lambda w, k, meta: (meta[0] ^ w, 0))
    by_shard = pl.BlockSpec((1, rows, 128), lambda w, k, meta: (2 * (meta[1] ^ k) + (meta[0] ^ w), 0, 0))
    extra = pl.BlockSpec((16, 128), lambda w, k, meta: (late_shards * rows // 16, 0))
    return pl.pallas_call(
        functools.partial(update_kernel, shards, late_shards, shard_rows),
        name="update",
        grid_spec=pltpu.PrefetchScalarGridSpec(
            num_scalar_prefetch=1,
            grid=(2, shards),
            in_specs=[pl.BlockSpec(memory_space=pltpu.SMEM)]
            + [pl.BlockSpec((rows, 128), early_map(side)) for side in range(2)]
            + [pl.BlockSpec((rows, 128), late_map(side)) for side in range(2)]
            + [extra, extra, by_shard, by_half, by_half]
            + [by_half] * (2 * shards),
            out_specs=[pl.BlockSpec(memory_space=ANY), by_half, by_half, by_half],
            scratch_shapes=[
                VECTOR((rows, 128), jnp.float32),
                VECTOR((shards * shard_rows + 2 * rows, 128), jnp.float32),
                VECTOR((2, shards * shard_rows // 9, 128), jnp.bfloat16),
                pltpu.SemaphoreType.DMA((2,)),
            ],
        ),
        out_shape=[jax.ShapeDtypeStruct((shards * shard_rows, 128), jnp.bfloat16)]
        + [jax.ShapeDtypeStruct((shard_rows, 128), jnp.float32)] * 3,
        compiler_params=pltpu.CompilerParams(vmem_limit_bytes=60 * 2**20),
        cost_estimate=BRIEF,
    )(
        meta,
        jnp.stack([1.0 / norm, norm]),
        *early,
        *late,
        *late,
        weights,
        first_moment.reshape(-1, 128),
        second_moment.reshape(-1, 128),
        *moments,
    )


def narrow_kernel(shard_rows, turn_ref, one_ref, two_ref, first_out, second_out):
    shape = first_out.shape
    begin = pl.program_id(0) * shape[0]
    inside = begin + lax.broadcasted_iota(jnp.int32, shape, 0) < shard_rows
    one = jnp.where(inside, one_ref[...], 0.0).astype(jnp.bfloat16)
    two = jnp.where(inside, two_ref[...], 0.0).astype(jnp.bfloat16)
    turned = turn_ref[0] == 1
    first_out[...] = jnp.where(turned, two, one)
    second_out[...] = jnp.where(turned, one, two)


def narrowed(one, two, half, turn):
    block = pl.BlockSpec((half // 2, 128), lambda i: (i, 0))
    return pl.pallas_call(
        functools.partial(narrow_kernel, one.shape[0]),
        name="narrow",
        grid=(4,),
        in_specs=[pl.BlockSpec(memory_space=pltpu.SMEM), block, block],
        out_specs=[block, block],
        out_shape=[jax.ShapeDtypeStruct((2 * half, 128), jnp.bfloat16)] * 2,
        cost_estimate=BRIEF,
    )(turn.reshape(1), one, two)


def bit_of(bit):
    return (lax.axis_index(LINE) // bit) % 2


def on_device(inputs, weights, cotangent, clip_lengths, first_moment, second_moment):
    tok_rows = inputs.shape[0]
    reach = (MOST + tok_rows - 2) // tok_rows
    shard_rows = first_moment.shape[0] // 128
    half = halves_rows(shard_rows)
    (
        first_gain,
        first_bias,
        query_weight,
        query_bias,
        key_weight,
        value_weight,
        value_bias,
        out_weight,
        out_bias,
        second_gain,
        second_bias,
        up_weight,
        up_bias,
        down_weight,
        down_bias,
        padded_weights,
    ) = unpacked(weights, shard_rows)
    base_slot = lax.axis_index(LINE) * tok_rows
    positions = base_slot + jnp.arange(tok_rows, dtype=jnp.int32)
    lower_slot, upper_slot = bounds(positions, clip_lengths)
    low = lower_slot - base_slot + reach * tok_rows
    high = upper_slot - base_slot + reach * tok_rows
    first_block = low.reshape(-1, ROWS_AT)[:, 0] // tok_rows
    last_block = (high.reshape(-1, ROWS_AT)[:, -1] + tok_rows - 1) // tok_rows
    ranges = (first_block, last_block, slot_table(), tok_rows)
    places = base_slot + block_distances()[:, None] * tok_rows + jnp.arange(tok_rows, dtype=jnp.int32)[None]
    marks = clip_marks(places.reshape(-1), clip_lengths)
    closed = penalty(clip_marks(positions, clip_lengths))

    inner = lax.axis_size("inner")
    turn = (lax.axis_index(LINE) // inner) % 2
    first_half, second_half = narrowed(first_moment.reshape(-1, 128), second_moment.reshape(-1, 128), half, turn)
    blocks = halo(inputs, (padded_weights,))
    fetched, *blocks = lax.optimization_barrier((first_half, *blocks))
    rows = projected(
        blocks, query_weight, key_weight, value_weight, first_gain, first_bias, query_bias, value_bias
    )
    fetched = swapped(fetched, 2)
    input_rows = inputs.astype(jnp.float32)
    first_hat, first_dev = standard(input_rows)
    normed = (first_hat * first_gain + first_bias).astype(jnp.bfloat16)

    attended, lse = attend(
        forward_kernel,
        ranges,
        [
            (rows, ("pair", 0)),
            (rows, ("pair", -5)),
            (rows, ("pair", -9)),
            (marks, ("all", 0)),
            (closed, ("all", 0)),
        ],
        [jnp.float32, jnp.float32],
        [pltpu.VMEM((2, 2 * reach + 1, ROWS_AT, tok_rows), jnp.float32)],
    )
    attended, lse, fetched = lax.optimization_barrier((attended, lse, fetched))
    held = {0: (first_half, second_half), 2: (fetched, swapped(fetched, inner))}
    bit = 4
    while bit < inner:
        for place in list(held):
            held[place + bit] = tuple(swapped(piece, bit) for piece in held[place])
        bit = 2 * bit
    moments = []
    for place in range(inner):
        if place % 2 == 0:
            moments += held[place]
        else:
            moments += [swapped(piece, 1) for piece in held[place - 1]]
    mixed = attended.astype(jnp.bfloat16)
    middle = input_rows + plain_dot(mixed, out_weight) + out_bias
    second_hat, second_dev = standard(middle)
    hidden_in = (second_hat * second_gain + second_bias).astype(jnp.bfloat16)
    up_rows = plain_dot(hidden_in, up_weight) + up_bias
    cdf_part = 0.5 * (1.0 + lax.erf(up_rows * INV_ROOT_TWO))
    activated = (up_rows * cdf_part).astype(jnp.bfloat16)
    layer_output = (middle + plain_dot(activated, down_weight) + down_bias).astype(jnp.bfloat16)
    grad_out = cotangent.astype(jnp.float32)
    down_bias_grad = jnp.sum(grad_out, axis=0)
    grad_act = back_dot(cotangent, down_weight)
    pdf_part = jnp.exp(-0.5 * up_rows * up_rows) * INV_ROOT_TWO_PI
    grad_up = (grad_act * (cdf_part + up_rows * pdf_part)).astype(jnp.bfloat16)
    up_bias_grad = jnp.sum(grad_up.astype(jnp.float32), axis=0)
    grad_hidden = back_dot(grad_up, up_weight)
    second_gain_grad = jnp.sum(grad_hidden * second_hat, axis=0)
    second_bias_grad = jnp.sum(grad_hidden, axis=0)
    grad_middle = grad_out + norm_back(grad_hidden, second_hat, second_dev, second_gain)
    grad_branch = grad_middle.astype(jnp.bfloat16)
    out_bias_grad = jnp.sum(grad_branch.astype(jnp.float32), axis=0)
    grad_branch, *moments[4:6] = lax.optimization_barrier((grad_branch, *moments[4:6]))
    sent = mixed_grad(grad_branch, out_weight, attended, lse, clip_marks(positions, clip_lengths))
    line = lax.axis_size(LINE)
    shards = inner
    late_shards = shards // 4
    groups = bit_groups()

    def rounded(count, unit):
        return -(-count // unit) * unit

    def shard_spans(first, last, base):
        spans = ([], [])
        for shard in range(first, last):
            begin = (shard - first) * shard_rows + base
            spans[0].append((begin, half, half))
            spans[1].append((begin + half, shard_rows - half, half))
        return spans

    def query_step(pairs, after):
        return attend(
            query_kernel,
            ranges,
            [
                (rows, ("pair", 0)),
                (rows, ("pair", -5)),
                (rows, ("pair", -9)),
                (sent, ("pair", 0)),
                (sent, ("column", 4)),
                (marks, ("all", 0)),
                (closed, ("all", 0)),
            ],
            [jnp.bfloat16],
            [],
            pairs,
            after,
        )

    def key_step(pairs, after):
        return attend(
            key_kernel,
            ranges,
            [
                (rows, ("pair", 4)),
                (rows, ("pair", 8)),
                (rows, ("pair", -1)),
                (closed, ("all", 0)),
            ]
            + [(block, ("pair", 0)) for block in grad_blocks]
            + [(block, ("column", 4)) for block in grad_blocks],
            [jnp.bfloat16, jnp.bfloat16],
            [pltpu.VMEM((len(grad_blocks), tok_rows, 128), jnp.bfloat16)] * 2,
            pairs,
            after,
        )

    query_parts = query_step((0, 2), ())
    grad_blocks = halo(sent, query_parts)
    activated, hidden_in, mixed = (behind(array, query_parts) for array in (activated, hidden_in, mixed))
    down_grad = rows_dot(activated, cotangent)
    up_grad = rows_dot(hidden_in, grad_up)
    out_grad = rows_dot(mixed, grad_branch)

    early_rows = [
        out_grad,
        out_bias_grad,
        second_gain_grad,
        second_bias_grad,
        up_grad,
        up_bias_grad,
        down_grad,
        down_bias_grad,
    ]
    early_rows = [section.reshape(-1, section.shape[-1]) for section in early_rows]
    early_half = rounded((shards - late_shards) * half, 8 * line)
    spans = shard_spans(late_shards, shards, 0)
    for span in spans:
        span.append((0, 0, early_half - (shards - late_shards) * half))
    early_keep, early_give = packed_halves(early_rows, D // 128, spans, early_half)
    early_got = swapped(early_give, 1)

    query_parts += query_step((2, 2), (early_give,))
    parts = combine([early_keep, early_got], groups[0], query_parts)
    got = exchanged(parts, groups[0])
    query_low = jnp.concatenate(query_parts, axis=1)
    work = [(1, 1), (2, 1), (3, 1)]
    done = key_step((0, 1), parts[:1])
    key_parts, value_parts = [done[0]], [done[1]]
    held_back = done[:1]
    for at, group in enumerate(groups):
        parts = combine(got, groups[at + 1] if at + 1 < len(groups) else [], held_back)
        if at + 1 < len(groups):
            got = exchanged(parts, groups[at + 1])
        if work:
            done = key_step(work.pop(0), parts[:1])
            key_parts.append(done[0])
            value_parts.append(done[1])
            held_back = done[:1]
    piece = parts[0]
    for at, group in enumerate(groups[::-1]):
        got = exchanged([piece], group)
        if work and at > 0:
            done = key_step(work.pop(0), [piece])
            key_parts.append(done[0])
            value_parts.append(done[1])
            held_back = done[:1]
        piece = stack(got, group, held_back)
    early_other = swapped(piece, 1)
    for pairs in work:
        done = key_step(pairs, [piece])
        key_parts.append(done[0])
        value_parts.append(done[1])
    early = (piece, early_other)
    key_low = jnp.concatenate(key_parts, axis=1)
    value_low = jnp.concatenate(value_parts, axis=1)
    query_grad = rows_dot(normed, query_low)
    query_bias_grad = jnp.sum(query_low.astype(jnp.float32), axis=0)
    key_grad = rows_dot(normed, key_low)
    value_grad = rows_dot(normed, value_low)
    value_bias_grad = jnp.sum(value_low.astype(jnp.float32), axis=0)
    grad_normed = (
        back_dot(query_low, query_weight)
        + back_dot(key_low, key_weight)
        + back_dot(value_low, value_weight)
    )
    first_gain_grad = jnp.sum(grad_normed * first_hat, axis=0)
    first_bias_grad = jnp.sum(grad_normed, axis=0)
    input_grad = (grad_middle + norm_back(grad_normed, first_hat, first_dev, first_gain)).astype(
        jnp.bfloat16
    )

    late_rows = [
        first_gain_grad,
        first_bias_grad,
        query_grad,
        query_bias_grad,
        key_grad,
        value_grad,
        value_bias_grad,
    ]
    late_rows = [section.reshape(-1, section.shape[-1]) for section in late_rows]
    tail = max(1, 1 << (len(groups[0])))
    late_half = rounded(late_shards * half + 16, 16 * tail)
    spans = shard_spans(0, late_shards, 0)
    spare = late_half - late_shards * half
    spans[0].append((late_shards * shard_rows, D // 128, spare))
    spans[1].append((0, 0, spare))
    keep, give = packed_halves(late_rows, 0, spans, late_half)
    parts = combine([keep, swapped(give, 1)], groups[0], ())
    (piece,) = combine(exchanged(parts, groups[0]), [], ())
    for group in groups[1:]:
        (piece,) = combine(exchanged([piece], group), [], ())
    piece = stack(exchanged([piece], groups[0]), groups[0], ())
    late = (piece, swapped(piece, 1))

    def square_sum(pair):
        sums = [jnp.sum(jnp.square(part.astype(jnp.float32))) for part in pair]
        return sums[0] + sums[1]

    grad_norm = jnp.sqrt(square_sum(early) + square_sum(late))
    steps, grad_shard, moment_one, moment_two = updated(
        jnp.maximum(grad_norm, 1.0), early, late, late_shards, padded_weights, first_moment, second_moment, moments
    )
    weight_step = steps.reshape(-1)
    return (
        layer_output,
        input_grad,
        grad_shard.reshape(-1),
        grad_norm,
        moment_one.reshape(-1),
        moment_two.reshape(-1),
        weight_step,
    )


def solution(mesh):
    return jax.shard_map(
        on_device,
        mesh=mesh,
        in_specs=(
            P(("outer", "inner"), None),
            P(),
            P(("outer", "inner"), None),
            P(),
            P("inner"),
            P("inner"),
        ),
        out_specs=(
            P(("outer", "inner"), None),
            P(("outer", "inner"), None),
            P("inner"),
            P(),
            P("inner"),
            P("inner"),
            P(),
        ),
        check_vma=False,
    )
```

```python
import functools
import math

import jax
import jax.numpy as jnp
from jax import lax
from jax.experimental import pallas as pl
from jax.experimental.pallas import tpu as pltpu
from jax.sharding import PartitionSpec as P

D = 512
HEADS = 8
FF = 2048
MOST = 1500


BETA_ONE = 0.9
BETA_TWO = 0.999
FIX_ONE = 1.0 - (0.9**10) ** 10
FIX_TWO = 1.0 - (0.999**10) ** 10
DECAY = 0.1
INV_ROOT_TWO = 1.0 / math.sqrt(2.0)
INV_ROOT_TWO_PI = 1.0 / math.sqrt(2.0 * math.pi)


def layouts():
    return [
        (D,),
        (D,),
        (D, D),
        (D,),
        (D, D),
        (D, D),
        (D,),
        (D, D),
        (D,),
        (D,),
        (D,),
        (D, FF),
        (FF,),
        (FF, D),
        (D,),
    ]


def plain_dot(matrix_one, matrix_two):
    return jnp.dot(matrix_one, matrix_two, preferred_element_type=jnp.float32)


def rows_dot(matrix_one, matrix_two):
    return lax.dot_general(
        matrix_one, matrix_two, (((0,), (0,)), ((), ())), preferred_element_type=jnp.float32
    )


def back_dot(matrix_one, matrix_two):
    return lax.dot_general(
        matrix_one, matrix_two, (((1,), (1,)), ((), ())), preferred_element_type=jnp.float32
    )


def standard(values):
    center = jnp.mean(values, axis=-1, keepdims=True)
    centered = values - center
    inverse_dev = lax.rsqrt(jnp.mean(centered * centered, axis=-1, keepdims=True) + 1e-05)
    return (centered * inverse_dev, inverse_dev)


def norm_back(grad_normed, normed_hat, inverse_dev, gain):
    scaled = grad_normed * gain
    return inverse_dev * (
        scaled
        - jnp.mean(scaled, axis=-1, keepdims=True)
        - normed_hat * jnp.mean(scaled * normed_hat, axis=-1, keepdims=True)
    )


def bounds(positions, clip_lengths):
    starts = jnp.cumsum(clip_lengths, dtype=jnp.int32) - clip_lengths
    member = (
        jnp.sum((positions[:, None] >= starts[None, :]).astype(jnp.int32), axis=1, dtype=jnp.int32)
        - 1
    )
    onehot = (
        jnp.arange(clip_lengths.shape[0], dtype=jnp.int32)[None, :] == member[:, None]
    ).astype(jnp.int32)
    lower_slot = jnp.sum(onehot * starts[None, :], axis=1, dtype=jnp.int32)
    upper_slot = lower_slot + jnp.sum(onehot * clip_lengths[None, :], axis=1, dtype=jnp.int32)
    return (lower_slot, upper_slot)


LINE = ("outer", "inner")
NEG = -1e30
BRIEF = pl.CostEstimate(flops=1000, bytes_accessed=1000, transcendentals=0)


def shifted(block, distance):
    n = lax.axis_size(LINE)
    return lax.ppermute(block, LINE, [(i + distance, i) for i in range(n) if 0 <= i + distance < n])


def swapped(block, bit):
    n = lax.axis_size(LINE)
    return lax.ppermute(block, LINE, [(i ^ bit, i) for i in range(n)])


def halo(block, before=()):
    n = lax.axis_size(LINE)
    left = shifted(block, -2)
    right = shifted(block, 2)
    partner = swapped(block, 1)
    route = [(i + (3 if i % 2 else -3), i) for i in range(n)]
    far = lax.ppermute(block, LINE, [(s, t) for s, t in route if 0 <= s < n])
    passed_left, passed_right, *_ = lax.optimization_barrier((left, right, *before))
    turned = [swapped(passed_left, 1), swapped(passed_right, 1)]
    return [block, partner, left, right, *turned, far]


def block_distances():
    odd = lax.axis_index(LINE) % 2
    even_far = jnp.array([0, 1, -2, 2, -1, 3, -3], jnp.int32)
    odd_far = jnp.array([0, -1, -2, 2, -3, 1, 3], jnp.int32)
    return jnp.where(odd == 1, odd_far, even_far)


def slot_table():
    odd = lax.axis_index(LINE) % 2
    even_slots = jnp.array([6, 2, 4, 0, 1, 3, 5], jnp.int32)
    odd_slots = jnp.array([4, 2, 1, 0, 5, 3, 6], jnp.int32)
    return jnp.where(odd == 1, odd_slots, even_slots)


def dot_nt(a, b):
    return lax.dot_general(a, b, (((1,), (1,)), ((), ())), preferred_element_type=jnp.float32)


def head_halves(pair):
    first = lax.broadcasted_iota(jnp.int32, pair.shape, 1) < pair.shape[1] // 2
    zero = jnp.zeros_like(pair)
    return jnp.where(first, pair, zero), jnp.where(first, zero, pair)


def over_lanes(tile, op):
    parts = [tile[:, 128 * j : 128 * (j + 1)] for j in range(tile.shape[1] // 128)]
    while len(parts) > 1:
        rest = parts[len(parts) // 2 * 2 :]
        parts = [op(parts[2 * j], parts[2 * j + 1]) for j in range(len(parts) // 2)] + rest
    return parts[0]


LSE_PARTS, DELTA_PARTS = 3, 2
DELTA_AT = LSE_PARTS * HEADS
CLIPS_AT = DELTA_AT + DELTA_PARTS * HEADS


def lane_of(shape):
    return lax.broadcasted_iota(jnp.int32, shape, 1)


def among(lane, begin, count):
    return (lane >= begin) & (lane < begin + count)


def beside(pair, marks):
    return jnp.concatenate([pair, marks.astype(pair.dtype)], axis=1)


def clip_marks(positions, clip_lengths):
    ends = jnp.cumsum(clip_lengths, dtype=jnp.int32)
    starts = ends - clip_lengths
    spare = 128 - CLIPS_AT - clip_lengths.shape[0]
    assert spare >= 0
    big = jnp.iinfo(jnp.int32).max
    lower = jnp.concatenate([jnp.full((CLIPS_AT,), -big, jnp.int32), starts, jnp.full((spare,), big, jnp.int32)])
    upper = jnp.concatenate([jnp.full((CLIPS_AT,), big, jnp.int32), ends, jnp.full((spare,), big, jnp.int32)])
    inside = (positions[:, None] >= lower[None]) & (positions[:, None] < upper[None])
    return inside.astype(jnp.bfloat16)


def penalty(marks):
    closed = (lane_of(marks.shape) >= CLIPS_AT) & (marks == 0)
    return jnp.where(closed, NEG, 0.0).astype(jnp.bfloat16)


def forward_kernel(
    begin, rows_at, first_ref, last_ref, slot_ref, q_ref, k_ref, v_ref, mark_ref, closed_ref, o_ref, lse_ref, s_ref
):
    width = q_ref.shape[0]
    for i in range(width // rows_at):
        rows = pl.ds(i * rows_at, rows_at)
        queries = [
            beside(half, closed_ref[rows, :]) for half in head_halves(q_ref[rows, :] * jnp.bfloat16(0.125))
        ]

        def scores(block, peaks):
            at = pl.ds(pl.multiple_of(slot_ref[block] * width, width), width)
            keys = beside(k_ref[at, :], mark_ref[at, :])
            found = []
            for h in range(2):
                score = dot_nt(queries[h], keys)
                s_ref[h, block] = score
                found.append(jnp.maximum(peaks[h], over_lanes(score, jnp.maximum)))
            return tuple(found)

        start = jnp.full((rows_at, 128), NEG, jnp.float32)
        peaks = lax.fori_loop(first_ref[i], last_ref[i], scores, (start, start))
        peaks = [jnp.max(peak, axis=1, keepdims=True) for peak in peaks]

        def mix(block, sums):
            at = pl.ds(pl.multiple_of(slot_ref[block] * width, width), width)
            values = beside(v_ref[at, :], mark_ref[at, :])
            found = []
            for h in range(2):
                soft = jnp.exp(s_ref[h, block] - peaks[h]).astype(jnp.bfloat16)
                found.append(sums[h] + jnp.dot(soft, values, preferred_element_type=jnp.float32))
            return tuple(found)

        zero = jnp.zeros((rows_at, 256), jnp.float32)
        sums = lax.fori_loop(first_ref[i], last_ref[i], mix, (zero, zero))
        totals = [part[:, 128:129] for part in sums]
        even = lane_of((rows_at, 128)) < 64
        o_ref[rows, :] = jnp.where(even, sums[0][:, :128] / totals[0], sums[1][:, :128] / totals[1])
        lse_ref[rows, :] = jnp.where(even, peaks[0] + jnp.log(totals[0]), peaks[1] + jnp.log(totals[1]))


def query_kernel(
    begin, rows_at, first_ref, last_ref, slot_ref, q_ref, k_ref, v_ref, g_ref, own_ref, mark_ref, closed_ref, dq_ref
):
    width = q_ref.shape[0]
    pair = pl.program_id(0) + begin
    for i in range(width // rows_at):
        rows = pl.ds(i * rows_at, rows_at)
        own, closed = own_ref[rows, :], closed_ref[rows, :]
        lane = lane_of(own.shape)
        zero = jnp.zeros_like(own)
        queries, grads = [], []
        halves = zip(head_halves(q_ref[rows, :] * jnp.bfloat16(0.125)), head_halves(g_ref[rows, :]))
        for h, (query, grad) in enumerate(halves):
            head = 2 * pair + h
            queries.append(beside(query, jnp.where(among(lane, LSE_PARTS * head, LSE_PARTS), own, closed)))
            grads.append(beside(grad, jnp.where(among(lane, DELTA_AT + DELTA_PARTS * head, DELTA_PARTS), own, zero)))

        def step(block, carried):
            at = pl.ds(pl.multiple_of(slot_ref[block] * width, width), width)
            keys = k_ref[at, :]
            values = beside(v_ref[at, :], mark_ref[at, :])
            marked = beside(keys, mark_ref[at, :])
            found = []
            for h in range(2):
                soft = jnp.exp(dot_nt(queries[h], marked))
                grad = (soft * dot_nt(grads[h], values)).astype(jnp.bfloat16)
                found.append(carried[h] + jnp.dot(grad, keys, preferred_element_type=jnp.float32))
            return tuple(found)

        start = jnp.zeros((rows_at, 128), jnp.float32)
        sums = lax.fori_loop(first_ref[i], last_ref[i], step, (start, start))
        dq_ref[rows, :] = (jnp.where(lane < 64, sums[0], sums[1]) * 0.125).astype(jnp.bfloat16)


def key_kernel(begin, rows_at, first_ref, last_ref, slot_ref, k_ref, v_ref, q_ref, closed_ref, *refs):
    dk_ref, dv_ref, grad_ref, mark_ref = refs[-4:]
    width = k_ref.shape[0]
    pair = pl.program_id(0) + begin
    blocks = grad_ref.shape[0]
    for j in range(blocks):
        grad_ref[j] = refs[j][...]

    @pl.when(pl.program_id(0) == 0)
    def _():
        for j in range(blocks):
            mark_ref[j] = refs[blocks + j][...]

    for i in range(width // rows_at):
        rows = pl.ds(i * rows_at, rows_at)
        closed = closed_ref[rows, :]
        lane = lane_of(closed.shape)
        one, zero = jnp.ones_like(closed), jnp.zeros_like(closed)
        keys, values = [], []
        halves = zip(head_halves(k_ref[rows, :] * jnp.bfloat16(0.125)), head_halves(v_ref[rows, :]))
        for h, (key, value) in enumerate(halves):
            head = 2 * pair + h
            keys.append(beside(key, jnp.where(among(lane, LSE_PARTS * head, LSE_PARTS), one, closed)))
            values.append(beside(value, jnp.where(among(lane, DELTA_AT + DELTA_PARTS * head, DELTA_PARTS), one, zero)))

        def step(block, carried):
            slot = slot_ref[block]
            queries = q_ref[pl.ds(pl.multiple_of(slot * width, width), width), :]
            grads, marks = grad_ref[slot], mark_ref[slot]
            marked, graded = beside(queries, marks), beside(grads, marks)
            key_sums, value_sums = [], []
            for h in range(2):
                soft = jnp.exp(dot_nt(keys[h], marked))
                value_sums.append(
                    carried[1][h] + jnp.dot(soft.astype(jnp.bfloat16), grads, preferred_element_type=jnp.float32)
                )
                grad = (soft * dot_nt(values[h], graded)).astype(jnp.bfloat16)
                key_sums.append(carried[0][h] + jnp.dot(grad, queries, preferred_element_type=jnp.float32))
            return tuple(key_sums), tuple(value_sums)

        start = jnp.zeros((rows_at, 128), jnp.float32)
        key_sums, value_sums = lax.fori_loop(first_ref[i], last_ref[i], step, ((start, start), (start, start)))
        dk_ref[rows, :] = (jnp.where(lane < 64, key_sums[0], key_sums[1]) * 0.125).astype(jnp.bfloat16)
        dv_ref[rows, :] = jnp.where(lane < 64, value_sums[0], value_sums[1]).astype(jnp.bfloat16)


def mixed_grad_kernel(branch_ref, weight_ref, mixed_ref, lse_ref, own_ref, sent_ref, mark_ref):
    step = pl.program_id(0)

    @pl.when(step == 0)
    def _():
        mark_ref[...] = own_ref[...].astype(jnp.float32)

    @pl.when(step < D // 128)
    def _():
        grad = dot_nt(branch_ref[...], weight_ref[...]).astype(jnp.bfloat16)
        sent_ref[...] = grad
        product = grad.astype(jnp.float32) * mixed_ref[...]
        lane = lane_of(product.shape)
        for h, part in enumerate(head_halves(product)):
            head = 2 * step + h
            delta = -jnp.sum(part, axis=1, keepdims=True)
            lse = -lse_ref[:, 64 * h : 64 * h + 1]
            for value, begin, count in (
                (lse, LSE_PARTS * head, LSE_PARTS),
                (delta, DELTA_AT + DELTA_PARTS * head, DELTA_PARTS),
            ):
                for k in range(count):
                    rounded = value.astype(jnp.bfloat16).astype(jnp.float32)
                    mark_ref[...] = jnp.where(lane == begin + k, rounded, mark_ref[...])
                    value = value - rounded

    @pl.when(step == D // 128)
    def _():
        sent_ref[...] = mark_ref[...].astype(jnp.bfloat16)


def mixed_grad(branch, out_weight, mixed, lse, own_marks):
    width = branch.shape[0]
    last = D // 128 - 1
    column = pl.BlockSpec((width, 128), lambda h: (0, jnp.minimum(h, last)))
    return pl.pallas_call(
        mixed_grad_kernel,
        name="mixed_grad",
        grid=(D // 128 + 1,),
        in_specs=[
            pl.BlockSpec((width, D), lambda h: (0, 0)),
            pl.BlockSpec((128, D), lambda h: (jnp.minimum(h, last), 0)),
            column,
            column,
            pl.BlockSpec((width, 128), lambda h: (0, 0)),
        ],
        out_specs=pl.BlockSpec((width, 128), lambda h: (0, h)),
        out_shape=jax.ShapeDtypeStruct((width, D + 128), jnp.bfloat16),
        scratch_shapes=[pltpu.VMEM((width, 128), jnp.float32)],
        cost_estimate=BRIEF,
    )(branch, out_weight, mixed, lse, own_marks)


def project_kernel(count, *refs):
    query_ref, key_ref, value_ref, gain_ref, bias_ref, query_bias_ref, value_bias_ref, out_ref, row_ref = refs[count:]
    step = pl.program_id(0)
    for j in range(count):

        @pl.when(step == j)
        def _():
            row_ref[...] = refs[j][...]

    rows = 256
    for i in range(row_ref.shape[0] // rows):
        at = pl.ds(i * rows, rows)
        hat, _ = standard(row_ref[at, :].astype(jnp.float32))
        normed = (hat * gain_ref[...] + bias_ref[...]).astype(jnp.bfloat16)
        out_ref[at, 0:D] = (plain_dot(normed, query_ref[...]) + query_bias_ref[...]).astype(jnp.bfloat16)
        out_ref[at, D : 2 * D] = plain_dot(normed, key_ref[...]).astype(jnp.bfloat16)
        out_ref[at, 2 * D :] = (plain_dot(normed, value_ref[...]) + value_bias_ref[...]).astype(jnp.bfloat16)


def projected(blocks, *weights):
    width = blocks[0].shape[0]
    whole = [pl.BlockSpec(array.shape, lambda i: (0, 0)) for array in (*blocks, *weights)]
    return pl.pallas_call(
        functools.partial(project_kernel, len(blocks)),
        name="project",
        grid=(len(blocks),),
        in_specs=whole,
        out_specs=pl.BlockSpec((width, 3 * D), lambda i: (i, 0)),
        out_shape=jax.ShapeDtypeStruct((len(blocks) * width, 3 * D), jnp.bfloat16),
        scratch_shapes=[pltpu.VMEM((width, D), jnp.bfloat16)],
        compiler_params=pltpu.CompilerParams(vmem_limit_bytes=63 * 2**20),
        cost_estimate=BRIEF,
    )(*blocks, *weights)


ROWS_AT = 512


def attend(kernel, ranges, operands, results, scratch, pairs=(0, D // 128), after=()):
    begin, count = pairs
    tok_rows = ranges[3]
    specs = []
    for array, (kind, at) in operands:
        if kind == "pair":
            rows = array.shape[0] if at < 0 else tok_rows
            at = (abs(at) - 1 if at < 0 else at) + begin
            specs.append(pl.BlockSpec((rows, 128), lambda h, *_, at=at: (0, at + h)))
        elif kind == "column":
            specs.append(pl.BlockSpec((tok_rows, 128), lambda h, *_, at=at: (0, at)))
        else:
            specs.append(pl.BlockSpec(array.shape, lambda h, *_, n=array.ndim: (0,) * n))
    return pl.pallas_call(
        functools.partial(kernel, begin, ROWS_AT),
        grid_spec=pltpu.PrefetchScalarGridSpec(
            num_scalar_prefetch=3,
            grid=(count,),
            in_specs=specs,
            out_specs=[pl.BlockSpec((tok_rows, 128), lambda h, *_: (0, h))] * len(results),
            scratch_shapes=scratch,
        ),
        out_shape=[jax.ShapeDtypeStruct((tok_rows, 128 * count), kept) for kept in results],
        compiler_params=pltpu.CompilerParams(vmem_limit_bytes=48 * 2**20),
        cost_estimate=BRIEF,
    )(*[behind(bound, after) for bound in ranges[:1]], *ranges[1:3], *[array for array, _ in operands])


VECTOR = pltpu.VMEM
ANY = pl.ANY


def behind(value, others):
    return lax.optimization_barrier((value, *others))[0]


def halves_rows(shard_rows):
    return -(-shard_rows // 128) * 64


def unpack_kernel(plan, shard_rows, flat_ref, *refs):
    wide_ref = refs[-1]
    padded_ref = refs[-2]
    total = flat_ref.shape[0]
    chunk = 432

    def widen(i, _):
        rows = pl.ds(pl.multiple_of(i * chunk, 16), chunk)
        wide_ref[rows, :] = flat_ref[rows, :].astype(jnp.float32)
        return 0

    lax.fori_loop(0, total // chunk, widen, 0)
    wide_ref[pl.ds(total, wide_ref.shape[0] - total), :] = jnp.zeros((wide_ref.shape[0] - total, 128), jnp.float32)
    for (offset, rows, columns, begin), ref in zip(plan, refs[:-2]):
        pieces = columns // 128
        if rows == 1:
            for j in range(pieces):
                ref[:, 128 * j : 128 * (j + 1)] = wide_ref[pl.ds(offset + j, 1), :]
            continue

        def matrix(i, _):
            at = pl.multiple_of(i * 64, 64)
            for j in range(pieces):
                part = wide_ref[pl.ds(offset + j + at * pieces, 64, stride=pieces), :]
                ref[pl.ds(at, 64), begin + 128 * j : begin + 128 * (j + 1)] = part.astype(jnp.bfloat16)
            return 0

        lax.fori_loop(0, rows // 64, matrix, 0)
    shards = total // shard_rows
    half = halves_rows(shard_rows)
    for s in range(shards):
        for h in range(2):

            def pad(i, _):
                part = wide_ref[pl.ds(s * shard_rows + h * half + i * 64, 64), :]
                padded_ref[s * 2 + h, pl.ds(pl.multiple_of(i * 64, 64), 64), :] = part.astype(jnp.bfloat16)
                return 0

            lax.fori_loop(0, half // 64, pad, 0)


def unpacked(weights, shard_rows):
    flat = weights.reshape(-1, 128)
    half = halves_rows(shard_rows)
    plan, outs = [], []
    offset = 0
    for layout in layouts():
        rows, columns = layout if len(layout) == 2 else (1, layout[0])
        plan.append([offset, rows, columns, 0])
        outs.append(jax.ShapeDtypeStruct((rows, columns), jnp.bfloat16 if rows > 1 else jnp.float32))
        offset = offset + rows * columns // 128
    shards = flat.shape[0] // shard_rows
    outs.append(jax.ShapeDtypeStruct((2 * shards, half, 128), jnp.bfloat16))
    return pl.pallas_call(
        functools.partial(unpack_kernel, plan, shard_rows),
        name="unpack",
        in_specs=[pl.BlockSpec(memory_space=VECTOR)],
        out_specs=[pl.BlockSpec(memory_space=VECTOR)] * len(outs),
        out_shape=outs,
        scratch_shapes=[VECTOR((flat.shape[0] + 2 * half, 128), jnp.float32)],
        compiler_params=pltpu.CompilerParams(vmem_limit_bytes=60 * 2**20),
        cost_estimate=BRIEF,
    )(flat)


def pack_kernel(plan, spans, place_ref, *refs):
    count = len(plan)
    keep_ref, give_ref, flat_ref, out_ref, sems = refs[-5:]
    end = max(offset + rows * columns // 128 for offset, rows, columns in plan)
    begin = min(offset for offset, _, _ in plan)
    if begin:
        flat_ref[pl.ds(0, begin), :] = jnp.zeros((begin, 128), jnp.float32)
    for (offset, rows, columns), ref in zip(plan, refs[:count]):
        pieces = columns // 128
        if rows == 1:
            for j in range(pieces):
                flat_ref[pl.ds(offset + j, 1), :] = ref[:, 128 * j : 128 * (j + 1)]
            continue

        def matrix(i, _):
            at = pl.multiple_of(i * 64, 64)
            for j in range(pieces):
                flat_ref[pl.ds(offset + j + at * pieces, 64, stride=pieces), :] = ref[pl.ds(at, 64), 128 * j : 128 * (j + 1)]
            return 0

        lax.fori_loop(0, rows // 64, matrix, 0)
    for h in range(2):
        at = h ^ place_ref[0]
        filled = 0
        for source, rows, room in spans[h]:
            whole = rows // 64

            def move(i, _):
                to = pl.ds(pl.multiple_of(filled + i * 64, 16), 64)
                out_ref[at, to, :] = flat_ref[pl.ds(source + i * 64, 64), :].astype(jnp.bfloat16)
                return 0

            lax.fori_loop(0, whole, move, 0)
            rest = rows - 64 * whole
            tail = room - 64 * whole
            if tail:
                parts = []
                if rest:
                    parts.append(flat_ref[pl.ds(source + 64 * whole, rest), :])
                if tail > rest:
                    parts.append(jnp.zeros((tail - rest, 128), jnp.float32))
                last = parts[0] if len(parts) == 1 else jnp.concatenate(parts, axis=0)
                out_ref[at, pl.ds(filled + 64 * whole, tail), :] = last.astype(jnp.bfloat16)
            filled = filled + room
    copies = [
        pltpu.make_async_copy(out_ref.at[0], keep_ref, sems.at[0]),
        pltpu.make_async_copy(out_ref.at[1], give_ref, sems.at[1]),
    ]
    for copy in copies:
        copy.start()
    for copy in copies:
        copy.wait()


def packed_halves(grads, begin, spans, half):
    plan = []
    offset = begin
    for grad in grads:
        plan.append((offset, *grad.shape))
        offset = offset + grad.shape[0] * grad.shape[1] // 128
    return pl.pallas_call(
        functools.partial(pack_kernel, plan, spans),
        name="pack",
        in_specs=[pl.BlockSpec(memory_space=pltpu.SMEM)] + [pl.BlockSpec(memory_space=VECTOR)] * len(grads),
        out_specs=[pl.BlockSpec(memory_space=ANY)] * 2,
        out_shape=[jax.ShapeDtypeStruct((half, 128), jnp.bfloat16)] * 2,
        scratch_shapes=[
            VECTOR((offset, 128), jnp.float32),
            VECTOR((2, half, 128), jnp.bfloat16),
            pltpu.SemaphoreType.DMA((2,)),
        ],
        compiler_params=pltpu.CompilerParams(vmem_limit_bytes=60 * 2**20),
        cost_estimate=BRIEF,
    )(bit_of(1).reshape(1), *grads)


def combine_kernel(count, places_ref, *refs):
    parts, outs = refs[:count], refs[-places_ref.shape[0] :]
    rows = outs[0].shape[0]
    for k, out in enumerate(outs):
        at = pl.ds(pl.multiple_of(places_ref[k] * rows, 16), rows)
        terms = [part[at, :].astype(jnp.float32) for part in parts]
        while len(terms) > 1:
            terms = [terms[2 * j] + terms[2 * j + 1] for j in range(len(terms) // 2)]
        out[...] = terms[0].astype(jnp.bfloat16)


def places_of(group):
    if not group:
        return jnp.zeros((1,), jnp.int32)
    place = (lax.axis_index(LINE) // group[0]) % (1 << len(group))
    return place ^ jnp.arange(1 << len(group), dtype=jnp.int32)


def combine(parts, group, after):
    count = 1 << len(group)
    rows = parts[0].shape[0] // count
    outs = pl.pallas_call(
        functools.partial(combine_kernel, len(parts)),
        name="combine",
        in_specs=[pl.BlockSpec(memory_space=pltpu.SMEM)]
        + [pl.BlockSpec(memory_space=VECTOR)] * len(parts),
        out_specs=[pl.BlockSpec(memory_space=VECTOR)] * count,
        out_shape=[jax.ShapeDtypeStruct((rows, 128), jnp.bfloat16)] * count,
        cost_estimate=BRIEF,
    )(behind(places_of(group), after), *parts)
    return list(outs)


def stack_kernel(count, places_ref, *refs):
    out_ref = refs[-1]
    rows = refs[0].shape[0]
    for k in range(count):
        out_ref[pl.ds(pl.multiple_of(places_ref[k] * rows, 16), rows), :] = refs[k][...]


def stack(parts, group, after):
    rows = parts[0].shape[0] * len(parts)
    return pl.pallas_call(
        functools.partial(stack_kernel, len(parts)),
        name="stack",
        in_specs=[pl.BlockSpec(memory_space=pltpu.SMEM)]
        + [pl.BlockSpec(memory_space=VECTOR)] * len(parts),
        out_specs=pl.BlockSpec(memory_space=VECTOR),
        out_shape=jax.ShapeDtypeStruct((rows, 128), jnp.bfloat16),
        cost_estimate=BRIEF,
    )(behind(places_of(group), after), *parts)


def exchanged(parts, group):
    return [parts[0]] + [swapped(parts[k % len(parts)], group[0] * k) for k in range(1, 1 << len(group))]


def bit_groups():
    bits = [1 << k for k in range(1, lax.axis_size(LINE).bit_length() - 1)]
    return [bits[k : k + 2] for k in range(0, len(bits), 2)]


def square_sum_kernel(one_ref, two_ref, out_ref):
    sums = []
    for ref in (one_ref, two_ref):
        rows = ref.shape[0]
        chunk = 128 if rows % 128 == 0 else 64

        def add(i, total):
            part = ref[pl.ds(pl.multiple_of(i * chunk, 64), chunk), :].astype(jnp.float32)
            part = part * part
            while part.shape[0] > 8:
                part = part[: part.shape[0] // 2] + part[part.shape[0] // 2 :]
            return total + part

        sums.append(jnp.sum(lax.fori_loop(0, rows // chunk, add, jnp.zeros((8, 128), jnp.float32)), keepdims=True))
    out_ref[...] = jnp.broadcast_to(sums[0] + sums[1], (1, 128))


def square_sum(pair):
    return pl.pallas_call(
        square_sum_kernel,
        name="square_sum",
        in_specs=[pl.BlockSpec(memory_space=VECTOR)] * 2,
        out_specs=pl.BlockSpec(memory_space=VECTOR),
        out_shape=jax.ShapeDtypeStruct((1, 128), jnp.float32),
        cost_estimate=BRIEF,
    )(*pair)


def update_kernel(
    shards, late, shard_rows, meta_ref, scale_ref, early_own, early_other, late_own, late_other, extra_own, extra_other,
    weight_ref, one_ref, two_ref, *refs
):
    moments = refs[: 2 * shards]
    step_ref, grad_ref, new_one_ref, new_two_ref, sum_ref, wide_ref, stage_ref, sems = refs[2 * shards :]
    which, k = pl.program_id(0), pl.program_id(1)
    core, me, turn = meta_ref[0], meta_ref[1], meta_ref[2]
    shard = me ^ k
    half = core ^ which
    rows = sum_ref.shape[0]
    chunk = rows // 7 if rows % 112 == 0 else 64
    scale = scale_ref[0]

    def by_chunks(body):
        def move(i, _):
            body(pl.multiple_of(i * chunk, 16))
            return 0

        lax.fori_loop(0, rows // chunk, move, 0)

    def load(ref):
        def body(at):
            sum_ref[pl.ds(at, chunk), :] = ref[pl.ds(at, chunk), :].astype(jnp.float32)

        by_chunks(body)

    for array, side, is_late in ((early_own, 0, 0), (early_other, 1, 0), (late_own, 0, 1), (late_other, 1, 1)):
        pl.when((which == side) & ((shard < late) == (is_late == 1)))(functools.partial(load, array))
    for array, side in ((extra_own, 0), (extra_other, 1)):

        @pl.when((which == side) & (shard == late) & (half == 0))
        def _():
            sum_ref[pl.ds(0, 8), :] = sum_ref[pl.ds(0, 8), :] + array[pl.ds(0, 8), :].astype(jnp.float32)

    slope_one = (1.0 - BETA_ONE) * scale
    slope_two = (1.0 - BETA_TWO) * scale * scale

    base = shard * shard_rows + half * rows
    limit = jnp.where(half == 1, shard_rows - rows, rows)
    for j in range(shards):

        @pl.when(k == j)
        def _():
            def body(start):
                at = pl.ds(start, chunk)
                first, second = moments[2 * j][at, :], moments[2 * j + 1][at, :]
                one, two = jnp.where(turn == 1, second, first), jnp.where(turn == 1, first, second)
                grad = sum_ref[at, :]
                one = (BETA_ONE / FIX_ONE) * one.astype(jnp.float32) + (slope_one * (1.0 / FIX_ONE)) * grad
                two = (BETA_TWO / FIX_TWO) * two.astype(jnp.float32) + (slope_two * (1.0 / FIX_TWO)) * grad * grad
                root = two * lax.rsqrt(jnp.maximum(two, 1e-37))
                update = one / (root + 1e-08) + DECAY * weight_ref[0, at, :].astype(jnp.float32)
                to = pl.ds(base + start, chunk)
                inside = start + lax.broadcasted_iota(jnp.int32, update.shape, 0) < limit
                wide_ref[to, :] = jnp.where(inside, update, wide_ref[to, :])

            by_chunks(body)

    @pl.when(k == 0)
    def _():
        def body(start):
            at = pl.ds(start, chunk)
            grad = sum_ref[at, :]
            grad_ref[at, :] = grad
            new_one_ref[at, :] = BETA_ONE * one_ref[at, :] + slope_one * grad
            new_two_ref[at, :] = BETA_TWO * two_ref[at, :] + slope_two * grad * grad

        by_chunks(body)

    @pl.when((which == 1) & (k == shards - 1))
    def _():
        piece = stage_ref.shape[1]
        total = step_ref.shape[0]

        def sending(i, slot):
            return pltpu.make_async_copy(
                stage_ref.at[slot], step_ref.at[pl.ds(pl.multiple_of(i * piece, 16), piece), :], sems.at[slot]
            )

        count = total // piece
        for i in range(count):
            if i >= 2:
                sending(i - 2, i % 2).wait()
            stage_ref[i % 2] = wide_ref[pl.ds(i * piece, piece), :].astype(jnp.bfloat16)
            sending(i, i % 2).start()
        for i in range(count - 2, count):
            sending(i, i % 2).wait()


def updated(norm, early, late, late_shards, weights, first_moment, second_moment, moments):
    shards = len(moments) // 2
    rows = weights.shape[1]
    shard_rows = first_moment.shape[0] // 128
    line = lax.axis_index(LINE)
    inner = lax.axis_size("inner")
    meta = jnp.stack([line % 2, lax.axis_index("inner"), (line // inner) % 2]).astype(jnp.int32)
    last = shards - 1

    def early_map(side):
        def index(w, k, meta):
            k = jnp.where(w == side, k, last if side == 0 else 0)
            return (jnp.clip((meta[1] ^ k) - late_shards, 0, shards - late_shards - 1), 0)

        return index

    def late_map(side):
        def index(w, k, meta):
            k = jnp.where(w == side, k, last if side == 0 else 0)
            return (jnp.clip(meta[1] ^ k, 0, late_shards - 1), 0)

        return index

    by_half = pl.BlockSpec((rows, 128), lambda w, k, meta: (meta[0] ^ w, 0))
    by_shard = pl.BlockSpec((1, rows, 128), lambda w, k, meta: (2 * (meta[1] ^ k) + (meta[0] ^ w), 0, 0))
    extra = pl.BlockSpec((16, 128), lambda w, k, meta: (late_shards * rows // 16, 0))
    return pl.pallas_call(
        functools.partial(update_kernel, shards, late_shards, shard_rows),
        name="update",
        grid_spec=pltpu.PrefetchScalarGridSpec(
            num_scalar_prefetch=1,
            grid=(2, shards),
            in_specs=[pl.BlockSpec(memory_space=pltpu.SMEM)]
            + [pl.BlockSpec((rows, 128), early_map(side)) for side in range(2)]
            + [pl.BlockSpec((rows, 128), late_map(side)) for side in range(2)]
            + [extra, extra, by_shard, by_half, by_half]
            + [by_half] * (2 * shards),
            out_specs=[pl.BlockSpec(memory_space=ANY), by_half, by_half, by_half],
            scratch_shapes=[
                VECTOR((rows, 128), jnp.float32),
                VECTOR((shards * shard_rows + 2 * rows, 128), jnp.float32),
                VECTOR((2, shards * shard_rows // 9, 128), jnp.bfloat16),
                pltpu.SemaphoreType.DMA((2,)),
            ],
        ),
        out_shape=[jax.ShapeDtypeStruct((shards * shard_rows, 128), jnp.bfloat16)]
        + [jax.ShapeDtypeStruct((shard_rows, 128), jnp.float32)] * 3,
        compiler_params=pltpu.CompilerParams(vmem_limit_bytes=60 * 2**20),
        cost_estimate=BRIEF,
    )(
        meta,
        norm,
        *early,
        *late,
        *late,
        weights,
        first_moment.reshape(-1, 128),
        second_moment.reshape(-1, 128),
        *moments,
    )


def narrow_kernel(shard_rows, turn_ref, one_ref, two_ref, first_out, second_out):
    shape = first_out.shape
    begin = pl.program_id(0) * shape[0]
    inside = begin + lax.broadcasted_iota(jnp.int32, shape, 0) < shard_rows
    one = jnp.where(inside, one_ref[...], 0.0).astype(jnp.bfloat16)
    two = jnp.where(inside, two_ref[...], 0.0).astype(jnp.bfloat16)
    turned = turn_ref[0] == 1
    first_out[...] = jnp.where(turned, two, one)
    second_out[...] = jnp.where(turned, one, two)


def narrowed(one, two, half, turn):
    block = pl.BlockSpec((half // 2, 128), lambda i: (i, 0))
    return pl.pallas_call(
        functools.partial(narrow_kernel, one.shape[0]),
        name="narrow",
        grid=(4,),
        in_specs=[pl.BlockSpec(memory_space=pltpu.SMEM), block, block],
        out_specs=[block, block],
        out_shape=[jax.ShapeDtypeStruct((2 * half, 128), jnp.bfloat16)] * 2,
        cost_estimate=BRIEF,
    )(turn.reshape(1), one, two)


def bit_of(bit):
    return (lax.axis_index(LINE) // bit) % 2


def on_device(inputs, weights, cotangent, clip_lengths, first_moment, second_moment):
    tok_rows = inputs.shape[0]
    reach = (MOST + tok_rows - 2) // tok_rows
    shard_rows = first_moment.shape[0] // 128
    half = halves_rows(shard_rows)
    (
        first_gain,
        first_bias,
        query_weight,
        query_bias,
        key_weight,
        value_weight,
        value_bias,
        out_weight,
        out_bias,
        second_gain,
        second_bias,
        up_weight,
        up_bias,
        down_weight,
        down_bias,
        padded_weights,
    ) = unpacked(weights, shard_rows)
    base_slot = lax.axis_index(LINE) * tok_rows
    positions = base_slot + jnp.arange(tok_rows, dtype=jnp.int32)
    lower_slot, upper_slot = bounds(positions, clip_lengths)
    low = lower_slot - base_slot + reach * tok_rows
    high = upper_slot - base_slot + reach * tok_rows
    first_block = low.reshape(-1, ROWS_AT)[:, 0] // tok_rows
    last_block = (high.reshape(-1, ROWS_AT)[:, -1] + tok_rows - 1) // tok_rows
    ranges = (first_block, last_block, slot_table(), tok_rows)
    places = base_slot + block_distances()[:, None] * tok_rows + jnp.arange(tok_rows, dtype=jnp.int32)[None]
    marks = clip_marks(places.reshape(-1), clip_lengths)
    closed = penalty(clip_marks(positions, clip_lengths))

    inner = lax.axis_size("inner")
    turn = (lax.axis_index(LINE) // inner) % 2
    first_half, second_half = narrowed(first_moment.reshape(-1, 128), second_moment.reshape(-1, 128), half, turn)
    blocks = halo(inputs, (padded_weights,))
    fetched, *blocks = lax.optimization_barrier((first_half, *blocks))
    rows = projected(
        blocks, query_weight, key_weight, value_weight, first_gain, first_bias, query_bias, value_bias
    )
    fetched = swapped(fetched, 2)
    input_rows = inputs.astype(jnp.float32)
    first_hat, first_dev = standard(input_rows)
    normed = (first_hat * first_gain + first_bias).astype(jnp.bfloat16)

    attended, lse = attend(
        forward_kernel,
        ranges,
        [
            (rows, ("pair", 0)),
            (rows, ("pair", -5)),
            (rows, ("pair", -9)),
            (marks, ("all", 0)),
            (closed, ("all", 0)),
        ],
        [jnp.float32, jnp.float32],
        [pltpu.VMEM((2, 2 * reach + 1, ROWS_AT, tok_rows), jnp.float32)],
    )
    attended, lse, fetched = lax.optimization_barrier((attended, lse, fetched))
    passed = swapped(fetched, inner)
    held = {0: (first_half, second_half), 2: (fetched, passed)}
    bit = 4
    while bit < inner:
        for place in list(held):
            held[place + bit] = tuple(swapped(piece, bit) for piece in held[place])
        bit = 2 * bit
    moments = []
    for place in range(inner):
        if place % 2 == 0:
            moments += held[place]
        else:
            moments += [swapped(piece, 1) for piece in held[place - 1]]
    mixed = attended.astype(jnp.bfloat16)
    middle = input_rows + plain_dot(mixed, out_weight) + out_bias
    second_hat, second_dev = standard(middle)
    hidden_in = (second_hat * second_gain + second_bias).astype(jnp.bfloat16)
    up_rows = plain_dot(hidden_in, up_weight) + up_bias
    cdf_part = 0.5 * (1.0 + lax.erf(up_rows * INV_ROOT_TWO))
    activated = (up_rows * cdf_part).astype(jnp.bfloat16)
    layer_output = (middle + plain_dot(activated, down_weight) + down_bias).astype(jnp.bfloat16)
    grad_out = cotangent.astype(jnp.float32)
    down_bias_grad = jnp.sum(grad_out, axis=0)
    grad_act = back_dot(cotangent, down_weight)
    pdf_part = jnp.exp(-0.5 * up_rows * up_rows) * INV_ROOT_TWO_PI
    grad_up = (grad_act * (cdf_part + up_rows * pdf_part)).astype(jnp.bfloat16)
    up_bias_grad = jnp.sum(grad_up.astype(jnp.float32), axis=0)
    grad_hidden = back_dot(grad_up, up_weight)
    second_gain_grad = jnp.sum(grad_hidden * second_hat, axis=0)
    second_bias_grad = jnp.sum(grad_hidden, axis=0)
    grad_middle = grad_out + norm_back(grad_hidden, second_hat, second_dev, second_gain)
    grad_branch = grad_middle.astype(jnp.bfloat16)
    out_bias_grad = jnp.sum(grad_branch.astype(jnp.float32), axis=0)
    sent = mixed_grad(grad_branch, out_weight, attended, lse, clip_marks(positions, clip_lengths))
    line = lax.axis_size(LINE)
    shards = inner
    late_shards = shards // 4
    groups = bit_groups()

    def rounded(count, unit):
        return -(-count // unit) * unit

    def shard_spans(first, last, base):
        spans = ([], [])
        for shard in range(first, last):
            begin = (shard - first) * shard_rows + base
            spans[0].append((begin, half, half))
            spans[1].append((begin + half, shard_rows - half, half))
        return spans

    def query_step(pairs, after):
        return attend(
            query_kernel,
            ranges,
            [
                (rows, ("pair", 0)),
                (rows, ("pair", -5)),
                (rows, ("pair", -9)),
                (sent, ("pair", 0)),
                (sent, ("column", 4)),
                (marks, ("all", 0)),
                (closed, ("all", 0)),
            ],
            [jnp.bfloat16],
            [],
            pairs,
            after,
        )

    def key_step(pairs, after):
        return attend(
            key_kernel,
            ranges,
            [
                (rows, ("pair", 4)),
                (rows, ("pair", 8)),
                (rows, ("pair", -1)),
                (closed, ("all", 0)),
            ]
            + [(block, ("pair", 0)) for block in grad_blocks]
            + [(block, ("column", 4)) for block in grad_blocks],
            [jnp.bfloat16, jnp.bfloat16],
            [pltpu.VMEM((len(grad_blocks), tok_rows, 128), jnp.bfloat16)] * 2,
            pairs,
            after,
        )

    query_parts = query_step((0, 2), ())
    grad_blocks = halo(sent, query_parts)
    activated, hidden_in, mixed = (behind(array, query_parts) for array in (activated, hidden_in, mixed))
    down_grad = rows_dot(activated, cotangent)
    up_grad = rows_dot(hidden_in, grad_up)
    out_grad = rows_dot(mixed, grad_branch)

    early_rows = [
        out_grad,
        out_bias_grad,
        second_gain_grad,
        second_bias_grad,
        up_grad,
        up_bias_grad,
        down_grad,
        down_bias_grad,
    ]
    early_rows = [section.reshape(-1, section.shape[-1]) for section in early_rows]
    early_half = rounded((shards - late_shards) * half, 8 * line)
    spans = shard_spans(late_shards, shards, 0)
    for span in spans:
        span.append((0, 0, early_half - (shards - late_shards) * half))
    early_keep, early_give = packed_halves(early_rows, D // 128, spans, early_half)
    early_got = swapped(early_give, 1)

    query_parts += query_step((2, 2), (early_give,))
    parts = combine([early_keep, early_got], groups[0], query_parts)
    got = exchanged(parts, groups[0])
    query_low = jnp.concatenate(query_parts, axis=1)
    work = [(1, 1), (2, 1), (3, 1)]
    done = key_step((0, 1), parts[:1])
    key_parts, value_parts = [done[0]], [done[1]]
    held_back = done[:1]
    for at, group in enumerate(groups):
        parts = combine(got, groups[at + 1] if at + 1 < len(groups) else [], held_back)
        if at + 1 < len(groups):
            got = exchanged(parts, groups[at + 1])
        if work:
            done = key_step(work.pop(0), parts[:1])
            key_parts.append(done[0])
            value_parts.append(done[1])
            held_back = done[:1]
    piece = parts[0]
    for at, group in enumerate(groups[::-1]):
        got = exchanged([piece], group)
        if work and at > 0:
            done = key_step(work.pop(0), [piece])
            key_parts.append(done[0])
            value_parts.append(done[1])
            held_back = done[:1]
        piece = stack(got, group, held_back)
    early_other = swapped(piece, 1)
    for pairs in work:
        done = key_step(pairs, [piece])
        key_parts.append(done[0])
        value_parts.append(done[1])
    early = (piece, early_other)
    key_low = jnp.concatenate(key_parts, axis=1)
    value_low = jnp.concatenate(value_parts, axis=1)
    query_grad = rows_dot(normed, query_low)
    query_bias_grad = jnp.sum(query_low.astype(jnp.float32), axis=0)
    key_grad = rows_dot(normed, key_low)
    value_grad = rows_dot(normed, value_low)
    value_bias_grad = jnp.sum(value_low.astype(jnp.float32), axis=0)
    grad_normed = (
        back_dot(query_low, query_weight)
        + back_dot(key_low, key_weight)
        + back_dot(value_low, value_weight)
    )
    first_gain_grad = jnp.sum(grad_normed * first_hat, axis=0)
    first_bias_grad = jnp.sum(grad_normed, axis=0)
    input_grad = (grad_middle + norm_back(grad_normed, first_hat, first_dev, first_gain)).astype(
        jnp.bfloat16
    )

    late_rows = [
        first_gain_grad,
        first_bias_grad,
        query_grad,
        query_bias_grad,
        key_grad,
        value_grad,
        value_bias_grad,
    ]
    late_rows = [section.reshape(-1, section.shape[-1]) for section in late_rows]
    tail = max(1, 1 << (len(groups[0])))
    late_half = rounded(late_shards * half + 16, 16 * tail)
    spans = shard_spans(0, late_shards, 0)
    spare = late_half - late_shards * half
    spans[0].append((late_shards * shard_rows, D // 128, spare))
    spans[1].append((0, 0, spare))
    keep, give = packed_halves(late_rows, 0, spans, late_half)
    early_square = square_sum(early)
    parts = combine([keep, swapped(give, 1)], groups[0], ())
    (piece,) = combine(exchanged(parts, groups[0]), [], ())
    for group in groups[1:]:
        (piece,) = combine(exchanged([piece], group), [], (early_square,))
    piece = stack(exchanged([piece], groups[0]), groups[0], ())
    late = (piece, swapped(piece, 1))

    grad_norm = jnp.sqrt(early_square + square_sum(late))[0, 0]
    steps, grad_shard, moment_one, moment_two = updated(
        (1.0 / jnp.maximum(grad_norm, 1.0)).reshape(1),
        early,
        late,
        late_shards,
        padded_weights,
        first_moment,
        second_moment,
        moments,
    )
    weight_step = steps.reshape(-1)
    return (
        layer_output,
        input_grad,
        grad_shard.reshape(-1),
        grad_norm,
        moment_one.reshape(-1),
        moment_two.reshape(-1),
        weight_step,
    )


def solution(mesh):
    return jax.shard_map(
        on_device,
        mesh=mesh,
        in_specs=(
            P(("outer", "inner"), None),
            P(),
            P(("outer", "inner"), None),
            P(),
            P("inner"),
            P("inner"),
        ),
        out_specs=(
            P(("outer", "inner"), None),
            P(("outer", "inner"), None),
            P("inner"),
            P(),
            P("inner"),
            P("inner"),
            P(),
        ),
        check_vma=False,
    )
```

```python
import functools
import math

import jax
import jax.numpy as jnp
from jax import lax
from jax.experimental import pallas as pl
from jax.experimental.pallas import tpu as pltpu
from jax.sharding import PartitionSpec as P

D = 512
HEADS = 8
FF = 2048
MOST = 1500


BETA_ONE = 0.9
BETA_TWO = 0.999
FIX_ONE = 1.0 - (0.9**10) ** 10
FIX_TWO = 1.0 - (0.999**10) ** 10
DECAY = 0.1
INV_ROOT_TWO = 1.0 / math.sqrt(2.0)
INV_ROOT_TWO_PI = 1.0 / math.sqrt(2.0 * math.pi)


def layouts():
    return [
        (D,),
        (D,),
        (D, D),
        (D,),
        (D, D),
        (D, D),
        (D,),
        (D, D),
        (D,),
        (D,),
        (D,),
        (D, FF),
        (FF,),
        (FF, D),
        (D,),
    ]


def plain_dot(matrix_one, matrix_two):
    return jnp.dot(matrix_one, matrix_two, preferred_element_type=jnp.float32)


def rows_dot(matrix_one, matrix_two):
    return lax.dot_general(
        matrix_one, matrix_two, (((0,), (0,)), ((), ())), preferred_element_type=jnp.float32
    )


def back_dot(matrix_one, matrix_two):
    return lax.dot_general(
        matrix_one, matrix_two, (((1,), (1,)), ((), ())), preferred_element_type=jnp.float32
    )


def standard(values):
    center = jnp.mean(values, axis=-1, keepdims=True)
    centered = values - center
    inverse_dev = lax.rsqrt(jnp.mean(centered * centered, axis=-1, keepdims=True) + 1e-05)
    return (centered * inverse_dev, inverse_dev)


def norm_back(grad_normed, normed_hat, inverse_dev, gain):
    scaled = grad_normed * gain
    return inverse_dev * (
        scaled
        - jnp.mean(scaled, axis=-1, keepdims=True)
        - normed_hat * jnp.mean(scaled * normed_hat, axis=-1, keepdims=True)
    )


def bounds(positions, clip_lengths):
    starts = jnp.cumsum(clip_lengths, dtype=jnp.int32) - clip_lengths
    member = (
        jnp.sum((positions[:, None] >= starts[None, :]).astype(jnp.int32), axis=1, dtype=jnp.int32)
        - 1
    )
    onehot = (
        jnp.arange(clip_lengths.shape[0], dtype=jnp.int32)[None, :] == member[:, None]
    ).astype(jnp.int32)
    lower_slot = jnp.sum(onehot * starts[None, :], axis=1, dtype=jnp.int32)
    upper_slot = lower_slot + jnp.sum(onehot * clip_lengths[None, :], axis=1, dtype=jnp.int32)
    return (lower_slot, upper_slot)


LINE = ("outer", "inner")
NEG = -1e30
BRIEF = pl.CostEstimate(flops=1000, bytes_accessed=1000, transcendentals=0)


def shifted(block, distance):
    n = lax.axis_size(LINE)
    return lax.ppermute(block, LINE, [(i + distance, i) for i in range(n) if 0 <= i + distance < n])


def swapped(block, bit):
    n = lax.axis_size(LINE)
    return lax.ppermute(block, LINE, [(i ^ bit, i) for i in range(n)])


def halo(block, before=()):
    n = lax.axis_size(LINE)
    left = shifted(block, -2)
    right = shifted(block, 2)
    partner = swapped(block, 1)
    route = [(i + (3 if i % 2 else -3), i) for i in range(n)]
    far = lax.ppermute(block, LINE, [(s, t) for s, t in route if 0 <= s < n])
    passed_left, passed_right, *_ = lax.optimization_barrier((left, right, *before))
    turned = [swapped(passed_left, 1), swapped(passed_right, 1)]
    return [block, partner, left, right, *turned, far]


def block_distances():
    odd = lax.axis_index(LINE) % 2
    even_far = jnp.array([0, 1, -2, 2, -1, 3, -3], jnp.int32)
    odd_far = jnp.array([0, -1, -2, 2, -3, 1, 3], jnp.int32)
    return jnp.where(odd == 1, odd_far, even_far)


def slot_table():
    odd = lax.axis_index(LINE) % 2
    even_slots = jnp.array([6, 2, 4, 0, 1, 3, 5], jnp.int32)
    odd_slots = jnp.array([4, 2, 1, 0, 5, 3, 6], jnp.int32)
    return jnp.where(odd == 1, odd_slots, even_slots)


def dot_nt(a, b):
    return lax.dot_general(a, b, (((1,), (1,)), ((), ())), preferred_element_type=jnp.float32)


def head_halves(pair):
    first = lax.broadcasted_iota(jnp.int32, pair.shape, 1) < pair.shape[1] // 2
    zero = jnp.zeros_like(pair)
    return jnp.where(first, pair, zero), jnp.where(first, zero, pair)


def over_lanes(tile, op):
    parts = [tile[:, 128 * j : 128 * (j + 1)] for j in range(tile.shape[1] // 128)]
    while len(parts) > 1:
        rest = parts[len(parts) // 2 * 2 :]
        parts = [op(parts[2 * j], parts[2 * j + 1]) for j in range(len(parts) // 2)] + rest
    return parts[0]


LSE_PARTS, DELTA_PARTS = 3, 2
DELTA_AT = LSE_PARTS * HEADS
CLIPS_AT = DELTA_AT + DELTA_PARTS * HEADS


def lane_of(shape):
    return lax.broadcasted_iota(jnp.int32, shape, 1)


def among(lane, begin, count):
    return (lane >= begin) & (lane < begin + count)


def beside(pair, marks):
    return jnp.concatenate([pair, marks.astype(pair.dtype)], axis=1)


def clip_marks(positions, clip_lengths):
    ends = jnp.cumsum(clip_lengths, dtype=jnp.int32)
    starts = ends - clip_lengths
    spare = 128 - CLIPS_AT - clip_lengths.shape[0]
    assert spare >= 0
    big = jnp.iinfo(jnp.int32).max
    lower = jnp.concatenate([jnp.full((CLIPS_AT,), -big, jnp.int32), starts, jnp.full((spare,), big, jnp.int32)])
    upper = jnp.concatenate([jnp.full((CLIPS_AT,), big, jnp.int32), ends, jnp.full((spare,), big, jnp.int32)])
    inside = (positions[:, None] >= lower[None]) & (positions[:, None] < upper[None])
    return inside.astype(jnp.bfloat16)


def penalty(marks):
    closed = (lane_of(marks.shape) >= CLIPS_AT) & (marks == 0)
    return jnp.where(closed, NEG, 0.0).astype(jnp.bfloat16)


def over_blocks(first_ref, last_ref, rows, work, start):
    half = rows // 2
    carried = (start, start)
    spans = (
        (first_ref[0], first_ref[1], 0, half),
        (first_ref[1], last_ref[0], 0, rows),
        (last_ref[0], last_ref[1], half, half),
    )
    for lower, upper, begin, count in spans:

        def step(block, carried):
            found = work(block, begin, count)
            upper_half, lower_half = carried
            if begin == 0:
                upper_half = tuple(join(old, new[:half]) for (join, new), old in zip(found, upper_half))
            if begin + count == rows:
                lower_half = tuple(join(old, new[count - half :]) for (join, new), old in zip(found, lower_half))
            return upper_half, lower_half

        carried = lax.fori_loop(lower, upper, step, carried)
    return [jnp.concatenate(halves, axis=0) for halves in zip(*carried)]


def forward_kernel(begin, first_ref, last_ref, slot_ref, q_ref, k_ref, v_ref, mark_ref, closed_ref, o_ref, lse_ref, s_ref):
    width = q_ref.shape[0]
    queries = [beside(half, closed_ref[...]) for half in head_halves(q_ref[...] * jnp.bfloat16(0.125))]

    def scores(block, begin, count):
        at = pl.ds(pl.multiple_of(slot_ref[block] * width, width), width)
        keys = beside(k_ref[at, :], mark_ref[at, :])
        found = []
        for h in range(2):
            score = dot_nt(queries[h][begin : begin + count], keys)
            s_ref[h, block, pl.ds(begin, count), :] = score
            found.append((jnp.maximum, over_lanes(score, jnp.maximum)))
        return found

    start = jnp.full((width // 2, 128), NEG, jnp.float32)
    peaks = over_blocks(first_ref, last_ref, width, scores, (start, start))
    peaks = [jnp.max(peak, axis=1, keepdims=True) for peak in peaks]

    def mix(block, begin, count):
        at = pl.ds(pl.multiple_of(slot_ref[block] * width, width), width)
        values = beside(v_ref[at, :], mark_ref[at, :])
        found = []
        for h in range(2):
            score = s_ref[h, block, pl.ds(begin, count), :]
            soft = jnp.exp(score - peaks[h][begin : begin + count]).astype(jnp.bfloat16)
            found.append((jnp.add, jnp.dot(soft, values, preferred_element_type=jnp.float32)))
        return found

    start = jnp.zeros((width // 2, 256), jnp.float32)
    sums = over_blocks(first_ref, last_ref, width, mix, (start, start))
    totals = [part[:, 128:129] for part in sums]
    even = lane_of((width, 128)) < 64
    o_ref[...] = jnp.where(even, sums[0][:, :128] / totals[0], sums[1][:, :128] / totals[1])
    lse_ref[...] = jnp.where(even, peaks[0] + jnp.log(totals[0]), peaks[1] + jnp.log(totals[1]))


def query_kernel(
    begin, first_ref, last_ref, slot_ref, q_ref, k_ref, v_ref, g_ref, own_ref, mark_ref, closed_ref, dq_ref
):
    width = q_ref.shape[0]
    pair = pl.program_id(0) + begin
    own, closed = own_ref[...], closed_ref[...]
    lane = lane_of(own.shape)
    zero = jnp.zeros_like(own)
    queries, grads = [], []
    halves = zip(head_halves(q_ref[...] * jnp.bfloat16(0.125)), head_halves(g_ref[...]))
    for h, (query, grad) in enumerate(halves):
        head = 2 * pair + h
        queries.append(beside(query, jnp.where(among(lane, LSE_PARTS * head, LSE_PARTS), own, closed)))
        grads.append(beside(grad, jnp.where(among(lane, DELTA_AT + DELTA_PARTS * head, DELTA_PARTS), own, zero)))

    def work(block, begin, count):
        at = pl.ds(pl.multiple_of(slot_ref[block] * width, width), width)
        keys = k_ref[at, :]
        values = beside(v_ref[at, :], mark_ref[at, :])
        marked = beside(keys, mark_ref[at, :])
        found = []
        for h in range(2):
            soft = jnp.exp(dot_nt(queries[h][begin : begin + count], marked))
            grad = (soft * dot_nt(grads[h][begin : begin + count], values)).astype(jnp.bfloat16)
            found.append((jnp.add, jnp.dot(grad, keys, preferred_element_type=jnp.float32)))
        return found

    start = jnp.zeros((width // 2, 128), jnp.float32)
    sums = over_blocks(first_ref, last_ref, width, work, (start, start))
    dq_ref[...] = (jnp.where(lane < 64, sums[0], sums[1]) * 0.125).astype(jnp.bfloat16)


def key_kernel(begin, first_ref, last_ref, slot_ref, k_ref, v_ref, q_ref, closed_ref, *refs):
    dk_ref, dv_ref, grad_ref, mark_ref = refs[-4:]
    width = k_ref.shape[0]
    pair = pl.program_id(0) + begin
    blocks = grad_ref.shape[0]
    for j in range(blocks):
        grad_ref[j] = refs[j][...]

    @pl.when(pl.program_id(0) == 0)
    def _():
        for j in range(blocks):
            mark_ref[j] = refs[blocks + j][...]

    closed = closed_ref[...]
    lane = lane_of(closed.shape)
    one, zero = jnp.ones_like(closed), jnp.zeros_like(closed)
    keys, values = [], []
    halves = zip(head_halves(k_ref[...] * jnp.bfloat16(0.125)), head_halves(v_ref[...]))
    for h, (key, value) in enumerate(halves):
        head = 2 * pair + h
        keys.append(beside(key, jnp.where(among(lane, LSE_PARTS * head, LSE_PARTS), one, closed)))
        values.append(beside(value, jnp.where(among(lane, DELTA_AT + DELTA_PARTS * head, DELTA_PARTS), one, zero)))

    def work(block, begin, count):
        slot = slot_ref[block]
        queries = q_ref[pl.ds(pl.multiple_of(slot * width, width), width), :]
        grads, marks = grad_ref[slot], mark_ref[slot]
        marked, graded = beside(queries, marks), beside(grads, marks)
        found = []
        for h in range(2):
            soft = jnp.exp(dot_nt(keys[h][begin : begin + count], marked))
            grad = (soft * dot_nt(values[h][begin : begin + count], graded)).astype(jnp.bfloat16)
            found.append((jnp.add, jnp.dot(grad, queries, preferred_element_type=jnp.float32)))
            found.append((jnp.add, jnp.dot(soft.astype(jnp.bfloat16), grads, preferred_element_type=jnp.float32)))
        return found

    start = jnp.zeros((width // 2, 128), jnp.float32)
    sums = over_blocks(first_ref, last_ref, width, work, (start,) * 4)
    dk_ref[...] = (jnp.where(lane < 64, sums[0], sums[2]) * 0.125).astype(jnp.bfloat16)
    dv_ref[...] = jnp.where(lane < 64, sums[1], sums[3]).astype(jnp.bfloat16)


def mixed_grad_kernel(branch_ref, weight_ref, mixed_ref, lse_ref, own_ref, sent_ref, mark_ref):
    step = pl.program_id(0)

    @pl.when(step == 0)
    def _():
        mark_ref[...] = own_ref[...].astype(jnp.float32)

    @pl.when(step < D // 128)
    def _():
        grad = dot_nt(branch_ref[...], weight_ref[...]).astype(jnp.bfloat16)
        sent_ref[...] = grad
        product = grad.astype(jnp.float32) * mixed_ref[...]
        lane = lane_of(product.shape)
        for h, part in enumerate(head_halves(product)):
            head = 2 * step + h
            delta = -jnp.sum(part, axis=1, keepdims=True)
            lse = -lse_ref[:, 64 * h : 64 * h + 1]
            for value, begin, count in (
                (lse, LSE_PARTS * head, LSE_PARTS),
                (delta, DELTA_AT + DELTA_PARTS * head, DELTA_PARTS),
            ):
                for k in range(count):
                    rounded = value.astype(jnp.bfloat16).astype(jnp.float32)
                    mark_ref[...] = jnp.where(lane == begin + k, rounded, mark_ref[...])
                    value = value - rounded

    @pl.when(step == D // 128)
    def _():
        sent_ref[...] = mark_ref[...].astype(jnp.bfloat16)


def mixed_grad(branch, out_weight, mixed, lse, own_marks):
    width = branch.shape[0]
    last = D // 128 - 1
    column = pl.BlockSpec((width, 128), lambda h: (0, jnp.minimum(h, last)))
    return pl.pallas_call(
        mixed_grad_kernel,
        name="mixed_grad",
        grid=(D // 128 + 1,),
        in_specs=[
            pl.BlockSpec((width, D), lambda h: (0, 0)),
            pl.BlockSpec((128, D), lambda h: (jnp.minimum(h, last), 0)),
            column,
            column,
            pl.BlockSpec((width, 128), lambda h: (0, 0)),
        ],
        out_specs=pl.BlockSpec((width, 128), lambda h: (0, h)),
        out_shape=jax.ShapeDtypeStruct((width, D + 128), jnp.bfloat16),
        scratch_shapes=[pltpu.VMEM((width, 128), jnp.float32)],
        cost_estimate=BRIEF,
    )(branch, out_weight, mixed, lse, own_marks)


def project_kernel(count, *refs):
    query_ref, key_ref, value_ref, gain_ref, bias_ref, query_bias_ref, value_bias_ref, out_ref, row_ref = refs[count:]
    step = pl.program_id(0)
    for j in range(count):

        @pl.when(step == j)
        def _():
            row_ref[...] = refs[j][...]

    rows = 256
    for i in range(row_ref.shape[0] // rows):
        at = pl.ds(i * rows, rows)
        hat, _ = standard(row_ref[at, :].astype(jnp.float32))
        normed = (hat * gain_ref[...] + bias_ref[...]).astype(jnp.bfloat16)
        out_ref[at, 0:D] = (plain_dot(normed, query_ref[...]) + query_bias_ref[...]).astype(jnp.bfloat16)
        out_ref[at, D : 2 * D] = plain_dot(normed, key_ref[...]).astype(jnp.bfloat16)
        out_ref[at, 2 * D :] = (plain_dot(normed, value_ref[...]) + value_bias_ref[...]).astype(jnp.bfloat16)


def projected(blocks, *weights):
    width = blocks[0].shape[0]
    whole = [pl.BlockSpec(array.shape, lambda i: (0, 0)) for array in (*blocks, *weights)]
    return pl.pallas_call(
        functools.partial(project_kernel, len(blocks)),
        name="project",
        grid=(len(blocks),),
        in_specs=whole,
        out_specs=pl.BlockSpec((width, 3 * D), lambda i: (i, 0)),
        out_shape=jax.ShapeDtypeStruct((len(blocks) * width, 3 * D), jnp.bfloat16),
        scratch_shapes=[pltpu.VMEM((width, D), jnp.bfloat16)],
        compiler_params=pltpu.CompilerParams(vmem_limit_bytes=63 * 2**20),
        cost_estimate=BRIEF,
    )(*blocks, *weights)


def attend(kernel, ranges, operands, results, scratch, pairs=(0, D // 128), after=()):
    begin, count = pairs
    tok_rows = ranges[3]
    specs = []
    for array, (kind, at) in operands:
        if kind == "pair":
            rows = array.shape[0] if at < 0 else tok_rows
            at = (abs(at) - 1 if at < 0 else at) + begin
            specs.append(pl.BlockSpec((rows, 128), lambda h, *_, at=at: (0, at + h)))
        elif kind == "column":
            specs.append(pl.BlockSpec((tok_rows, 128), lambda h, *_, at=at: (0, at)))
        else:
            specs.append(pl.BlockSpec(array.shape, lambda h, *_, n=array.ndim: (0,) * n))
    return pl.pallas_call(
        functools.partial(kernel, begin),
        grid_spec=pltpu.PrefetchScalarGridSpec(
            num_scalar_prefetch=3,
            grid=(count,),
            in_specs=specs,
            out_specs=[pl.BlockSpec((tok_rows, 128), lambda h, *_: (0, h))] * len(results),
            scratch_shapes=scratch,
        ),
        out_shape=[jax.ShapeDtypeStruct((tok_rows, 128 * count), kept) for kept in results],
        compiler_params=pltpu.CompilerParams(vmem_limit_bytes=48 * 2**20),
        cost_estimate=BRIEF,
    )(*[behind(bound, after) for bound in ranges[:1]], *ranges[1:3], *[array for array, _ in operands])


VECTOR = pltpu.VMEM
ANY = pl.ANY


def behind(value, others):
    return lax.optimization_barrier((value, *others))[0]


def halves_rows(shard_rows):
    return -(-shard_rows // 128) * 64


def unpack_kernel(plan, shard_rows, flat_ref, *refs):
    wide_ref = refs[-1]
    padded_ref = refs[-2]
    total = flat_ref.shape[0]
    chunk = 432

    def widen(i, _):
        rows = pl.ds(pl.multiple_of(i * chunk, 16), chunk)
        wide_ref[rows, :] = flat_ref[rows, :].astype(jnp.float32)
        return 0

    lax.fori_loop(0, total // chunk, widen, 0)
    wide_ref[pl.ds(total, wide_ref.shape[0] - total), :] = jnp.zeros((wide_ref.shape[0] - total, 128), jnp.float32)
    for (offset, rows, columns, begin), ref in zip(plan, refs[:-2]):
        pieces = columns // 128
        if rows == 1:
            for j in range(pieces):
                ref[:, 128 * j : 128 * (j + 1)] = wide_ref[pl.ds(offset + j, 1), :]
            continue

        def matrix(i, _):
            at = pl.multiple_of(i * 64, 64)
            for j in range(pieces):
                part = wide_ref[pl.ds(offset + j + at * pieces, 64, stride=pieces), :]
                ref[pl.ds(at, 64), begin + 128 * j : begin + 128 * (j + 1)] = part.astype(jnp.bfloat16)
            return 0

        lax.fori_loop(0, rows // 64, matrix, 0)
    shards = total // shard_rows
    half = halves_rows(shard_rows)
    for s in range(shards):
        for h in range(2):

            def pad(i, _):
                part = wide_ref[pl.ds(s * shard_rows + h * half + i * 64, 64), :]
                padded_ref[s * 2 + h, pl.ds(pl.multiple_of(i * 64, 64), 64), :] = part.astype(jnp.bfloat16)
                return 0

            lax.fori_loop(0, half // 64, pad, 0)


def unpacked(weights, shard_rows):
    flat = weights.reshape(-1, 128)
    half = halves_rows(shard_rows)
    plan, outs = [], []
    offset = 0
    for layout in layouts():
        rows, columns = layout if len(layout) == 2 else (1, layout[0])
        plan.append([offset, rows, columns, 0])
        outs.append(jax.ShapeDtypeStruct((rows, columns), jnp.bfloat16 if rows > 1 else jnp.float32))
        offset = offset + rows * columns // 128
    shards = flat.shape[0] // shard_rows
    outs.append(jax.ShapeDtypeStruct((2 * shards, half, 128), jnp.bfloat16))
    return pl.pallas_call(
        functools.partial(unpack_kernel, plan, shard_rows),
        name="unpack",
        in_specs=[pl.BlockSpec(memory_space=VECTOR)],
        out_specs=[pl.BlockSpec(memory_space=VECTOR)] * len(outs),
        out_shape=outs,
        scratch_shapes=[VECTOR((flat.shape[0] + 2 * half, 128), jnp.float32)],
        compiler_params=pltpu.CompilerParams(vmem_limit_bytes=60 * 2**20),
        cost_estimate=BRIEF,
    )(flat)


def pack_kernel(plan, spans, place_ref, *refs):
    count = len(plan)
    keep_ref, give_ref, flat_ref, out_ref, sems = refs[-5:]
    end = max(offset + rows * columns // 128 for offset, rows, columns in plan)
    begin = min(offset for offset, _, _ in plan)
    if begin:
        flat_ref[pl.ds(0, begin), :] = jnp.zeros((begin, 128), jnp.float32)
    for (offset, rows, columns), ref in zip(plan, refs[:count]):
        pieces = columns // 128
        if rows == 1:
            for j in range(pieces):
                flat_ref[pl.ds(offset + j, 1), :] = ref[:, 128 * j : 128 * (j + 1)]
            continue

        def matrix(i, _):
            at = pl.multiple_of(i * 64, 64)
            for j in range(pieces):
                flat_ref[pl.ds(offset + j + at * pieces, 64, stride=pieces), :] = ref[pl.ds(at, 64), 128 * j : 128 * (j + 1)]
            return 0

        lax.fori_loop(0, rows // 64, matrix, 0)
    for h in range(2):
        at = h ^ place_ref[0]
        filled = 0
        for source, rows, room in spans[h]:
            whole = rows // 64

            def move(i, _):
                to = pl.ds(pl.multiple_of(filled + i * 64, 16), 64)
                out_ref[at, to, :] = flat_ref[pl.ds(source + i * 64, 64), :].astype(jnp.bfloat16)
                return 0

            lax.fori_loop(0, whole, move, 0)
            rest = rows - 64 * whole
            tail = room - 64 * whole
            if tail:
                parts = []
                if rest:
                    parts.append(flat_ref[pl.ds(source + 64 * whole, rest), :])
                if tail > rest:
                    parts.append(jnp.zeros((tail - rest, 128), jnp.float32))
                last = parts[0] if len(parts) == 1 else jnp.concatenate(parts, axis=0)
                out_ref[at, pl.ds(filled + 64 * whole, tail), :] = last.astype(jnp.bfloat16)
            filled = filled + room
    copies = [
        pltpu.make_async_copy(out_ref.at[0], keep_ref, sems.at[0]),
        pltpu.make_async_copy(out_ref.at[1], give_ref, sems.at[1]),
    ]
    for copy in copies:
        copy.start()
    for copy in copies:
        copy.wait()


def packed_halves(grads, begin, spans, half):
    plan = []
    offset = begin
    for grad in grads:
        plan.append((offset, *grad.shape))
        offset = offset + grad.shape[0] * grad.shape[1] // 128
    return pl.pallas_call(
        functools.partial(pack_kernel, plan, spans),
        name="pack",
        in_specs=[pl.BlockSpec(memory_space=pltpu.SMEM)] + [pl.BlockSpec(memory_space=VECTOR)] * len(grads),
        out_specs=[pl.BlockSpec(memory_space=ANY)] * 2,
        out_shape=[jax.ShapeDtypeStruct((half, 128), jnp.bfloat16)] * 2,
        scratch_shapes=[
            VECTOR((offset, 128), jnp.float32),
            VECTOR((2, half, 128), jnp.bfloat16),
            pltpu.SemaphoreType.DMA((2,)),
        ],
        compiler_params=pltpu.CompilerParams(vmem_limit_bytes=60 * 2**20),
        cost_estimate=BRIEF,
    )(bit_of(1).reshape(1), *grads)


def combine_kernel(count, places_ref, *refs):
    parts, outs = refs[:count], refs[-places_ref.shape[0] :]
    rows = outs[0].shape[0]
    for k, out in enumerate(outs):
        at = pl.ds(pl.multiple_of(places_ref[k] * rows, 16), rows)
        terms = [part[at, :].astype(jnp.float32) for part in parts]
        while len(terms) > 1:
            terms = [terms[2 * j] + terms[2 * j + 1] for j in range(len(terms) // 2)]
        out[...] = terms[0].astype(jnp.bfloat16)


def places_of(group):
    if not group:
        return jnp.zeros((1,), jnp.int32)
    place = (lax.axis_index(LINE) // group[0]) % (1 << len(group))
    return place ^ jnp.arange(1 << len(group), dtype=jnp.int32)


def combine(parts, group, after):
    count = 1 << len(group)
    rows = parts[0].shape[0] // count
    outs = pl.pallas_call(
        functools.partial(combine_kernel, len(parts)),
        name="combine",
        in_specs=[pl.BlockSpec(memory_space=pltpu.SMEM)]
        + [pl.BlockSpec(memory_space=VECTOR)] * len(parts),
        out_specs=[pl.BlockSpec(memory_space=VECTOR)] * count,
        out_shape=[jax.ShapeDtypeStruct((rows, 128), jnp.bfloat16)] * count,
        cost_estimate=BRIEF,
    )(behind(places_of(group), after), *parts)
    return list(outs)


def stack_kernel(count, places_ref, *refs):
    out_ref = refs[-1]
    rows = refs[0].shape[0]
    for k in range(count):
        out_ref[pl.ds(pl.multiple_of(places_ref[k] * rows, 16), rows), :] = refs[k][...]


def stack(parts, group, after):
    rows = parts[0].shape[0] * len(parts)
    return pl.pallas_call(
        functools.partial(stack_kernel, len(parts)),
        name="stack",
        in_specs=[pl.BlockSpec(memory_space=pltpu.SMEM)]
        + [pl.BlockSpec(memory_space=VECTOR)] * len(parts),
        out_specs=pl.BlockSpec(memory_space=VECTOR),
        out_shape=jax.ShapeDtypeStruct((rows, 128), jnp.bfloat16),
        cost_estimate=BRIEF,
    )(behind(places_of(group), after), *parts)


def exchanged(parts, group):
    return [parts[0]] + [swapped(parts[k % len(parts)], group[0] * k) for k in range(1, 1 << len(group))]


def bit_groups():
    bits = [1 << k for k in range(1, lax.axis_size(LINE).bit_length() - 1)]
    return [bits[k : k + 2] for k in range(0, len(bits), 2)]


def square_sum_kernel(one_ref, two_ref, out_ref):
    sums = []
    for ref in (one_ref, two_ref):
        rows = ref.shape[0]
        chunk = 128 if rows % 128 == 0 else 64

        def add(i, total):
            part = ref[pl.ds(pl.multiple_of(i * chunk, 64), chunk), :].astype(jnp.float32)
            part = part * part
            while part.shape[0] > 8:
                part = part[: part.shape[0] // 2] + part[part.shape[0] // 2 :]
            return total + part

        sums.append(jnp.sum(lax.fori_loop(0, rows // chunk, add, jnp.zeros((8, 128), jnp.float32)), keepdims=True))
    out_ref[...] = jnp.broadcast_to(sums[0] + sums[1], (1, 128))


def square_sum(pair):
    return pl.pallas_call(
        square_sum_kernel,
        name="square_sum",
        in_specs=[pl.BlockSpec(memory_space=VECTOR)] * 2,
        out_specs=pl.BlockSpec(memory_space=VECTOR),
        out_shape=jax.ShapeDtypeStruct((1, 128), jnp.float32),
        cost_estimate=BRIEF,
    )(*pair)


def update_kernel(
    shards, late, shard_rows, meta_ref, scale_ref, early_own, early_other, late_own, late_other, extra_own, extra_other,
    weight_ref, one_ref, two_ref, *refs
):
    moments = refs[: 2 * shards]
    step_ref, grad_ref, new_one_ref, new_two_ref, sum_ref, wide_ref, stage_ref, sems = refs[2 * shards :]
    which, k = pl.program_id(0), pl.program_id(1)
    core, me, turn = meta_ref[0], meta_ref[1], meta_ref[2]
    shard = me ^ k
    half = core ^ which
    rows = sum_ref.shape[0]
    chunk = rows // 7 if rows % 112 == 0 else 64
    scale = scale_ref[0]

    def by_chunks(body):
        def move(i, _):
            body(pl.multiple_of(i * chunk, 16))
            return 0

        lax.fori_loop(0, rows // chunk, move, 0)

    def load(ref):
        def body(at):
            sum_ref[pl.ds(at, chunk), :] = ref[pl.ds(at, chunk), :].astype(jnp.float32)

        by_chunks(body)

    for array, side, is_late in ((early_own, 0, 0), (early_other, 1, 0), (late_own, 0, 1), (late_other, 1, 1)):
        pl.when((which == side) & ((shard < late) == (is_late == 1)))(functools.partial(load, array))
    for array, side in ((extra_own, 0), (extra_other, 1)):

        @pl.when((which == side) & (shard == late) & (half == 0))
        def _():
            sum_ref[pl.ds(0, 8), :] = sum_ref[pl.ds(0, 8), :] + array[pl.ds(0, 8), :].astype(jnp.float32)

    slope_one = (1.0 - BETA_ONE) * scale
    slope_two = (1.0 - BETA_TWO) * scale * scale

    base = shard * shard_rows + half * rows
    limit = jnp.where(half == 1, shard_rows - rows, rows)
    for j in range(shards):

        @pl.when(k == j)
        def _():
            def body(start):
                at = pl.ds(start, chunk)
                first, second = moments[2 * j][at, :], moments[2 * j + 1][at, :]
                one, two = jnp.where(turn == 1, second, first), jnp.where(turn == 1, first, second)
                grad = sum_ref[at, :]
                one = (BETA_ONE / FIX_ONE) * one.astype(jnp.float32) + (slope_one * (1.0 / FIX_ONE)) * grad
                two = (BETA_TWO / FIX_TWO) * two.astype(jnp.float32) + (slope_two * (1.0 / FIX_TWO)) * grad * grad
                root = two * lax.rsqrt(jnp.maximum(two, 1e-37))
                update = one / (root + 1e-08) + DECAY * weight_ref[0, at, :].astype(jnp.float32)
                to = pl.ds(base + start, chunk)
                inside = start + lax.broadcasted_iota(jnp.int32, update.shape, 0) < limit
                wide_ref[to, :] = jnp.where(inside, update, wide_ref[to, :])

            by_chunks(body)

    @pl.when(k == 0)
    def _():
        def body(start):
            at = pl.ds(start, chunk)
            grad = sum_ref[at, :]
            grad_ref[at, :] = grad
            new_one_ref[at, :] = BETA_ONE * one_ref[at, :] + slope_one * grad
            new_two_ref[at, :] = BETA_TWO * two_ref[at, :] + slope_two * grad * grad

        by_chunks(body)

    @pl.when((which == 1) & (k == shards - 1))
    def _():
        piece = stage_ref.shape[1]
        total = step_ref.shape[0]

        def sending(i, slot):
            return pltpu.make_async_copy(
                stage_ref.at[slot], step_ref.at[pl.ds(pl.multiple_of(i * piece, 16), piece), :], sems.at[slot]
            )

        count = total // piece
        for i in range(count):
            if i >= 2:
                sending(i - 2, i % 2).wait()
            stage_ref[i % 2] = wide_ref[pl.ds(i * piece, piece), :].astype(jnp.bfloat16)
            sending(i, i % 2).start()
        for i in range(count - 2, count):
            sending(i, i % 2).wait()


def updated(norm, early, late, late_shards, weights, first_moment, second_moment, moments):
    shards = len(moments) // 2
    rows = weights.shape[1]
    shard_rows = first_moment.shape[0] // 128
    line = lax.axis_index(LINE)
    inner = lax.axis_size("inner")
    meta = jnp.stack([line % 2, lax.axis_index("inner"), (line // inner) % 2]).astype(jnp.int32)
    last = shards - 1

    def early_map(side):
        def index(w, k, meta):
            k = jnp.where(w == side, k, last if side == 0 else 0)
            return (jnp.clip((meta[1] ^ k) - late_shards, 0, shards - late_shards - 1), 0)

        return index

    def late_map(side):
        def index(w, k, meta):
            k = jnp.where(w == side, k, last if side == 0 else 0)
            return (jnp.clip(meta[1] ^ k, 0, late_shards - 1), 0)

        return index

    by_half = pl.BlockSpec((rows, 128), lambda w, k, meta: (meta[0] ^ w, 0))

    def in_turn(j):
        return pl.BlockSpec((rows, 128), lambda w, k, meta: (meta[0] ^ jnp.where(k >= j - 1, w, 0), 0))

    by_shard = pl.BlockSpec((1, rows, 128), lambda w, k, meta: (2 * (meta[1] ^ k) + (meta[0] ^ w), 0, 0))
    extra = pl.BlockSpec((16, 128), lambda w, k, meta: (late_shards * rows // 16, 0))
    return pl.pallas_call(
        functools.partial(update_kernel, shards, late_shards, shard_rows),
        name="update",
        grid_spec=pltpu.PrefetchScalarGridSpec(
            num_scalar_prefetch=1,
            grid=(2, shards),
            in_specs=[pl.BlockSpec(memory_space=pltpu.SMEM)]
            + [pl.BlockSpec((rows, 128), early_map(side)) for side in range(2)]
            + [pl.BlockSpec((rows, 128), late_map(side)) for side in range(2)]
            + [extra, extra, by_shard, by_half, by_half]
            + [in_turn(j // 2) for j in range(2 * shards)],
            out_specs=[pl.BlockSpec(memory_space=ANY), by_half, by_half, by_half],
            scratch_shapes=[
                VECTOR((rows, 128), jnp.float32),
                VECTOR((shards * shard_rows + 2 * rows, 128), jnp.float32),
                VECTOR((2, shards * shard_rows // 9, 128), jnp.bfloat16),
                pltpu.SemaphoreType.DMA((2,)),
            ],
        ),
        out_shape=[jax.ShapeDtypeStruct((shards * shard_rows, 128), jnp.bfloat16)]
        + [jax.ShapeDtypeStruct((shard_rows, 128), jnp.float32)] * 3,
        compiler_params=pltpu.CompilerParams(vmem_limit_bytes=60 * 2**20),
        cost_estimate=BRIEF,
    )(
        meta,
        norm,
        *early,
        *late,
        *late,
        weights,
        first_moment.reshape(-1, 128),
        second_moment.reshape(-1, 128),
        *moments,
    )


def narrow_kernel(shard_rows, turn_ref, one_ref, two_ref, first_out, second_out):
    shape = first_out.shape
    begin = pl.program_id(0) * shape[0]
    inside = begin + lax.broadcasted_iota(jnp.int32, shape, 0) < shard_rows
    one = jnp.where(inside, one_ref[...], 0.0).astype(jnp.bfloat16)
    two = jnp.where(inside, two_ref[...], 0.0).astype(jnp.bfloat16)
    turned = turn_ref[0] == 1
    first_out[...] = jnp.where(turned, two, one)
    second_out[...] = jnp.where(turned, one, two)


def narrowed(one, two, half, turn):
    block = pl.BlockSpec((half // 2, 128), lambda i: (i, 0))
    return pl.pallas_call(
        functools.partial(narrow_kernel, one.shape[0]),
        name="narrow",
        grid=(4,),
        in_specs=[pl.BlockSpec(memory_space=pltpu.SMEM), block, block],
        out_specs=[block, block],
        out_shape=[jax.ShapeDtypeStruct((2 * half, 128), jnp.bfloat16)] * 2,
        cost_estimate=BRIEF,
    )(turn.reshape(1), one, two)


def bit_of(bit):
    return (lax.axis_index(LINE) // bit) % 2


def on_device(inputs, weights, cotangent, clip_lengths, first_moment, second_moment):
    tok_rows = inputs.shape[0]
    reach = (MOST + tok_rows - 2) // tok_rows
    shard_rows = first_moment.shape[0] // 128
    half = halves_rows(shard_rows)
    (
        first_gain,
        first_bias,
        query_weight,
        query_bias,
        key_weight,
        value_weight,
        value_bias,
        out_weight,
        out_bias,
        second_gain,
        second_bias,
        up_weight,
        up_bias,
        down_weight,
        down_bias,
        padded_weights,
    ) = unpacked(weights, shard_rows)
    base_slot = lax.axis_index(LINE) * tok_rows
    positions = base_slot + jnp.arange(tok_rows, dtype=jnp.int32)
    lower_slot, upper_slot = bounds(positions, clip_lengths)
    low = lower_slot - base_slot + reach * tok_rows
    high = upper_slot - base_slot + reach * tok_rows
    first_block = low.reshape(2, -1)[:, 0] // tok_rows
    last_block = (high.reshape(2, -1)[:, -1] + tok_rows - 1) // tok_rows
    ranges = (first_block, last_block, slot_table(), tok_rows)
    places = base_slot + block_distances()[:, None] * tok_rows + jnp.arange(tok_rows, dtype=jnp.int32)[None]
    marks = clip_marks(places.reshape(-1), clip_lengths)
    closed = penalty(clip_marks(positions, clip_lengths))

    inner = lax.axis_size("inner")
    turn = (lax.axis_index(LINE) // inner) % 2
    first_half, second_half = narrowed(first_moment.reshape(-1, 128), second_moment.reshape(-1, 128), half, turn)
    blocks = halo(inputs, (padded_weights,))
    fetched, *blocks = lax.optimization_barrier((first_half, *blocks))
    rows = projected(
        blocks, query_weight, key_weight, value_weight, first_gain, first_bias, query_bias, value_bias
    )
    fetched = swapped(fetched, 2)
    input_rows = inputs.astype(jnp.float32)
    first_hat, first_dev = standard(input_rows)
    normed = (first_hat * first_gain + first_bias).astype(jnp.bfloat16)

    attended, lse = attend(
        forward_kernel,
        ranges,
        [
            (rows, ("pair", 0)),
            (rows, ("pair", -5)),
            (rows, ("pair", -9)),
            (marks, ("all", 0)),
            (closed, ("all", 0)),
        ],
        [jnp.float32, jnp.float32],
        [pltpu.VMEM((2, 2 * reach + 1, tok_rows, tok_rows), jnp.float32)],
    )
    attended, lse, fetched = lax.optimization_barrier((attended, lse, fetched))
    passed = swapped(fetched, inner)
    held = {0: (first_half, second_half), 2: (fetched, passed)}
    bit = 4
    while bit < inner:
        for place in list(held):
            held[place + bit] = tuple(swapped(piece, bit) for piece in held[place])
        bit = 2 * bit
    moments = []
    for place in range(inner):
        if place % 2 == 0:
            moments += held[place]
        else:
            moments += [swapped(piece, 1) for piece in held[place - 1]]
    mixed = attended.astype(jnp.bfloat16)
    middle = input_rows + plain_dot(mixed, out_weight) + out_bias
    second_hat, second_dev = standard(middle)
    hidden_in = (second_hat * second_gain + second_bias).astype(jnp.bfloat16)
    up_rows = plain_dot(hidden_in, up_weight) + up_bias
    cdf_part = 0.5 * (1.0 + lax.erf(up_rows * INV_ROOT_TWO))
    activated = (up_rows * cdf_part).astype(jnp.bfloat16)
    layer_output = (middle + plain_dot(activated, down_weight) + down_bias).astype(jnp.bfloat16)
    grad_out = cotangent.astype(jnp.float32)
    down_bias_grad = jnp.sum(grad_out, axis=0)
    grad_act = back_dot(cotangent, down_weight)
    pdf_part = jnp.exp(-0.5 * up_rows * up_rows) * INV_ROOT_TWO_PI
    grad_up = (grad_act * (cdf_part + up_rows * pdf_part)).astype(jnp.bfloat16)
    up_bias_grad = jnp.sum(grad_up.astype(jnp.float32), axis=0)
    grad_hidden = back_dot(grad_up, up_weight)
    second_gain_grad = jnp.sum(grad_hidden * second_hat, axis=0)
    second_bias_grad = jnp.sum(grad_hidden, axis=0)
    grad_middle = grad_out + norm_back(grad_hidden, second_hat, second_dev, second_gain)
    grad_branch = grad_middle.astype(jnp.bfloat16)
    out_bias_grad = jnp.sum(grad_branch.astype(jnp.float32), axis=0)
    sent = mixed_grad(grad_branch, out_weight, attended, lse, clip_marks(positions, clip_lengths))
    line = lax.axis_size(LINE)
    shards = inner
    late_shards = shards // 4
    groups = bit_groups()

    def rounded(count, unit):
        return -(-count // unit) * unit

    def shard_spans(first, last, base):
        spans = ([], [])
        for shard in range(first, last):
            begin = (shard - first) * shard_rows + base
            spans[0].append((begin, half, half))
            spans[1].append((begin + half, shard_rows - half, half))
        return spans

    def query_step(pairs, after):
        return attend(
            query_kernel,
            ranges,
            [
                (rows, ("pair", 0)),
                (rows, ("pair", -5)),
                (rows, ("pair", -9)),
                (sent, ("pair", 0)),
                (sent, ("column", 4)),
                (marks, ("all", 0)),
                (closed, ("all", 0)),
            ],
            [jnp.bfloat16],
            [],
            pairs,
            after,
        )

    def key_step(pairs, after):
        return attend(
            key_kernel,
            ranges,
            [
                (rows, ("pair", 4)),
                (rows, ("pair", 8)),
                (rows, ("pair", -1)),
                (closed, ("all", 0)),
            ]
            + [(block, ("pair", 0)) for block in grad_blocks]
            + [(block, ("column", 4)) for block in grad_blocks],
            [jnp.bfloat16, jnp.bfloat16],
            [pltpu.VMEM((len(grad_blocks), tok_rows, 128), jnp.bfloat16)] * 2,
            pairs,
            after,
        )

    query_parts = query_step((0, 2), ())
    grad_blocks = halo(sent, query_parts)
    activated, hidden_in, mixed = (behind(array, query_parts) for array in (activated, hidden_in, mixed))
    down_grad = rows_dot(activated, cotangent)
    up_grad = rows_dot(hidden_in, grad_up)
    out_grad = rows_dot(mixed, grad_branch)

    early_rows = [
        out_grad,
        out_bias_grad,
        second_gain_grad,
        second_bias_grad,
        up_grad,
        up_bias_grad,
        down_grad,
        down_bias_grad,
    ]
    early_rows = [section.reshape(-1, section.shape[-1]) for section in early_rows]
    early_half = rounded((shards - late_shards) * half, 8 * line)
    spans = shard_spans(late_shards, shards, 0)
    for span in spans:
        span.append((0, 0, early_half - (shards - late_shards) * half))
    early_keep, early_give = packed_halves(early_rows, D // 128, spans, early_half)
    early_got = swapped(early_give, 1)

    query_parts += query_step((2, 2), (early_give,))
    parts = combine([early_keep, early_got], groups[0], query_parts)
    got = exchanged(parts, groups[0])
    query_low = jnp.concatenate(query_parts, axis=1)
    work = [(1, 1), (2, 1), (3, 1)]
    done = key_step((0, 1), parts[:1])
    key_parts, value_parts = [done[0]], [done[1]]
    held_back = done[:1]
    for at, group in enumerate(groups):
        parts = combine(got, groups[at + 1] if at + 1 < len(groups) else [], held_back)
        if at + 1 < len(groups):
            got = exchanged(parts, groups[at + 1])
        if work:
            done = key_step(work.pop(0), parts[:1])
            key_parts.append(done[0])
            value_parts.append(done[1])
            held_back = done[:1]
    piece = parts[0]
    for at, group in enumerate(groups[::-1]):
        got = exchanged([piece], group)
        if work and at > 0:
            done = key_step(work.pop(0), [piece])
            key_parts.append(done[0])
            value_parts.append(done[1])
            held_back = done[:1]
        piece = stack(got, group, held_back)
    early_other = swapped(piece, 1)
    for pairs in work:
        done = key_step(pairs, [piece])
        key_parts.append(done[0])
        value_parts.append(done[1])
    early = (piece, early_other)
    key_low = jnp.concatenate(key_parts, axis=1)
    value_low = jnp.concatenate(value_parts, axis=1)
    query_grad = rows_dot(normed, query_low)
    query_bias_grad = jnp.sum(query_low.astype(jnp.float32), axis=0)
    key_grad = rows_dot(normed, key_low)
    value_grad = rows_dot(normed, value_low)
    value_bias_grad = jnp.sum(value_low.astype(jnp.float32), axis=0)
    grad_normed = (
        back_dot(query_low, query_weight)
        + back_dot(key_low, key_weight)
        + back_dot(value_low, value_weight)
    )
    first_gain_grad = jnp.sum(grad_normed * first_hat, axis=0)
    first_bias_grad = jnp.sum(grad_normed, axis=0)
    input_grad = (grad_middle + norm_back(grad_normed, first_hat, first_dev, first_gain)).astype(
        jnp.bfloat16
    )

    late_rows = [
        first_gain_grad,
        first_bias_grad,
        query_grad,
        query_bias_grad,
        key_grad,
        value_grad,
        value_bias_grad,
    ]
    late_rows = [section.reshape(-1, section.shape[-1]) for section in late_rows]
    tail = max(1, 1 << (len(groups[0])))
    late_half = rounded(late_shards * half + 16, 16 * tail)
    spans = shard_spans(0, late_shards, 0)
    spare = late_half - late_shards * half
    spans[0].append((late_shards * shard_rows, D // 128, spare))
    spans[1].append((0, 0, spare))
    keep, give = packed_halves(late_rows, 0, spans, late_half)
    early_square = square_sum(early)
    parts = combine([keep, swapped(give, 1)], groups[0], ())
    (piece,) = combine(exchanged(parts, groups[0]), [], ())
    for group in groups[1:]:
        (piece,) = combine(exchanged([piece], group), [], (early_square,))
    piece = stack(exchanged([piece], groups[0]), groups[0], ())
    late = (piece, swapped(piece, 1))

    grad_norm = jnp.sqrt(early_square + square_sum(late))[0, 0]
    steps, grad_shard, moment_one, moment_two = updated(
        (1.0 / jnp.maximum(grad_norm, 1.0)).reshape(1),
        early,
        late,
        late_shards,
        padded_weights,
        first_moment,
        second_moment,
        moments,
    )
    weight_step = steps.reshape(-1)
    return (
        layer_output,
        input_grad,
        grad_shard.reshape(-1),
        grad_norm,
        moment_one.reshape(-1),
        moment_two.reshape(-1),
        weight_step,
    )


def solution(mesh):
    return jax.shard_map(
        on_device,
        mesh=mesh,
        in_specs=(
            P(("outer", "inner"), None),
            P(),
            P(("outer", "inner"), None),
            P(),
            P("inner"),
            P("inner"),
        ),
        out_specs=(
            P(("outer", "inner"), None),
            P(("outer", "inner"), None),
            P("inner"),
            P(),
            P("inner"),
            P("inner"),
            P(),
        ),
        check_vma=False,
    )
```

```python
import functools
import math

import jax
import jax.numpy as jnp
from jax import lax
from jax.experimental import pallas as pl
from jax.experimental.pallas import tpu as pltpu
from jax.sharding import PartitionSpec as P

D = 512
HEADS = 8
FF = 2048
MOST = 1500


BETA_ONE = 0.9
BETA_TWO = 0.999
FIX_ONE = 1.0 - (0.9**10) ** 10
FIX_TWO = 1.0 - (0.999**10) ** 10
DECAY = 0.1
INV_ROOT_TWO = 1.0 / math.sqrt(2.0)
INV_ROOT_TWO_PI = 1.0 / math.sqrt(2.0 * math.pi)


def layouts():
    return [
        (D,),
        (D,),
        (D, D),
        (D,),
        (D, D),
        (D, D),
        (D,),
        (D, D),
        (D,),
        (D,),
        (D,),
        (D, FF),
        (FF,),
        (FF, D),
        (D,),
    ]


def plain_dot(matrix_one, matrix_two):
    return jnp.dot(matrix_one, matrix_two, preferred_element_type=jnp.float32)


def rows_dot(matrix_one, matrix_two):
    return lax.dot_general(
        matrix_one, matrix_two, (((0,), (0,)), ((), ())), preferred_element_type=jnp.float32
    )


def back_dot(matrix_one, matrix_two):
    return lax.dot_general(
        matrix_one, matrix_two, (((1,), (1,)), ((), ())), preferred_element_type=jnp.float32
    )


def standard(values):
    center = jnp.mean(values, axis=-1, keepdims=True)
    centered = values - center
    inverse_dev = lax.rsqrt(jnp.mean(centered * centered, axis=-1, keepdims=True) + 1e-05)
    return (centered * inverse_dev, inverse_dev)


def norm_back(grad_normed, normed_hat, inverse_dev, gain):
    scaled = grad_normed * gain
    return inverse_dev * (
        scaled
        - jnp.mean(scaled, axis=-1, keepdims=True)
        - normed_hat * jnp.mean(scaled * normed_hat, axis=-1, keepdims=True)
    )


def bounds(positions, clip_lengths):
    starts = jnp.cumsum(clip_lengths, dtype=jnp.int32) - clip_lengths
    member = (
        jnp.sum((positions[:, None] >= starts[None, :]).astype(jnp.int32), axis=1, dtype=jnp.int32)
        - 1
    )
    onehot = (
        jnp.arange(clip_lengths.shape[0], dtype=jnp.int32)[None, :] == member[:, None]
    ).astype(jnp.int32)
    lower_slot = jnp.sum(onehot * starts[None, :], axis=1, dtype=jnp.int32)
    upper_slot = lower_slot + jnp.sum(onehot * clip_lengths[None, :], axis=1, dtype=jnp.int32)
    return (lower_slot, upper_slot)


LINE = ("outer", "inner")
NEG = -1e30
BRIEF = pl.CostEstimate(flops=1000, bytes_accessed=1000, transcendentals=0)


def shifted(block, distance):
    n = lax.axis_size(LINE)
    return lax.ppermute(block, LINE, [(i + distance, i) for i in range(n) if 0 <= i + distance < n])


def swapped(block, bit):
    n = lax.axis_size(LINE)
    return lax.ppermute(block, LINE, [(i ^ bit, i) for i in range(n)])


def halo(block, before=()):
    n = lax.axis_size(LINE)
    left = shifted(block, -2)
    right = shifted(block, 2)
    partner = swapped(block, 1)
    route = [(i + (3 if i % 2 else -3), i) for i in range(n)]
    far = lax.ppermute(block, LINE, [(s, t) for s, t in route if 0 <= s < n])
    passed_left, passed_right, *_ = lax.optimization_barrier((left, right, *before))
    turned = [swapped(passed_left, 1), swapped(passed_right, 1)]
    return [block, partner, left, right, *turned, far]


def block_distances():
    odd = lax.axis_index(LINE) % 2
    even_far = jnp.array([0, 1, -2, 2, -1, 3, -3], jnp.int32)
    odd_far = jnp.array([0, -1, -2, 2, -3, 1, 3], jnp.int32)
    return jnp.where(odd == 1, odd_far, even_far)


def slot_table():
    odd = lax.axis_index(LINE) % 2
    even_slots = jnp.array([6, 2, 4, 0, 1, 3, 5], jnp.int32)
    odd_slots = jnp.array([4, 2, 1, 0, 5, 3, 6], jnp.int32)
    return jnp.where(odd == 1, odd_slots, even_slots)


def dot_nt(a, b):
    return lax.dot_general(a, b, (((1,), (1,)), ((), ())), preferred_element_type=jnp.float32)


def head_halves(pair):
    first = lax.broadcasted_iota(jnp.int32, pair.shape, 1) < pair.shape[1] // 2
    zero = jnp.zeros_like(pair)
    return jnp.where(first, pair, zero), jnp.where(first, zero, pair)


def over_lanes(tile, op):
    parts = [tile[:, 128 * j : 128 * (j + 1)] for j in range(tile.shape[1] // 128)]
    while len(parts) > 1:
        rest = parts[len(parts) // 2 * 2 :]
        parts = [op(parts[2 * j], parts[2 * j + 1]) for j in range(len(parts) // 2)] + rest
    return parts[0]


LSE_PARTS, DELTA_PARTS = 3, 2
DELTA_AT = LSE_PARTS * HEADS
CLIPS_AT = DELTA_AT + DELTA_PARTS * HEADS


def lane_of(shape):
    return lax.broadcasted_iota(jnp.int32, shape, 1)


def among(lane, begin, count):
    return (lane >= begin) & (lane < begin + count)


def beside(pair, marks):
    return jnp.concatenate([pair, marks.astype(pair.dtype)], axis=1)


def clip_marks(positions, clip_lengths):
    ends = jnp.cumsum(clip_lengths, dtype=jnp.int32)
    starts = ends - clip_lengths
    spare = 128 - CLIPS_AT - clip_lengths.shape[0]
    assert spare >= 0
    big = jnp.iinfo(jnp.int32).max
    lower = jnp.concatenate([jnp.full((CLIPS_AT,), -big, jnp.int32), starts, jnp.full((spare,), big, jnp.int32)])
    upper = jnp.concatenate([jnp.full((CLIPS_AT,), big, jnp.int32), ends, jnp.full((spare,), big, jnp.int32)])
    inside = (positions[:, None] >= lower[None]) & (positions[:, None] < upper[None])
    return inside.astype(jnp.bfloat16)


def penalty(marks):
    closed = (lane_of(marks.shape) >= CLIPS_AT) & (marks == 0)
    return jnp.where(closed, NEG, 0.0).astype(jnp.bfloat16)


def over_blocks(first_ref, last_ref, rows, work, start):
    half = rows // 2
    carried = (start, start)
    spans = (
        (first_ref[0], first_ref[1], 0, half),
        (first_ref[1], last_ref[0], 0, rows),
        (last_ref[0], last_ref[1], half, half),
    )
    for lower, upper, begin, count in spans:

        def step(block, carried):
            found = work(block, begin, count)
            upper_half, lower_half = carried
            if begin == 0:
                upper_half = tuple(join(old, new[:half]) for (join, new), old in zip(found, upper_half))
            if begin + count == rows:
                lower_half = tuple(join(old, new[count - half :]) for (join, new), old in zip(found, lower_half))
            return upper_half, lower_half

        carried = lax.fori_loop(lower, upper, step, carried)
    return [jnp.concatenate(halves, axis=0) for halves in zip(*carried)]


def forward_kernel(begin, first_ref, last_ref, slot_ref, q_ref, k_ref, v_ref, mark_ref, closed_ref, o_ref, lse_ref, s_ref):
    width = q_ref.shape[0]
    queries = [beside(half, closed_ref[...]) for half in head_halves(q_ref[...] * jnp.bfloat16(0.125))]

    def scores(block, begin, count):
        at = pl.ds(pl.multiple_of(slot_ref[block] * width, width), width)
        keys = beside(k_ref[at, :], mark_ref[at, :])
        found = []
        for h in range(2):
            score = dot_nt(queries[h][begin : begin + count], keys)
            s_ref[h, block, pl.ds(begin, count), :] = score
            found.append((jnp.maximum, over_lanes(score, jnp.maximum)))
        return found

    start = jnp.full((width // 2, 128), NEG, jnp.float32)
    peaks = over_blocks(first_ref, last_ref, width, scores, (start, start))
    peaks = [jnp.max(peak, axis=1, keepdims=True) for peak in peaks]

    def mix(block, begin, count):
        at = pl.ds(pl.multiple_of(slot_ref[block] * width, width), width)
        values = beside(v_ref[at, :], mark_ref[at, :])
        found = []
        for h in range(2):
            score = s_ref[h, block, pl.ds(begin, count), :]
            soft = jnp.exp(score - peaks[h][begin : begin + count]).astype(jnp.bfloat16)
            found.append((jnp.add, jnp.dot(soft, values, preferred_element_type=jnp.float32)))
        return found

    start = jnp.zeros((width // 2, 256), jnp.float32)
    sums = over_blocks(first_ref, last_ref, width, mix, (start, start))
    totals = [part[:, 128:129] for part in sums]
    even = lane_of((width, 128)) < 64
    o_ref[...] = jnp.where(even, sums[0][:, :128] / totals[0], sums[1][:, :128] / totals[1])
    lse_ref[...] = jnp.where(even, peaks[0] + jnp.log(totals[0]), peaks[1] + jnp.log(totals[1]))


def query_kernel(
    begin, first_ref, last_ref, slot_ref, q_ref, k_ref, v_ref, g_ref, own_ref, mark_ref, closed_ref, dq_ref
):
    width = q_ref.shape[0]
    pair = pl.program_id(0) + begin
    own, closed = own_ref[...], closed_ref[...]
    lane = lane_of(own.shape)
    zero = jnp.zeros_like(own)
    queries, grads = [], []
    halves = zip(head_halves(q_ref[...] * jnp.bfloat16(0.125)), head_halves(g_ref[...]))
    for h, (query, grad) in enumerate(halves):
        head = 2 * pair + h
        queries.append(beside(query, jnp.where(among(lane, LSE_PARTS * head, LSE_PARTS), own, closed)))
        grads.append(beside(grad, jnp.where(among(lane, DELTA_AT + DELTA_PARTS * head, DELTA_PARTS), own, zero)))

    def work(block, begin, count):
        at = pl.ds(pl.multiple_of(slot_ref[block] * width, width), width)
        keys = k_ref[at, :]
        values = beside(v_ref[at, :], mark_ref[at, :])
        marked = beside(keys, mark_ref[at, :])
        found = []
        for h in range(2):
            soft = jnp.exp(dot_nt(queries[h][begin : begin + count], marked))
            grad = (soft * dot_nt(grads[h][begin : begin + count], values)).astype(jnp.bfloat16)
            found.append((jnp.add, jnp.dot(grad, keys, preferred_element_type=jnp.float32)))
        return found

    start = jnp.zeros((width // 2, 128), jnp.float32)
    sums = over_blocks(first_ref, last_ref, width, work, (start, start))
    dq_ref[...] = (jnp.where(lane < 64, sums[0], sums[1]) * 0.125).astype(jnp.bfloat16)


def key_kernel(begin, first_ref, last_ref, slot_ref, k_ref, v_ref, q_ref, closed_ref, *refs):
    dk_ref, dv_ref, grad_ref, mark_ref = refs[-4:]
    width = k_ref.shape[0]
    pair = pl.program_id(0) + begin
    blocks = grad_ref.shape[0]
    for j in range(blocks):
        grad_ref[j] = refs[j][...]

    @pl.when(pl.program_id(0) == 0)
    def _():
        for j in range(blocks):
            mark_ref[j] = refs[blocks + j][...]

    closed = closed_ref[...]
    lane = lane_of(closed.shape)
    one, zero = jnp.ones_like(closed), jnp.zeros_like(closed)
    keys, values = [], []
    halves = zip(head_halves(k_ref[...] * jnp.bfloat16(0.125)), head_halves(v_ref[...]))
    for h, (key, value) in enumerate(halves):
        head = 2 * pair + h
        keys.append(beside(key, jnp.where(among(lane, LSE_PARTS * head, LSE_PARTS), one, closed)))
        values.append(beside(value, jnp.where(among(lane, DELTA_AT + DELTA_PARTS * head, DELTA_PARTS), one, zero)))

    def work(block, begin, count):
        slot = slot_ref[block]
        queries = q_ref[pl.ds(pl.multiple_of(slot * width, width), width), :]
        grads, marks = grad_ref[slot], mark_ref[slot]
        marked, graded = beside(queries, marks), beside(grads, marks)
        found = []
        for h in range(2):
            soft = jnp.exp(dot_nt(keys[h][begin : begin + count], marked))
            grad = (soft * dot_nt(values[h][begin : begin + count], graded)).astype(jnp.bfloat16)
            found.append((jnp.add, jnp.dot(grad, queries, preferred_element_type=jnp.float32)))
            found.append((jnp.add, jnp.dot(soft.astype(jnp.bfloat16), grads, preferred_element_type=jnp.float32)))
        return found

    start = jnp.zeros((width // 2, 128), jnp.float32)
    sums = over_blocks(first_ref, last_ref, width, work, (start,) * 4)
    dk_ref[...] = (jnp.where(lane < 64, sums[0], sums[2]) * 0.125).astype(jnp.bfloat16)
    dv_ref[...] = jnp.where(lane < 64, sums[1], sums[3]).astype(jnp.bfloat16)


def mixed_grad_kernel(branch_ref, weight_ref, mixed_ref, lse_ref, own_ref, sent_ref, mark_ref):
    step = pl.program_id(0)

    @pl.when(step == 0)
    def _():
        mark_ref[...] = own_ref[...].astype(jnp.float32)

    @pl.when(step < D // 128)
    def _():
        grad = dot_nt(branch_ref[...], weight_ref[...]).astype(jnp.bfloat16)
        sent_ref[...] = grad
        product = grad.astype(jnp.float32) * mixed_ref[...]
        lane = lane_of(product.shape)
        marks = mark_ref[...]
        for h, part in enumerate(head_halves(product)):
            head = 2 * step + h
            delta = -jnp.sum(part, axis=1, keepdims=True)
            lse = -lse_ref[:, 64 * h : 64 * h + 1]
            for value, begin, count in (
                (lse, LSE_PARTS * head, LSE_PARTS),
                (delta, DELTA_AT + DELTA_PARTS * head, DELTA_PARTS),
            ):
                for k in range(count):
                    rounded = value.astype(jnp.bfloat16).astype(jnp.float32)
                    marks = jnp.where(lane == begin + k, rounded, marks)
                    value = value - rounded
        mark_ref[...] = marks

    @pl.when(step == D // 128)
    def _():
        sent_ref[...] = mark_ref[...].astype(jnp.bfloat16)


def mixed_grad(branch, out_weight, mixed, lse, own_marks):
    width = branch.shape[0]
    last = D // 128 - 1
    column = pl.BlockSpec((width, 128), lambda h: (0, jnp.minimum(h, last)))
    return pl.pallas_call(
        mixed_grad_kernel,
        name="mixed_grad",
        grid=(D // 128 + 1,),
        in_specs=[
            pl.BlockSpec((width, D), lambda h: (0, 0)),
            pl.BlockSpec((128, D), lambda h: (jnp.minimum(h, last), 0)),
            column,
            column,
            pl.BlockSpec((width, 128), lambda h: (0, 0)),
        ],
        out_specs=pl.BlockSpec((width, 128), lambda h: (0, h)),
        out_shape=jax.ShapeDtypeStruct((width, D + 128), jnp.bfloat16),
        scratch_shapes=[pltpu.VMEM((width, 128), jnp.float32)],
        cost_estimate=BRIEF,
    )(branch, out_weight, mixed, lse, own_marks)


def project_kernel(count, *refs):
    query_ref, key_ref, value_ref, gain_ref, bias_ref, query_bias_ref, value_bias_ref, out_ref, row_ref = refs[count:]
    step = pl.program_id(0)
    for j in range(count):

        @pl.when(step == j)
        def _():
            row_ref[...] = refs[j][...]

    rows = 256
    for i in range(row_ref.shape[0] // rows):
        at = pl.ds(i * rows, rows)
        hat, _ = standard(row_ref[at, :].astype(jnp.float32))
        normed = (hat * gain_ref[...] + bias_ref[...]).astype(jnp.bfloat16)
        out_ref[at, 0:D] = (plain_dot(normed, query_ref[...]) + query_bias_ref[...]).astype(jnp.bfloat16)
        out_ref[at, D : 2 * D] = plain_dot(normed, key_ref[...]).astype(jnp.bfloat16)
        out_ref[at, 2 * D :] = (plain_dot(normed, value_ref[...]) + value_bias_ref[...]).astype(jnp.bfloat16)


def projected(blocks, *weights):
    width = blocks[0].shape[0]
    whole = [pl.BlockSpec(array.shape, lambda i: (0, 0)) for array in (*blocks, *weights)]
    return pl.pallas_call(
        functools.partial(project_kernel, len(blocks)),
        name="project",
        grid=(len(blocks),),
        in_specs=whole,
        out_specs=pl.BlockSpec((width, 3 * D), lambda i: (i, 0)),
        out_shape=jax.ShapeDtypeStruct((len(blocks) * width, 3 * D), jnp.bfloat16),
        scratch_shapes=[pltpu.VMEM((width, D), jnp.bfloat16)],
        compiler_params=pltpu.CompilerParams(vmem_limit_bytes=63 * 2**20),
        cost_estimate=BRIEF,
    )(*blocks, *weights)


def attend(kernel, ranges, operands, results, scratch, pairs=(0, D // 128), after=()):
    begin, count = pairs
    tok_rows = ranges[3]
    specs = []
    for array, (kind, at) in operands:
        if kind == "pair":
            rows = array.shape[0] if at < 0 else tok_rows
            at = (abs(at) - 1 if at < 0 else at) + begin
            specs.append(pl.BlockSpec((rows, 128), lambda h, *_, at=at: (0, at + h)))
        elif kind == "column":
            specs.append(pl.BlockSpec((tok_rows, 128), lambda h, *_, at=at: (0, at)))
        else:
            specs.append(pl.BlockSpec(array.shape, lambda h, *_, n=array.ndim: (0,) * n))
    return pl.pallas_call(
        functools.partial(kernel, begin),
        grid_spec=pltpu.PrefetchScalarGridSpec(
            num_scalar_prefetch=3,
            grid=(count,),
            in_specs=specs,
            out_specs=[pl.BlockSpec((tok_rows, 128), lambda h, *_: (0, h))] * len(results),
            scratch_shapes=scratch,
        ),
        out_shape=[jax.ShapeDtypeStruct((tok_rows, 128 * count), kept) for kept in results],
        compiler_params=pltpu.CompilerParams(vmem_limit_bytes=48 * 2**20),
        cost_estimate=BRIEF,
    )(*[behind(bound, after) for bound in ranges[:1]], *ranges[1:3], *[array for array, _ in operands])


VECTOR = pltpu.VMEM
ANY = pl.ANY


def behind(value, others):
    return lax.optimization_barrier((value, *others))[0]


def halves_rows(shard_rows):
    return -(-shard_rows // 128) * 64


def unpack_kernel(plan, shard_rows, flat_ref, *refs):
    wide_ref = refs[-1]
    padded_ref = refs[-2]
    total = flat_ref.shape[0]
    chunk = 432

    def widen(i, _):
        rows = pl.ds(pl.multiple_of(i * chunk, 16), chunk)
        wide_ref[rows, :] = flat_ref[rows, :].astype(jnp.float32)
        return 0

    lax.fori_loop(0, total // chunk, widen, 0)
    wide_ref[pl.ds(total, wide_ref.shape[0] - total), :] = jnp.zeros((wide_ref.shape[0] - total, 128), jnp.float32)
    for (offset, rows, columns, begin), ref in zip(plan, refs[:-2]):
        pieces = columns // 128
        if rows == 1:
            for j in range(pieces):
                ref[:, 128 * j : 128 * (j + 1)] = wide_ref[pl.ds(offset + j, 1), :]
            continue

        taken = 1024 // pieces

        def matrix(i, _):
            at = pl.multiple_of(i * taken, 64)
            for j in range(pieces):
                part = wide_ref[pl.ds(offset + j + at * pieces, taken, stride=pieces), :]
                ref[pl.ds(at, taken), begin + 128 * j : begin + 128 * (j + 1)] = part.astype(jnp.bfloat16)
            return 0

        lax.fori_loop(0, rows // taken, matrix, 0)
    shards = total // shard_rows
    half = halves_rows(shard_rows)
    for s in range(shards):
        for h in range(2):

            run = 448 if half % 448 == 0 else 64

            def pad(i, _):
                part = wide_ref[pl.ds(s * shard_rows + h * half + i * run, run), :]
                padded_ref[s * 2 + h, pl.ds(pl.multiple_of(i * run, 64), run), :] = part.astype(jnp.bfloat16)
                return 0

            lax.fori_loop(0, half // run, pad, 0)


def unpacked(weights, shard_rows):
    flat = weights.reshape(-1, 128)
    half = halves_rows(shard_rows)
    plan, outs = [], []
    offset = 0
    for layout in layouts():
        rows, columns = layout if len(layout) == 2 else (1, layout[0])
        plan.append([offset, rows, columns, 0])
        outs.append(jax.ShapeDtypeStruct((rows, columns), jnp.bfloat16 if rows > 1 else jnp.float32))
        offset = offset + rows * columns // 128
    shards = flat.shape[0] // shard_rows
    outs.append(jax.ShapeDtypeStruct((2 * shards, half, 128), jnp.bfloat16))
    return pl.pallas_call(
        functools.partial(unpack_kernel, plan, shard_rows),
        name="unpack",
        in_specs=[pl.BlockSpec(memory_space=VECTOR)],
        out_specs=[pl.BlockSpec(memory_space=VECTOR)] * len(outs),
        out_shape=outs,
        scratch_shapes=[VECTOR((flat.shape[0] + 2 * half, 128), jnp.float32)],
        compiler_params=pltpu.CompilerParams(vmem_limit_bytes=60 * 2**20),
        cost_estimate=BRIEF,
    )(flat)


def pack_kernel(plan, spans, place_ref, *refs):
    count = len(plan)
    keep_ref, give_ref, flat_ref, out_ref, sems = refs[-5:]
    end = max(offset + rows * columns // 128 for offset, rows, columns in plan)
    begin = min(offset for offset, _, _ in plan)
    if begin:
        flat_ref[pl.ds(0, begin), :] = jnp.zeros((begin, 128), jnp.float32)
    for (offset, rows, columns), ref in zip(plan, refs[:count]):
        pieces = columns // 128
        if rows == 1:
            for j in range(pieces):
                flat_ref[pl.ds(offset + j, 1), :] = ref[:, 128 * j : 128 * (j + 1)]
            continue

        taken = 1024 // pieces

        def matrix(i, _):
            at = pl.multiple_of(i * taken, 64)
            for j in range(pieces):
                part = ref[pl.ds(at, taken), 128 * j : 128 * (j + 1)]
                flat_ref[pl.ds(offset + j + at * pieces, taken, stride=pieces), :] = part
            return 0

        lax.fori_loop(0, rows // taken, matrix, 0)
    for h in range(2):
        at = h ^ place_ref[0]
        filled = 0
        for source, rows, room in spans[h]:
            run = 448 if rows >= 448 else 64
            whole = rows // run

            def move(i, _):
                to = pl.ds(pl.multiple_of(filled + i * run, 16), run)
                out_ref[at, to, :] = flat_ref[pl.ds(source + i * run, run), :].astype(jnp.bfloat16)
                return 0

            lax.fori_loop(0, whole, move, 0)
            rest = rows - run * whole
            tail = room - run * whole
            if tail:
                parts = []
                if rest:
                    parts.append(flat_ref[pl.ds(source + run * whole, rest), :])
                if tail > rest:
                    parts.append(jnp.zeros((tail - rest, 128), jnp.float32))
                last = parts[0] if len(parts) == 1 else jnp.concatenate(parts, axis=0)
                out_ref[at, pl.ds(filled + run * whole, tail), :] = last.astype(jnp.bfloat16)
            filled = filled + room
    copies = [
        pltpu.make_async_copy(out_ref.at[0], keep_ref, sems.at[0]),
        pltpu.make_async_copy(out_ref.at[1], give_ref, sems.at[1]),
    ]
    for copy in copies:
        copy.start()
    for copy in copies:
        copy.wait()


def packed_halves(grads, begin, spans, half):
    plan = []
    offset = begin
    for grad in grads:
        plan.append((offset, *grad.shape))
        offset = offset + grad.shape[0] * grad.shape[1] // 128
    return pl.pallas_call(
        functools.partial(pack_kernel, plan, spans),
        name="pack",
        in_specs=[pl.BlockSpec(memory_space=pltpu.SMEM)] + [pl.BlockSpec(memory_space=VECTOR)] * len(grads),
        out_specs=[pl.BlockSpec(memory_space=ANY)] * 2,
        out_shape=[jax.ShapeDtypeStruct((half, 128), jnp.bfloat16)] * 2,
        scratch_shapes=[
            VECTOR((offset, 128), jnp.float32),
            VECTOR((2, half, 128), jnp.bfloat16),
            pltpu.SemaphoreType.DMA((2,)),
        ],
        compiler_params=pltpu.CompilerParams(vmem_limit_bytes=60 * 2**20),
        cost_estimate=BRIEF,
    )(bit_of(1).reshape(1), *grads)


def combine_kernel(count, places_ref, *refs):
    parts, outs = refs[:count], refs[-places_ref.shape[0] :]
    rows = outs[0].shape[0]
    for k, out in enumerate(outs):
        at = pl.ds(pl.multiple_of(places_ref[k] * rows, 16), rows)
        terms = [part[at, :].astype(jnp.float32) for part in parts]
        while len(terms) > 1:
            terms = [terms[2 * j] + terms[2 * j + 1] for j in range(len(terms) // 2)]
        out[...] = terms[0].astype(jnp.bfloat16)


def places_of(group):
    if not group:
        return jnp.zeros((1,), jnp.int32)
    place = (lax.axis_index(LINE) // group[0]) % (1 << len(group))
    return place ^ jnp.arange(1 << len(group), dtype=jnp.int32)


def combine(parts, group, after):
    count = 1 << len(group)
    rows = parts[0].shape[0] // count
    outs = pl.pallas_call(
        functools.partial(combine_kernel, len(parts)),
        name="combine",
        in_specs=[pl.BlockSpec(memory_space=pltpu.SMEM)]
        + [pl.BlockSpec(memory_space=VECTOR)] * len(parts),
        out_specs=[pl.BlockSpec(memory_space=VECTOR)] * count,
        out_shape=[jax.ShapeDtypeStruct((rows, 128), jnp.bfloat16)] * count,
        cost_estimate=BRIEF,
    )(behind(places_of(group), after), *parts)
    return list(outs)


def stack_kernel(count, places_ref, *refs):
    out_ref = refs[-1]
    rows = refs[0].shape[0]
    for k in range(count):
        out_ref[pl.ds(pl.multiple_of(places_ref[k] * rows, 16), rows), :] = refs[k][...]


def stack(parts, group, after):
    rows = parts[0].shape[0] * len(parts)
    return pl.pallas_call(
        functools.partial(stack_kernel, len(parts)),
        name="stack",
        in_specs=[pl.BlockSpec(memory_space=pltpu.SMEM)]
        + [pl.BlockSpec(memory_space=VECTOR)] * len(parts),
        out_specs=pl.BlockSpec(memory_space=VECTOR),
        out_shape=jax.ShapeDtypeStruct((rows, 128), jnp.bfloat16),
        cost_estimate=BRIEF,
    )(behind(places_of(group), after), *parts)


def exchanged(parts, group):
    return [parts[0]] + [swapped(parts[k % len(parts)], group[0] * k) for k in range(1, 1 << len(group))]


def bit_groups():
    bits = [1 << k for k in range(1, lax.axis_size(LINE).bit_length() - 1)]
    return [bits[k : k + 2] for k in range(0, len(bits), 2)]


def square_sum_kernel(one_ref, two_ref, out_ref):
    sums = []
    for ref in (one_ref, two_ref):
        rows = ref.shape[0]
        chunk = rows // 8 if rows % 128 == 0 else 64

        def add(i, total):
            part = ref[pl.ds(pl.multiple_of(i * chunk, 16), chunk), :].astype(jnp.float32)
            return total + jnp.sum((part * part).reshape(-1, 32, 128), axis=0)

        zero = jnp.zeros((32, 128), jnp.float32)
        if chunk % 32:
            chunk = 32
        sums.append(jnp.sum(lax.fori_loop(0, rows // chunk, add, zero), keepdims=True))
    out_ref[...] = jnp.broadcast_to(sums[0] + sums[1], (1, 128))


def square_sum(pair):
    return pl.pallas_call(
        square_sum_kernel,
        name="square_sum",
        in_specs=[pl.BlockSpec(memory_space=VECTOR)] * 2,
        out_specs=pl.BlockSpec(memory_space=VECTOR),
        out_shape=jax.ShapeDtypeStruct((1, 128), jnp.float32),
        cost_estimate=BRIEF,
    )(*pair)


def update_kernel(
    shards, late, shard_rows, meta_ref, scale_ref, early_own, early_other, late_own, late_other, extra_own, extra_other,
    weight_ref, one_ref, two_ref, *refs
):
    moments = refs[: 2 * shards]
    step_ref, grad_ref, new_one_ref, new_two_ref, sum_ref, wide_ref, stage_ref, sems = refs[2 * shards :]
    which, k = pl.program_id(0), pl.program_id(1)
    core, me, turn = meta_ref[0], meta_ref[1], meta_ref[2]
    shard = me ^ k
    half = core ^ which
    rows = sum_ref.shape[0]
    chunk = rows // 7 if rows % 112 == 0 else 64
    scale = scale_ref[0]

    def by_chunks(body, first=0, last=rows // chunk):
        def move(i, _):
            body(pl.multiple_of(i * chunk, 16))
            return 0

        lax.fori_loop(first, last, move, 0)

    def load(ref):
        def body(at):
            sum_ref[pl.ds(at, chunk), :] = ref[pl.ds(at, chunk), :].astype(jnp.float32)

        by_chunks(body)

    for array, side, is_late in ((early_own, 0, 0), (early_other, 1, 0), (late_own, 0, 1), (late_other, 1, 1)):
        pl.when((which == side) & ((shard < late) == (is_late == 1)))(functools.partial(load, array))
    for array, side in ((extra_own, 0), (extra_other, 1)):

        @pl.when((which == side) & (shard == late) & (half == 0))
        def _():
            sum_ref[pl.ds(0, 8), :] = sum_ref[pl.ds(0, 8), :] + array[pl.ds(0, 8), :].astype(jnp.float32)

    slope_one = (1.0 - BETA_ONE) * scale
    slope_two = (1.0 - BETA_TWO) * scale * scale

    base = shard * shard_rows + half * rows
    limit = jnp.where(half == 1, shard_rows - rows, rows)
    for j in range(shards):

        @pl.when(k == j)
        def _():
            def body(start, masked=False):
                at = pl.ds(start, chunk)
                first, second = moments[2 * j][at, :], moments[2 * j + 1][at, :]
                one, two = jnp.where(turn == 1, second, first), jnp.where(turn == 1, first, second)
                grad = sum_ref[at, :]
                one = one.astype(jnp.float32) + (slope_one * (1.0 / FIX_ONE)) * grad
                two = two.astype(jnp.float32) + (slope_two * (1.0 / FIX_TWO)) * grad * grad
                root = two * lax.rsqrt(jnp.maximum(two, 1e-37))
                update = one / (root + 1e-08) + DECAY * weight_ref[0, at, :].astype(jnp.float32)
                to = pl.ds(base + start, chunk)
                if masked:
                    inside = start + lax.broadcasted_iota(jnp.int32, update.shape, 0) < limit
                    update = jnp.where(inside, update, wide_ref[to, :])
                wide_ref[to, :] = update

            whole = (shard_rows - rows) // chunk
            by_chunks(body, 0, whole)
            by_chunks(functools.partial(body, masked=True), whole, rows // chunk)

    @pl.when(k == 0)
    def _():
        def body(start):
            at = pl.ds(start, chunk)
            grad = sum_ref[at, :]
            grad_ref[at, :] = grad
            new_one_ref[at, :] = BETA_ONE * one_ref[at, :] + slope_one * grad
            new_two_ref[at, :] = BETA_TWO * two_ref[at, :] + slope_two * grad * grad

        by_chunks(body)

    @pl.when((which == 1) & (k == shards - 1))
    def _():
        piece = stage_ref.shape[1]
        total = step_ref.shape[0]

        def sending(i, slot):
            return pltpu.make_async_copy(
                stage_ref.at[slot], step_ref.at[pl.ds(pl.multiple_of(i * piece, 16), piece), :], sems.at[slot]
            )

        count = total // piece
        for i in range(count):
            if i >= 2:
                sending(i - 2, i % 2).wait()
            stage_ref[i % 2] = wide_ref[pl.ds(i * piece, piece), :].astype(jnp.bfloat16)
            sending(i, i % 2).start()
        for i in range(count - 2, count):
            sending(i, i % 2).wait()


def updated(norm, early, late, late_shards, weights, first_moment, second_moment, moments):
    shards = len(moments) // 2
    rows = weights.shape[1]
    shard_rows = first_moment.shape[0] // 128
    line = lax.axis_index(LINE)
    inner = lax.axis_size("inner")
    meta = jnp.stack([line % 2, lax.axis_index("inner"), (line // inner) % 2]).astype(jnp.int32)
    last = shards - 1

    def early_map(side):
        def index(w, k, meta):
            k = jnp.where(w == side, k, last if side == 0 else 0)
            return (jnp.clip((meta[1] ^ k) - late_shards, 0, shards - late_shards - 1), 0)

        return index

    def late_map(side):
        def index(w, k, meta):
            k = jnp.where(w == side, k, last if side == 0 else 0)
            return (jnp.clip(meta[1] ^ k, 0, late_shards - 1), 0)

        return index

    by_half = pl.BlockSpec((rows, 128), lambda w, k, meta: (meta[0] ^ w, 0))

    def in_turn(j):
        return pl.BlockSpec((rows, 128), lambda w, k, meta: (meta[0] ^ jnp.where(k >= j - 1, w, 0), 0))

    by_shard = pl.BlockSpec((1, rows, 128), lambda w, k, meta: (2 * (meta[1] ^ k) + (meta[0] ^ w), 0, 0))
    extra = pl.BlockSpec((16, 128), lambda w, k, meta: (late_shards * rows // 16, 0))
    return pl.pallas_call(
        functools.partial(update_kernel, shards, late_shards, shard_rows),
        name="update",
        grid_spec=pltpu.PrefetchScalarGridSpec(
            num_scalar_prefetch=1,
            grid=(2, shards),
            in_specs=[pl.BlockSpec(memory_space=pltpu.SMEM)]
            + [pl.BlockSpec((rows, 128), early_map(side)) for side in range(2)]
            + [pl.BlockSpec((rows, 128), late_map(side)) for side in range(2)]
            + [extra, extra, by_shard, by_half, by_half]
            + [in_turn(j // 2) for j in range(2 * shards)],
            out_specs=[pl.BlockSpec(memory_space=ANY), by_half, by_half, by_half],
            scratch_shapes=[
                VECTOR((rows, 128), jnp.float32),
                VECTOR((shards * shard_rows + 2 * rows, 128), jnp.float32),
                VECTOR((2, shards * shard_rows // 9, 128), jnp.bfloat16),
                pltpu.SemaphoreType.DMA((2,)),
            ],
        ),
        out_shape=[jax.ShapeDtypeStruct((shards * shard_rows, 128), jnp.bfloat16)]
        + [jax.ShapeDtypeStruct((shard_rows, 128), jnp.float32)] * 3,
        compiler_params=pltpu.CompilerParams(vmem_limit_bytes=60 * 2**20),
        cost_estimate=BRIEF,
    )(
        meta,
        norm,
        *early,
        *late,
        *late,
        weights,
        first_moment.reshape(-1, 128),
        second_moment.reshape(-1, 128),
        *moments,
    )


def narrow_kernel(shard_rows, turn_ref, one_ref, two_ref, first_out, second_out):
    shape = first_out.shape
    begin = pl.program_id(0) * shape[0]
    inside = begin + lax.broadcasted_iota(jnp.int32, shape, 0) < shard_rows
    one = jnp.where(inside, one_ref[...] * (BETA_ONE / FIX_ONE), 0.0).astype(jnp.bfloat16)
    two = jnp.where(inside, two_ref[...] * (BETA_TWO / FIX_TWO), 0.0).astype(jnp.bfloat16)
    turned = turn_ref[0] == 1
    first_out[...] = jnp.where(turned, two, one)
    second_out[...] = jnp.where(turned, one, two)


def narrowed(one, two, half, turn):
    block = pl.BlockSpec((half // 2, 128), lambda i: (i, 0))
    return pl.pallas_call(
        functools.partial(narrow_kernel, one.shape[0]),
        name="narrow",
        grid=(4,),
        in_specs=[pl.BlockSpec(memory_space=pltpu.SMEM), block, block],
        out_specs=[block, block],
        out_shape=[jax.ShapeDtypeStruct((2 * half, 128), jnp.bfloat16)] * 2,
        cost_estimate=BRIEF,
    )(turn.reshape(1), one, two)


def bit_of(bit):
    return (lax.axis_index(LINE) // bit) % 2


def on_device(inputs, weights, cotangent, clip_lengths, first_moment, second_moment):
    tok_rows = inputs.shape[0]
    reach = (MOST + tok_rows - 2) // tok_rows
    shard_rows = first_moment.shape[0] // 128
    half = halves_rows(shard_rows)
    (
        first_gain,
        first_bias,
        query_weight,
        query_bias,
        key_weight,
        value_weight,
        value_bias,
        out_weight,
        out_bias,
        second_gain,
        second_bias,
        up_weight,
        up_bias,
        down_weight,
        down_bias,
        padded_weights,
    ) = unpacked(weights, shard_rows)
    base_slot = lax.axis_index(LINE) * tok_rows
    positions = base_slot + jnp.arange(tok_rows, dtype=jnp.int32)
    lower_slot, upper_slot = bounds(positions, clip_lengths)
    low = lower_slot - base_slot + reach * tok_rows
    high = upper_slot - base_slot + reach * tok_rows
    first_block = low.reshape(2, -1)[:, 0] // tok_rows
    last_block = (high.reshape(2, -1)[:, -1] + tok_rows - 1) // tok_rows
    ranges = (first_block, last_block, slot_table(), tok_rows)
    places = base_slot + block_distances()[:, None] * tok_rows + jnp.arange(tok_rows, dtype=jnp.int32)[None]
    marks = clip_marks(places.reshape(-1), clip_lengths)
    closed = penalty(clip_marks(positions, clip_lengths))

    inner = lax.axis_size("inner")
    turn = (lax.axis_index(LINE) // inner) % 2
    first_half, second_half = narrowed(first_moment.reshape(-1, 128), second_moment.reshape(-1, 128), half, turn)
    blocks = halo(inputs, (padded_weights,))
    fetched, *blocks = lax.optimization_barrier((first_half, *blocks))
    rows = projected(
        blocks, query_weight, key_weight, value_weight, first_gain, first_bias, query_bias, value_bias
    )
    fetched = swapped(fetched, 2)
    input_rows = inputs.astype(jnp.float32)
    first_hat, first_dev = standard(input_rows)
    normed = (first_hat * first_gain + first_bias).astype(jnp.bfloat16)

    attended, lse = attend(
        forward_kernel,
        ranges,
        [
            (rows, ("pair", 0)),
            (rows, ("pair", -5)),
            (rows, ("pair", -9)),
            (marks, ("all", 0)),
            (closed, ("all", 0)),
        ],
        [jnp.float32, jnp.float32],
        [pltpu.VMEM((2, 2 * reach + 1, tok_rows, tok_rows), jnp.float32)],
    )
    attended, lse, fetched = lax.optimization_barrier((attended, lse, fetched))
    passed = swapped(fetched, inner)
    held = {0: (first_half, second_half), 2: (fetched, passed)}
    bit = 4
    while bit < inner:
        for place in list(held):
            held[place + bit] = tuple(swapped(piece, bit) for piece in held[place])
        bit = 2 * bit
    moments = []
    for place in range(inner):
        if place % 2 == 0:
            moments += held[place]
        else:
            moments += [swapped(piece, 1) for piece in held[place - 1]]
    mixed = attended.astype(jnp.bfloat16)
    middle = input_rows + plain_dot(mixed, out_weight) + out_bias
    second_hat, second_dev = standard(middle)
    hidden_in = (second_hat * second_gain + second_bias).astype(jnp.bfloat16)
    up_rows = plain_dot(hidden_in, up_weight) + up_bias
    cdf_part = 0.5 * (1.0 + lax.erf(up_rows * INV_ROOT_TWO))
    activated = (up_rows * cdf_part).astype(jnp.bfloat16)
    layer_output = (middle + plain_dot(activated, down_weight) + down_bias).astype(jnp.bfloat16)
    grad_out = cotangent.astype(jnp.float32)
    down_bias_grad = jnp.sum(grad_out, axis=0)
    grad_act = back_dot(cotangent, down_weight)
    pdf_part = jnp.exp(-0.5 * up_rows * up_rows) * INV_ROOT_TWO_PI
    grad_up = (grad_act * (cdf_part + up_rows * pdf_part)).astype(jnp.bfloat16)
    up_bias_grad = jnp.sum(grad_up.astype(jnp.float32), axis=0)
    grad_hidden = back_dot(grad_up, up_weight)
    second_gain_grad = jnp.sum(grad_hidden * second_hat, axis=0)
    second_bias_grad = jnp.sum(grad_hidden, axis=0)
    grad_middle = grad_out + norm_back(grad_hidden, second_hat, second_dev, second_gain)
    grad_branch = grad_middle.astype(jnp.bfloat16)
    out_bias_grad = jnp.sum(grad_branch.astype(jnp.float32), axis=0)
    sent = mixed_grad(grad_branch, out_weight, attended, lse, clip_marks(positions, clip_lengths))
    line = lax.axis_size(LINE)
    shards = inner
    late_shards = shards // 4
    groups = bit_groups()

    def rounded(count, unit):
        return -(-count // unit) * unit

    def shard_spans(first, last, base):
        spans = ([], [])
        for shard in range(first, last):
            begin = (shard - first) * shard_rows + base
            spans[0].append((begin, half, half))
            spans[1].append((begin + half, shard_rows - half, half))
        return spans

    def query_step(pairs, after):
        return attend(
            query_kernel,
            ranges,
            [
                (rows, ("pair", 0)),
                (rows, ("pair", -5)),
                (rows, ("pair", -9)),
                (sent, ("pair", 0)),
                (sent, ("column", 4)),
                (marks, ("all", 0)),
                (closed, ("all", 0)),
            ],
            [jnp.bfloat16],
            [],
            pairs,
            after,
        )

    def key_step(pairs, after):
        return attend(
            key_kernel,
            ranges,
            [
                (rows, ("pair", 4)),
                (rows, ("pair", 8)),
                (rows, ("pair", -1)),
                (closed, ("all", 0)),
            ]
            + [(block, ("pair", 0)) for block in grad_blocks]
            + [(block, ("column", 4)) for block in grad_blocks],
            [jnp.bfloat16, jnp.bfloat16],
            [pltpu.VMEM((len(grad_blocks), tok_rows, 128), jnp.bfloat16)] * 2,
            pairs,
            after,
        )

    query_parts = query_step((0, 2), ())
    grad_blocks = halo(sent, query_parts)
    activated, hidden_in, mixed = (behind(array, query_parts) for array in (activated, hidden_in, mixed))
    down_grad = rows_dot(activated, cotangent)
    up_grad = rows_dot(hidden_in, grad_up)
    out_grad = rows_dot(mixed, grad_branch)

    early_rows = [
        out_grad,
        out_bias_grad,
        second_gain_grad,
        second_bias_grad,
        up_grad,
        up_bias_grad,
        down_grad,
        down_bias_grad,
    ]
    early_rows = [section.reshape(-1, section.shape[-1]) for section in early_rows]
    early_half = rounded((shards - late_shards) * half, 8 * line)
    spans = shard_spans(late_shards, shards, 0)
    for span in spans:
        span.append((0, 0, early_half - (shards - late_shards) * half))
    early_keep, early_give = packed_halves(early_rows, D // 128, spans, early_half)
    early_got = swapped(early_give, 1)

    query_parts += query_step((2, 2), (early_give,))
    parts = combine([early_keep, early_got], groups[0], query_parts)
    got = exchanged(parts, groups[0])
    query_low = jnp.concatenate(query_parts, axis=1)
    work = [(1, 1), (2, 1), (3, 1)]
    done = key_step((0, 1), parts[:1])
    key_parts, value_parts = [done[0]], [done[1]]
    held_back = done[:1]
    for at, group in enumerate(groups):
        parts = combine(got, groups[at + 1] if at + 1 < len(groups) else [], held_back)
        if at + 1 < len(groups):
            got = exchanged(parts, groups[at + 1])
        if work:
            done = key_step(work.pop(0), parts[:1])
            key_parts.append(done[0])
            value_parts.append(done[1])
            held_back = done[:1]
    piece = parts[0]
    for at, group in enumerate(groups[::-1]):
        got = exchanged([piece], group)
        if work and at > 0:
            done = key_step(work.pop(0), [piece])
            key_parts.append(done[0])
            value_parts.append(done[1])
            held_back = done[:1]
        piece = stack(got, group, held_back)
    early_other = swapped(piece, 1)
    for pairs in work:
        done = key_step(pairs, [piece])
        key_parts.append(done[0])
        value_parts.append(done[1])
    early = (piece, early_other)
    key_low = jnp.concatenate(key_parts, axis=1)
    value_low = jnp.concatenate(value_parts, axis=1)
    query_grad = rows_dot(normed, query_low)
    query_bias_grad = jnp.sum(query_low.astype(jnp.float32), axis=0)
    key_grad = rows_dot(normed, key_low)
    value_grad = rows_dot(normed, value_low)
    value_bias_grad = jnp.sum(value_low.astype(jnp.float32), axis=0)
    grad_normed = (
        back_dot(query_low, query_weight)
        + back_dot(key_low, key_weight)
        + back_dot(value_low, value_weight)
    )
    first_gain_grad = jnp.sum(grad_normed * first_hat, axis=0)
    first_bias_grad = jnp.sum(grad_normed, axis=0)
    input_grad = (grad_middle + norm_back(grad_normed, first_hat, first_dev, first_gain)).astype(
        jnp.bfloat16
    )

    late_rows = [
        first_gain_grad,
        first_bias_grad,
        query_grad,
        query_bias_grad,
        key_grad,
        value_grad,
        value_bias_grad,
    ]
    late_rows = [section.reshape(-1, section.shape[-1]) for section in late_rows]
    tail = max(1, 1 << (len(groups[0])))
    late_half = rounded(late_shards * half + 16, 16 * tail)
    spans = shard_spans(0, late_shards, 0)
    spare = late_half - late_shards * half
    spans[0].append((late_shards * shard_rows, D // 128, spare))
    spans[1].append((0, 0, spare))
    keep, give = packed_halves(late_rows, 0, spans, late_half)
    early_square = square_sum(early)
    parts = combine([keep, swapped(give, 1)], groups[0], ())
    (piece,) = combine(exchanged(parts, groups[0]), [], ())
    for group in groups[1:]:
        (piece,) = combine(exchanged([piece], group), [], (early_square,))
    piece = stack(exchanged([piece], groups[0]), groups[0], ())
    late = (piece, swapped(piece, 1))

    grad_norm = jnp.sqrt(early_square + square_sum(late))[0, 0]
    steps, grad_shard, moment_one, moment_two = updated(
        (1.0 / jnp.maximum(grad_norm, 1.0)).reshape(1),
        early,
        late,
        late_shards,
        padded_weights,
        first_moment,
        second_moment,
        moments,
    )
    weight_step = steps.reshape(-1)
    return (
        layer_output,
        input_grad,
        grad_shard.reshape(-1),
        grad_norm,
        moment_one.reshape(-1),
        moment_two.reshape(-1),
        weight_step,
    )


def solution(mesh):
    return jax.shard_map(
        on_device,
        mesh=mesh,
        in_specs=(
            P(("outer", "inner"), None),
            P(),
            P(("outer", "inner"), None),
            P(),
            P("inner"),
            P("inner"),
        ),
        out_specs=(
            P(("outer", "inner"), None),
            P(("outer", "inner"), None),
            P("inner"),
            P(),
            P("inner"),
            P("inner"),
            P(),
        ),
        check_vma=False,
    )
```

```python
import functools
import math

import jax
import jax.numpy as jnp
from jax import lax
from jax.experimental import pallas as pl
from jax.experimental.pallas import tpu as pltpu
from jax.sharding import PartitionSpec as P

D = 512
HEADS = 8
FF = 2048
MOST = 1500


BETA_ONE = 0.9
BETA_TWO = 0.999
FIX_ONE = 1.0 - (0.9**10) ** 10
FIX_TWO = 1.0 - (0.999**10) ** 10
DECAY = 0.1
INV_ROOT_TWO = 1.0 / math.sqrt(2.0)
INV_ROOT_TWO_PI = 1.0 / math.sqrt(2.0 * math.pi)


def layouts():
    return [
        (D,),
        (D,),
        (D, D),
        (D,),
        (D, D),
        (D, D),
        (D,),
        (D, D),
        (D,),
        (D,),
        (D,),
        (D, FF),
        (FF,),
        (FF, D),
        (D,),
    ]


def plain_dot(matrix_one, matrix_two):
    return jnp.dot(matrix_one, matrix_two, preferred_element_type=jnp.float32)


def rows_dot(matrix_one, matrix_two):
    return lax.dot_general(
        matrix_one, matrix_two, (((0,), (0,)), ((), ())), preferred_element_type=jnp.float32
    )


def back_dot(matrix_one, matrix_two):
    return lax.dot_general(
        matrix_one, matrix_two, (((1,), (1,)), ((), ())), preferred_element_type=jnp.float32
    )


def standard(values):
    center = jnp.mean(values, axis=-1, keepdims=True)
    centered = values - center
    inverse_dev = lax.rsqrt(jnp.mean(centered * centered, axis=-1, keepdims=True) + 1e-05)
    return (centered * inverse_dev, inverse_dev)


def norm_back(grad_normed, normed_hat, inverse_dev, gain):
    scaled = grad_normed * gain
    return inverse_dev * (
        scaled
        - jnp.mean(scaled, axis=-1, keepdims=True)
        - normed_hat * jnp.mean(scaled * normed_hat, axis=-1, keepdims=True)
    )


def bounds(positions, clip_lengths):
    starts = jnp.cumsum(clip_lengths, dtype=jnp.int32) - clip_lengths
    member = (
        jnp.sum((positions[:, None] >= starts[None, :]).astype(jnp.int32), axis=1, dtype=jnp.int32)
        - 1
    )
    onehot = (
        jnp.arange(clip_lengths.shape[0], dtype=jnp.int32)[None, :] == member[:, None]
    ).astype(jnp.int32)
    lower_slot = jnp.sum(onehot * starts[None, :], axis=1, dtype=jnp.int32)
    upper_slot = lower_slot + jnp.sum(onehot * clip_lengths[None, :], axis=1, dtype=jnp.int32)
    return (lower_slot, upper_slot)


LINE = ("outer", "inner")
NEG = -1e30
BRIEF = pl.CostEstimate(flops=1000, bytes_accessed=1000, transcendentals=0)


def shifted(block, distance):
    n = lax.axis_size(LINE)
    return lax.ppermute(block, LINE, [(i + distance, i) for i in range(n) if 0 <= i + distance < n])


def swapped(block, bit):
    n = lax.axis_size(LINE)
    return lax.ppermute(block, LINE, [(i ^ bit, i) for i in range(n)])


def halo(block, before=()):
    n = lax.axis_size(LINE)
    left = shifted(block, -2)
    right = shifted(block, 2)
    partner = swapped(block, 1)
    route = [(i + (3 if i % 2 else -3), i) for i in range(n)]
    far = lax.ppermute(block, LINE, [(s, t) for s, t in route if 0 <= s < n])
    passed_left, passed_right, *_ = lax.optimization_barrier((left, right, *before))
    turned = [swapped(passed_left, 1), swapped(passed_right, 1)]
    return [block, partner, left, right, *turned, far]


def block_distances():
    odd = lax.axis_index(LINE) % 2
    even_far = jnp.array([0, 1, -2, 2, -1, 3, -3], jnp.int32)
    odd_far = jnp.array([0, -1, -2, 2, -3, 1, 3], jnp.int32)
    return jnp.where(odd == 1, odd_far, even_far)


def slot_table():
    odd = lax.axis_index(LINE) % 2
    even_slots = jnp.array([6, 2, 4, 0, 1, 3, 5], jnp.int32)
    odd_slots = jnp.array([4, 2, 1, 0, 5, 3, 6], jnp.int32)
    return jnp.where(odd == 1, odd_slots, even_slots)


def dot_nt(a, b):
    return lax.dot_general(a, b, (((1,), (1,)), ((), ())), preferred_element_type=jnp.float32)


def head_halves(pair):
    first = lax.broadcasted_iota(jnp.int32, pair.shape, 1) < pair.shape[1] // 2
    zero = jnp.zeros_like(pair)
    return jnp.where(first, pair, zero), jnp.where(first, zero, pair)


def over_lanes(tile, op):
    parts = [tile[:, 128 * j : 128 * (j + 1)] for j in range(tile.shape[1] // 128)]
    while len(parts) > 1:
        rest = parts[len(parts) // 2 * 2 :]
        parts = [op(parts[2 * j], parts[2 * j + 1]) for j in range(len(parts) // 2)] + rest
    return parts[0]


LSE_PARTS, DELTA_PARTS = 3, 2
DELTA_AT = LSE_PARTS * HEADS
CLIPS_AT = DELTA_AT + DELTA_PARTS * HEADS


def lane_of(shape):
    return lax.broadcasted_iota(jnp.int32, shape, 1)


def among(lane, begin, count):
    return (lane >= begin) & (lane < begin + count)


def beside(pair, marks):
    return jnp.concatenate([pair, marks.astype(pair.dtype)], axis=1)


def clip_marks(positions, clip_lengths):
    ends = jnp.cumsum(clip_lengths, dtype=jnp.int32)
    starts = ends - clip_lengths
    spare = 128 - CLIPS_AT - clip_lengths.shape[0]
    assert spare >= 0
    big = jnp.iinfo(jnp.int32).max
    lower = jnp.concatenate([jnp.full((CLIPS_AT,), -big, jnp.int32), starts, jnp.full((spare,), big, jnp.int32)])
    upper = jnp.concatenate([jnp.full((CLIPS_AT,), big, jnp.int32), ends, jnp.full((spare,), big, jnp.int32)])
    inside = (positions[:, None] >= lower[None]) & (positions[:, None] < upper[None])
    return inside.astype(jnp.bfloat16)


def penalty(marks):
    closed = (lane_of(marks.shape) >= CLIPS_AT) & (marks == 0)
    return jnp.where(closed, NEG, 0.0).astype(jnp.bfloat16)


def over_blocks(first_ref, last_ref, rows, work, start):
    half = rows // 2
    carried = (start, start)
    spans = (
        (first_ref[0], first_ref[1], 0, half),
        (first_ref[1], last_ref[0], 0, rows),
        (last_ref[0], last_ref[1], half, half),
    )
    for lower, upper, begin, count in spans:

        def step(block, carried):
            found = work(block, begin, count)
            upper_half, lower_half = carried
            if begin == 0:
                upper_half = tuple(join(old, new[:half]) for (join, new), old in zip(found, upper_half))
            if begin + count == rows:
                lower_half = tuple(join(old, new[count - half :]) for (join, new), old in zip(found, lower_half))
            return upper_half, lower_half

        carried = lax.fori_loop(lower, upper, step, carried)
    return [jnp.concatenate(halves, axis=0) for halves in zip(*carried)]


def forward_kernel(begin, first_ref, last_ref, slot_ref, q_ref, k_ref, v_ref, mark_ref, closed_ref, o_ref, lse_ref, s_ref):
    width = q_ref.shape[0]
    queries = [beside(half, closed_ref[...]) for half in head_halves(q_ref[...] * jnp.bfloat16(0.125))]

    def scores(block, begin, count):
        at = pl.ds(pl.multiple_of(slot_ref[block] * width, width), width)
        keys = beside(k_ref[at, :], mark_ref[at, :])
        found = []
        for h in range(2):
            score = dot_nt(queries[h][begin : begin + count], keys)
            s_ref[h, block, pl.ds(begin, count), :] = score
            found.append((jnp.maximum, over_lanes(score, jnp.maximum)))
        return found

    start = jnp.full((width // 2, 128), NEG, jnp.float32)
    peaks = over_blocks(first_ref, last_ref, width, scores, (start, start))
    peaks = [jnp.max(peak, axis=1, keepdims=True) for peak in peaks]

    def mix(block, begin, count):
        at = pl.ds(pl.multiple_of(slot_ref[block] * width, width), width)
        values = beside(v_ref[at, :], mark_ref[at, :])
        found = []
        for h in range(2):
            score = s_ref[h, block, pl.ds(begin, count), :]
            soft = jnp.exp(score - peaks[h][begin : begin + count]).astype(jnp.bfloat16)
            found.append((jnp.add, jnp.dot(soft, values, preferred_element_type=jnp.float32)))
        return found

    start = jnp.zeros((width // 2, 256), jnp.float32)
    sums = over_blocks(first_ref, last_ref, width, mix, (start, start))
    totals = [part[:, 128:129] for part in sums]
    even = lane_of((width, 128)) < 64
    o_ref[...] = jnp.where(even, sums[0][:, :128] / totals[0], sums[1][:, :128] / totals[1])
    lse_ref[...] = jnp.where(even, peaks[0] + jnp.log(totals[0]), peaks[1] + jnp.log(totals[1]))


def query_kernel(
    begin, first_ref, last_ref, slot_ref, q_ref, k_ref, v_ref, g_ref, own_ref, mark_ref, closed_ref, dq_ref
):
    width = q_ref.shape[0]
    pair = pl.program_id(0) + begin
    own, closed = own_ref[...], closed_ref[...]
    lane = lane_of(own.shape)
    zero = jnp.zeros_like(own)
    queries, grads = [], []
    halves = zip(head_halves(q_ref[...] * jnp.bfloat16(0.125)), head_halves(g_ref[...]))
    for h, (query, grad) in enumerate(halves):
        head = 2 * pair + h
        queries.append(beside(query, jnp.where(among(lane, LSE_PARTS * head, LSE_PARTS), own, closed)))
        grads.append(beside(grad, jnp.where(among(lane, DELTA_AT + DELTA_PARTS * head, DELTA_PARTS), own, zero)))

    def work(block, begin, count):
        at = pl.ds(pl.multiple_of(slot_ref[block] * width, width), width)
        keys = k_ref[at, :]
        values = beside(v_ref[at, :], mark_ref[at, :])
        marked = beside(keys, mark_ref[at, :])
        found = []
        for h in range(2):
            soft = jnp.exp(dot_nt(queries[h][begin : begin + count], marked))
            grad = (soft * dot_nt(grads[h][begin : begin + count], values)).astype(jnp.bfloat16)
            found.append((jnp.add, jnp.dot(grad, keys, preferred_element_type=jnp.float32)))
        return found

    start = jnp.zeros((width // 2, 128), jnp.float32)
    sums = over_blocks(first_ref, last_ref, width, work, (start, start))
    dq_ref[...] = (jnp.where(lane < 64, sums[0], sums[1]) * 0.125).astype(jnp.bfloat16)


def key_kernel(begin, first_ref, last_ref, slot_ref, k_ref, v_ref, q_ref, closed_ref, *refs):
    dk_ref, dv_ref, grad_ref, mark_ref = refs[-4:]
    width = k_ref.shape[0]
    pair = pl.program_id(0) + begin
    blocks = grad_ref.shape[0]
    for j in range(blocks):
        grad_ref[j] = refs[j][...]

    @pl.when(pl.program_id(0) == 0)
    def _():
        for j in range(blocks):
            mark_ref[j] = refs[blocks + j][...]

    closed = closed_ref[...]
    lane = lane_of(closed.shape)
    one, zero = jnp.ones_like(closed), jnp.zeros_like(closed)
    keys, values = [], []
    halves = zip(head_halves(k_ref[...] * jnp.bfloat16(0.125)), head_halves(v_ref[...]))
    for h, (key, value) in enumerate(halves):
        head = 2 * pair + h
        keys.append(beside(key, jnp.where(among(lane, LSE_PARTS * head, LSE_PARTS), one, closed)))
        values.append(beside(value, jnp.where(among(lane, DELTA_AT + DELTA_PARTS * head, DELTA_PARTS), one, zero)))

    def work(block, begin, count):
        slot = slot_ref[block]
        queries = q_ref[pl.ds(pl.multiple_of(slot * width, width), width), :]
        grads, marks = grad_ref[slot], mark_ref[slot]
        marked, graded = beside(queries, marks), beside(grads, marks)
        found = []
        for h in range(2):
            soft = jnp.exp(dot_nt(keys[h][begin : begin + count], marked))
            grad = (soft * dot_nt(values[h][begin : begin + count], graded)).astype(jnp.bfloat16)
            found.append((jnp.add, jnp.dot(grad, queries, preferred_element_type=jnp.float32)))
            found.append((jnp.add, jnp.dot(soft.astype(jnp.bfloat16), grads, preferred_element_type=jnp.float32)))
        return found

    start = jnp.zeros((width // 2, 128), jnp.float32)
    sums = over_blocks(first_ref, last_ref, width, work, (start,) * 4)
    dk_ref[...] = (jnp.where(lane < 64, sums[0], sums[2]) * 0.125).astype(jnp.bfloat16)
    dv_ref[...] = jnp.where(lane < 64, sums[1], sums[3]).astype(jnp.bfloat16)


def mixed_grad_kernel(branch_ref, weight_ref, mixed_ref, lse_ref, own_ref, sent_ref, mark_ref):
    step = pl.program_id(0)

    @pl.when(step == 0)
    def _():
        mark_ref[...] = own_ref[...].astype(jnp.float32)

    @pl.when(step < D // 128)
    def _():
        grad = dot_nt(branch_ref[...], weight_ref[...]).astype(jnp.bfloat16)
        sent_ref[...] = grad
        product = grad.astype(jnp.float32) * mixed_ref[...]
        lane = lane_of(product.shape)
        marks = mark_ref[...]
        for h, part in enumerate(head_halves(product)):
            head = 2 * step + h
            delta = -jnp.sum(part, axis=1, keepdims=True)
            lse = -lse_ref[:, 64 * h : 64 * h + 1]
            for value, begin, count in (
                (lse, LSE_PARTS * head, LSE_PARTS),
                (delta, DELTA_AT + DELTA_PARTS * head, DELTA_PARTS),
            ):
                for k in range(count):
                    rounded = value.astype(jnp.bfloat16).astype(jnp.float32)
                    marks = jnp.where(lane == begin + k, rounded, marks)
                    value = value - rounded
        mark_ref[...] = marks

    @pl.when(step == D // 128)
    def _():
        sent_ref[...] = mark_ref[...].astype(jnp.bfloat16)


def mixed_grad(branch, out_weight, mixed, lse, own_marks):
    width = branch.shape[0]
    last = D // 128 - 1
    column = pl.BlockSpec((width, 128), lambda h: (0, jnp.minimum(h, last)))
    return pl.pallas_call(
        mixed_grad_kernel,
        name="mixed_grad",
        grid=(D // 128 + 1,),
        in_specs=[
            pl.BlockSpec((width, D), lambda h: (0, 0)),
            pl.BlockSpec((128, D), lambda h: (jnp.minimum(h, last), 0)),
            column,
            column,
            pl.BlockSpec((width, 128), lambda h: (0, 0)),
        ],
        out_specs=pl.BlockSpec((width, 128), lambda h: (0, h)),
        out_shape=jax.ShapeDtypeStruct((width, D + 128), jnp.bfloat16),
        scratch_shapes=[pltpu.VMEM((width, 128), jnp.float32)],
        cost_estimate=BRIEF,
    )(branch, out_weight, mixed, lse, own_marks)


def project_kernel(count, *refs):
    query_ref, key_ref, value_ref, gain_ref, bias_ref, query_bias_ref, value_bias_ref, out_ref, row_ref = refs[count:]
    step = pl.program_id(0)
    for j in range(count):

        @pl.when(step == j)
        def _():
            row_ref[...] = refs[j][...]

    rows = 256
    for i in range(row_ref.shape[0] // rows):
        at = pl.ds(i * rows, rows)
        hat, _ = standard(row_ref[at, :].astype(jnp.float32))
        normed = (hat * gain_ref[...] + bias_ref[...]).astype(jnp.bfloat16)
        out_ref[at, 0:D] = (plain_dot(normed, query_ref[...]) + query_bias_ref[...]).astype(jnp.bfloat16)
        out_ref[at, D : 2 * D] = plain_dot(normed, key_ref[...]).astype(jnp.bfloat16)
        out_ref[at, 2 * D :] = (plain_dot(normed, value_ref[...]) + value_bias_ref[...]).astype(jnp.bfloat16)


def projected(blocks, *weights):
    width = blocks[0].shape[0]
    whole = [pl.BlockSpec(array.shape, lambda i: (0, 0)) for array in (*blocks, *weights)]
    return pl.pallas_call(
        functools.partial(project_kernel, len(blocks)),
        name="project",
        grid=(len(blocks),),
        in_specs=whole,
        out_specs=pl.BlockSpec((width, 3 * D), lambda i: (i, 0)),
        out_shape=jax.ShapeDtypeStruct((len(blocks) * width, 3 * D), jnp.bfloat16),
        scratch_shapes=[pltpu.VMEM((width, D), jnp.bfloat16)],
        compiler_params=pltpu.CompilerParams(vmem_limit_bytes=63 * 2**20),
        cost_estimate=BRIEF,
    )(*blocks, *weights)


def attend(kernel, ranges, operands, results, scratch, pairs=(0, D // 128), after=()):
    begin, count = pairs
    tok_rows = ranges[3]
    specs = []
    for array, (kind, at) in operands:
        if kind == "pair":
            rows = array.shape[0] if at < 0 else tok_rows
            at = (abs(at) - 1 if at < 0 else at) + begin
            specs.append(pl.BlockSpec((rows, 128), lambda h, *_, at=at: (0, at + h)))
        elif kind == "column":
            specs.append(pl.BlockSpec((tok_rows, 128), lambda h, *_, at=at: (0, at)))
        else:
            specs.append(pl.BlockSpec(array.shape, lambda h, *_, n=array.ndim: (0,) * n))
    return pl.pallas_call(
        functools.partial(kernel, begin),
        grid_spec=pltpu.PrefetchScalarGridSpec(
            num_scalar_prefetch=3,
            grid=(count,),
            in_specs=specs,
            out_specs=[pl.BlockSpec((tok_rows, 128), lambda h, *_: (0, h))] * len(results),
            scratch_shapes=scratch,
        ),
        out_shape=[jax.ShapeDtypeStruct((tok_rows, 128 * count), kept) for kept in results],
        compiler_params=pltpu.CompilerParams(vmem_limit_bytes=48 * 2**20),
        cost_estimate=BRIEF,
    )(*[behind(bound, after) for bound in ranges[:1]], *ranges[1:3], *[array for array, _ in operands])


VECTOR = pltpu.VMEM
ANY = pl.ANY


def behind(value, others):
    return lax.optimization_barrier((value, *others))[0]


def halves_rows(shard_rows):
    return -(-shard_rows // 128) * 64


def unpack_kernel(plan, shard_rows, flat_ref, *refs):
    wide_ref = refs[-1]
    padded_ref = refs[-2]
    total = flat_ref.shape[0]
    chunk = 432

    def widen(i, _):
        rows = pl.ds(pl.multiple_of(i * chunk, 16), chunk)
        wide_ref[rows, :] = flat_ref[rows, :].astype(jnp.float32)
        return 0

    lax.fori_loop(0, total // chunk, widen, 0)
    wide_ref[pl.ds(total, wide_ref.shape[0] - total), :] = jnp.zeros((wide_ref.shape[0] - total, 128), jnp.float32)
    for (offset, rows, columns, begin), ref in zip(plan, refs[:-2]):
        pieces = columns // 128
        if rows == 1:
            for j in range(pieces):
                ref[:, 128 * j : 128 * (j + 1)] = wide_ref[pl.ds(offset + j, 1), :]
            continue

        taken = 1024 // pieces

        def matrix(i, _):
            at = pl.multiple_of(i * taken, 64)
            for j in range(pieces):
                part = wide_ref[pl.ds(offset + j + at * pieces, taken, stride=pieces), :]
                ref[pl.ds(at, taken), begin + 128 * j : begin + 128 * (j + 1)] = part.astype(jnp.bfloat16)
            return 0

        lax.fori_loop(0, rows // taken, matrix, 0)
    shards = total // shard_rows
    half = halves_rows(shard_rows)
    for s in range(shards):
        for h in range(2):

            run = 448 if half % 448 == 0 else 64

            def pad(i, _):
                part = wide_ref[pl.ds(s * shard_rows + h * half + i * run, run), :]
                padded_ref[s * 2 + h, pl.ds(pl.multiple_of(i * run, 64), run), :] = part.astype(jnp.bfloat16)
                return 0

            lax.fori_loop(0, half // run, pad, 0)


def unpacked(weights, shard_rows):
    flat = weights.reshape(-1, 128)
    half = halves_rows(shard_rows)
    plan, outs = [], []
    offset = 0
    for layout in layouts():
        rows, columns = layout if len(layout) == 2 else (1, layout[0])
        plan.append([offset, rows, columns, 0])
        outs.append(jax.ShapeDtypeStruct((rows, columns), jnp.bfloat16 if rows > 1 else jnp.float32))
        offset = offset + rows * columns // 128
    shards = flat.shape[0] // shard_rows
    outs.append(jax.ShapeDtypeStruct((2 * shards, half, 128), jnp.bfloat16))
    return pl.pallas_call(
        functools.partial(unpack_kernel, plan, shard_rows),
        name="unpack",
        in_specs=[pl.BlockSpec(memory_space=VECTOR)],
        out_specs=[pl.BlockSpec(memory_space=VECTOR)] * len(outs),
        out_shape=outs,
        scratch_shapes=[VECTOR((flat.shape[0] + 2 * half, 128), jnp.float32)],
        compiler_params=pltpu.CompilerParams(vmem_limit_bytes=60 * 2**20),
        cost_estimate=BRIEF,
    )(flat)


def pack_kernel(plan, spans, place_ref, *refs):
    keep_ref, give_ref, flat_ref, out_ref, sems = refs[-5:]
    end = max(offset + rows * columns // 128 for offset, rows, columns in plan)
    begin = min(offset for offset, _, _ in plan)
    if begin:
        flat_ref[pl.ds(0, begin), :] = jnp.zeros((begin, 128), jnp.float32)
    given = iter(refs)
    for offset, rows, columns in plan:
        pieces = columns // 128
        ref = next(given)
        if rows == 1:
            for j in range(pieces):
                flat_ref[pl.ds(offset + j, 1), :] = ref[:, 128 * j : 128 * (j + 1)]
            continue

        other = next(given)
        taken = 256

        def product(i, _):
            at = pl.multiple_of(i * taken, 128)
            found = rows_dot(ref[:, pl.ds(at, taken)], other[...])
            for j in range(pieces):
                part = found[:, 128 * j : 128 * (j + 1)]
                flat_ref[pl.ds(offset + j + at * pieces, taken, stride=pieces), :] = part
            return 0

        lax.fori_loop(0, rows // taken, product, 0)
    for h in range(2):
        at = h ^ place_ref[0]
        filled = 0
        for source, rows, room in spans[h]:
            run = 448 if rows >= 448 else 64
            whole = rows // run

            def move(i, _):
                to = pl.ds(pl.multiple_of(filled + i * run, 16), run)
                out_ref[at, to, :] = flat_ref[pl.ds(source + i * run, run), :].astype(jnp.bfloat16)
                return 0

            lax.fori_loop(0, whole, move, 0)
            rest = rows - run * whole
            tail = room - run * whole
            if tail:
                parts = []
                if rest:
                    parts.append(flat_ref[pl.ds(source + run * whole, rest), :])
                if tail > rest:
                    parts.append(jnp.zeros((tail - rest, 128), jnp.float32))
                last = parts[0] if len(parts) == 1 else jnp.concatenate(parts, axis=0)
                out_ref[at, pl.ds(filled + run * whole, tail), :] = last.astype(jnp.bfloat16)
            filled = filled + room
    copies = [
        pltpu.make_async_copy(out_ref.at[0], keep_ref, sems.at[0]),
        pltpu.make_async_copy(out_ref.at[1], give_ref, sems.at[1]),
    ]
    for copy in copies:
        copy.start()
    for copy in copies:
        copy.wait()


def packed_halves(grads, begin, spans, half):
    plan, arrays = [], []
    offset = begin
    for grad in grads:
        rows, columns = (grad[0].shape[1], grad[1].shape[1]) if len(grad) == 2 else (1, grad[0].size)
        plan.append((offset, rows, columns))
        arrays += [array.reshape(-1, array.shape[-1]) for array in grad]
        offset = offset + rows * columns // 128
    return pl.pallas_call(
        functools.partial(pack_kernel, plan, spans),
        name="pack",
        in_specs=[pl.BlockSpec(memory_space=pltpu.SMEM)] + [pl.BlockSpec(memory_space=VECTOR)] * len(arrays),
        out_specs=[pl.BlockSpec(memory_space=ANY)] * 2,
        out_shape=[jax.ShapeDtypeStruct((half, 128), jnp.bfloat16)] * 2,
        scratch_shapes=[
            VECTOR((offset, 128), jnp.float32),
            VECTOR((2, half, 128), jnp.bfloat16),
            pltpu.SemaphoreType.DMA((2,)),
        ],
        compiler_params=pltpu.CompilerParams(vmem_limit_bytes=60 * 2**20),
        cost_estimate=BRIEF,
    )(bit_of(1).reshape(1), *arrays)


def combine_kernel(count, places_ref, *refs):
    parts, outs = refs[:count], refs[-places_ref.shape[0] :]
    rows = outs[0].shape[0]
    for k, out in enumerate(outs):
        at = pl.ds(pl.multiple_of(places_ref[k] * rows, 16), rows)
        terms = [part[at, :].astype(jnp.float32) for part in parts]
        while len(terms) > 1:
            terms = [terms[2 * j] + terms[2 * j + 1] for j in range(len(terms) // 2)]
        out[...] = terms[0].astype(jnp.bfloat16)


def places_of(group):
    if not group:
        return jnp.zeros((1,), jnp.int32)
    place = (lax.axis_index(LINE) // group[0]) % (1 << len(group))
    return place ^ jnp.arange(1 << len(group), dtype=jnp.int32)


def combine(parts, group, after):
    count = 1 << len(group)
    rows = parts[0].shape[0] // count
    outs = pl.pallas_call(
        functools.partial(combine_kernel, len(parts)),
        name="combine",
        in_specs=[pl.BlockSpec(memory_space=pltpu.SMEM)]
        + [pl.BlockSpec(memory_space=VECTOR)] * len(parts),
        out_specs=[pl.BlockSpec(memory_space=VECTOR)] * count,
        out_shape=[jax.ShapeDtypeStruct((rows, 128), jnp.bfloat16)] * count,
        cost_estimate=BRIEF,
    )(behind(places_of(group), after), *parts)
    return list(outs)


def stack_kernel(count, places_ref, *refs):
    out_ref = refs[-1]
    rows = refs[0].shape[0]
    for k in range(count):
        out_ref[pl.ds(pl.multiple_of(places_ref[k] * rows, 16), rows), :] = refs[k][...]


def stack(parts, group, after):
    rows = parts[0].shape[0] * len(parts)
    return pl.pallas_call(
        functools.partial(stack_kernel, len(parts)),
        name="stack",
        in_specs=[pl.BlockSpec(memory_space=pltpu.SMEM)]
        + [pl.BlockSpec(memory_space=VECTOR)] * len(parts),
        out_specs=pl.BlockSpec(memory_space=VECTOR),
        out_shape=jax.ShapeDtypeStruct((rows, 128), jnp.bfloat16),
        cost_estimate=BRIEF,
    )(behind(places_of(group), after), *parts)


def exchanged(parts, group):
    return [parts[0]] + [swapped(parts[k % len(parts)], group[0] * k) for k in range(1, 1 << len(group))]


def bit_groups():
    bits = [1 << k for k in range(1, lax.axis_size(LINE).bit_length() - 1)]
    return [bits[k : k + 2] for k in range(0, len(bits), 2)]


def square_sum_kernel(one_ref, two_ref, out_ref):
    sums = []
    for ref in (one_ref, two_ref):
        rows = ref.shape[0]
        chunk = rows // 8 if rows % 128 == 0 else 64

        def add(i, total):
            part = ref[pl.ds(pl.multiple_of(i * chunk, 16), chunk), :].astype(jnp.float32)
            return total + jnp.sum((part * part).reshape(-1, 32, 128), axis=0)

        zero = jnp.zeros((32, 128), jnp.float32)
        if chunk % 32:
            chunk = 32
        sums.append(jnp.sum(lax.fori_loop(0, rows // chunk, add, zero), keepdims=True))
    out_ref[...] = jnp.broadcast_to(sums[0] + sums[1], (1, 128))


def square_sum(pair):
    return pl.pallas_call(
        square_sum_kernel,
        name="square_sum",
        in_specs=[pl.BlockSpec(memory_space=VECTOR)] * 2,
        out_specs=pl.BlockSpec(memory_space=VECTOR),
        out_shape=jax.ShapeDtypeStruct((1, 128), jnp.float32),
        cost_estimate=BRIEF,
    )(*pair)


def update_kernel(
    shards, late, shard_rows, meta_ref, scale_ref, early_own, early_other, late_own, late_other, extra_own, extra_other,
    weight_ref, one_ref, two_ref, *refs
):
    moments = refs[: 2 * shards]
    step_ref, grad_ref, new_one_ref, new_two_ref, sum_ref, wide_ref, stage_ref, sems = refs[2 * shards :]
    which, k = pl.program_id(0), pl.program_id(1)
    core, me = meta_ref[0], meta_ref[1]
    shard = me ^ k
    half = core ^ which
    rows = sum_ref.shape[0]
    chunk = rows // 7 if rows % 112 == 0 else 64
    scale = scale_ref[0]

    def by_chunks(body, first=0, last=rows // chunk):
        def move(i, _):
            body(pl.multiple_of(i * chunk, 16))
            return 0

        lax.fori_loop(first, last, move, 0)

    def load(ref):
        def body(at):
            sum_ref[pl.ds(at, chunk), :] = ref[pl.ds(at, chunk), :].astype(jnp.float32)

        by_chunks(body)

    for array, side, is_late in ((early_own, 0, 0), (early_other, 1, 0), (late_own, 0, 1), (late_other, 1, 1)):
        pl.when((which == side) & ((shard < late) == (is_late == 1)))(functools.partial(load, array))
    for array, side in ((extra_own, 0), (extra_other, 1)):

        @pl.when((which == side) & (shard == late) & (half == 0))
        def _():
            sum_ref[pl.ds(0, 8), :] = sum_ref[pl.ds(0, 8), :] + array[pl.ds(0, 8), :].astype(jnp.float32)

    slope_one = (1.0 - BETA_ONE) * scale
    slope_two = (1.0 - BETA_TWO) * scale * scale

    base = shard * shard_rows + half * rows
    limit = jnp.where(half == 1, shard_rows - rows, rows)
    for j in range(shards):

        @pl.when(k == j)
        def _():
            def body(start, masked=False):
                at = pl.ds(start, chunk)
                one, two = moments[2 * j][at, :], moments[2 * j + 1][at, :]
                grad = sum_ref[at, :]
                one = one.astype(jnp.float32) + (slope_one * (1.0 / FIX_ONE)) * grad
                two = two.astype(jnp.float32) + (slope_two * (1.0 / FIX_TWO)) * grad * grad
                root = two * lax.rsqrt(jnp.maximum(two, 1e-37))
                update = one / (root + 1e-08) + DECAY * weight_ref[0, at, :].astype(jnp.float32)
                to = pl.ds(base + start, chunk)
                if masked:
                    inside = start + lax.broadcasted_iota(jnp.int32, update.shape, 0) < limit
                    update = jnp.where(inside, update, wide_ref[to, :])
                wide_ref[to, :] = update

            whole = (shard_rows - rows) // chunk
            by_chunks(body, 0, whole)
            by_chunks(functools.partial(body, masked=True), whole, rows // chunk)

    @pl.when(k == 0)
    def _():
        def body(start):
            at = pl.ds(start, chunk)
            grad = sum_ref[at, :]
            grad_ref[at, :] = grad
            new_one_ref[at, :] = BETA_ONE * one_ref[at, :] + slope_one * grad
            new_two_ref[at, :] = BETA_TWO * two_ref[at, :] + slope_two * grad * grad

        by_chunks(body)

    @pl.when((which == 1) & (k == shards - 1))
    def _():
        piece = stage_ref.shape[1]
        total = step_ref.shape[0]

        def sending(i, slot):
            return pltpu.make_async_copy(
                stage_ref.at[slot], step_ref.at[pl.ds(pl.multiple_of(i * piece, 16), piece), :], sems.at[slot]
            )

        count = total // piece
        for i in range(count):
            if i >= 2:
                sending(i - 2, i % 2).wait()
            stage_ref[i % 2] = wide_ref[pl.ds(i * piece, piece), :].astype(jnp.bfloat16)
            sending(i, i % 2).start()
        for i in range(count - 2, count):
            sending(i, i % 2).wait()


def updated(norm, early, late, late_shards, weights, first_moment, second_moment, moments):
    shards = len(moments) // 2
    rows = weights.shape[1]
    shard_rows = first_moment.shape[0] // 128
    line = lax.axis_index(LINE)
    meta = jnp.stack([line % 2, lax.axis_index("inner")]).astype(jnp.int32)
    last = shards - 1

    def early_map(side):
        def index(w, k, meta):
            k = jnp.where(w == side, k, last if side == 0 else 0)
            return (jnp.clip((meta[1] ^ k) - late_shards, 0, shards - late_shards - 1), 0)

        return index

    def late_map(side):
        def index(w, k, meta):
            k = jnp.where(w == side, k, last if side == 0 else 0)
            return (jnp.clip(meta[1] ^ k, 0, late_shards - 1), 0)

        return index

    by_half = pl.BlockSpec((rows, 128), lambda w, k, meta: (meta[0] ^ w, 0))

    def in_turn(j):
        return pl.BlockSpec((rows, 128), lambda w, k, meta: (meta[0] ^ jnp.where(k >= j - 1, w, 0), 0))

    by_shard = pl.BlockSpec((1, rows, 128), lambda w, k, meta: (2 * (meta[1] ^ k) + (meta[0] ^ w), 0, 0))
    extra = pl.BlockSpec((16, 128), lambda w, k, meta: (late_shards * rows // 16, 0))
    return pl.pallas_call(
        functools.partial(update_kernel, shards, late_shards, shard_rows),
        name="update",
        grid_spec=pltpu.PrefetchScalarGridSpec(
            num_scalar_prefetch=1,
            grid=(2, shards),
            in_specs=[pl.BlockSpec(memory_space=pltpu.SMEM)]
            + [pl.BlockSpec((rows, 128), early_map(side)) for side in range(2)]
            + [pl.BlockSpec((rows, 128), late_map(side)) for side in range(2)]
            + [extra, extra, by_shard, by_half, by_half]
            + [in_turn(j // 2) for j in range(2 * shards)],
            out_specs=[pl.BlockSpec(memory_space=ANY), by_half, by_half, by_half],
            scratch_shapes=[
                VECTOR((rows, 128), jnp.float32),
                VECTOR((shards * shard_rows + 2 * rows, 128), jnp.float32),
                VECTOR((2, shards * shard_rows // 9, 128), jnp.bfloat16),
                pltpu.SemaphoreType.DMA((2,)),
            ],
        ),
        out_shape=[jax.ShapeDtypeStruct((shards * shard_rows, 128), jnp.bfloat16)]
        + [jax.ShapeDtypeStruct((shard_rows, 128), jnp.float32)] * 3,
        compiler_params=pltpu.CompilerParams(vmem_limit_bytes=60 * 2**20),
        cost_estimate=BRIEF,
    )(
        meta,
        norm,
        *early,
        *late,
        *late,
        weights,
        first_moment.reshape(-1, 128),
        second_moment.reshape(-1, 128),
        *moments,
    )


def narrow_kernel(shard_rows, one_ref, two_ref, first_out, second_out):
    shape = first_out.shape
    begin = pl.program_id(0) * shape[0]
    inside = begin + lax.broadcasted_iota(jnp.int32, shape, 0) < shard_rows
    one = jnp.where(inside, one_ref[...] * (BETA_ONE / FIX_ONE), 0.0).astype(jnp.bfloat16)
    two = jnp.where(inside, two_ref[...] * (BETA_TWO / FIX_TWO), 0.0).astype(jnp.bfloat16)
    first_out[...] = one
    second_out[...] = two


def narrowed(one, two, half):
    block = pl.BlockSpec((half // 2, 128), lambda i: (i, 0))
    return pl.pallas_call(
        functools.partial(narrow_kernel, one.shape[0]),
        name="narrow",
        grid=(4,),
        in_specs=[block, block],
        out_specs=[block, block],
        out_shape=[jax.ShapeDtypeStruct((2 * half, 128), jnp.bfloat16)] * 2,
        cost_estimate=BRIEF,
    )(one, two)


def bit_of(bit):
    return (lax.axis_index(LINE) // bit) % 2


def on_device(inputs, weights, cotangent, clip_lengths, first_moment, second_moment):
    tok_rows = inputs.shape[0]
    reach = (MOST + tok_rows - 2) // tok_rows
    shard_rows = first_moment.shape[0] // 128
    half = halves_rows(shard_rows)
    (
        first_gain,
        first_bias,
        query_weight,
        query_bias,
        key_weight,
        value_weight,
        value_bias,
        out_weight,
        out_bias,
        second_gain,
        second_bias,
        up_weight,
        up_bias,
        down_weight,
        down_bias,
        padded_weights,
    ) = unpacked(weights, shard_rows)
    base_slot = lax.axis_index(LINE) * tok_rows
    positions = base_slot + jnp.arange(tok_rows, dtype=jnp.int32)
    lower_slot, upper_slot = bounds(positions, clip_lengths)
    low = lower_slot - base_slot + reach * tok_rows
    high = upper_slot - base_slot + reach * tok_rows
    first_block = low.reshape(2, -1)[:, 0] // tok_rows
    last_block = (high.reshape(2, -1)[:, -1] + tok_rows - 1) // tok_rows
    ranges = (first_block, last_block, slot_table(), tok_rows)
    places = base_slot + block_distances()[:, None] * tok_rows + jnp.arange(tok_rows, dtype=jnp.int32)[None]
    marks = clip_marks(places.reshape(-1), clip_lengths)
    closed = penalty(clip_marks(positions, clip_lengths))

    inner = lax.axis_size("inner")
    first_half, second_half = narrowed(first_moment.reshape(-1, 128), second_moment.reshape(-1, 128), half)
    blocks = halo(inputs, (padded_weights,))
    first_sent, second_sent, *blocks = lax.optimization_barrier((first_half, second_half, *blocks))
    rows = projected(
        blocks, query_weight, key_weight, value_weight, first_gain, first_bias, query_bias, value_bias
    )
    first_got = swapped(first_sent, 2)
    second_got = swapped(second_sent, 2)
    input_rows = inputs.astype(jnp.float32)
    first_hat, first_dev = standard(input_rows)
    normed = (first_hat * first_gain + first_bias).astype(jnp.bfloat16)

    attended, lse = attend(
        forward_kernel,
        ranges,
        [
            (rows, ("pair", 0)),
            (rows, ("pair", -5)),
            (rows, ("pair", -9)),
            (marks, ("all", 0)),
            (closed, ("all", 0)),
        ],
        [jnp.float32, jnp.float32],
        [pltpu.VMEM((2, 2 * reach + 1, tok_rows, tok_rows), jnp.float32)],
    )
    held = {0: (first_half, second_half), 2: (first_got, second_got)}
    bit = 4
    while bit < inner:
        for place in list(held):
            held[place + bit] = tuple(swapped(piece, bit) for piece in held[place])
        bit = 2 * bit
    moments = []
    for place in range(inner):
        if place % 2 == 0:
            moments += held[place]
        else:
            moments += [swapped(piece, 1) for piece in held[place - 1]]
    mixed = attended.astype(jnp.bfloat16)
    middle = input_rows + plain_dot(mixed, out_weight) + out_bias
    second_hat, second_dev = standard(middle)
    hidden_in = (second_hat * second_gain + second_bias).astype(jnp.bfloat16)
    up_rows = plain_dot(hidden_in, up_weight) + up_bias
    cdf_part = 0.5 * (1.0 + lax.erf(up_rows * INV_ROOT_TWO))
    activated = (up_rows * cdf_part).astype(jnp.bfloat16)
    layer_output = (middle + plain_dot(activated, down_weight) + down_bias).astype(jnp.bfloat16)
    grad_out = cotangent.astype(jnp.float32)
    down_bias_grad = jnp.sum(grad_out, axis=0)
    grad_act = back_dot(cotangent, down_weight)
    pdf_part = jnp.exp(-0.5 * up_rows * up_rows) * INV_ROOT_TWO_PI
    grad_up = (grad_act * (cdf_part + up_rows * pdf_part)).astype(jnp.bfloat16)
    up_bias_grad = jnp.sum(grad_up.astype(jnp.float32), axis=0)
    grad_hidden = back_dot(grad_up, up_weight)
    second_gain_grad = jnp.sum(grad_hidden * second_hat, axis=0)
    second_bias_grad = jnp.sum(grad_hidden, axis=0)
    grad_middle = grad_out + norm_back(grad_hidden, second_hat, second_dev, second_gain)
    grad_branch = grad_middle.astype(jnp.bfloat16)
    out_bias_grad = jnp.sum(grad_branch.astype(jnp.float32), axis=0)
    sent = mixed_grad(grad_branch, out_weight, attended, lse, clip_marks(positions, clip_lengths))
    line = lax.axis_size(LINE)
    shards = inner
    late_shards = shards // 4
    groups = bit_groups()

    def rounded(count, unit):
        return -(-count // unit) * unit

    def shard_spans(first, last, base):
        spans = ([], [])
        for shard in range(first, last):
            begin = (shard - first) * shard_rows + base
            spans[0].append((begin, half, half))
            spans[1].append((begin + half, shard_rows - half, half))
        return spans

    def query_step(pairs, after):
        return attend(
            query_kernel,
            ranges,
            [
                (rows, ("pair", 0)),
                (rows, ("pair", -5)),
                (rows, ("pair", -9)),
                (sent, ("pair", 0)),
                (sent, ("column", 4)),
                (marks, ("all", 0)),
                (closed, ("all", 0)),
            ],
            [jnp.bfloat16],
            [],
            pairs,
            after,
        )

    def key_step(pairs, after):
        return attend(
            key_kernel,
            ranges,
            [
                (rows, ("pair", 4)),
                (rows, ("pair", 8)),
                (rows, ("pair", -1)),
                (closed, ("all", 0)),
            ]
            + [(block, ("pair", 0)) for block in grad_blocks]
            + [(block, ("column", 4)) for block in grad_blocks],
            [jnp.bfloat16, jnp.bfloat16],
            [pltpu.VMEM((len(grad_blocks), tok_rows, 128), jnp.bfloat16)] * 2,
            pairs,
            after,
        )

    query_parts = query_step((0, 2), ())
    grad_blocks = halo(sent, query_parts)
    activated, hidden_in, mixed = (behind(array, query_parts) for array in (activated, hidden_in, mixed))

    early_rows = [
        (mixed, grad_branch),
        (out_bias_grad,),
        (second_gain_grad,),
        (second_bias_grad,),
        (hidden_in, grad_up),
        (up_bias_grad,),
        (activated, cotangent),
        (down_bias_grad,),
    ]
    early_half = rounded((shards - late_shards) * half, 8 * line)
    spans = shard_spans(late_shards, shards, 0)
    for span in spans:
        span.append((0, 0, early_half - (shards - late_shards) * half))
    early_keep, early_give = packed_halves(early_rows, D // 128, spans, early_half)
    early_got = swapped(early_give, 1)

    query_parts += query_step((2, 2), (early_give,))
    parts = combine([early_keep, early_got], groups[0], query_parts)
    got = exchanged(parts, groups[0])
    query_low = jnp.concatenate(query_parts, axis=1)
    work = [(1, 1), (2, 1), (3, 1)]
    done = key_step((0, 1), parts[:1])
    key_parts, value_parts = [done[0]], [done[1]]
    held_back = done[:1]
    for at, group in enumerate(groups):
        parts = combine(got, groups[at + 1] if at + 1 < len(groups) else [], held_back)
        if at + 1 < len(groups):
            got = exchanged(parts, groups[at + 1])
        if work:
            done = key_step(work.pop(0), parts[:1])
            key_parts.append(done[0])
            value_parts.append(done[1])
            held_back = done[:1]
    piece = parts[0]
    for at, group in enumerate(groups[::-1]):
        got = exchanged([piece], group)
        if work and at > 0:
            done = key_step(work.pop(0), [piece])
            key_parts.append(done[0])
            value_parts.append(done[1])
            held_back = done[:1]
        piece = stack(got, group, held_back)
    early_other = swapped(piece, 1)
    for pairs in work:
        done = key_step(pairs, [piece])
        key_parts.append(done[0])
        value_parts.append(done[1])
    early = (piece, early_other)
    key_low = jnp.concatenate(key_parts, axis=1)
    value_low = jnp.concatenate(value_parts, axis=1)
    query_bias_grad = jnp.sum(query_low.astype(jnp.float32), axis=0)
    value_bias_grad = jnp.sum(value_low.astype(jnp.float32), axis=0)
    grad_normed = (
        back_dot(query_low, query_weight)
        + back_dot(key_low, key_weight)
        + back_dot(value_low, value_weight)
    )
    first_gain_grad = jnp.sum(grad_normed * first_hat, axis=0)
    first_bias_grad = jnp.sum(grad_normed, axis=0)
    input_grad = (grad_middle + norm_back(grad_normed, first_hat, first_dev, first_gain)).astype(
        jnp.bfloat16
    )

    late_rows = [
        (first_gain_grad,),
        (first_bias_grad,),
        (normed, query_low),
        (query_bias_grad,),
        (normed, key_low),
        (normed, value_low),
        (value_bias_grad,),
    ]
    tail = max(1, 1 << (len(groups[0])))
    late_half = rounded(late_shards * half + 16, 16 * tail)
    spans = shard_spans(0, late_shards, 0)
    spare = late_half - late_shards * half
    spans[0].append((late_shards * shard_rows, D // 128, spare))
    spans[1].append((0, 0, spare))
    keep, give = packed_halves(late_rows, 0, spans, late_half)
    early_square = square_sum(early)
    parts = combine([keep, swapped(give, 1)], groups[0], ())
    (piece,) = combine(exchanged(parts, groups[0]), [], ())
    for group in groups[1:]:
        (piece,) = combine(exchanged([piece], group), [], (early_square,))
    piece = stack(exchanged([piece], groups[0]), groups[0], ())
    late = (piece, swapped(piece, 1))

    grad_norm = jnp.sqrt(early_square + square_sum(late))[0, 0]
    steps, grad_shard, moment_one, moment_two = updated(
        (1.0 / jnp.maximum(grad_norm, 1.0)).reshape(1),
        early,
        late,
        late_shards,
        padded_weights,
        first_moment,
        second_moment,
        moments,
    )
    weight_step = steps.reshape(-1)
    return (
        layer_output,
        input_grad,
        grad_shard.reshape(-1),
        grad_norm,
        moment_one.reshape(-1),
        moment_two.reshape(-1),
        weight_step,
    )


def solution(mesh):
    return jax.shard_map(
        on_device,
        mesh=mesh,
        in_specs=(
            P(("outer", "inner"), None),
            P(),
            P(("outer", "inner"), None),
            P(),
            P("inner"),
            P("inner"),
        ),
        out_specs=(
            P(("outer", "inner"), None),
            P(("outer", "inner"), None),
            P("inner"),
            P(),
            P("inner"),
            P("inner"),
            P(),
        ),
        check_vma=False,
    )
```

```python
import functools
import math

import jax
import jax.numpy as jnp
from jax import lax
from jax.experimental import pallas as pl
from jax.experimental.pallas import tpu as pltpu
from jax.sharding import PartitionSpec as P

D = 512
HEADS = 8
FF = 2048
MOST = 1500


BETA_ONE = 0.9
BETA_TWO = 0.999
FIX_ONE = 1.0 - (0.9**10) ** 10
FIX_TWO = 1.0 - (0.999**10) ** 10
DECAY = 0.1
INV_ROOT_TWO = 1.0 / math.sqrt(2.0)
INV_ROOT_TWO_PI = 1.0 / math.sqrt(2.0 * math.pi)


def layouts():
    return [
        (D,),
        (D,),
        (D, D),
        (D,),
        (D, D),
        (D, D),
        (D,),
        (D, D),
        (D,),
        (D,),
        (D,),
        (D, FF),
        (FF,),
        (FF, D),
        (D,),
    ]


def plain_dot(matrix_one, matrix_two):
    return jnp.dot(matrix_one, matrix_two, preferred_element_type=jnp.float32)


def rows_dot(matrix_one, matrix_two):
    return lax.dot_general(
        matrix_one, matrix_two, (((0,), (0,)), ((), ())), preferred_element_type=jnp.float32
    )


def back_dot(matrix_one, matrix_two):
    return lax.dot_general(
        matrix_one, matrix_two, (((1,), (1,)), ((), ())), preferred_element_type=jnp.float32
    )


def standard(values):
    center = jnp.mean(values, axis=-1, keepdims=True)
    centered = values - center
    inverse_dev = lax.rsqrt(jnp.mean(centered * centered, axis=-1, keepdims=True) + 1e-05)
    return (centered * inverse_dev, inverse_dev)


def norm_back(grad_normed, normed_hat, inverse_dev, gain):
    scaled = grad_normed * gain
    return inverse_dev * (
        scaled
        - jnp.mean(scaled, axis=-1, keepdims=True)
        - normed_hat * jnp.mean(scaled * normed_hat, axis=-1, keepdims=True)
    )


def bounds(positions, clip_lengths):
    starts = jnp.cumsum(clip_lengths, dtype=jnp.int32) - clip_lengths
    member = (
        jnp.sum((positions[:, None] >= starts[None, :]).astype(jnp.int32), axis=1, dtype=jnp.int32)
        - 1
    )
    onehot = (
        jnp.arange(clip_lengths.shape[0], dtype=jnp.int32)[None, :] == member[:, None]
    ).astype(jnp.int32)
    lower_slot = jnp.sum(onehot * starts[None, :], axis=1, dtype=jnp.int32)
    upper_slot = lower_slot + jnp.sum(onehot * clip_lengths[None, :], axis=1, dtype=jnp.int32)
    return (lower_slot, upper_slot)


LINE = ("outer", "inner")
NEG = -1e30
BRIEF = pl.CostEstimate(flops=1000, bytes_accessed=1000, transcendentals=0)


def shifted(block, distance):
    n = lax.axis_size(LINE)
    return lax.ppermute(block, LINE, [(i + distance, i) for i in range(n) if 0 <= i + distance < n])


def swapped(block, bit):
    n = lax.axis_size(LINE)
    return lax.ppermute(block, LINE, [(i ^ bit, i) for i in range(n)])


def halo(block, before=()):
    n = lax.axis_size(LINE)
    left = shifted(block, -2)
    right = shifted(block, 2)
    partner = swapped(block, 1)
    route = [(i + (3 if i % 2 else -3), i) for i in range(n)]
    far = lax.ppermute(block, LINE, [(s, t) for s, t in route if 0 <= s < n])
    passed_left, passed_right, *_ = lax.optimization_barrier((left, right, *before))
    turned = [swapped(passed_left, 1), swapped(passed_right, 1)]
    return [block, partner, left, right, *turned, far]


def block_distances():
    odd = lax.axis_index(LINE) % 2
    even_far = jnp.array([0, 1, -2, 2, -1, 3, -3], jnp.int32)
    odd_far = jnp.array([0, -1, -2, 2, -3, 1, 3], jnp.int32)
    return jnp.where(odd == 1, odd_far, even_far)


def slot_table():
    odd = lax.axis_index(LINE) % 2
    even_slots = jnp.array([6, 2, 4, 0, 1, 3, 5], jnp.int32)
    odd_slots = jnp.array([4, 2, 1, 0, 5, 3, 6], jnp.int32)
    return jnp.where(odd == 1, odd_slots, even_slots)


def dot_nt(a, b):
    return lax.dot_general(a, b, (((1,), (1,)), ((), ())), preferred_element_type=jnp.float32)


def head_halves(pair):
    first = lax.broadcasted_iota(jnp.int32, pair.shape, 1) < pair.shape[1] // 2
    zero = jnp.zeros_like(pair)
    return jnp.where(first, pair, zero), jnp.where(first, zero, pair)


def over_lanes(tile, op):
    parts = [tile[:, 128 * j : 128 * (j + 1)] for j in range(tile.shape[1] // 128)]
    while len(parts) > 1:
        rest = parts[len(parts) // 2 * 2 :]
        parts = [op(parts[2 * j], parts[2 * j + 1]) for j in range(len(parts) // 2)] + rest
    return parts[0]


LSE_PARTS, DELTA_PARTS = 3, 2
DELTA_AT = LSE_PARTS * HEADS
CLIPS_AT = DELTA_AT + DELTA_PARTS * HEADS


def lane_of(shape):
    return lax.broadcasted_iota(jnp.int32, shape, 1)


def among(lane, begin, count):
    return (lane >= begin) & (lane < begin + count)


def beside(pair, marks):
    return jnp.concatenate([pair, marks.astype(pair.dtype)], axis=1)


def clip_marks(positions, clip_lengths):
    ends = jnp.cumsum(clip_lengths, dtype=jnp.int32)
    starts = ends - clip_lengths
    spare = 128 - CLIPS_AT - clip_lengths.shape[0]
    assert spare >= 0
    big = jnp.iinfo(jnp.int32).max
    lower = jnp.concatenate([jnp.full((CLIPS_AT,), -big, jnp.int32), starts, jnp.full((spare,), big, jnp.int32)])
    upper = jnp.concatenate([jnp.full((CLIPS_AT,), big, jnp.int32), ends, jnp.full((spare,), big, jnp.int32)])
    inside = (positions[:, None] >= lower[None]) & (positions[:, None] < upper[None])
    return inside.astype(jnp.bfloat16)


def penalty(marks):
    closed = (lane_of(marks.shape) >= CLIPS_AT) & (marks == 0)
    return jnp.where(closed, NEG, 0.0).astype(jnp.bfloat16)


def over_blocks(first_ref, last_ref, rows, work, start):
    half = rows // 2
    carried = (start, start)
    spans = (
        (first_ref[0], first_ref[1], 0, half),
        (first_ref[1], last_ref[0], 0, rows),
        (last_ref[0], last_ref[1], half, half),
    )
    for lower, upper, begin, count in spans:

        def step(block, carried):
            found = work(block, begin, count)
            upper_half, lower_half = carried
            if begin == 0:
                upper_half = tuple(join(old, new[:half]) for (join, new), old in zip(found, upper_half))
            if begin + count == rows:
                lower_half = tuple(join(old, new[count - half :]) for (join, new), old in zip(found, lower_half))
            return upper_half, lower_half

        carried = lax.fori_loop(lower, upper, step, carried)
    return [jnp.concatenate(halves, axis=0) for halves in zip(*carried)]


def forward_kernel(begin, first_ref, last_ref, slot_ref, q_ref, k_ref, v_ref, mark_ref, closed_ref, o_ref, lse_ref, s_ref):
    width = q_ref.shape[0]
    queries = [beside(half, closed_ref[...]) for half in head_halves(q_ref[...] * jnp.bfloat16(0.125))]

    def scores(block, begin, count):
        at = pl.ds(pl.multiple_of(slot_ref[block] * width, width), width)
        keys = beside(k_ref[at, :], mark_ref[at, :])
        found = []
        for h in range(2):
            score = dot_nt(queries[h][begin : begin + count], keys)
            s_ref[h, block, pl.ds(begin, count), :] = score
            found.append((jnp.maximum, over_lanes(score, jnp.maximum)))
        return found

    start = jnp.full((width // 2, 128), NEG, jnp.float32)
    peaks = over_blocks(first_ref, last_ref, width, scores, (start, start))
    peaks = [jnp.max(peak, axis=1, keepdims=True) for peak in peaks]

    def mix(block, begin, count):
        at = pl.ds(pl.multiple_of(slot_ref[block] * width, width), width)
        values = beside(v_ref[at, :], mark_ref[at, :])
        found = []
        for h in range(2):
            score = s_ref[h, block, pl.ds(begin, count), :]
            soft = jnp.exp(score - peaks[h][begin : begin + count]).astype(jnp.bfloat16)
            found.append((jnp.add, jnp.dot(soft, values, preferred_element_type=jnp.float32)))
        return found

    start = jnp.zeros((width // 2, 256), jnp.float32)
    sums = over_blocks(first_ref, last_ref, width, mix, (start, start))
    totals = [part[:, 128:129] for part in sums]
    even = lane_of((width, 128)) < 64
    o_ref[...] = jnp.where(even, sums[0][:, :128] / totals[0], sums[1][:, :128] / totals[1])
    lse_ref[...] = jnp.where(even, peaks[0] + jnp.log(totals[0]), peaks[1] + jnp.log(totals[1]))


def query_kernel(
    begin, first_ref, last_ref, slot_ref, q_ref, k_ref, v_ref, g_ref, own_ref, mark_ref, closed_ref, dq_ref
):
    width = q_ref.shape[0]
    pair = pl.program_id(0) + begin
    own, closed = own_ref[...], closed_ref[...]
    lane = lane_of(own.shape)
    zero = jnp.zeros_like(own)
    queries, grads = [], []
    halves = zip(head_halves(q_ref[...] * jnp.bfloat16(0.125)), head_halves(g_ref[...]))
    for h, (query, grad) in enumerate(halves):
        head = 2 * pair + h
        queries.append(beside(query, jnp.where(among(lane, LSE_PARTS * head, LSE_PARTS), own, closed)))
        grads.append(beside(grad, jnp.where(among(lane, DELTA_AT + DELTA_PARTS * head, DELTA_PARTS), own, zero)))

    def work(block, begin, count):
        at = pl.ds(pl.multiple_of(slot_ref[block] * width, width), width)
        keys = k_ref[at, :]
        values = beside(v_ref[at, :], mark_ref[at, :])
        marked = beside(keys, mark_ref[at, :])
        found = []
        for h in range(2):
            soft = jnp.exp(dot_nt(queries[h][begin : begin + count], marked))
            grad = (soft * dot_nt(grads[h][begin : begin + count], values)).astype(jnp.bfloat16)
            found.append((jnp.add, jnp.dot(grad, keys, preferred_element_type=jnp.float32)))
        return found

    start = jnp.zeros((width // 2, 128), jnp.float32)
    sums = over_blocks(first_ref, last_ref, width, work, (start, start))
    dq_ref[...] = (jnp.where(lane < 64, sums[0], sums[1]) * 0.125).astype(jnp.bfloat16)


def key_kernel(begin, first_ref, last_ref, slot_ref, k_ref, v_ref, q_ref, closed_ref, *refs):
    dk_ref, dv_ref, grad_ref, mark_ref = refs[-4:]
    width = k_ref.shape[0]
    pair = pl.program_id(0) + begin
    blocks = grad_ref.shape[0]
    for j in range(blocks):
        grad_ref[j] = refs[j][...]

    @pl.when(pl.program_id(0) == 0)
    def _():
        for j in range(blocks):
            mark_ref[j] = refs[blocks + j][...]

    closed = closed_ref[...]
    lane = lane_of(closed.shape)
    one, zero = jnp.ones_like(closed), jnp.zeros_like(closed)
    keys, values = [], []
    halves = zip(head_halves(k_ref[...] * jnp.bfloat16(0.125)), head_halves(v_ref[...]))
    for h, (key, value) in enumerate(halves):
        head = 2 * pair + h
        keys.append(beside(key, jnp.where(among(lane, LSE_PARTS * head, LSE_PARTS), one, closed)))
        values.append(beside(value, jnp.where(among(lane, DELTA_AT + DELTA_PARTS * head, DELTA_PARTS), one, zero)))

    def work(block, begin, count):
        slot = slot_ref[block]
        queries = q_ref[pl.ds(pl.multiple_of(slot * width, width), width), :]
        grads, marks = grad_ref[slot], mark_ref[slot]
        marked, graded = beside(queries, marks), beside(grads, marks)
        found = []
        for h in range(2):
            soft = jnp.exp(dot_nt(keys[h][begin : begin + count], marked))
            grad = (soft * dot_nt(values[h][begin : begin + count], graded)).astype(jnp.bfloat16)
            found.append((jnp.add, jnp.dot(grad, queries, preferred_element_type=jnp.float32)))
            found.append((jnp.add, jnp.dot(soft.astype(jnp.bfloat16), grads, preferred_element_type=jnp.float32)))
        return found

    start = jnp.zeros((width // 2, 128), jnp.float32)
    sums = over_blocks(first_ref, last_ref, width, work, (start,) * 4)
    dk_ref[...] = (jnp.where(lane < 64, sums[0], sums[2]) * 0.125).astype(jnp.bfloat16)
    dv_ref[...] = jnp.where(lane < 64, sums[1], sums[3]).astype(jnp.bfloat16)


def mixed_grad_kernel(branch_ref, weight_ref, mixed_ref, lse_ref, own_ref, sent_ref, mark_ref):
    step = pl.program_id(0)

    @pl.when(step == 0)
    def _():
        mark_ref[...] = own_ref[...].astype(jnp.float32)

    @pl.when(step < D // 128)
    def _():
        grad = dot_nt(branch_ref[...], weight_ref[...]).astype(jnp.bfloat16)
        sent_ref[...] = grad
        product = grad.astype(jnp.float32) * mixed_ref[...]
        lane = lane_of(product.shape)
        marks = mark_ref[...]
        for h, part in enumerate(head_halves(product)):
            head = 2 * step + h
            delta = -jnp.sum(part, axis=1, keepdims=True)
            lse = -lse_ref[:, 64 * h : 64 * h + 1]
            for value, begin, count in (
                (lse, LSE_PARTS * head, LSE_PARTS),
                (delta, DELTA_AT + DELTA_PARTS * head, DELTA_PARTS),
            ):
                for k in range(count):
                    rounded = value.astype(jnp.bfloat16).astype(jnp.float32)
                    marks = jnp.where(lane == begin + k, rounded, marks)
                    value = value - rounded
        mark_ref[...] = marks

    @pl.when(step == D // 128)
    def _():
        sent_ref[...] = mark_ref[...].astype(jnp.bfloat16)


def mixed_grad(branch, out_weight, mixed, lse, own_marks):
    width = branch.shape[0]
    last = D // 128 - 1
    column = pl.BlockSpec((width, 128), lambda h: (0, jnp.minimum(h, last)))
    return pl.pallas_call(
        mixed_grad_kernel,
        name="mixed_grad",
        grid=(D // 128 + 1,),
        in_specs=[
            pl.BlockSpec((width, D), lambda h: (0, 0)),
            pl.BlockSpec((128, D), lambda h: (jnp.minimum(h, last), 0)),
            column,
            column,
            pl.BlockSpec((width, 128), lambda h: (0, 0)),
        ],
        out_specs=pl.BlockSpec((width, 128), lambda h: (0, h)),
        out_shape=jax.ShapeDtypeStruct((width, D + 128), jnp.bfloat16),
        scratch_shapes=[pltpu.VMEM((width, 128), jnp.float32)],
        cost_estimate=BRIEF,
    )(branch, out_weight, mixed, lse, own_marks)


def project_kernel(count, *refs):
    query_ref, key_ref, value_ref, gain_ref, bias_ref, query_bias_ref, value_bias_ref, out_ref, row_ref = refs[count:]
    step = pl.program_id(0)
    for j in range(count):

        @pl.when(step == j)
        def _():
            row_ref[...] = refs[j][...]

    rows = 256
    for i in range(row_ref.shape[0] // rows):
        at = pl.ds(i * rows, rows)
        hat, _ = standard(row_ref[at, :].astype(jnp.float32))
        normed = (hat * gain_ref[...] + bias_ref[...]).astype(jnp.bfloat16)
        out_ref[at, 0:D] = (plain_dot(normed, query_ref[...]) + query_bias_ref[...]).astype(jnp.bfloat16)
        out_ref[at, D : 2 * D] = plain_dot(normed, key_ref[...]).astype(jnp.bfloat16)
        out_ref[at, 2 * D :] = (plain_dot(normed, value_ref[...]) + value_bias_ref[...]).astype(jnp.bfloat16)


def projected(blocks, *weights):
    width = blocks[0].shape[0]
    whole = [pl.BlockSpec(array.shape, lambda i: (0, 0)) for array in (*blocks, *weights)]
    return pl.pallas_call(
        functools.partial(project_kernel, len(blocks)),
        name="project",
        grid=(len(blocks),),
        in_specs=whole,
        out_specs=pl.BlockSpec((width, 3 * D), lambda i: (i, 0)),
        out_shape=jax.ShapeDtypeStruct((len(blocks) * width, 3 * D), jnp.bfloat16),
        scratch_shapes=[pltpu.VMEM((width, D), jnp.bfloat16)],
        compiler_params=pltpu.CompilerParams(vmem_limit_bytes=63 * 2**20),
        cost_estimate=BRIEF,
    )(*blocks, *weights)


def attend(kernel, ranges, operands, results, scratch, pairs=(0, D // 128), after=()):
    begin, count = pairs
    tok_rows = ranges[3]
    specs = []
    for array, (kind, at) in operands:
        if kind == "pair":
            rows = array.shape[0] if at < 0 else tok_rows
            at = (abs(at) - 1 if at < 0 else at) + begin
            specs.append(pl.BlockSpec((rows, 128), lambda h, *_, at=at: (0, at + h)))
        elif kind == "column":
            specs.append(pl.BlockSpec((tok_rows, 128), lambda h, *_, at=at: (0, at)))
        else:
            specs.append(pl.BlockSpec(array.shape, lambda h, *_, n=array.ndim: (0,) * n))
    return pl.pallas_call(
        functools.partial(kernel, begin),
        grid_spec=pltpu.PrefetchScalarGridSpec(
            num_scalar_prefetch=3,
            grid=(count,),
            in_specs=specs,
            out_specs=[pl.BlockSpec((tok_rows, 128), lambda h, *_: (0, h))] * len(results),
            scratch_shapes=scratch,
        ),
        out_shape=[jax.ShapeDtypeStruct((tok_rows, 128 * count), kept) for kept in results],
        compiler_params=pltpu.CompilerParams(vmem_limit_bytes=48 * 2**20),
        cost_estimate=BRIEF,
    )(*[behind(bound, after) for bound in ranges[:1]], *ranges[1:3], *[array for array, _ in operands])


VECTOR = pltpu.VMEM
ANY = pl.ANY


def behind(value, others):
    return lax.optimization_barrier((value, *others))[0]


def halves_rows(shard_rows):
    return -(-shard_rows // 128) * 64


def unpack_kernel(plan, shard_rows, flat_ref, *refs):
    wide_ref = refs[-1]
    padded_ref = refs[-2]
    total = flat_ref.shape[0]
    chunk = 432

    def widen(i, _):
        rows = pl.ds(pl.multiple_of(i * chunk, 16), chunk)
        wide_ref[rows, :] = flat_ref[rows, :].astype(jnp.float32)
        return 0

    lax.fori_loop(0, total // chunk, widen, 0)
    wide_ref[pl.ds(total, wide_ref.shape[0] - total), :] = jnp.zeros((wide_ref.shape[0] - total, 128), jnp.float32)
    for (offset, rows, columns, begin), ref in zip(plan, refs[:-2]):
        pieces = columns // 128
        if rows == 1:
            for j in range(pieces):
                ref[:, 128 * j : 128 * (j + 1)] = wide_ref[pl.ds(offset + j, 1), :]
            continue

        taken = 1024 // pieces

        def matrix(i, _):
            at = pl.multiple_of(i * taken, 64)
            for j in range(pieces):
                part = wide_ref[pl.ds(offset + j + at * pieces, taken, stride=pieces), :]
                ref[pl.ds(at, taken), begin + 128 * j : begin + 128 * (j + 1)] = part.astype(jnp.bfloat16)
            return 0

        lax.fori_loop(0, rows // taken, matrix, 0)
    shards = total // shard_rows
    half = halves_rows(shard_rows)
    for s in range(shards):
        for h in range(2):

            run = 448 if half % 448 == 0 else 64

            def pad(i, _):
                part = wide_ref[pl.ds(s * shard_rows + h * half + i * run, run), :]
                padded_ref[s * 2 + h, pl.ds(pl.multiple_of(i * run, 64), run), :] = part.astype(jnp.bfloat16)
                return 0

            lax.fori_loop(0, half // run, pad, 0)


def unpacked(weights, shard_rows):
    flat = weights.reshape(-1, 128)
    half = halves_rows(shard_rows)
    plan, outs = [], []
    offset = 0
    for layout in layouts():
        rows, columns = layout if len(layout) == 2 else (1, layout[0])
        plan.append([offset, rows, columns, 0])
        outs.append(jax.ShapeDtypeStruct((rows, columns), jnp.bfloat16 if rows > 1 else jnp.float32))
        offset = offset + rows * columns // 128
    shards = flat.shape[0] // shard_rows
    outs.append(jax.ShapeDtypeStruct((2 * shards, half, 128), jnp.bfloat16))
    return pl.pallas_call(
        functools.partial(unpack_kernel, plan, shard_rows),
        name="unpack",
        in_specs=[pl.BlockSpec(memory_space=VECTOR)],
        out_specs=[pl.BlockSpec(memory_space=VECTOR)] * len(outs),
        out_shape=outs,
        scratch_shapes=[VECTOR((flat.shape[0] + 2 * half, 128), jnp.float32)],
        compiler_params=pltpu.CompilerParams(vmem_limit_bytes=60 * 2**20),
        cost_estimate=BRIEF,
    )(flat)


def pack_kernel(plan, spans, place_ref, *refs):
    keep_ref, give_ref, flat_ref, out_ref, sems = refs[-5:]
    begin = min(entry[0] for entry in plan)
    if begin:
        flat_ref[pl.ds(0, begin), :] = jnp.zeros((begin, 128), jnp.float32)
    given = iter(refs)
    for offset, rows, columns, factors in plan:
        pieces = columns // 128
        ref = next(given)
        if rows == 1:
            for j in range(pieces):
                flat_ref[pl.ds(offset + j, 1), :] = ref[:, 128 * j : 128 * (j + 1)]
            continue

        others = [next(given) for _ in range(factors - 1)]
        other = others[0][...] if len(others) == 1 else jnp.concatenate([part[...] for part in others], axis=1)
        taken = 256

        def product(i, _):
            at = pl.multiple_of(i * taken, 128)
            found = rows_dot(ref[:, pl.ds(at, taken)], other)
            for j in range(pieces):
                part = found[:, 128 * j : 128 * (j + 1)]
                flat_ref[pl.ds(offset + j + at * pieces, taken, stride=pieces), :] = part
            return 0

        lax.fori_loop(0, rows // taken, product, 0)
    for h in range(2):
        at = h ^ place_ref[0]
        filled = 0
        for source, rows, room in spans[h]:
            run = 448 if rows >= 448 else 64
            whole = rows // run

            def move(i, _):
                to = pl.ds(pl.multiple_of(filled + i * run, 16), run)
                out_ref[at, to, :] = flat_ref[pl.ds(source + i * run, run), :].astype(jnp.bfloat16)
                return 0

            lax.fori_loop(0, whole, move, 0)
            rest = rows - run * whole
            tail = room - run * whole
            if tail:
                parts = []
                if rest:
                    parts.append(flat_ref[pl.ds(source + run * whole, rest), :])
                if tail > rest:
                    parts.append(jnp.zeros((tail - rest, 128), jnp.float32))
                last = parts[0] if len(parts) == 1 else jnp.concatenate(parts, axis=0)
                out_ref[at, pl.ds(filled + run * whole, tail), :] = last.astype(jnp.bfloat16)
            filled = filled + room
    copies = [
        pltpu.make_async_copy(out_ref.at[0], keep_ref, sems.at[0]),
        pltpu.make_async_copy(out_ref.at[1], give_ref, sems.at[1]),
    ]
    for copy in copies:
        copy.start()
    for copy in copies:
        copy.wait()


def packed_halves(grads, begin, spans, half):
    plan, arrays = [], []
    offset = begin
    for grad in grads:
        rows, columns = 1, grad[0].size
        if len(grad) > 1:
            rows, columns = grad[0].shape[1], sum(part.shape[1] for part in grad[1:])
        plan.append((offset, rows, columns, len(grad)))
        arrays += [array.reshape(-1, array.shape[-1]) for array in grad]
        offset = offset + rows * columns // 128
    return pl.pallas_call(
        functools.partial(pack_kernel, plan, spans),
        name="pack",
        in_specs=[pl.BlockSpec(memory_space=pltpu.SMEM)] + [pl.BlockSpec(memory_space=VECTOR)] * len(arrays),
        out_specs=[pl.BlockSpec(memory_space=ANY)] * 2,
        out_shape=[jax.ShapeDtypeStruct((half, 128), jnp.bfloat16)] * 2,
        scratch_shapes=[
            VECTOR((offset, 128), jnp.float32),
            VECTOR((2, half, 128), jnp.bfloat16),
            pltpu.SemaphoreType.DMA((2,)),
        ],
        compiler_params=pltpu.CompilerParams(vmem_limit_bytes=60 * 2**20),
        cost_estimate=BRIEF,
    )(bit_of(1).reshape(1), *arrays)


def combine_kernel(count, places_ref, *refs):
    parts, outs = refs[:count], refs[-places_ref.shape[0] :]
    rows = outs[0].shape[0]
    for k, out in enumerate(outs):
        at = pl.ds(pl.multiple_of(places_ref[k] * rows, 16), rows)
        terms = [part[at, :].astype(jnp.float32) for part in parts]
        while len(terms) > 1:
            terms = [terms[2 * j] + terms[2 * j + 1] for j in range(len(terms) // 2)]
        out[...] = terms[0].astype(jnp.bfloat16)


def places_of(group):
    if not group:
        return jnp.zeros((1,), jnp.int32)
    place = (lax.axis_index(LINE) // group[0]) % (1 << len(group))
    return place ^ jnp.arange(1 << len(group), dtype=jnp.int32)


def combine(parts, group, after):
    count = 1 << len(group)
    rows = parts[0].shape[0] // count
    outs = pl.pallas_call(
        functools.partial(combine_kernel, len(parts)),
        name="combine",
        in_specs=[pl.BlockSpec(memory_space=pltpu.SMEM)]
        + [pl.BlockSpec(memory_space=VECTOR)] * len(parts),
        out_specs=[pl.BlockSpec(memory_space=VECTOR)] * count,
        out_shape=[jax.ShapeDtypeStruct((rows, 128), jnp.bfloat16)] * count,
        cost_estimate=BRIEF,
    )(behind(places_of(group), after), *parts)
    return list(outs)


def stack_kernel(count, places_ref, *refs):
    out_ref = refs[-1]
    rows = refs[0].shape[0]
    for k in range(count):
        out_ref[pl.ds(pl.multiple_of(places_ref[k] * rows, 16), rows), :] = refs[k][...]


def stack(parts, group, after):
    rows = parts[0].shape[0] * len(parts)
    return pl.pallas_call(
        functools.partial(stack_kernel, len(parts)),
        name="stack",
        in_specs=[pl.BlockSpec(memory_space=pltpu.SMEM)]
        + [pl.BlockSpec(memory_space=VECTOR)] * len(parts),
        out_specs=pl.BlockSpec(memory_space=VECTOR),
        out_shape=jax.ShapeDtypeStruct((rows, 128), jnp.bfloat16),
        cost_estimate=BRIEF,
    )(behind(places_of(group), after), *parts)


def exchanged(parts, group):
    return [parts[0]] + [swapped(parts[k % len(parts)], group[0] * k) for k in range(1, 1 << len(group))]


def bit_groups():
    bits = [1 << k for k in range(1, lax.axis_size(LINE).bit_length() - 1)]
    return [bits[k : k + 2] for k in range(0, len(bits), 2)]


def square_sum_kernel(ref, out_ref):
    rows = ref.shape[0]
    chunk = rows // 8 if rows % 256 == 0 else 32

    def add(i, total):
        part = ref[pl.ds(pl.multiple_of(i * chunk, 16), chunk), :].astype(jnp.float32)
        return total + jnp.sum((part * part).reshape(-1, 32, 128), axis=0)

    total = lax.fori_loop(0, rows // chunk, add, jnp.zeros((32, 128), jnp.float32))
    out_ref[...] = jnp.broadcast_to(jnp.sum(total, keepdims=True), (8, 128))


def square_sum(half):
    own = pl.pallas_call(
        square_sum_kernel,
        name="square_sum",
        in_specs=[pl.BlockSpec(memory_space=VECTOR)],
        out_specs=pl.BlockSpec(memory_space=VECTOR),
        out_shape=jax.ShapeDtypeStruct((8, 128), jnp.float32),
        cost_estimate=BRIEF,
    )(half)
    return own + swapped(own, 1)


def finish_kernel(counts, x_ref, middle_ref, gain_ref, *refs):
    weights, parts, outs = refs[:3], refs[3:-5], refs[-5:]
    grad_ref, gain_out, bias_out, query_out, value_out = outs
    for out in outs[1:]:
        out[...] = jnp.zeros_like(out)
    rows = 256
    for i in range(x_ref.shape[0] // rows):
        at = pl.ds(i * rows, rows)
        hat, dev = standard(x_ref[at, :].astype(jnp.float32))
        grads, begin = [], 0
        for count in counts:
            grads.append(jnp.concatenate([part[at, :] for part in parts[begin : begin + count]], axis=1))
            begin = begin + count
        normed = sum(dot_nt(grad, weight[...]) for grad, weight in zip(grads, weights))
        for out, value in (
            (gain_out, normed * hat),
            (bias_out, normed),
            (query_out, grads[0].astype(jnp.float32)),
            (value_out, grads[2].astype(jnp.float32)),
        ):
            out[...] = out[...] + jnp.sum(value, axis=0, keepdims=True)
        grad_ref[at, :] = (middle_ref[at, :] + norm_back(normed, hat, dev, gain_ref[...])).astype(jnp.bfloat16)


def finished(inputs, grad_middle, gain, weights, parts):
    arrays = [inputs, grad_middle, gain, *weights, *(part for group in parts for part in group)]
    return pl.pallas_call(
        functools.partial(finish_kernel, [len(group) for group in parts]),
        name="finish",
        in_specs=[pl.BlockSpec(memory_space=VECTOR)] * len(arrays),
        out_specs=[pl.BlockSpec(memory_space=VECTOR)] * 5,
        out_shape=[jax.ShapeDtypeStruct(inputs.shape, jnp.bfloat16)] + [jax.ShapeDtypeStruct((1, D), jnp.float32)] * 4,
        compiler_params=pltpu.CompilerParams(vmem_limit_bytes=60 * 2**20),
        cost_estimate=BRIEF,
    )(*arrays)


def update_kernel(
    shards, late, shard_rows, meta_ref, scale_ref, early_own, early_other, late_own, late_other, extra_own, extra_other,
    weight_ref, one_ref, two_ref, *refs
):
    moments = refs[: 2 * shards]
    step_ref, grad_ref, new_one_ref, new_two_ref, sum_ref, wide_ref, stage_ref, sems = refs[2 * shards :]
    which, k = pl.program_id(0), pl.program_id(1)
    core, me = meta_ref[0], meta_ref[1]
    shard = me ^ k
    half = core ^ which
    rows = sum_ref.shape[0]
    chunk = rows // 7 if rows % 112 == 0 else 64
    scale = scale_ref[0]

    def by_chunks(body, first=0, last=rows // chunk):
        def move(i, _):
            body(pl.multiple_of(i * chunk, 16))
            return 0

        lax.fori_loop(first, last, move, 0)

    def load(ref):
        def body(at):
            sum_ref[pl.ds(at, chunk), :] = ref[pl.ds(at, chunk), :].astype(jnp.float32)

        by_chunks(body)

    for array, side, is_late in ((early_own, 0, 0), (early_other, 1, 0), (late_own, 0, 1), (late_other, 1, 1)):
        pl.when((which == side) & ((shard < late) == (is_late == 1)))(functools.partial(load, array))
    for array, side in ((extra_own, 0), (extra_other, 1)):

        @pl.when((which == side) & (shard == late) & (half == 0))
        def _():
            sum_ref[pl.ds(0, 8), :] = sum_ref[pl.ds(0, 8), :] + array[pl.ds(0, 8), :].astype(jnp.float32)

    slope_one = (1.0 - BETA_ONE) * scale
    slope_two = (1.0 - BETA_TWO) * scale * scale

    base = shard * shard_rows + half * rows
    limit = jnp.where(half == 1, shard_rows - rows, rows)
    for j in range(shards):

        @pl.when(k == j)
        def _():
            def body(start, masked=False):
                at = pl.ds(start, chunk)
                one, two = moments[2 * j][at, :], moments[2 * j + 1][at, :]
                grad = sum_ref[at, :]
                one = one.astype(jnp.float32) + (slope_one * (1.0 / FIX_ONE)) * grad
                two = two.astype(jnp.float32) + (slope_two * (1.0 / FIX_TWO)) * grad * grad
                root = two * lax.rsqrt(jnp.maximum(two, 1e-37))
                update = one / (root + 1e-08) + DECAY * weight_ref[0, at, :].astype(jnp.float32)
                to = pl.ds(base + start, chunk)
                if masked:
                    inside = start + lax.broadcasted_iota(jnp.int32, update.shape, 0) < limit
                    update = jnp.where(inside, update, wide_ref[to, :])
                wide_ref[to, :] = update

            whole = (shard_rows - rows) // chunk
            by_chunks(body, 0, whole)
            by_chunks(functools.partial(body, masked=True), whole, rows // chunk)

    @pl.when(k == 0)
    def _():
        def body(start):
            at = pl.ds(start, chunk)
            grad = sum_ref[at, :]
            grad_ref[at, :] = grad
            new_one_ref[at, :] = BETA_ONE * one_ref[at, :] + slope_one * grad
            new_two_ref[at, :] = BETA_TWO * two_ref[at, :] + slope_two * grad * grad

        by_chunks(body)

    @pl.when((which == 1) & (k == shards - 1))
    def _():
        piece = stage_ref.shape[1]
        total = step_ref.shape[0]

        def sending(i, slot):
            return pltpu.make_async_copy(
                stage_ref.at[slot], step_ref.at[pl.ds(pl.multiple_of(i * piece, 16), piece), :], sems.at[slot]
            )

        count = total // piece
        for i in range(count):
            if i >= 2:
                sending(i - 2, i % 2).wait()
            stage_ref[i % 2] = wide_ref[pl.ds(i * piece, piece), :].astype(jnp.bfloat16)
            sending(i, i % 2).start()
        for i in range(count - 2, count):
            sending(i, i % 2).wait()


def updated(norm, early, late, late_shards, weights, first_moment, second_moment, moments):
    shards = len(moments) // 2
    rows = weights.shape[1]
    shard_rows = first_moment.shape[0] // 128
    line = lax.axis_index(LINE)
    meta = jnp.stack([line % 2, lax.axis_index("inner")]).astype(jnp.int32)
    last = shards - 1

    def early_map(side):
        def index(w, k, meta):
            k = jnp.where(w == side, k, last if side == 0 else 0)
            return (jnp.clip((meta[1] ^ k) - late_shards, 0, shards - late_shards - 1), 0)

        return index

    def late_map(side):
        def index(w, k, meta):
            k = jnp.where(w == side, k, last if side == 0 else 0)
            return (jnp.clip(meta[1] ^ k, 0, late_shards - 1), 0)

        return index

    by_half = pl.BlockSpec((rows, 128), lambda w, k, meta: (meta[0] ^ w, 0))

    def in_turn(j):
        return pl.BlockSpec((rows, 128), lambda w, k, meta: (meta[0] ^ jnp.where(k >= j - 1, w, 0), 0))

    by_shard = pl.BlockSpec((1, rows, 128), lambda w, k, meta: (2 * (meta[1] ^ k) + (meta[0] ^ w), 0, 0))
    extra = pl.BlockSpec((16, 128), lambda w, k, meta: (late_shards * rows // 16, 0))
    return pl.pallas_call(
        functools.partial(update_kernel, shards, late_shards, shard_rows),
        name="update",
        grid_spec=pltpu.PrefetchScalarGridSpec(
            num_scalar_prefetch=1,
            grid=(2, shards),
            in_specs=[pl.BlockSpec(memory_space=pltpu.SMEM)]
            + [pl.BlockSpec((rows, 128), early_map(side)) for side in range(2)]
            + [pl.BlockSpec((rows, 128), late_map(side)) for side in range(2)]
            + [extra, extra, by_shard, by_half, by_half]
            + [in_turn(j // 2) for j in range(2 * shards)],
            out_specs=[pl.BlockSpec(memory_space=ANY), by_half, by_half, by_half],
            scratch_shapes=[
                VECTOR((rows, 128), jnp.float32),
                VECTOR((shards * shard_rows + 2 * rows, 128), jnp.float32),
                VECTOR((2, shards * shard_rows // 9, 128), jnp.bfloat16),
                pltpu.SemaphoreType.DMA((2,)),
            ],
        ),
        out_shape=[jax.ShapeDtypeStruct((shards * shard_rows, 128), jnp.bfloat16)]
        + [jax.ShapeDtypeStruct((shard_rows, 128), jnp.float32)] * 3,
        compiler_params=pltpu.CompilerParams(vmem_limit_bytes=60 * 2**20),
        cost_estimate=BRIEF,
    )(
        meta,
        norm,
        *early,
        *late,
        *late,
        weights,
        first_moment.reshape(-1, 128),
        second_moment.reshape(-1, 128),
        *moments,
    )


def narrow_kernel(shard_rows, one_ref, two_ref, first_out, second_out):
    shape = first_out.shape
    begin = pl.program_id(0) * shape[0]
    inside = begin + lax.broadcasted_iota(jnp.int32, shape, 0) < shard_rows
    one = jnp.where(inside, one_ref[...] * (BETA_ONE / FIX_ONE), 0.0).astype(jnp.bfloat16)
    two = jnp.where(inside, two_ref[...] * (BETA_TWO / FIX_TWO), 0.0).astype(jnp.bfloat16)
    first_out[...] = one
    second_out[...] = two


def narrowed(one, two, half):
    block = pl.BlockSpec((half // 2, 128), lambda i: (i, 0))
    return pl.pallas_call(
        functools.partial(narrow_kernel, one.shape[0]),
        name="narrow",
        grid=(4,),
        in_specs=[block, block],
        out_specs=[block, block],
        out_shape=[jax.ShapeDtypeStruct((2 * half, 128), jnp.bfloat16)] * 2,
        cost_estimate=BRIEF,
    )(one, two)


def bit_of(bit):
    return (lax.axis_index(LINE) // bit) % 2


def on_device(inputs, weights, cotangent, clip_lengths, first_moment, second_moment):
    tok_rows = inputs.shape[0]
    reach = (MOST + tok_rows - 2) // tok_rows
    shard_rows = first_moment.shape[0] // 128
    half = halves_rows(shard_rows)
    (
        first_gain,
        first_bias,
        query_weight,
        query_bias,
        key_weight,
        value_weight,
        value_bias,
        out_weight,
        out_bias,
        second_gain,
        second_bias,
        up_weight,
        up_bias,
        down_weight,
        down_bias,
        padded_weights,
    ) = unpacked(weights, shard_rows)
    base_slot = lax.axis_index(LINE) * tok_rows
    positions = base_slot + jnp.arange(tok_rows, dtype=jnp.int32)
    lower_slot, upper_slot = bounds(positions, clip_lengths)
    low = lower_slot - base_slot + reach * tok_rows
    high = upper_slot - base_slot + reach * tok_rows
    first_block = low.reshape(2, -1)[:, 0] // tok_rows
    last_block = (high.reshape(2, -1)[:, -1] + tok_rows - 1) // tok_rows
    ranges = (first_block, last_block, slot_table(), tok_rows)
    places = base_slot + block_distances()[:, None] * tok_rows + jnp.arange(tok_rows, dtype=jnp.int32)[None]
    marks = clip_marks(places.reshape(-1), clip_lengths)
    closed = penalty(clip_marks(positions, clip_lengths))

    inner = lax.axis_size("inner")
    first_half, second_half = narrowed(first_moment.reshape(-1, 128), second_moment.reshape(-1, 128), half)
    blocks = halo(inputs, (padded_weights,))
    first_sent, second_sent, *blocks = lax.optimization_barrier((first_half, second_half, *blocks))
    rows = projected(
        blocks, query_weight, key_weight, value_weight, first_gain, first_bias, query_bias, value_bias
    )
    first_got = swapped(first_sent, 2)
    second_got = swapped(second_sent, 2)
    input_rows = inputs.astype(jnp.float32)
    first_hat, _ = standard(input_rows)
    normed = (first_hat * first_gain + first_bias).astype(jnp.bfloat16)

    attended, lse = attend(
        forward_kernel,
        ranges,
        [
            (rows, ("pair", 0)),
            (rows, ("pair", -5)),
            (rows, ("pair", -9)),
            (marks, ("all", 0)),
            (closed, ("all", 0)),
        ],
        [jnp.float32, jnp.float32],
        [pltpu.VMEM((2, 2 * reach + 1, tok_rows, tok_rows), jnp.float32)],
    )
    held = {0: (first_half, second_half), 2: (first_got, second_got)}
    bit = 4
    while bit < inner:
        for place in list(held):
            held[place + bit] = tuple(swapped(piece, bit) for piece in held[place])
        bit = 2 * bit
    moments = []
    for place in range(inner):
        if place % 2 == 0:
            moments += held[place]
        else:
            moments += [swapped(piece, 1) for piece in held[place - 1]]
    mixed = attended.astype(jnp.bfloat16)
    middle = input_rows + plain_dot(mixed, out_weight) + out_bias
    second_hat, second_dev = standard(middle)
    hidden_in = (second_hat * second_gain + second_bias).astype(jnp.bfloat16)
    up_rows = plain_dot(hidden_in, up_weight) + up_bias
    cdf_part = 0.5 * (1.0 + lax.erf(up_rows * INV_ROOT_TWO))
    activated = (up_rows * cdf_part).astype(jnp.bfloat16)
    layer_output = (middle + plain_dot(activated, down_weight) + down_bias).astype(jnp.bfloat16)
    grad_out = cotangent.astype(jnp.float32)
    down_bias_grad = jnp.sum(grad_out, axis=0)
    grad_act = back_dot(cotangent, down_weight)
    pdf_part = jnp.exp(-0.5 * up_rows * up_rows) * INV_ROOT_TWO_PI
    grad_up = (grad_act * (cdf_part + up_rows * pdf_part)).astype(jnp.bfloat16)
    up_bias_grad = jnp.sum(grad_up.astype(jnp.float32), axis=0)
    grad_hidden = back_dot(grad_up, up_weight)
    second_gain_grad = jnp.sum(grad_hidden * second_hat, axis=0)
    second_bias_grad = jnp.sum(grad_hidden, axis=0)
    grad_middle = grad_out + norm_back(grad_hidden, second_hat, second_dev, second_gain)
    grad_branch = grad_middle.astype(jnp.bfloat16)
    out_bias_grad = jnp.sum(grad_branch.astype(jnp.float32), axis=0)
    sent = mixed_grad(grad_branch, out_weight, attended, lse, clip_marks(positions, clip_lengths))
    line = lax.axis_size(LINE)
    shards = inner
    late_shards = shards // 4
    groups = bit_groups()

    def rounded(count, unit):
        return -(-count // unit) * unit

    def shard_spans(first, last, base):
        spans = ([], [])
        for shard in range(first, last):
            begin = (shard - first) * shard_rows + base
            spans[0].append((begin, half, half))
            spans[1].append((begin + half, shard_rows - half, half))
        return spans

    def query_step(pairs, after):
        return attend(
            query_kernel,
            ranges,
            [
                (rows, ("pair", 0)),
                (rows, ("pair", -5)),
                (rows, ("pair", -9)),
                (sent, ("pair", 0)),
                (sent, ("column", 4)),
                (marks, ("all", 0)),
                (closed, ("all", 0)),
            ],
            [jnp.bfloat16],
            [],
            pairs,
            after,
        )

    def key_step(pairs, after):
        return attend(
            key_kernel,
            ranges,
            [
                (rows, ("pair", 4)),
                (rows, ("pair", 8)),
                (rows, ("pair", -1)),
                (closed, ("all", 0)),
            ]
            + [(block, ("pair", 0)) for block in grad_blocks]
            + [(block, ("column", 4)) for block in grad_blocks],
            [jnp.bfloat16, jnp.bfloat16],
            [pltpu.VMEM((len(grad_blocks), tok_rows, 128), jnp.bfloat16)] * 2,
            pairs,
            after,
        )

    query_parts = query_step((0, 2), ())
    grad_blocks = halo(sent, query_parts)
    activated, hidden_in, mixed = (behind(array, query_parts) for array in (activated, hidden_in, mixed))

    early_rows = [
        (mixed, grad_branch),
        (out_bias_grad,),
        (second_gain_grad,),
        (second_bias_grad,),
        (hidden_in, grad_up),
        (up_bias_grad,),
        (activated, cotangent),
        (down_bias_grad,),
    ]
    early_half = rounded((shards - late_shards) * half, 8 * line)
    spans = shard_spans(late_shards, shards, 0)
    for span in spans:
        span.append((0, 0, early_half - (shards - late_shards) * half))
    early_keep, early_give = packed_halves(early_rows, D // 128, spans, early_half)
    early_got = swapped(early_give, 1)

    query_parts += query_step((2, 2), (early_give,))
    parts = combine([early_keep, early_got], groups[0], query_parts)
    got = exchanged(parts, groups[0])
    work = [(1, 1), (2, 1), (3, 1)]
    done = key_step((0, 1), parts[:1])
    key_parts, value_parts = [done[0]], [done[1]]
    held_back = done[:1]
    for at, group in enumerate(groups):
        parts = combine(got, groups[at + 1] if at + 1 < len(groups) else [], held_back)
        if at + 1 < len(groups):
            got = exchanged(parts, groups[at + 1])
        if work:
            done = key_step(work.pop(0), parts[:1])
            key_parts.append(done[0])
            value_parts.append(done[1])
            held_back = done[:1]
    piece = parts[0]
    for at, group in enumerate(groups[::-1]):
        got = exchanged([piece], group)
        if work and at > 0:
            done = key_step(work.pop(0), [piece])
            key_parts.append(done[0])
            value_parts.append(done[1])
            held_back = done[:1]
        piece = stack(got, group, held_back)
    early_other = swapped(piece, 1)
    for pairs in work:
        done = key_step(pairs, [piece])
        key_parts.append(done[0])
        value_parts.append(done[1])
    early = (piece, early_other)
    input_grad, first_gain_grad, first_bias_grad, query_bias_grad, value_bias_grad = finished(
        inputs,
        grad_middle,
        first_gain,
        (query_weight, key_weight, value_weight),
        (query_parts, key_parts, value_parts),
    )
    late_rows = [
        (first_gain_grad,),
        (first_bias_grad,),
        (normed, *query_parts),
        (query_bias_grad,),
        (normed, *key_parts),
        (normed, *value_parts),
        (value_bias_grad,),
    ]
    tail = max(1, 1 << (len(groups[0])))
    late_half = rounded(late_shards * half + 16, 16 * tail)
    spans = shard_spans(0, late_shards, 0)
    spare = late_half - late_shards * half
    spans[0].append((late_shards * shard_rows, D // 128, spare))
    spans[1].append((0, 0, spare))
    keep, give = packed_halves(late_rows, 0, spans, late_half)
    early_square = square_sum(early[0])
    parts = combine([keep, swapped(give, 1)], groups[0], ())
    (piece,) = combine(exchanged(parts, groups[0]), [], ())
    for group in groups[1:]:
        (piece,) = combine(exchanged([piece], group), [], (early_square, layer_output))
    piece = stack(exchanged([piece], groups[0]), groups[0], ())
    late = (piece, swapped(piece, 1))

    grad_norm = jnp.sqrt(early_square + square_sum(late[0]))[0, 0]
    steps, grad_shard, moment_one, moment_two = updated(
        (1.0 / jnp.maximum(grad_norm, 1.0)).reshape(1),
        early,
        late,
        late_shards,
        padded_weights,
        first_moment,
        second_moment,
        moments,
    )
    weight_step = steps.reshape(-1)
    return (
        layer_output,
        input_grad,
        grad_shard.reshape(-1),
        grad_norm,
        moment_one.reshape(-1),
        moment_two.reshape(-1),
        weight_step,
    )


def solution(mesh):
    return jax.shard_map(
        on_device,
        mesh=mesh,
        in_specs=(
            P(("outer", "inner"), None),
            P(),
            P(("outer", "inner"), None),
            P(),
            P("inner"),
            P("inner"),
        ),
        out_specs=(
            P(("outer", "inner"), None),
            P(("outer", "inner"), None),
            P("inner"),
            P(),
            P("inner"),
            P("inner"),
            P(),
        ),
        check_vma=False,
    )
```

```python
import functools
import math

import jax
import jax.numpy as jnp
from jax import lax
from jax.experimental import pallas as pl
from jax.experimental.pallas import tpu as pltpu
from jax.sharding import PartitionSpec as P

D = 512
HEADS = 8
FF = 2048
MOST = 1500


BETA_ONE = 0.9
BETA_TWO = 0.999
FIX_ONE = 1.0 - (0.9**10) ** 10
FIX_TWO = 1.0 - (0.999**10) ** 10
DECAY = 0.1
INV_ROOT_TWO = 1.0 / math.sqrt(2.0)
INV_ROOT_TWO_PI = 1.0 / math.sqrt(2.0 * math.pi)


def layouts():
    return [
        (D,),
        (D,),
        (D, D),
        (D,),
        (D, D),
        (D, D),
        (D,),
        (D, D),
        (D,),
        (D,),
        (D,),
        (D, FF),
        (FF,),
        (FF, D),
        (D,),
    ]


def plain_dot(matrix_one, matrix_two):
    return jnp.dot(matrix_one, matrix_two, preferred_element_type=jnp.float32)


def rows_dot(matrix_one, matrix_two):
    return lax.dot_general(
        matrix_one, matrix_two, (((0,), (0,)), ((), ())), preferred_element_type=jnp.float32
    )


def back_dot(matrix_one, matrix_two):
    return lax.dot_general(
        matrix_one, matrix_two, (((1,), (1,)), ((), ())), preferred_element_type=jnp.float32
    )


def standard(values):
    center = jnp.mean(values, axis=-1, keepdims=True)
    centered = values - center
    inverse_dev = lax.rsqrt(jnp.mean(centered * centered, axis=-1, keepdims=True) + 1e-05)
    return (centered * inverse_dev, inverse_dev)


def norm_back(grad_normed, normed_hat, inverse_dev, gain):
    scaled = grad_normed * gain
    return inverse_dev * (
        scaled
        - jnp.mean(scaled, axis=-1, keepdims=True)
        - normed_hat * jnp.mean(scaled * normed_hat, axis=-1, keepdims=True)
    )


def bounds(positions, clip_lengths):
    starts = jnp.cumsum(clip_lengths, dtype=jnp.int32) - clip_lengths
    member = (
        jnp.sum((positions[:, None] >= starts[None, :]).astype(jnp.int32), axis=1, dtype=jnp.int32)
        - 1
    )
    onehot = (
        jnp.arange(clip_lengths.shape[0], dtype=jnp.int32)[None, :] == member[:, None]
    ).astype(jnp.int32)
    lower_slot = jnp.sum(onehot * starts[None, :], axis=1, dtype=jnp.int32)
    upper_slot = lower_slot + jnp.sum(onehot * clip_lengths[None, :], axis=1, dtype=jnp.int32)
    return (lower_slot, upper_slot)


LINE = ("outer", "inner")
NEG = -1e30
BRIEF = pl.CostEstimate(flops=1000, bytes_accessed=1000, transcendentals=0)


def shifted(block, distance):
    n = lax.axis_size(LINE)
    return lax.ppermute(block, LINE, [(i + distance, i) for i in range(n) if 0 <= i + distance < n])


def swapped(block, bit):
    n = lax.axis_size(LINE)
    return lax.ppermute(block, LINE, [(i ^ bit, i) for i in range(n)])


def halo(block, before=()):
    n = lax.axis_size(LINE)
    left = shifted(block, -2)
    right = shifted(block, 2)
    partner = swapped(block, 1)
    route = [(i + (3 if i % 2 else -3), i) for i in range(n)]
    far = lax.ppermute(block, LINE, [(s, t) for s, t in route if 0 <= s < n])
    passed_left, passed_right, *_ = lax.optimization_barrier((left, right, *before))
    turned = [swapped(passed_left, 1), swapped(passed_right, 1)]
    return [block, partner, left, right, *turned, far]


def block_distances():
    odd = lax.axis_index(LINE) % 2
    even_far = jnp.array([0, 1, -2, 2, -1, 3, -3], jnp.int32)
    odd_far = jnp.array([0, -1, -2, 2, -3, 1, 3], jnp.int32)
    return jnp.where(odd == 1, odd_far, even_far)


def slot_table():
    odd = lax.axis_index(LINE) % 2
    even_slots = jnp.array([6, 2, 4, 0, 1, 3, 5], jnp.int32)
    odd_slots = jnp.array([4, 2, 1, 0, 5, 3, 6], jnp.int32)
    return jnp.where(odd == 1, odd_slots, even_slots)


def dot_nt(a, b):
    return lax.dot_general(a, b, (((1,), (1,)), ((), ())), preferred_element_type=jnp.float32)


def head_halves(pair):
    first = lax.broadcasted_iota(jnp.int32, pair.shape, 1) < pair.shape[1] // 2
    zero = jnp.zeros_like(pair)
    return jnp.where(first, pair, zero), jnp.where(first, zero, pair)


def over_lanes(tile, op):
    parts = [tile[:, 128 * j : 128 * (j + 1)] for j in range(tile.shape[1] // 128)]
    while len(parts) > 1:
        rest = parts[len(parts) // 2 * 2 :]
        parts = [op(parts[2 * j], parts[2 * j + 1]) for j in range(len(parts) // 2)] + rest
    return parts[0]


LSE_PARTS, DELTA_PARTS = 3, 2
DELTA_AT = LSE_PARTS * HEADS
CLIPS_AT = DELTA_AT + DELTA_PARTS * HEADS


def lane_of(shape):
    return lax.broadcasted_iota(jnp.int32, shape, 1)


def among(lane, begin, count):
    return (lane >= begin) & (lane < begin + count)


def beside(pair, marks):
    return jnp.concatenate([pair, marks.astype(pair.dtype)], axis=1)


def clip_marks(positions, clip_lengths):
    ends = jnp.cumsum(clip_lengths, dtype=jnp.int32)
    starts = ends - clip_lengths
    spare = 128 - CLIPS_AT - clip_lengths.shape[0]
    assert spare >= 0
    big = jnp.iinfo(jnp.int32).max
    lower = jnp.concatenate([jnp.full((CLIPS_AT,), -big, jnp.int32), starts, jnp.full((spare,), big, jnp.int32)])
    upper = jnp.concatenate([jnp.full((CLIPS_AT,), big, jnp.int32), ends, jnp.full((spare,), big, jnp.int32)])
    inside = (positions[:, None] >= lower[None]) & (positions[:, None] < upper[None])
    return inside.astype(jnp.bfloat16)


def penalty(marks):
    closed = (lane_of(marks.shape) >= CLIPS_AT) & (marks == 0)
    return jnp.where(closed, NEG, 0.0).astype(jnp.bfloat16)


def over_blocks(first_ref, last_ref, rows, work, start):
    half = rows // 2
    carried = (start, start)
    spans = (
        (first_ref[0], first_ref[1], 0, half),
        (first_ref[1], last_ref[0], 0, rows),
        (last_ref[0], last_ref[1], half, half),
    )
    for lower, upper, begin, count in spans:

        def step(block, carried):
            found = work(block, begin, count)
            upper_half, lower_half = carried
            if begin == 0:
                upper_half = tuple(join(old, new[:half]) for (join, new), old in zip(found, upper_half))
            if begin + count == rows:
                lower_half = tuple(join(old, new[count - half :]) for (join, new), old in zip(found, lower_half))
            return upper_half, lower_half

        carried = lax.fori_loop(lower, upper, step, carried)
    return [jnp.concatenate(halves, axis=0) for halves in zip(*carried)]


def forward_kernel(begin, first_ref, last_ref, slot_ref, q_ref, k_ref, v_ref, mark_ref, closed_ref, o_ref, lse_ref, s_ref):
    width = q_ref.shape[0]
    queries = [beside(half, closed_ref[...]) for half in head_halves(q_ref[...] * jnp.bfloat16(0.125))]

    def scores(block, begin, count):
        at = pl.ds(pl.multiple_of(slot_ref[block] * width, width), width)
        keys = beside(k_ref[at, :], mark_ref[at, :])
        found = []
        for h in range(2):
            score = dot_nt(queries[h][begin : begin + count], keys)
            s_ref[h, block, pl.ds(begin, count), :] = score
            found.append((jnp.maximum, over_lanes(score, jnp.maximum)))
        return found

    start = jnp.full((width // 2, 128), NEG, jnp.float32)
    peaks = over_blocks(first_ref, last_ref, width, scores, (start, start))
    peaks = [jnp.max(peak, axis=1, keepdims=True) for peak in peaks]

    def mix(block, begin, count):
        at = pl.ds(pl.multiple_of(slot_ref[block] * width, width), width)
        values = beside(v_ref[at, :], mark_ref[at, :])
        found = []
        for h in range(2):
            score = s_ref[h, block, pl.ds(begin, count), :]
            soft = jnp.exp(score - peaks[h][begin : begin + count]).astype(jnp.bfloat16)
            found.append((jnp.add, jnp.dot(soft, values, preferred_element_type=jnp.float32)))
        return found

    start = jnp.zeros((width // 2, 256), jnp.float32)
    sums = over_blocks(first_ref, last_ref, width, mix, (start, start))
    totals = [part[:, 128:129] for part in sums]
    even = lane_of((width, 128)) < 64
    o_ref[...] = jnp.where(even, sums[0][:, :128] / totals[0], sums[1][:, :128] / totals[1])
    lse_ref[...] = jnp.where(even, peaks[0] + jnp.log(totals[0]), peaks[1] + jnp.log(totals[1]))


def query_kernel(
    begin, first_ref, last_ref, slot_ref, q_ref, k_ref, v_ref, g_ref, own_ref, mark_ref, closed_ref, dq_ref
):
    width = q_ref.shape[0]
    pair = pl.program_id(0) + begin
    own, closed = own_ref[...], closed_ref[...]
    lane = lane_of(own.shape)
    zero = jnp.zeros_like(own)
    queries, grads = [], []
    halves = zip(head_halves(q_ref[...] * jnp.bfloat16(0.125)), head_halves(g_ref[...]))
    for h, (query, grad) in enumerate(halves):
        head = 2 * pair + h
        queries.append(beside(query, jnp.where(among(lane, LSE_PARTS * head, LSE_PARTS), own, closed)))
        grads.append(beside(grad, jnp.where(among(lane, DELTA_AT + DELTA_PARTS * head, DELTA_PARTS), own, zero)))

    def work(block, begin, count):
        at = pl.ds(pl.multiple_of(slot_ref[block] * width, width), width)
        keys = k_ref[at, :]
        values = beside(v_ref[at, :], mark_ref[at, :])
        marked = beside(keys, mark_ref[at, :])
        found = []
        for h in range(2):
            soft = jnp.exp(dot_nt(queries[h][begin : begin + count], marked))
            grad = (soft * dot_nt(grads[h][begin : begin + count], values)).astype(jnp.bfloat16)
            found.append((jnp.add, jnp.dot(grad, keys, preferred_element_type=jnp.float32)))
        return found

    start = jnp.zeros((width // 2, 128), jnp.float32)
    sums = over_blocks(first_ref, last_ref, width, work, (start, start))
    dq_ref[...] = (jnp.where(lane < 64, sums[0], sums[1]) * 0.125).astype(jnp.bfloat16)


def key_kernel(begin, first_ref, last_ref, slot_ref, k_ref, v_ref, q_ref, closed_ref, *refs):
    dk_ref, dv_ref, grad_ref, mark_ref = refs[-4:]
    width = k_ref.shape[0]
    pair = pl.program_id(0) + begin
    blocks = grad_ref.shape[0]
    for j in range(blocks):
        grad_ref[j] = refs[j][...]

    @pl.when(pl.program_id(0) == 0)
    def _():
        for j in range(blocks):
            mark_ref[j] = refs[blocks + j][...]

    closed = closed_ref[...]
    lane = lane_of(closed.shape)
    one, zero = jnp.ones_like(closed), jnp.zeros_like(closed)
    keys, values = [], []
    halves = zip(head_halves(k_ref[...] * jnp.bfloat16(0.125)), head_halves(v_ref[...]))
    for h, (key, value) in enumerate(halves):
        head = 2 * pair + h
        keys.append(beside(key, jnp.where(among(lane, LSE_PARTS * head, LSE_PARTS), one, closed)))
        values.append(beside(value, jnp.where(among(lane, DELTA_AT + DELTA_PARTS * head, DELTA_PARTS), one, zero)))

    def work(block, begin, count):
        slot = slot_ref[block]
        queries = q_ref[pl.ds(pl.multiple_of(slot * width, width), width), :]
        grads, marks = grad_ref[slot], mark_ref[slot]
        marked, graded = beside(queries, marks), beside(grads, marks)
        found = []
        for h in range(2):
            soft = jnp.exp(dot_nt(keys[h][begin : begin + count], marked))
            grad = (soft * dot_nt(values[h][begin : begin + count], graded)).astype(jnp.bfloat16)
            found.append((jnp.add, jnp.dot(grad, queries, preferred_element_type=jnp.float32)))
            found.append((jnp.add, jnp.dot(soft.astype(jnp.bfloat16), grads, preferred_element_type=jnp.float32)))
        return found

    start = jnp.zeros((width // 2, 128), jnp.float32)
    sums = over_blocks(first_ref, last_ref, width, work, (start,) * 4)
    dk_ref[...] = (jnp.where(lane < 64, sums[0], sums[2]) * 0.125).astype(jnp.bfloat16)
    dv_ref[...] = jnp.where(lane < 64, sums[1], sums[3]).astype(jnp.bfloat16)


def mixed_grad_kernel(branch_ref, weight_ref, mixed_ref, lse_ref, own_ref, sent_ref, mark_ref):
    step = pl.program_id(0)

    @pl.when(step == 0)
    def _():
        mark_ref[...] = own_ref[...].astype(jnp.float32)

    @pl.when(step < D // 128)
    def _():
        grad = dot_nt(branch_ref[...], weight_ref[...]).astype(jnp.bfloat16)
        sent_ref[...] = grad
        product = grad.astype(jnp.float32) * mixed_ref[...]
        lane = lane_of(product.shape)
        marks = mark_ref[...]
        for h, part in enumerate(head_halves(product)):
            head = 2 * step + h
            delta = -jnp.sum(part, axis=1, keepdims=True)
            lse = -lse_ref[:, 64 * h : 64 * h + 1]
            for value, begin, count in (
                (lse, LSE_PARTS * head, LSE_PARTS),
                (delta, DELTA_AT + DELTA_PARTS * head, DELTA_PARTS),
            ):
                for k in range(count):
                    rounded = value.astype(jnp.bfloat16).astype(jnp.float32)
                    marks = jnp.where(lane == begin + k, rounded, marks)
                    value = value - rounded
        mark_ref[...] = marks

    @pl.when(step == D // 128)
    def _():
        sent_ref[...] = mark_ref[...].astype(jnp.bfloat16)


def mixed_grad(branch, out_weight, mixed, lse, own_marks):
    width = branch.shape[0]
    last = D // 128 - 1
    column = pl.BlockSpec((width, 128), lambda h: (0, jnp.minimum(h, last)))
    return pl.pallas_call(
        mixed_grad_kernel,
        name="mixed_grad",
        grid=(D // 128 + 1,),
        in_specs=[
            pl.BlockSpec((width, D), lambda h: (0, 0)),
            pl.BlockSpec((128, D), lambda h: (jnp.minimum(h, last), 0)),
            column,
            column,
            pl.BlockSpec((width, 128), lambda h: (0, 0)),
        ],
        out_specs=pl.BlockSpec((width, 128), lambda h: (0, h)),
        out_shape=jax.ShapeDtypeStruct((width, D + 128), jnp.bfloat16),
        scratch_shapes=[pltpu.VMEM((width, 128), jnp.float32)],
        cost_estimate=BRIEF,
    )(branch, out_weight, mixed, lse, own_marks)


def project_kernel(count, *refs):
    query_ref, key_ref, value_ref, gain_ref, bias_ref, query_bias_ref, value_bias_ref, out_ref, row_ref = refs[count:]
    step = pl.program_id(0)
    for j in range(count):

        @pl.when(step == j)
        def _():
            row_ref[...] = refs[j][...]

    rows = 256
    for i in range(row_ref.shape[0] // rows):
        at = pl.ds(i * rows, rows)
        hat, _ = standard(row_ref[at, :].astype(jnp.float32))
        normed = (hat * gain_ref[...] + bias_ref[...]).astype(jnp.bfloat16)
        out_ref[at, 0:D] = (plain_dot(normed, query_ref[...]) + query_bias_ref[...]).astype(jnp.bfloat16)
        out_ref[at, D : 2 * D] = plain_dot(normed, key_ref[...]).astype(jnp.bfloat16)
        out_ref[at, 2 * D :] = (plain_dot(normed, value_ref[...]) + value_bias_ref[...]).astype(jnp.bfloat16)


def projected(blocks, *weights):
    width = blocks[0].shape[0]
    whole = [pl.BlockSpec(array.shape, lambda i: (0, 0)) for array in (*blocks, *weights)]
    return pl.pallas_call(
        functools.partial(project_kernel, len(blocks)),
        name="project",
        grid=(len(blocks),),
        in_specs=whole,
        out_specs=pl.BlockSpec((width, 3 * D), lambda i: (i, 0)),
        out_shape=jax.ShapeDtypeStruct((len(blocks) * width, 3 * D), jnp.bfloat16),
        scratch_shapes=[pltpu.VMEM((width, D), jnp.bfloat16)],
        compiler_params=pltpu.CompilerParams(vmem_limit_bytes=63 * 2**20),
        cost_estimate=BRIEF,
    )(*blocks, *weights)


def attend(kernel, ranges, operands, results, scratch, pairs=(0, D // 128), after=()):
    begin, count = pairs
    tok_rows = ranges[3]
    specs = []
    for array, (kind, at) in operands:
        if kind == "pair":
            rows = array.shape[0] if at < 0 else tok_rows
            at = (abs(at) - 1 if at < 0 else at) + begin
            specs.append(pl.BlockSpec((rows, 128), lambda h, *_, at=at: (0, at + h)))
        elif kind == "column":
            specs.append(pl.BlockSpec((tok_rows, 128), lambda h, *_, at=at: (0, at)))
        else:
            specs.append(pl.BlockSpec(array.shape, lambda h, *_, n=array.ndim: (0,) * n))
    return pl.pallas_call(
        functools.partial(kernel, begin),
        grid_spec=pltpu.PrefetchScalarGridSpec(
            num_scalar_prefetch=3,
            grid=(count,),
            in_specs=specs,
            out_specs=[pl.BlockSpec((tok_rows, 128), lambda h, *_: (0, h))] * len(results),
            scratch_shapes=scratch,
        ),
        out_shape=[jax.ShapeDtypeStruct((tok_rows, 128 * count), kept) for kept in results],
        compiler_params=pltpu.CompilerParams(vmem_limit_bytes=48 * 2**20),
        cost_estimate=BRIEF,
    )(*[behind(bound, after) for bound in ranges[:1]], *ranges[1:3], *[array for array, _ in operands])


VECTOR = pltpu.VMEM
ANY = pl.ANY


def behind(value, others):
    return lax.optimization_barrier((value, *others))[0]


def halves_rows(shard_rows):
    return -(-shard_rows // 128) * 64


def unpack_kernel(plan, shard_rows, flat_ref, *refs):
    wide_ref = refs[-1]
    padded_ref = refs[-2]
    total = flat_ref.shape[0]
    chunk = 432

    def widen(i, _):
        rows = pl.ds(pl.multiple_of(i * chunk, 16), chunk)
        wide_ref[rows, :] = flat_ref[rows, :].astype(jnp.float32)
        return 0

    lax.fori_loop(0, total // chunk, widen, 0)
    wide_ref[pl.ds(total, wide_ref.shape[0] - total), :] = jnp.zeros((wide_ref.shape[0] - total, 128), jnp.float32)
    for (offset, rows, columns, begin), ref in zip(plan, refs[:-2]):
        pieces = columns // 128
        if rows == 1:
            for j in range(pieces):
                ref[:, 128 * j : 128 * (j + 1)] = wide_ref[pl.ds(offset + j, 1), :]
            continue

        taken = 1024 // pieces

        def matrix(i, _):
            at = pl.multiple_of(i * taken, 64)
            for j in range(pieces):
                part = wide_ref[pl.ds(offset + j + at * pieces, taken, stride=pieces), :]
                ref[pl.ds(at, taken), begin + 128 * j : begin + 128 * (j + 1)] = part.astype(jnp.bfloat16)
            return 0

        lax.fori_loop(0, rows // taken, matrix, 0)
    shards = total // shard_rows
    half = halves_rows(shard_rows)
    for s in range(shards):
        for h in range(2):

            run = 448 if half % 448 == 0 else 64

            def pad(i, _):
                part = wide_ref[pl.ds(s * shard_rows + h * half + i * run, run), :]
                padded_ref[s * 2 + h, pl.ds(pl.multiple_of(i * run, 64), run), :] = part.astype(jnp.bfloat16)
                return 0

            lax.fori_loop(0, half // run, pad, 0)


def unpacked(weights, shard_rows):
    flat = weights.reshape(-1, 128)
    half = halves_rows(shard_rows)
    plan, outs = [], []
    offset = 0
    for layout in layouts():
        rows, columns = layout if len(layout) == 2 else (1, layout[0])
        plan.append([offset, rows, columns, 0])
        outs.append(jax.ShapeDtypeStruct((rows, columns), jnp.bfloat16 if rows > 1 else jnp.float32))
        offset = offset + rows * columns // 128
    shards = flat.shape[0] // shard_rows
    outs.append(jax.ShapeDtypeStruct((2 * shards, half, 128), jnp.bfloat16))
    return pl.pallas_call(
        functools.partial(unpack_kernel, plan, shard_rows),
        name="unpack",
        in_specs=[pl.BlockSpec(memory_space=VECTOR)],
        out_specs=[pl.BlockSpec(memory_space=VECTOR)] * len(outs),
        out_shape=outs,
        scratch_shapes=[VECTOR((flat.shape[0] + 2 * half, 128), jnp.float32)],
        compiler_params=pltpu.CompilerParams(vmem_limit_bytes=60 * 2**20),
        cost_estimate=BRIEF,
    )(flat)


def pack_kernel(plan, spans, place_ref, *refs):
    keep_ref, give_ref, flat_ref, out_ref, sems = refs[-5:]
    begin = min(entry[0] for entry in plan)
    if begin:
        flat_ref[pl.ds(0, begin), :] = jnp.zeros((begin, 128), jnp.float32)
    given = iter(refs)
    for offset, rows, columns, factors in plan:
        pieces = columns // 128
        ref = next(given)
        if rows == 1:
            for j in range(pieces):
                flat_ref[pl.ds(offset + j, 1), :] = ref[:, 128 * j : 128 * (j + 1)]
            continue

        others = [next(given) for _ in range(factors - 1)]
        other = others[0][...] if len(others) == 1 else jnp.concatenate([part[...] for part in others], axis=1)
        taken = 256

        def product(i, _):
            at = pl.multiple_of(i * taken, 128)
            found = rows_dot(ref[:, pl.ds(at, taken)], other)
            for j in range(pieces):
                part = found[:, 128 * j : 128 * (j + 1)]
                flat_ref[pl.ds(offset + j + at * pieces, taken, stride=pieces), :] = part
            return 0

        lax.fori_loop(0, rows // taken, product, 0)
    for h in range(2):
        at = h ^ place_ref[0]
        filled = 0
        for source, rows, room in spans[h]:
            run = 448 if rows >= 448 else 64
            whole = rows // run

            def move(i, _):
                to = pl.ds(pl.multiple_of(filled + i * run, 16), run)
                out_ref[at, to, :] = flat_ref[pl.ds(source + i * run, run), :].astype(jnp.bfloat16)
                return 0

            lax.fori_loop(0, whole, move, 0)
            rest = rows - run * whole
            tail = room - run * whole
            if tail:
                parts = []
                if rest:
                    parts.append(flat_ref[pl.ds(source + run * whole, rest), :])
                if tail > rest:
                    parts.append(jnp.zeros((tail - rest, 128), jnp.float32))
                last = parts[0] if len(parts) == 1 else jnp.concatenate(parts, axis=0)
                out_ref[at, pl.ds(filled + run * whole, tail), :] = last.astype(jnp.bfloat16)
            filled = filled + room
    copies = [
        pltpu.make_async_copy(out_ref.at[0], keep_ref, sems.at[0]),
        pltpu.make_async_copy(out_ref.at[1], give_ref, sems.at[1]),
    ]
    for copy in copies:
        copy.start()
    for copy in copies:
        copy.wait()


def packed_halves(grads, begin, spans, half):
    plan, arrays = [], []
    offset = begin
    for grad in grads:
        rows, columns = 1, grad[0].size
        if len(grad) > 1:
            rows, columns = grad[0].shape[1], sum(part.shape[1] for part in grad[1:])
        plan.append((offset, rows, columns, len(grad)))
        arrays += [array.reshape(-1, array.shape[-1]) for array in grad]
        offset = offset + rows * columns // 128
    return pl.pallas_call(
        functools.partial(pack_kernel, plan, spans),
        name="pack",
        in_specs=[pl.BlockSpec(memory_space=pltpu.SMEM)] + [pl.BlockSpec(memory_space=VECTOR)] * len(arrays),
        out_specs=[pl.BlockSpec(memory_space=ANY)] * 2,
        out_shape=[jax.ShapeDtypeStruct((half, 128), jnp.bfloat16)] * 2,
        scratch_shapes=[
            VECTOR((offset, 128), jnp.float32),
            VECTOR((2, half, 128), jnp.bfloat16),
            pltpu.SemaphoreType.DMA((2,)),
        ],
        compiler_params=pltpu.CompilerParams(vmem_limit_bytes=60 * 2**20),
        cost_estimate=BRIEF,
    )(bit_of(1).reshape(1), *arrays)


def combine_kernel(count, places_ref, *refs):
    parts, outs = refs[:count], refs[-places_ref.shape[0] :]
    rows = outs[0].shape[0]
    for k, out in enumerate(outs):
        at = pl.ds(pl.multiple_of(places_ref[k] * rows, 16), rows)
        terms = [part[at, :].astype(jnp.float32) for part in parts]
        while len(terms) > 1:
            terms = [terms[2 * j] + terms[2 * j + 1] for j in range(len(terms) // 2)]
        out[...] = terms[0].astype(jnp.bfloat16)


def places_of(group):
    if not group:
        return jnp.zeros((1,), jnp.int32)
    place = (lax.axis_index(LINE) // group[0]) % (1 << len(group))
    return place ^ jnp.arange(1 << len(group), dtype=jnp.int32)


def combine(parts, group, after):
    count = 1 << len(group)
    rows = parts[0].shape[0] // count
    outs = pl.pallas_call(
        functools.partial(combine_kernel, len(parts)),
        name="combine",
        in_specs=[pl.BlockSpec(memory_space=pltpu.SMEM)]
        + [pl.BlockSpec(memory_space=VECTOR)] * len(parts),
        out_specs=[pl.BlockSpec(memory_space=VECTOR)] * count,
        out_shape=[jax.ShapeDtypeStruct((rows, 128), jnp.bfloat16)] * count,
        cost_estimate=BRIEF,
    )(behind(places_of(group), after), *parts)
    return list(outs)


def stack_kernel(count, places_ref, *refs):
    out_ref = refs[-1]
    rows = refs[0].shape[0]
    for k in range(count):
        out_ref[pl.ds(pl.multiple_of(places_ref[k] * rows, 16), rows), :] = refs[k][...]


def stack(parts, group, after):
    rows = parts[0].shape[0] * len(parts)
    return pl.pallas_call(
        functools.partial(stack_kernel, len(parts)),
        name="stack",
        in_specs=[pl.BlockSpec(memory_space=pltpu.SMEM)]
        + [pl.BlockSpec(memory_space=VECTOR)] * len(parts),
        out_specs=pl.BlockSpec(memory_space=VECTOR),
        out_shape=jax.ShapeDtypeStruct((rows, 128), jnp.bfloat16),
        cost_estimate=BRIEF,
    )(behind(places_of(group), after), *parts)


def exchanged(parts, group):
    return [parts[0]] + [swapped(parts[k % len(parts)], group[0] * k) for k in range(1, 1 << len(group))]


def bit_groups():
    bits = [1 << k for k in range(1, lax.axis_size(LINE).bit_length() - 1)]
    return [bits[k : k + 2] for k in range(0, len(bits), 2)]


def square_sum_kernel(ref, out_ref):
    rows = ref.shape[0]
    chunk = rows // 8 if rows % 256 == 0 else 32

    def add(i, total):
        part = ref[pl.ds(pl.multiple_of(i * chunk, 16), chunk), :].astype(jnp.float32)
        return total + jnp.sum((part * part).reshape(-1, 32, 128), axis=0)

    total = lax.fori_loop(0, rows // chunk, add, jnp.zeros((32, 128), jnp.float32))
    out_ref[...] = jnp.broadcast_to(jnp.sum(total, keepdims=True), (8, 128))


def square_sum(half):
    own = pl.pallas_call(
        square_sum_kernel,
        name="square_sum",
        in_specs=[pl.BlockSpec(memory_space=VECTOR)],
        out_specs=pl.BlockSpec(memory_space=VECTOR),
        out_shape=jax.ShapeDtypeStruct((8, 128), jnp.float32),
        cost_estimate=BRIEF,
    )(half)
    return own + swapped(own, 1)


def finish_kernel(counts, x_ref, middle_ref, gain_ref, *refs):
    weights, parts, outs = refs[:3], refs[3:-5], refs[-5:]
    grad_ref, gain_out, bias_out, query_out, value_out = outs
    for out in outs[1:]:
        out[...] = jnp.zeros_like(out)
    rows = 256
    for i in range(x_ref.shape[0] // rows):
        at = pl.ds(i * rows, rows)
        hat, dev = standard(x_ref[at, :].astype(jnp.float32))
        grads, begin = [], 0
        for count in counts:
            grads.append(jnp.concatenate([part[at, :] for part in parts[begin : begin + count]], axis=1))
            begin = begin + count
        normed = sum(dot_nt(grad, weight[...]) for grad, weight in zip(grads, weights))
        for out, value in (
            (gain_out, normed * hat),
            (bias_out, normed),
            (query_out, grads[0].astype(jnp.float32)),
            (value_out, grads[2].astype(jnp.float32)),
        ):
            out[...] = out[...] + jnp.sum(value, axis=0, keepdims=True)
        grad_ref[at, :] = (middle_ref[at, :] + norm_back(normed, hat, dev, gain_ref[...])).astype(jnp.bfloat16)


def finished(inputs, grad_middle, gain, weights, parts):
    arrays = [inputs, grad_middle, gain, *weights, *(part for group in parts for part in group)]
    return pl.pallas_call(
        functools.partial(finish_kernel, [len(group) for group in parts]),
        name="finish",
        in_specs=[pl.BlockSpec(memory_space=VECTOR)] * len(arrays),
        out_specs=[pl.BlockSpec(memory_space=VECTOR)] * 5,
        out_shape=[jax.ShapeDtypeStruct(inputs.shape, jnp.bfloat16)] + [jax.ShapeDtypeStruct((1, D), jnp.float32)] * 4,
        compiler_params=pltpu.CompilerParams(vmem_limit_bytes=60 * 2**20),
        cost_estimate=BRIEF,
    )(*arrays)


def update_kernel(
    shards, late, shard_rows, meta_ref, scale_ref, early_own, early_other, late_own, late_other, extra_own, extra_other,
    weight_ref, one_ref, two_ref, *refs
):
    moments = refs[: 2 * shards]
    step_ref, grad_ref, new_one_ref, new_two_ref, sum_ref, wide_ref, stage_ref, sems = refs[2 * shards :]
    which, k = pl.program_id(0), pl.program_id(1)
    core, me = meta_ref[0], meta_ref[1]
    shard = me ^ k
    half = core ^ which
    rows = sum_ref.shape[0]
    chunk = rows // 7 if rows % 112 == 0 else 64
    scale = scale_ref[0]

    def by_chunks(body, first=0, last=rows // chunk):
        def move(i, _):
            body(pl.multiple_of(i * chunk, 16))
            return 0

        lax.fori_loop(first, last, move, 0)

    def load(ref):
        def body(at):
            sum_ref[pl.ds(at, chunk), :] = ref[pl.ds(at, chunk), :].astype(jnp.float32)

        by_chunks(body)

    for array, side, is_late in ((early_own, 0, 0), (early_other, 1, 0), (late_own, 0, 1), (late_other, 1, 1)):
        pl.when((which == side) & ((shard < late) == (is_late == 1)))(functools.partial(load, array))
    for array, side in ((extra_own, 0), (extra_other, 1)):

        @pl.when((which == side) & (shard == late) & (half == 0))
        def _():
            sum_ref[pl.ds(0, 8), :] = sum_ref[pl.ds(0, 8), :] + array[pl.ds(0, 8), :].astype(jnp.float32)

    slope_one = (1.0 - BETA_ONE) * scale
    slope_two = (1.0 - BETA_TWO) * scale * scale

    base = shard * shard_rows + half * rows
    limit = jnp.where(half == 1, shard_rows - rows, rows)
    for j in range(shards):

        @pl.when(k == j)
        def _():
            def body(start, masked=False):
                at = pl.ds(start, chunk)
                one, two = moments[2 * j][at, :], moments[2 * j + 1][at, :]
                grad = sum_ref[at, :]
                one = one.astype(jnp.float32) + (slope_one * (1.0 / FIX_ONE)) * grad
                two = two.astype(jnp.float32) + (slope_two * (1.0 / FIX_TWO)) * grad * grad
                root = two * lax.rsqrt(jnp.maximum(two, 1e-37))
                update = one / (root + 1e-08) + DECAY * weight_ref[0, at, :].astype(jnp.float32)
                to = pl.ds(base + start, chunk)
                if masked:
                    inside = start + lax.broadcasted_iota(jnp.int32, update.shape, 0) < limit
                    update = jnp.where(inside, update, wide_ref[to, :])
                wide_ref[to, :] = update

            whole = (shard_rows - rows) // chunk
            by_chunks(body, 0, whole)
            by_chunks(functools.partial(body, masked=True), whole, rows // chunk)

    @pl.when(k == 0)
    def _():
        def body(start):
            at = pl.ds(start, chunk)
            grad = sum_ref[at, :]
            grad_ref[at, :] = grad
            new_one_ref[at, :] = BETA_ONE * one_ref[at, :] + slope_one * grad
            new_two_ref[at, :] = BETA_TWO * two_ref[at, :] + slope_two * grad * grad

        by_chunks(body)

    @pl.when((which == 1) & (k == shards - 1))
    def _():
        piece = stage_ref.shape[1]
        total = step_ref.shape[0]

        def sending(i, slot):
            return pltpu.make_async_copy(
                stage_ref.at[slot], step_ref.at[pl.ds(pl.multiple_of(i * piece, 16), piece), :], sems.at[slot]
            )

        count = total // piece
        for i in range(count):
            if i >= 2:
                sending(i - 2, i % 2).wait()
            stage_ref[i % 2] = wide_ref[pl.ds(i * piece, piece), :].astype(jnp.bfloat16)
            sending(i, i % 2).start()
        for i in range(count - 2, count):
            sending(i, i % 2).wait()


def updated(norm, early, late, late_shards, weights, first_moment, second_moment, moments):
    shards = len(moments) // 2
    rows = weights.shape[1]
    shard_rows = first_moment.shape[0] // 128
    line = lax.axis_index(LINE)
    meta = jnp.stack([line % 2, lax.axis_index("inner")]).astype(jnp.int32)
    last = shards - 1

    def early_map(side):
        def index(w, k, meta):
            k = jnp.where(w == side, k, last if side == 0 else 0)
            return (jnp.clip((meta[1] ^ k) - late_shards, 0, shards - late_shards - 1), 0)

        return index

    def late_map(side):
        def index(w, k, meta):
            k = jnp.where(w == side, k, last if side == 0 else 0)
            return (jnp.clip(meta[1] ^ k, 0, late_shards - 1), 0)

        return index

    by_half = pl.BlockSpec((rows, 128), lambda w, k, meta: (meta[0] ^ w, 0))

    def in_turn(j):
        return pl.BlockSpec((rows, 128), lambda w, k, meta: (meta[0] ^ jnp.where(k >= j - 1, w, 0), 0))

    by_shard = pl.BlockSpec((1, rows, 128), lambda w, k, meta: (2 * (meta[1] ^ k) + (meta[0] ^ w), 0, 0))
    extra = pl.BlockSpec((16, 128), lambda w, k, meta: (late_shards * rows // 16, 0))
    return pl.pallas_call(
        functools.partial(update_kernel, shards, late_shards, shard_rows),
        name="update",
        grid_spec=pltpu.PrefetchScalarGridSpec(
            num_scalar_prefetch=1,
            grid=(2, shards),
            in_specs=[pl.BlockSpec(memory_space=pltpu.SMEM)]
            + [pl.BlockSpec((rows, 128), early_map(side)) for side in range(2)]
            + [pl.BlockSpec((rows, 128), late_map(side)) for side in range(2)]
            + [extra, extra, by_shard, by_half, by_half]
            + [in_turn(j // 2) for j in range(2 * shards)],
            out_specs=[pl.BlockSpec(memory_space=ANY), by_half, by_half, by_half],
            scratch_shapes=[
                VECTOR((rows, 128), jnp.float32),
                VECTOR((shards * shard_rows + 2 * rows, 128), jnp.float32),
                VECTOR((2, shards * shard_rows // 9, 128), jnp.bfloat16),
                pltpu.SemaphoreType.DMA((2,)),
            ],
        ),
        out_shape=[jax.ShapeDtypeStruct((shards * shard_rows, 128), jnp.bfloat16)]
        + [jax.ShapeDtypeStruct((shard_rows, 128), jnp.float32)] * 3,
        compiler_params=pltpu.CompilerParams(vmem_limit_bytes=60 * 2**20),
        cost_estimate=BRIEF,
    )(
        meta,
        norm,
        *early,
        *late,
        *late,
        weights,
        first_moment.reshape(-1, 128),
        second_moment.reshape(-1, 128),
        *moments,
    )


def narrow_kernel(shard_rows, one_ref, two_ref, first_out, second_out):
    shape = first_out.shape
    begin = pl.program_id(0) * shape[0]
    inside = begin + lax.broadcasted_iota(jnp.int32, shape, 0) < shard_rows
    one = jnp.where(inside, one_ref[...] * (BETA_ONE / FIX_ONE), 0.0).astype(jnp.bfloat16)
    two = jnp.where(inside, two_ref[...] * (BETA_TWO / FIX_TWO), 0.0).astype(jnp.bfloat16)
    first_out[...] = one
    second_out[...] = two


def narrowed(one, two, half):
    block = pl.BlockSpec((half // 2, 128), lambda i: (i, 0))
    return pl.pallas_call(
        functools.partial(narrow_kernel, one.shape[0]),
        name="narrow",
        grid=(4,),
        in_specs=[block, block],
        out_specs=[block, block],
        out_shape=[jax.ShapeDtypeStruct((2 * half, 128), jnp.bfloat16)] * 2,
        cost_estimate=BRIEF,
    )(one, two)


def bit_of(bit):
    return (lax.axis_index(LINE) // bit) % 2


def on_device(inputs, weights, cotangent, clip_lengths, first_moment, second_moment):
    tok_rows = inputs.shape[0]
    reach = (MOST + tok_rows - 2) // tok_rows
    shard_rows = first_moment.shape[0] // 128
    half = halves_rows(shard_rows)
    (
        first_gain,
        first_bias,
        query_weight,
        query_bias,
        key_weight,
        value_weight,
        value_bias,
        out_weight,
        out_bias,
        second_gain,
        second_bias,
        up_weight,
        up_bias,
        down_weight,
        down_bias,
        padded_weights,
    ) = unpacked(weights, shard_rows)
    base_slot = lax.axis_index(LINE) * tok_rows
    positions = base_slot + jnp.arange(tok_rows, dtype=jnp.int32)
    lower_slot, upper_slot = bounds(positions, clip_lengths)
    low = lower_slot - base_slot + reach * tok_rows
    high = upper_slot - base_slot + reach * tok_rows
    first_block = low.reshape(2, -1)[:, 0] // tok_rows
    last_block = (high.reshape(2, -1)[:, -1] + tok_rows - 1) // tok_rows
    ranges = (first_block, last_block, slot_table(), tok_rows)
    places = base_slot + block_distances()[:, None] * tok_rows + jnp.arange(tok_rows, dtype=jnp.int32)[None]
    marks = clip_marks(places.reshape(-1), clip_lengths)
    closed = penalty(clip_marks(positions, clip_lengths))

    inner = lax.axis_size("inner")
    first_half, second_half = narrowed(first_moment.reshape(-1, 128), second_moment.reshape(-1, 128), half)
    blocks = halo(inputs, (padded_weights,))
    first_sent, second_sent, *blocks = lax.optimization_barrier((first_half, second_half, *blocks))
    rows = projected(
        blocks, query_weight, key_weight, value_weight, first_gain, first_bias, query_bias, value_bias
    )
    first_got = swapped(first_sent, 2)
    second_got = swapped(second_sent, 2)
    input_rows = inputs.astype(jnp.float32)
    first_hat, _ = standard(input_rows)
    normed = (first_hat * first_gain + first_bias).astype(jnp.bfloat16)

    attended, lse = attend(
        forward_kernel,
        ranges,
        [
            (rows, ("pair", 0)),
            (rows, ("pair", -5)),
            (rows, ("pair", -9)),
            (marks, ("all", 0)),
            (closed, ("all", 0)),
        ],
        [jnp.float32, jnp.float32],
        [pltpu.VMEM((2, 2 * reach + 1, tok_rows, tok_rows), jnp.float32)],
    )
    held = {0: (first_half, second_half), 2: (first_got, second_got)}
    bit = 4
    while bit < inner:
        for place in list(held):
            held[place + bit] = tuple(swapped(piece, bit) for piece in held[place])
        bit = 2 * bit
    moments = []
    for place in range(inner):
        if place % 2 == 0:
            moments += held[place]
        else:
            moments += [swapped(piece, 1) for piece in held[place - 1]]
    mixed = attended.astype(jnp.bfloat16)
    middle = input_rows + plain_dot(mixed, out_weight) + out_bias
    second_hat, second_dev = standard(middle)
    hidden_in = (second_hat * second_gain + second_bias).astype(jnp.bfloat16)
    up_rows = plain_dot(hidden_in, up_weight) + up_bias
    cdf_part = 0.5 * (1.0 + lax.erf(up_rows * INV_ROOT_TWO))
    activated = (up_rows * cdf_part).astype(jnp.bfloat16)
    layer_output = (middle + plain_dot(activated, down_weight) + down_bias).astype(jnp.bfloat16)
    grad_out = cotangent.astype(jnp.float32)
    down_bias_grad = jnp.sum(grad_out, axis=0)
    grad_act = back_dot(cotangent, down_weight)
    pdf_part = jnp.exp(-0.5 * up_rows * up_rows) * INV_ROOT_TWO_PI
    grad_up = (grad_act * (cdf_part + up_rows * pdf_part)).astype(jnp.bfloat16)
    up_bias_grad = jnp.sum(grad_up.astype(jnp.float32), axis=0)
    grad_hidden = back_dot(grad_up, up_weight)
    second_gain_grad = jnp.sum(grad_hidden * second_hat, axis=0)
    second_bias_grad = jnp.sum(grad_hidden, axis=0)
    grad_middle = grad_out + norm_back(grad_hidden, second_hat, second_dev, second_gain)
    grad_branch = grad_middle.astype(jnp.bfloat16)
    out_bias_grad = jnp.sum(grad_branch.astype(jnp.float32), axis=0)
    sent = mixed_grad(grad_branch, out_weight, attended, lse, clip_marks(positions, clip_lengths))
    line = lax.axis_size(LINE)
    shards = inner
    late_shards = shards // 4
    groups = bit_groups()

    def rounded(count, unit):
        return -(-count // unit) * unit

    def shard_spans(first, last, base):
        spans = ([], [])
        for shard in range(first, last):
            begin = (shard - first) * shard_rows + base
            spans[0].append((begin, half, half))
            spans[1].append((begin + half, shard_rows - half, half))
        return spans

    def query_step(pairs, after):
        return attend(
            query_kernel,
            ranges,
            [
                (rows, ("pair", 0)),
                (rows, ("pair", -5)),
                (rows, ("pair", -9)),
                (sent, ("pair", 0)),
                (sent, ("column", 4)),
                (marks, ("all", 0)),
                (closed, ("all", 0)),
            ],
            [jnp.bfloat16],
            [],
            pairs,
            after,
        )

    def key_step(pairs, after):
        return attend(
            key_kernel,
            ranges,
            [
                (rows, ("pair", 4)),
                (rows, ("pair", 8)),
                (rows, ("pair", -1)),
                (closed, ("all", 0)),
            ]
            + [(block, ("pair", 0)) for block in grad_blocks]
            + [(block, ("column", 4)) for block in grad_blocks],
            [jnp.bfloat16, jnp.bfloat16],
            [pltpu.VMEM((len(grad_blocks), tok_rows, 128), jnp.bfloat16)] * 2,
            pairs,
            after,
        )

    activated, hidden_in, mixed = (behind(array, (sent,)) for array in (activated, hidden_in, mixed))

    early_rows = [
        (mixed, grad_branch),
        (out_bias_grad,),
        (second_gain_grad,),
        (second_bias_grad,),
        (hidden_in, grad_up),
        (up_bias_grad,),
        (activated, cotangent),
        (down_bias_grad,),
    ]
    early_half = rounded((shards - late_shards) * half, 8 * line)
    spans = shard_spans(late_shards, shards, 0)
    for span in spans:
        span.append((0, 0, early_half - (shards - late_shards) * half))
    early_keep, early_give = packed_halves(early_rows, D // 128, spans, early_half)
    early_got = swapped(early_give, 1)

    query_parts = query_step((0, 2), (early_give,))
    grad_blocks = halo(sent, query_parts)
    parts = combine([early_keep, early_got], groups[0], query_parts)
    got = exchanged(parts, groups[0])
    work = [(1, 1), (2, 1), (3, 1)]
    query_parts += query_step((2, 2), parts[:1])
    done = key_step((0, 1), query_parts[-1:])
    key_parts, value_parts = [done[0]], [done[1]]
    held_back = done[:1]
    for at, group in enumerate(groups):
        parts = combine(got, groups[at + 1] if at + 1 < len(groups) else [], held_back)
        if at + 1 < len(groups):
            got = exchanged(parts, groups[at + 1])
        if work:
            done = key_step(work.pop(0), parts[:1])
            key_parts.append(done[0])
            value_parts.append(done[1])
            held_back = done[:1]
    piece = parts[0]
    for at, group in enumerate(groups[::-1]):
        got = exchanged([piece], group)
        if work and at > 0:
            done = key_step(work.pop(0), [piece])
            key_parts.append(done[0])
            value_parts.append(done[1])
            held_back = done[:1]
        piece = stack(got, group, held_back)
    early_other = swapped(piece, 1)
    for pairs in work:
        done = key_step(pairs, [piece])
        key_parts.append(done[0])
        value_parts.append(done[1])
    early = (piece, early_other)
    input_grad, first_gain_grad, first_bias_grad, query_bias_grad, value_bias_grad = finished(
        inputs,
        grad_middle,
        first_gain,
        (query_weight, key_weight, value_weight),
        (query_parts, key_parts, value_parts),
    )
    late_rows = [
        (first_gain_grad,),
        (first_bias_grad,),
        (normed, *query_parts),
        (query_bias_grad,),
        (normed, *key_parts),
        (normed, *value_parts),
        (value_bias_grad,),
    ]
    tail = max(1, 1 << (len(groups[0])))
    late_half = rounded(late_shards * half + 16, 16 * tail)
    spans = shard_spans(0, late_shards, 0)
    spare = late_half - late_shards * half
    spans[0].append((late_shards * shard_rows, D // 128, spare))
    spans[1].append((0, 0, spare))
    keep, give = packed_halves(late_rows, 0, spans, late_half)
    early_square = square_sum(early[0])
    parts = combine([keep, swapped(give, 1)], groups[0], ())
    (piece,) = combine(exchanged(parts, groups[0]), [], ())
    for group in groups[1:]:
        (piece,) = combine(exchanged([piece], group), [], (early_square, layer_output))
    piece = stack(exchanged([piece], groups[0]), groups[0], ())
    late = (piece, swapped(piece, 1))

    grad_norm = jnp.sqrt(early_square + square_sum(late[0]))[0, 0]
    steps, grad_shard, moment_one, moment_two = updated(
        (1.0 / jnp.maximum(grad_norm, 1.0)).reshape(1),
        early,
        late,
        late_shards,
        padded_weights,
        first_moment,
        second_moment,
        moments,
    )
    weight_step = steps.reshape(-1)
    return (
        layer_output,
        input_grad,
        grad_shard.reshape(-1),
        grad_norm,
        moment_one.reshape(-1),
        moment_two.reshape(-1),
        weight_step,
    )


def solution(mesh):
    return jax.shard_map(
        on_device,
        mesh=mesh,
        in_specs=(
            P(("outer", "inner"), None),
            P(),
            P(("outer", "inner"), None),
            P(),
            P("inner"),
            P("inner"),
        ),
        out_specs=(
            P(("outer", "inner"), None),
            P(("outer", "inner"), None),
            P("inner"),
            P(),
            P("inner"),
            P("inner"),
            P(),
        ),
        check_vma=False,
    )
```

```python
import functools
import math

import jax
import jax.numpy as jnp
from jax import lax
from jax.experimental import pallas as pl
from jax.experimental.pallas import tpu as pltpu
from jax.sharding import PartitionSpec as P

D = 512
HEADS = 8
FF = 2048
MOST = 1500


BETA_ONE = 0.9
BETA_TWO = 0.999
FIX_ONE = 1.0 - (0.9**10) ** 10
FIX_TWO = 1.0 - (0.999**10) ** 10
DECAY = 0.1
INV_ROOT_TWO = 1.0 / math.sqrt(2.0)
INV_ROOT_TWO_PI = 1.0 / math.sqrt(2.0 * math.pi)


def layouts():
    return [
        (D,),
        (D,),
        (D, D),
        (D,),
        (D, D),
        (D, D),
        (D,),
        (D, D),
        (D,),
        (D,),
        (D,),
        (D, FF),
        (FF,),
        (FF, D),
        (D,),
    ]


def plain_dot(matrix_one, matrix_two):
    return jnp.dot(matrix_one, matrix_two, preferred_element_type=jnp.float32)


def rows_dot(matrix_one, matrix_two):
    return lax.dot_general(
        matrix_one, matrix_two, (((0,), (0,)), ((), ())), preferred_element_type=jnp.float32
    )


def back_dot(matrix_one, matrix_two):
    return lax.dot_general(
        matrix_one, matrix_two, (((1,), (1,)), ((), ())), preferred_element_type=jnp.float32
    )


def standard(values):
    center = jnp.mean(values, axis=-1, keepdims=True)
    centered = values - center
    inverse_dev = lax.rsqrt(jnp.mean(centered * centered, axis=-1, keepdims=True) + 1e-05)
    return (centered * inverse_dev, inverse_dev)


def norm_back(grad_normed, normed_hat, inverse_dev, gain):
    scaled = grad_normed * gain
    return inverse_dev * (
        scaled
        - jnp.mean(scaled, axis=-1, keepdims=True)
        - normed_hat * jnp.mean(scaled * normed_hat, axis=-1, keepdims=True)
    )


def bounds(positions, clip_lengths):
    starts = jnp.cumsum(clip_lengths, dtype=jnp.int32) - clip_lengths
    member = (
        jnp.sum((positions[:, None] >= starts[None, :]).astype(jnp.int32), axis=1, dtype=jnp.int32)
        - 1
    )
    onehot = (
        jnp.arange(clip_lengths.shape[0], dtype=jnp.int32)[None, :] == member[:, None]
    ).astype(jnp.int32)
    lower_slot = jnp.sum(onehot * starts[None, :], axis=1, dtype=jnp.int32)
    upper_slot = lower_slot + jnp.sum(onehot * clip_lengths[None, :], axis=1, dtype=jnp.int32)
    return (lower_slot, upper_slot)


LINE = ("outer", "inner")
NEG = -1e30
BRIEF = pl.CostEstimate(flops=1000, bytes_accessed=1000, transcendentals=0)


def shifted(block, distance):
    n = lax.axis_size(LINE)
    return lax.ppermute(block, LINE, [(i + distance, i) for i in range(n) if 0 <= i + distance < n])


def swapped(block, bit):
    n = lax.axis_size(LINE)
    return lax.ppermute(block, LINE, [(i ^ bit, i) for i in range(n)])


def halo(block, before=()):
    n = lax.axis_size(LINE)
    left = shifted(block, -2)
    right = shifted(block, 2)
    partner = swapped(block, 1)
    route = [(i + (3 if i % 2 else -3), i) for i in range(n)]
    far = lax.ppermute(block, LINE, [(s, t) for s, t in route if 0 <= s < n])
    passed_left, passed_right, *_ = lax.optimization_barrier((left, right, *before))
    turned = [swapped(passed_left, 1), swapped(passed_right, 1)]
    return [block, partner, left, right, *turned, far]


def block_distances():
    odd = lax.axis_index(LINE) % 2
    even_far = jnp.array([0, 1, -2, 2, -1, 3, -3], jnp.int32)
    odd_far = jnp.array([0, -1, -2, 2, -3, 1, 3], jnp.int32)
    return jnp.where(odd == 1, odd_far, even_far)


def slot_table():
    odd = lax.axis_index(LINE) % 2
    even_slots = jnp.array([6, 2, 4, 0, 1, 3, 5], jnp.int32)
    odd_slots = jnp.array([4, 2, 1, 0, 5, 3, 6], jnp.int32)
    return jnp.where(odd == 1, odd_slots, even_slots)


def dot_nt(a, b):
    return lax.dot_general(a, b, (((1,), (1,)), ((), ())), preferred_element_type=jnp.float32)


def head_halves(pair):
    first = lax.broadcasted_iota(jnp.int32, pair.shape, 1) < pair.shape[1] // 2
    zero = jnp.zeros_like(pair)
    return jnp.where(first, pair, zero), jnp.where(first, zero, pair)


def over_lanes(tile, op):
    parts = [tile[:, 128 * j : 128 * (j + 1)] for j in range(tile.shape[1] // 128)]
    while len(parts) > 1:
        rest = parts[len(parts) // 2 * 2 :]
        parts = [op(parts[2 * j], parts[2 * j + 1]) for j in range(len(parts) // 2)] + rest
    return parts[0]


LSE_PARTS, DELTA_PARTS = 3, 2
DELTA_AT = LSE_PARTS * HEADS
CLIPS_AT = DELTA_AT + DELTA_PARTS * HEADS


def lane_of(shape):
    return lax.broadcasted_iota(jnp.int32, shape, 1)


def among(lane, begin, count):
    return (lane >= begin) & (lane < begin + count)


def beside(pair, marks):
    return jnp.concatenate([pair, marks.astype(pair.dtype)], axis=1)


def clip_marks(positions, clip_lengths):
    ends = jnp.cumsum(clip_lengths, dtype=jnp.int32)
    starts = ends - clip_lengths
    spare = 128 - CLIPS_AT - clip_lengths.shape[0]
    assert spare >= 0
    big = jnp.iinfo(jnp.int32).max
    lower = jnp.concatenate([jnp.full((CLIPS_AT,), -big, jnp.int32), starts, jnp.full((spare,), big, jnp.int32)])
    upper = jnp.concatenate([jnp.full((CLIPS_AT,), big, jnp.int32), ends, jnp.full((spare,), big, jnp.int32)])
    inside = (positions[:, None] >= lower[None]) & (positions[:, None] < upper[None])
    return inside.astype(jnp.bfloat16)


def penalty(marks):
    closed = (lane_of(marks.shape) >= CLIPS_AT) & (marks == 0)
    return jnp.where(closed, NEG, 0.0).astype(jnp.bfloat16)


def over_blocks(first_ref, last_ref, rows, work, start):
    half = rows // 2
    carried = (start, start)
    spans = (
        (first_ref[0], first_ref[1], 0, half),
        (first_ref[1], last_ref[0], 0, rows),
        (last_ref[0], last_ref[1], half, half),
    )
    for lower, upper, begin, count in spans:

        def step(block, carried):
            found = work(block, begin, count)
            upper_half, lower_half = carried
            if begin == 0:
                upper_half = tuple(join(old, new[:half]) for (join, new), old in zip(found, upper_half))
            if begin + count == rows:
                lower_half = tuple(join(old, new[count - half :]) for (join, new), old in zip(found, lower_half))
            return upper_half, lower_half

        carried = lax.fori_loop(lower, upper, step, carried)
    return [jnp.concatenate(halves, axis=0) for halves in zip(*carried)]


def forward_kernel(begin, first_ref, last_ref, slot_ref, q_ref, k_ref, v_ref, mark_ref, closed_ref, o_ref, lse_ref, s_ref):
    width = q_ref.shape[0]
    queries = [beside(half, closed_ref[...]) for half in head_halves(q_ref[...] * jnp.bfloat16(0.125))]

    def scores(block, begin, count):
        at = pl.ds(pl.multiple_of(slot_ref[block] * width, width), width)
        keys = beside(k_ref[at, :], mark_ref[at, :])
        found = []
        for h in range(2):
            score = dot_nt(queries[h][begin : begin + count], keys)
            s_ref[h, block, pl.ds(begin, count), :] = score
            found.append((jnp.maximum, over_lanes(score, jnp.maximum)))
        return found

    start = jnp.full((width // 2, 128), NEG, jnp.float32)
    peaks = over_blocks(first_ref, last_ref, width, scores, (start, start))
    peaks = [jnp.max(peak, axis=1, keepdims=True) for peak in peaks]

    def mix(block, begin, count):
        at = pl.ds(pl.multiple_of(slot_ref[block] * width, width), width)
        values = beside(v_ref[at, :], mark_ref[at, :])
        found = []
        for h in range(2):
            score = s_ref[h, block, pl.ds(begin, count), :]
            soft = jnp.exp(score - peaks[h][begin : begin + count]).astype(jnp.bfloat16)
            found.append((jnp.add, jnp.dot(soft, values, preferred_element_type=jnp.float32)))
        return found

    start = jnp.zeros((width // 2, 256), jnp.float32)
    sums = over_blocks(first_ref, last_ref, width, mix, (start, start))
    totals = [part[:, 128:129] for part in sums]
    even = lane_of((width, 128)) < 64
    o_ref[...] = jnp.where(even, sums[0][:, :128] / totals[0], sums[1][:, :128] / totals[1])
    lse_ref[...] = jnp.where(even, peaks[0] + jnp.log(totals[0]), peaks[1] + jnp.log(totals[1]))


def query_kernel(
    begin, first_ref, last_ref, slot_ref, q_ref, k_ref, v_ref, g_ref, own_ref, mark_ref, closed_ref, dq_ref
):
    width = q_ref.shape[0]
    pair = pl.program_id(0) + begin
    own, closed = own_ref[...], closed_ref[...]
    lane = lane_of(own.shape)
    zero = jnp.zeros_like(own)
    queries, grads = [], []
    halves = zip(head_halves(q_ref[...] * jnp.bfloat16(0.125)), head_halves(g_ref[...]))
    for h, (query, grad) in enumerate(halves):
        head = 2 * pair + h
        queries.append(beside(query, jnp.where(among(lane, LSE_PARTS * head, LSE_PARTS), own, closed)))
        grads.append(beside(grad, jnp.where(among(lane, DELTA_AT + DELTA_PARTS * head, DELTA_PARTS), own, zero)))

    def work(block, begin, count):
        at = pl.ds(pl.multiple_of(slot_ref[block] * width, width), width)
        keys = k_ref[at, :]
        values = beside(v_ref[at, :], mark_ref[at, :])
        marked = beside(keys, mark_ref[at, :])
        found = []
        for h in range(2):
            soft = jnp.exp(dot_nt(queries[h][begin : begin + count], marked))
            grad = (soft * dot_nt(grads[h][begin : begin + count], values)).astype(jnp.bfloat16)
            found.append((jnp.add, jnp.dot(grad, keys, preferred_element_type=jnp.float32)))
        return found

    start = jnp.zeros((width // 2, 128), jnp.float32)
    sums = over_blocks(first_ref, last_ref, width, work, (start, start))
    dq_ref[...] = (jnp.where(lane < 64, sums[0], sums[1]) * 0.125).astype(jnp.bfloat16)


def key_kernel(begin, first_ref, last_ref, slot_ref, k_ref, v_ref, q_ref, closed_ref, *refs):
    dk_ref, dv_ref, grad_ref, mark_ref = refs[-4:]
    width = k_ref.shape[0]
    pair = pl.program_id(0) + begin
    blocks = grad_ref.shape[0]
    for j in range(blocks):
        grad_ref[j] = refs[j][...]

    @pl.when(pl.program_id(0) == 0)
    def _():
        for j in range(blocks):
            mark_ref[j] = refs[blocks + j][...]

    closed = closed_ref[...]
    lane = lane_of(closed.shape)
    one, zero = jnp.ones_like(closed), jnp.zeros_like(closed)
    keys, values = [], []
    halves = zip(head_halves(k_ref[...] * jnp.bfloat16(0.125)), head_halves(v_ref[...]))
    for h, (key, value) in enumerate(halves):
        head = 2 * pair + h
        keys.append(beside(key, jnp.where(among(lane, LSE_PARTS * head, LSE_PARTS), one, closed)))
        values.append(beside(value, jnp.where(among(lane, DELTA_AT + DELTA_PARTS * head, DELTA_PARTS), one, zero)))

    def work(block, begin, count):
        slot = slot_ref[block]
        queries = q_ref[pl.ds(pl.multiple_of(slot * width, width), width), :]
        grads, marks = grad_ref[slot], mark_ref[slot]
        marked, graded = beside(queries, marks), beside(grads, marks)
        found = []
        for h in range(2):
            soft = jnp.exp(dot_nt(keys[h][begin : begin + count], marked))
            grad = (soft * dot_nt(values[h][begin : begin + count], graded)).astype(jnp.bfloat16)
            found.append((jnp.add, jnp.dot(grad, queries, preferred_element_type=jnp.float32)))
            found.append((jnp.add, jnp.dot(soft.astype(jnp.bfloat16), grads, preferred_element_type=jnp.float32)))
        return found

    start = jnp.zeros((width // 2, 128), jnp.float32)
    sums = over_blocks(first_ref, last_ref, width, work, (start,) * 4)
    dk_ref[...] = (jnp.where(lane < 64, sums[0], sums[2]) * 0.125).astype(jnp.bfloat16)
    dv_ref[...] = jnp.where(lane < 64, sums[1], sums[3]).astype(jnp.bfloat16)


def mixed_grad_kernel(branch_ref, weight_ref, mixed_ref, lse_ref, own_ref, sent_ref, mark_ref):
    step = pl.program_id(0)

    @pl.when(step == 0)
    def _():
        mark_ref[...] = own_ref[...].astype(jnp.float32)

    @pl.when(step < D // 128)
    def _():
        grad = dot_nt(branch_ref[...], weight_ref[...]).astype(jnp.bfloat16)
        sent_ref[...] = grad
        product = grad.astype(jnp.float32) * mixed_ref[...]
        lane = lane_of(product.shape)
        marks = mark_ref[...]
        for h, part in enumerate(head_halves(product)):
            head = 2 * step + h
            delta = -jnp.sum(part, axis=1, keepdims=True)
            lse = -lse_ref[:, 64 * h : 64 * h + 1]
            for value, begin, count in (
                (lse, LSE_PARTS * head, LSE_PARTS),
                (delta, DELTA_AT + DELTA_PARTS * head, DELTA_PARTS),
            ):
                for k in range(count):
                    rounded = value.astype(jnp.bfloat16).astype(jnp.float32)
                    marks = jnp.where(lane == begin + k, rounded, marks)
                    value = value - rounded
        mark_ref[...] = marks

    @pl.when(step == D // 128)
    def _():
        sent_ref[...] = mark_ref[...].astype(jnp.bfloat16)


def mixed_grad(branch, out_weight, mixed, lse, own_marks):
    width = branch.shape[0]
    last = D // 128 - 1
    column = pl.BlockSpec((width, 128), lambda h: (0, jnp.minimum(h, last)))
    return pl.pallas_call(
        mixed_grad_kernel,
        name="mixed_grad",
        grid=(D // 128 + 1,),
        in_specs=[
            pl.BlockSpec((width, D), lambda h: (0, 0)),
            pl.BlockSpec((128, D), lambda h: (jnp.minimum(h, last), 0)),
            column,
            column,
            pl.BlockSpec((width, 128), lambda h: (0, 0)),
        ],
        out_specs=pl.BlockSpec((width, 128), lambda h: (0, h)),
        out_shape=jax.ShapeDtypeStruct((width, D + 128), jnp.bfloat16),
        scratch_shapes=[pltpu.VMEM((width, 128), jnp.float32)],
        cost_estimate=BRIEF,
    )(branch, out_weight, mixed, lse, own_marks)


def project_kernel(count, *refs):
    query_ref, key_ref, value_ref, gain_ref, bias_ref, query_bias_ref, value_bias_ref, out_ref, row_ref = refs[count:]
    step = pl.program_id(0)
    for j in range(count):

        @pl.when(step == j)
        def _():
            row_ref[...] = refs[j][...]

    rows = 256
    for i in range(row_ref.shape[0] // rows):
        at = pl.ds(i * rows, rows)
        hat, _ = standard(row_ref[at, :].astype(jnp.float32))
        normed = (hat * gain_ref[...] + bias_ref[...]).astype(jnp.bfloat16)
        out_ref[at, 0:D] = (plain_dot(normed, query_ref[...]) + query_bias_ref[...]).astype(jnp.bfloat16)
        out_ref[at, D : 2 * D] = plain_dot(normed, key_ref[...]).astype(jnp.bfloat16)
        out_ref[at, 2 * D :] = (plain_dot(normed, value_ref[...]) + value_bias_ref[...]).astype(jnp.bfloat16)


def projected(blocks, weights, first, total, into=()):
    width = blocks[0].shape[0]
    count = len(blocks) + len(weights)
    whole = [pl.BlockSpec(array.shape, lambda i: (0, 0)) for array in (*blocks, *weights)]

    def body(*refs):
        project_kernel(len(blocks), *refs[:count], *refs[count + len(into) :])

    return pl.pallas_call(
        body,
        name="project",
        grid=(len(blocks),),
        in_specs=whole + [pl.BlockSpec(memory_space=ANY)] * len(into),
        out_specs=pl.BlockSpec((width, 3 * D), lambda i: (first + i, 0)),
        out_shape=jax.ShapeDtypeStruct((total * width, 3 * D), jnp.bfloat16),
        input_output_aliases={count: 0} if into else {},
        scratch_shapes=[pltpu.VMEM((width, D), jnp.bfloat16)],
        compiler_params=pltpu.CompilerParams(vmem_limit_bytes=63 * 2**20),
        cost_estimate=BRIEF,
    )(*blocks, *weights, *into)


def attend(kernel, ranges, operands, results, scratch, pairs=(0, D // 128), after=()):
    begin, count = pairs
    tok_rows = ranges[3]
    specs = []
    for array, (kind, at) in operands:
        if kind == "pair":
            rows = array.shape[0] if at < 0 else tok_rows
            at = (abs(at) - 1 if at < 0 else at) + begin
            specs.append(pl.BlockSpec((rows, 128), lambda h, *_, at=at: (0, at + h)))
        elif kind == "column":
            specs.append(pl.BlockSpec((tok_rows, 128), lambda h, *_, at=at: (0, at)))
        else:
            specs.append(pl.BlockSpec(array.shape, lambda h, *_, n=array.ndim: (0,) * n))
    return pl.pallas_call(
        functools.partial(kernel, begin),
        grid_spec=pltpu.PrefetchScalarGridSpec(
            num_scalar_prefetch=3,
            grid=(count,),
            in_specs=specs,
            out_specs=[pl.BlockSpec((tok_rows, 128), lambda h, *_: (0, h))] * len(results),
            scratch_shapes=scratch,
        ),
        out_shape=[jax.ShapeDtypeStruct((tok_rows, 128 * count), kept) for kept in results],
        compiler_params=pltpu.CompilerParams(vmem_limit_bytes=48 * 2**20),
        cost_estimate=BRIEF,
    )(*[behind(bound, after) for bound in ranges[:1]], *ranges[1:3], *[array for array, _ in operands])


VECTOR = pltpu.VMEM
ANY = pl.ANY


def behind(value, others):
    return lax.optimization_barrier((value, *others))[0]


def halves_rows(shard_rows):
    return -(-shard_rows // 128) * 64


def unpack_kernel(plan, shard_rows, flat_ref, *refs):
    wide_ref = refs[-1]
    padded_ref = refs[-2]
    total = flat_ref.shape[0]
    chunk = 432

    def widen(i, _):
        rows = pl.ds(pl.multiple_of(i * chunk, 16), chunk)
        wide_ref[rows, :] = flat_ref[rows, :].astype(jnp.float32)
        return 0

    lax.fori_loop(0, total // chunk, widen, 0)
    wide_ref[pl.ds(total, wide_ref.shape[0] - total), :] = jnp.zeros((wide_ref.shape[0] - total, 128), jnp.float32)
    for (offset, rows, columns, begin), ref in zip(plan, refs[:-2]):
        pieces = columns // 128
        if rows == 1:
            for j in range(pieces):
                ref[:, 128 * j : 128 * (j + 1)] = wide_ref[pl.ds(offset + j, 1), :]
            continue

        taken = 1024 // pieces

        def matrix(i, _):
            at = pl.multiple_of(i * taken, 64)
            for j in range(pieces):
                part = wide_ref[pl.ds(offset + j + at * pieces, taken, stride=pieces), :]
                ref[pl.ds(at, taken), begin + 128 * j : begin + 128 * (j + 1)] = part.astype(jnp.bfloat16)
            return 0

        lax.fori_loop(0, rows // taken, matrix, 0)
    shards = total // shard_rows
    half = halves_rows(shard_rows)
    for s in range(shards):
        for h in range(2):

            run = 448 if half % 448 == 0 else 64

            def pad(i, _):
                part = wide_ref[pl.ds(s * shard_rows + h * half + i * run, run), :]
                padded_ref[s * 2 + h, pl.ds(pl.multiple_of(i * run, 64), run), :] = part.astype(jnp.bfloat16)
                return 0

            lax.fori_loop(0, half // run, pad, 0)


def unpacked(weights, shard_rows):
    flat = weights.reshape(-1, 128)
    half = halves_rows(shard_rows)
    plan, outs = [], []
    offset = 0
    for layout in layouts():
        rows, columns = layout if len(layout) == 2 else (1, layout[0])
        plan.append([offset, rows, columns, 0])
        outs.append(jax.ShapeDtypeStruct((rows, columns), jnp.bfloat16 if rows > 1 else jnp.float32))
        offset = offset + rows * columns // 128
    shards = flat.shape[0] // shard_rows
    outs.append(jax.ShapeDtypeStruct((2 * shards, half, 128), jnp.bfloat16))
    return pl.pallas_call(
        functools.partial(unpack_kernel, plan, shard_rows),
        name="unpack",
        in_specs=[pl.BlockSpec(memory_space=VECTOR)],
        out_specs=[pl.BlockSpec(memory_space=VECTOR)] * len(outs),
        out_shape=outs,
        scratch_shapes=[VECTOR((flat.shape[0] + 2 * half, 128), jnp.float32)],
        compiler_params=pltpu.CompilerParams(vmem_limit_bytes=60 * 2**20),
        cost_estimate=BRIEF,
    )(flat)


def pack_kernel(plan, spans, place_ref, *refs):
    keep_ref, give_ref, flat_ref, out_ref, sems = refs[-5:]
    begin = min(entry[0] for entry in plan)
    if begin:
        flat_ref[pl.ds(0, begin), :] = jnp.zeros((begin, 128), jnp.float32)
    given = iter(refs)
    for offset, rows, columns, factors in plan:
        pieces = columns // 128
        ref = next(given)
        if rows == 1:
            for j in range(pieces):
                flat_ref[pl.ds(offset + j, 1), :] = ref[:, 128 * j : 128 * (j + 1)]
            continue

        others = [next(given) for _ in range(factors - 1)]
        other = others[0][...] if len(others) == 1 else jnp.concatenate([part[...] for part in others], axis=1)
        taken = 256

        def product(i, _):
            at = pl.multiple_of(i * taken, 128)
            found = rows_dot(ref[:, pl.ds(at, taken)], other)
            for j in range(pieces):
                part = found[:, 128 * j : 128 * (j + 1)]
                flat_ref[pl.ds(offset + j + at * pieces, taken, stride=pieces), :] = part
            return 0

        lax.fori_loop(0, rows // taken, product, 0)
    for h in range(2):
        at = h ^ place_ref[0]
        filled = 0
        for source, rows, room in spans[h]:
            run = 448 if rows >= 448 else 64
            whole = rows // run

            def move(i, _):
                to = pl.ds(pl.multiple_of(filled + i * run, 16), run)
                out_ref[at, to, :] = flat_ref[pl.ds(source + i * run, run), :].astype(jnp.bfloat16)
                return 0

            lax.fori_loop(0, whole, move, 0)
            rest = rows - run * whole
            tail = room - run * whole
            if tail:
                parts = []
                if rest:
                    parts.append(flat_ref[pl.ds(source + run * whole, rest), :])
                if tail > rest:
                    parts.append(jnp.zeros((tail - rest, 128), jnp.float32))
                last = parts[0] if len(parts) == 1 else jnp.concatenate(parts, axis=0)
                out_ref[at, pl.ds(filled + run * whole, tail), :] = last.astype(jnp.bfloat16)
            filled = filled + room
    copies = [
        pltpu.make_async_copy(out_ref.at[0], keep_ref, sems.at[0]),
        pltpu.make_async_copy(out_ref.at[1], give_ref, sems.at[1]),
    ]
    for copy in copies:
        copy.start()
    for copy in copies:
        copy.wait()


def packed_halves(grads, begin, spans, half):
    plan, arrays = [], []
    offset = begin
    for grad in grads:
        rows, columns = 1, grad[0].size
        if len(grad) > 1:
            rows, columns = grad[0].shape[1], sum(part.shape[1] for part in grad[1:])
        plan.append((offset, rows, columns, len(grad)))
        arrays += [array.reshape(-1, array.shape[-1]) for array in grad]
        offset = offset + rows * columns // 128
    return pl.pallas_call(
        functools.partial(pack_kernel, plan, spans),
        name="pack",
        in_specs=[pl.BlockSpec(memory_space=pltpu.SMEM)] + [pl.BlockSpec(memory_space=VECTOR)] * len(arrays),
        out_specs=[pl.BlockSpec(memory_space=ANY)] * 2,
        out_shape=[jax.ShapeDtypeStruct((half, 128), jnp.bfloat16)] * 2,
        scratch_shapes=[
            VECTOR((offset, 128), jnp.float32),
            VECTOR((2, half, 128), jnp.bfloat16),
            pltpu.SemaphoreType.DMA((2,)),
        ],
        compiler_params=pltpu.CompilerParams(vmem_limit_bytes=60 * 2**20),
        cost_estimate=BRIEF,
    )(bit_of(1).reshape(1), *arrays)


def combine_kernel(count, places_ref, *refs):
    parts, outs = refs[:count], refs[-places_ref.shape[0] :]
    rows = outs[0].shape[0]
    for k, out in enumerate(outs):
        at = pl.ds(pl.multiple_of(places_ref[k] * rows, 16), rows)
        terms = [part[at, :].astype(jnp.float32) for part in parts]
        while len(terms) > 1:
            terms = [terms[2 * j] + terms[2 * j + 1] for j in range(len(terms) // 2)]
        out[...] = terms[0].astype(jnp.bfloat16)


def places_of(group):
    if not group:
        return jnp.zeros((1,), jnp.int32)
    place = (lax.axis_index(LINE) // group[0]) % (1 << len(group))
    return place ^ jnp.arange(1 << len(group), dtype=jnp.int32)


def combine(parts, group, after):
    count = 1 << len(group)
    rows = parts[0].shape[0] // count
    outs = pl.pallas_call(
        functools.partial(combine_kernel, len(parts)),
        name="combine",
        in_specs=[pl.BlockSpec(memory_space=pltpu.SMEM)]
        + [pl.BlockSpec(memory_space=VECTOR)] * len(parts),
        out_specs=[pl.BlockSpec(memory_space=VECTOR)] * count,
        out_shape=[jax.ShapeDtypeStruct((rows, 128), jnp.bfloat16)] * count,
        cost_estimate=BRIEF,
    )(behind(places_of(group), after), *parts)
    return list(outs)


def stack_kernel(count, places_ref, *refs):
    out_ref = refs[-1]
    rows = refs[0].shape[0]
    for k in range(count):
        out_ref[pl.ds(pl.multiple_of(places_ref[k] * rows, 16), rows), :] = refs[k][...]


def stack(parts, group, after):
    rows = parts[0].shape[0] * len(parts)
    return pl.pallas_call(
        functools.partial(stack_kernel, len(parts)),
        name="stack",
        in_specs=[pl.BlockSpec(memory_space=pltpu.SMEM)]
        + [pl.BlockSpec(memory_space=VECTOR)] * len(parts),
        out_specs=pl.BlockSpec(memory_space=VECTOR),
        out_shape=jax.ShapeDtypeStruct((rows, 128), jnp.bfloat16),
        cost_estimate=BRIEF,
    )(behind(places_of(group), after), *parts)


def exchanged(parts, group):
    return [parts[0]] + [swapped(parts[k % len(parts)], group[0] * k) for k in range(1, 1 << len(group))]


def bit_groups():
    bits = [1 << k for k in range(1, lax.axis_size(LINE).bit_length() - 1)]
    return [bits[k : k + 2] for k in range(0, len(bits), 2)]


def square_sum_kernel(ref, out_ref):
    rows = ref.shape[0]
    chunk = rows // 8 if rows % 256 == 0 else 32

    def add(i, total):
        part = ref[pl.ds(pl.multiple_of(i * chunk, 16), chunk), :].astype(jnp.float32)
        return total + jnp.sum((part * part).reshape(-1, 32, 128), axis=0)

    total = lax.fori_loop(0, rows // chunk, add, jnp.zeros((32, 128), jnp.float32))
    out_ref[...] = jnp.broadcast_to(jnp.sum(total, keepdims=True), (8, 128))


def square_sum(half):
    own = pl.pallas_call(
        square_sum_kernel,
        name="square_sum",
        in_specs=[pl.BlockSpec(memory_space=VECTOR)],
        out_specs=pl.BlockSpec(memory_space=VECTOR),
        out_shape=jax.ShapeDtypeStruct((8, 128), jnp.float32),
        cost_estimate=BRIEF,
    )(half)
    return own + swapped(own, 1)


def finish_kernel(counts, x_ref, middle_ref, gain_ref, *refs):
    weights, parts, outs = refs[:3], refs[3:-5], refs[-5:]
    grad_ref, gain_out, bias_out, query_out, value_out = outs
    for out in outs[1:]:
        out[...] = jnp.zeros_like(out)
    rows = 256
    for i in range(x_ref.shape[0] // rows):
        at = pl.ds(i * rows, rows)
        hat, dev = standard(x_ref[at, :].astype(jnp.float32))
        grads, begin = [], 0
        for count in counts:
            grads.append(jnp.concatenate([part[at, :] for part in parts[begin : begin + count]], axis=1))
            begin = begin + count
        normed = sum(dot_nt(grad, weight[...]) for grad, weight in zip(grads, weights))
        for out, value in (
            (gain_out, normed * hat),
            (bias_out, normed),
            (query_out, grads[0].astype(jnp.float32)),
            (value_out, grads[2].astype(jnp.float32)),
        ):
            out[...] = out[...] + jnp.sum(value, axis=0, keepdims=True)
        grad_ref[at, :] = (middle_ref[at, :] + norm_back(normed, hat, dev, gain_ref[...])).astype(jnp.bfloat16)


def finished(inputs, grad_middle, gain, weights, parts):
    arrays = [inputs, grad_middle, gain, *weights, *(part for group in parts for part in group)]
    return pl.pallas_call(
        functools.partial(finish_kernel, [len(group) for group in parts]),
        name="finish",
        in_specs=[pl.BlockSpec(memory_space=VECTOR)] * len(arrays),
        out_specs=[pl.BlockSpec(memory_space=VECTOR)] * 5,
        out_shape=[jax.ShapeDtypeStruct(inputs.shape, jnp.bfloat16)] + [jax.ShapeDtypeStruct((1, D), jnp.float32)] * 4,
        compiler_params=pltpu.CompilerParams(vmem_limit_bytes=60 * 2**20),
        cost_estimate=BRIEF,
    )(*arrays)


def update_kernel(
    shards, late, shard_rows, meta_ref, scale_ref, early_own, early_other, late_own, late_other, extra_own, extra_other,
    weight_ref, one_ref, two_ref, *refs
):
    moments = refs[: 2 * shards]
    step_ref, grad_ref, new_one_ref, new_two_ref, sum_ref, wide_ref, stage_ref, sems = refs[2 * shards :]
    which, k = pl.program_id(0), pl.program_id(1)
    core, me = meta_ref[0], meta_ref[1]
    shard = me ^ k
    half = core ^ which
    rows = sum_ref.shape[0]
    chunk = rows // 7 if rows % 112 == 0 else 64
    scale = scale_ref[0]

    def by_chunks(body, first=0, last=rows // chunk):
        def move(i, _):
            body(pl.multiple_of(i * chunk, 16))
            return 0

        lax.fori_loop(first, last, move, 0)

    def load(ref):
        def body(at):
            sum_ref[pl.ds(at, chunk), :] = ref[pl.ds(at, chunk), :].astype(jnp.float32)

        by_chunks(body)

    for array, side, is_late in ((early_own, 0, 0), (early_other, 1, 0), (late_own, 0, 1), (late_other, 1, 1)):
        pl.when((which == side) & ((shard < late) == (is_late == 1)))(functools.partial(load, array))
    for array, side in ((extra_own, 0), (extra_other, 1)):

        @pl.when((which == side) & (shard == late) & (half == 0))
        def _():
            sum_ref[pl.ds(0, 8), :] = sum_ref[pl.ds(0, 8), :] + array[pl.ds(0, 8), :].astype(jnp.float32)

    slope_one = (1.0 - BETA_ONE) * scale
    slope_two = (1.0 - BETA_TWO) * scale * scale

    base = shard * shard_rows + half * rows
    limit = jnp.where(half == 1, shard_rows - rows, rows)
    for j in range(shards):

        @pl.when(k == j)
        def _():
            def body(start, masked=False):
                at = pl.ds(start, chunk)
                one, two = moments[2 * j][at, :], moments[2 * j + 1][at, :]
                grad = sum_ref[at, :]
                one = one.astype(jnp.float32) + (slope_one * (1.0 / FIX_ONE)) * grad
                two = two.astype(jnp.float32) + (slope_two * (1.0 / FIX_TWO)) * grad * grad
                root = two * lax.rsqrt(jnp.maximum(two, 1e-37))
                update = one / (root + 1e-08) + DECAY * weight_ref[0, at, :].astype(jnp.float32)
                to = pl.ds(base + start, chunk)
                if masked:
                    inside = start + lax.broadcasted_iota(jnp.int32, update.shape, 0) < limit
                    update = jnp.where(inside, update, wide_ref[to, :])
                wide_ref[to, :] = update

            whole = (shard_rows - rows) // chunk
            by_chunks(body, 0, whole)
            by_chunks(functools.partial(body, masked=True), whole, rows // chunk)

    @pl.when(k == 0)
    def _():
        def body(start):
            at = pl.ds(start, chunk)
            grad = sum_ref[at, :]
            grad_ref[at, :] = grad
            new_one_ref[at, :] = BETA_ONE * one_ref[at, :] + slope_one * grad
            new_two_ref[at, :] = BETA_TWO * two_ref[at, :] + slope_two * grad * grad

        by_chunks(body)

    @pl.when((which == 1) & (k == shards - 1))
    def _():
        piece = stage_ref.shape[1]
        total = step_ref.shape[0]

        def sending(i, slot):
            return pltpu.make_async_copy(
                stage_ref.at[slot], step_ref.at[pl.ds(pl.multiple_of(i * piece, 16), piece), :], sems.at[slot]
            )

        count = total // piece
        for i in range(count):
            if i >= 2:
                sending(i - 2, i % 2).wait()
            stage_ref[i % 2] = wide_ref[pl.ds(i * piece, piece), :].astype(jnp.bfloat16)
            sending(i, i % 2).start()
        for i in range(count - 2, count):
            sending(i, i % 2).wait()


def updated(norm, early, late, late_shards, weights, first_moment, second_moment, moments):
    shards = len(moments) // 2
    rows = weights.shape[1]
    shard_rows = first_moment.shape[0] // 128
    line = lax.axis_index(LINE)
    meta = jnp.stack([line % 2, lax.axis_index("inner")]).astype(jnp.int32)
    last = shards - 1

    def early_map(side):
        def index(w, k, meta):
            k = jnp.where(w == side, k, last if side == 0 else 0)
            return (jnp.clip((meta[1] ^ k) - late_shards, 0, shards - late_shards - 1), 0)

        return index

    def late_map(side):
        def index(w, k, meta):
            k = jnp.where(w == side, k, last if side == 0 else 0)
            return (jnp.clip(meta[1] ^ k, 0, late_shards - 1), 0)

        return index

    by_half = pl.BlockSpec((rows, 128), lambda w, k, meta: (meta[0] ^ w, 0))

    def in_turn(j):
        return pl.BlockSpec((rows, 128), lambda w, k, meta: (meta[0] ^ jnp.where(k >= j - 1, w, 0), 0))

    by_shard = pl.BlockSpec((1, rows, 128), lambda w, k, meta: (2 * (meta[1] ^ k) + (meta[0] ^ w), 0, 0))
    extra = pl.BlockSpec((16, 128), lambda w, k, meta: (late_shards * rows // 16, 0))
    return pl.pallas_call(
        functools.partial(update_kernel, shards, late_shards, shard_rows),
        name="update",
        grid_spec=pltpu.PrefetchScalarGridSpec(
            num_scalar_prefetch=1,
            grid=(2, shards),
            in_specs=[pl.BlockSpec(memory_space=pltpu.SMEM)]
            + [pl.BlockSpec((rows, 128), early_map(side)) for side in range(2)]
            + [pl.BlockSpec((rows, 128), late_map(side)) for side in range(2)]
            + [extra, extra, by_shard, by_half, by_half]
            + [in_turn(j // 2) for j in range(2 * shards)],
            out_specs=[pl.BlockSpec(memory_space=ANY), by_half, by_half, by_half],
            scratch_shapes=[
                VECTOR((rows, 128), jnp.float32),
                VECTOR((shards * shard_rows + 2 * rows, 128), jnp.float32),
                VECTOR((2, shards * shard_rows // 9, 128), jnp.bfloat16),
                pltpu.SemaphoreType.DMA((2,)),
            ],
        ),
        out_shape=[jax.ShapeDtypeStruct((shards * shard_rows, 128), jnp.bfloat16)]
        + [jax.ShapeDtypeStruct((shard_rows, 128), jnp.float32)] * 3,
        compiler_params=pltpu.CompilerParams(vmem_limit_bytes=60 * 2**20),
        cost_estimate=BRIEF,
    )(
        meta,
        norm,
        *early,
        *late,
        *late,
        weights,
        first_moment.reshape(-1, 128),
        second_moment.reshape(-1, 128),
        *moments,
    )


def narrow_kernel(shard_rows, one_ref, two_ref, first_out, second_out):
    shape = first_out.shape
    begin = pl.program_id(0) * shape[0]
    inside = begin + lax.broadcasted_iota(jnp.int32, shape, 0) < shard_rows
    one = jnp.where(inside, one_ref[...] * (BETA_ONE / FIX_ONE), 0.0).astype(jnp.bfloat16)
    two = jnp.where(inside, two_ref[...] * (BETA_TWO / FIX_TWO), 0.0).astype(jnp.bfloat16)
    first_out[...] = one
    second_out[...] = two


def narrowed(one, two, half):
    block = pl.BlockSpec((half // 2, 128), lambda i: (i, 0))
    return pl.pallas_call(
        functools.partial(narrow_kernel, one.shape[0]),
        name="narrow",
        grid=(4,),
        in_specs=[block, block],
        out_specs=[block, block],
        out_shape=[jax.ShapeDtypeStruct((2 * half, 128), jnp.bfloat16)] * 2,
        cost_estimate=BRIEF,
    )(one, two)


def bit_of(bit):
    return (lax.axis_index(LINE) // bit) % 2


def on_device(inputs, weights, cotangent, clip_lengths, first_moment, second_moment):
    tok_rows = inputs.shape[0]
    reach = (MOST + tok_rows - 2) // tok_rows
    shard_rows = first_moment.shape[0] // 128
    half = halves_rows(shard_rows)
    (
        first_gain,
        first_bias,
        query_weight,
        query_bias,
        key_weight,
        value_weight,
        value_bias,
        out_weight,
        out_bias,
        second_gain,
        second_bias,
        up_weight,
        up_bias,
        down_weight,
        down_bias,
        padded_weights,
    ) = unpacked(weights, shard_rows)
    base_slot = lax.axis_index(LINE) * tok_rows
    positions = base_slot + jnp.arange(tok_rows, dtype=jnp.int32)
    lower_slot, upper_slot = bounds(positions, clip_lengths)
    low = lower_slot - base_slot + reach * tok_rows
    high = upper_slot - base_slot + reach * tok_rows
    first_block = low.reshape(2, -1)[:, 0] // tok_rows
    last_block = (high.reshape(2, -1)[:, -1] + tok_rows - 1) // tok_rows
    ranges = (first_block, last_block, slot_table(), tok_rows)
    places = base_slot + block_distances()[:, None] * tok_rows + jnp.arange(tok_rows, dtype=jnp.int32)[None]
    marks = clip_marks(places.reshape(-1), clip_lengths)
    closed = penalty(clip_marks(positions, clip_lengths))

    inner = lax.axis_size("inner")
    first_half, second_half = narrowed(first_moment.reshape(-1, 128), second_moment.reshape(-1, 128), half)
    blocks = halo(inputs, (padded_weights,))
    weights_in = (query_weight, key_weight, value_weight, first_gain, first_bias, query_bias, value_bias)
    rows = projected(blocks[:4], weights_in, 0, len(blocks))
    first_sent, second_sent, *rest = lax.optimization_barrier((first_half, second_half, *blocks[4:]))
    rows = projected(rest, weights_in, 4, len(blocks), (rows,))
    first_got = swapped(first_sent, 2)
    second_got = swapped(second_sent, 2)
    input_rows = inputs.astype(jnp.float32)
    first_hat, _ = standard(input_rows)
    normed = (first_hat * first_gain + first_bias).astype(jnp.bfloat16)

    attended, lse = attend(
        forward_kernel,
        ranges,
        [
            (rows, ("pair", 0)),
            (rows, ("pair", -5)),
            (rows, ("pair", -9)),
            (marks, ("all", 0)),
            (closed, ("all", 0)),
        ],
        [jnp.float32, jnp.float32],
        [pltpu.VMEM((2, 2 * reach + 1, tok_rows, tok_rows), jnp.float32)],
    )
    held = {0: (first_half, second_half), 2: (first_got, second_got)}
    bit = 4
    while bit < inner:
        for place in list(held):
            held[place + bit] = tuple(swapped(piece, bit) for piece in held[place])
        bit = 2 * bit
    moments = []
    for place in range(inner):
        if place % 2 == 0:
            moments += held[place]
        else:
            moments += [swapped(piece, 1) for piece in held[place - 1]]
    mixed = attended.astype(jnp.bfloat16)
    middle = input_rows + plain_dot(mixed, out_weight) + out_bias
    second_hat, second_dev = standard(middle)
    hidden_in = (second_hat * second_gain + second_bias).astype(jnp.bfloat16)
    up_rows = plain_dot(hidden_in, up_weight) + up_bias
    cdf_part = 0.5 * (1.0 + lax.erf(up_rows * INV_ROOT_TWO))
    activated = (up_rows * cdf_part).astype(jnp.bfloat16)
    layer_output = (middle + plain_dot(activated, down_weight) + down_bias).astype(jnp.bfloat16)
    grad_out = cotangent.astype(jnp.float32)
    down_bias_grad = jnp.sum(grad_out, axis=0)
    grad_act = back_dot(cotangent, down_weight)
    pdf_part = jnp.exp(-0.5 * up_rows * up_rows) * INV_ROOT_TWO_PI
    grad_up = (grad_act * (cdf_part + up_rows * pdf_part)).astype(jnp.bfloat16)
    up_bias_grad = jnp.sum(grad_up.astype(jnp.float32), axis=0)
    grad_hidden = back_dot(grad_up, up_weight)
    second_gain_grad = jnp.sum(grad_hidden * second_hat, axis=0)
    second_bias_grad = jnp.sum(grad_hidden, axis=0)
    grad_middle = grad_out + norm_back(grad_hidden, second_hat, second_dev, second_gain)
    grad_branch = grad_middle.astype(jnp.bfloat16)
    out_bias_grad = jnp.sum(grad_branch.astype(jnp.float32), axis=0)
    sent = mixed_grad(grad_branch, out_weight, attended, lse, clip_marks(positions, clip_lengths))
    line = lax.axis_size(LINE)
    shards = inner
    late_shards = shards // 4
    groups = bit_groups()

    def rounded(count, unit):
        return -(-count // unit) * unit

    def shard_spans(first, last, base):
        spans = ([], [])
        for shard in range(first, last):
            begin = (shard - first) * shard_rows + base
            spans[0].append((begin, half, half))
            spans[1].append((begin + half, shard_rows - half, half))
        return spans

    def query_step(pairs, after):
        return attend(
            query_kernel,
            ranges,
            [
                (rows, ("pair", 0)),
                (rows, ("pair", -5)),
                (rows, ("pair", -9)),
                (sent, ("pair", 0)),
                (sent, ("column", 4)),
                (marks, ("all", 0)),
                (closed, ("all", 0)),
            ],
            [jnp.bfloat16],
            [],
            pairs,
            after,
        )

    def key_step(pairs, after):
        return attend(
            key_kernel,
            ranges,
            [
                (rows, ("pair", 4)),
                (rows, ("pair", 8)),
                (rows, ("pair", -1)),
                (closed, ("all", 0)),
            ]
            + [(block, ("pair", 0)) for block in grad_blocks]
            + [(block, ("column", 4)) for block in grad_blocks],
            [jnp.bfloat16, jnp.bfloat16],
            [pltpu.VMEM((len(grad_blocks), tok_rows, 128), jnp.bfloat16)] * 2,
            pairs,
            after,
        )

    activated, hidden_in, mixed = (behind(array, (sent,)) for array in (activated, hidden_in, mixed))

    early_rows = [
        (mixed, grad_branch),
        (out_bias_grad,),
        (second_gain_grad,),
        (second_bias_grad,),
        (hidden_in, grad_up),
        (up_bias_grad,),
        (activated, cotangent),
        (down_bias_grad,),
    ]
    early_half = rounded((shards - late_shards) * half, 8 * line)
    spans = shard_spans(late_shards, shards, 0)
    for span in spans:
        span.append((0, 0, early_half - (shards - late_shards) * half))
    early_keep, early_give = packed_halves(early_rows, D // 128, spans, early_half)
    early_got = swapped(early_give, 1)

    query_parts = query_step((0, 2), (early_give,))
    grad_blocks = halo(sent, query_parts)
    parts = combine([early_keep, early_got], groups[0], query_parts)
    got = exchanged(parts, groups[0])
    work = [(1, 1), (2, 1), (3, 1)]
    query_parts += query_step((2, 2), parts[:1])
    done = key_step((0, 1), query_parts[-1:])
    key_parts, value_parts = [done[0]], [done[1]]
    held_back = done[:1]
    for at, group in enumerate(groups):
        parts = combine(got, groups[at + 1] if at + 1 < len(groups) else [], held_back)
        if at + 1 < len(groups):
            got = exchanged(parts, groups[at + 1])
        if work:
            done = key_step(work.pop(0), parts[:1])
            key_parts.append(done[0])
            value_parts.append(done[1])
            held_back = done[:1]
    piece = parts[0]
    for at, group in enumerate(groups[::-1]):
        got = exchanged([piece], group)
        if work and at > 0:
            done = key_step(work.pop(0), [piece])
            key_parts.append(done[0])
            value_parts.append(done[1])
            held_back = done[:1]
        piece = stack(got, group, held_back)
    early_other = swapped(piece, 1)
    for pairs in work:
        done = key_step(pairs, [piece])
        key_parts.append(done[0])
        value_parts.append(done[1])
    early = (piece, early_other)
    input_grad, first_gain_grad, first_bias_grad, query_bias_grad, value_bias_grad = finished(
        inputs,
        grad_middle,
        first_gain,
        (query_weight, key_weight, value_weight),
        (query_parts, key_parts, value_parts),
    )
    late_rows = [
        (first_gain_grad,),
        (first_bias_grad,),
        (normed, *query_parts),
        (query_bias_grad,),
        (normed, *key_parts),
        (normed, *value_parts),
        (value_bias_grad,),
    ]
    tail = max(1, 1 << (len(groups[0])))
    late_half = rounded(late_shards * half + 16, 16 * tail)
    spans = shard_spans(0, late_shards, 0)
    spare = late_half - late_shards * half
    spans[0].append((late_shards * shard_rows, D // 128, spare))
    spans[1].append((0, 0, spare))
    keep, give = packed_halves(late_rows, 0, spans, late_half)
    early_square = square_sum(early[0])
    parts = combine([keep, swapped(give, 1)], groups[0], ())
    (piece,) = combine(exchanged(parts, groups[0]), [], ())
    for group in groups[1:]:
        (piece,) = combine(exchanged([piece], group), [], (early_square, layer_output))
    piece = stack(exchanged([piece], groups[0]), groups[0], ())
    late = (piece, swapped(piece, 1))

    grad_norm = jnp.sqrt(early_square + square_sum(late[0]))[0, 0]
    steps, grad_shard, moment_one, moment_two = updated(
        (1.0 / jnp.maximum(grad_norm, 1.0)).reshape(1),
        early,
        late,
        late_shards,
        padded_weights,
        first_moment,
        second_moment,
        moments,
    )
    weight_step = steps.reshape(-1)
    return (
        layer_output,
        input_grad,
        grad_shard.reshape(-1),
        grad_norm,
        moment_one.reshape(-1),
        moment_two.reshape(-1),
        weight_step,
    )


def solution(mesh):
    return jax.shard_map(
        on_device,
        mesh=mesh,
        in_specs=(
            P(("outer", "inner"), None),
            P(),
            P(("outer", "inner"), None),
            P(),
            P("inner"),
            P("inner"),
        ),
        out_specs=(
            P(("outer", "inner"), None),
            P(("outer", "inner"), None),
            P("inner"),
            P(),
            P("inner"),
            P("inner"),
            P(),
        ),
        check_vma=False,
    )
```
